32 devices in a mesh: dp: 16 (over z, x, core), mp: 2 (over y).
Axes of the slice: x: 2, y: 2, z: 4, core: 2. Of those that a mesh axis runs over, the one named last changes fastest.
Arguments:
- tokens: bfloat16 [16384, 768], P('dp', 'mp'), may hold values from -6 to 6
- norm_gain: bfloat16 [768], P('mp'), may hold values from 0.5 to 1.5
- proj_gate: bfloat16 [768, 1536], P(None, 'mp'), may hold values from -0.21875 to 0.21875
- proj_inner: bfloat16 [768, 1536], P(None, 'mp'), may hold values from -0.21875 to 0.21875
- proj_state: bfloat16 [768, 256], replicated, may hold values from -0.21875 to 0.21875
- proj_step: bfloat16 [768, 2, 24], P(None, None, 'mp'), may hold values from -0.21875 to 0.21875
- conv_inner: float32 [4, 1536], P(None, 'mp'), may hold values from -3 to 3
- conv_inner_bias: float32 [1536], P('mp'), may hold values from -3 to 3
- conv_state: float32 [4, 256], replicated, may hold values from -3 to 3
- conv_state_bias: float32 [256], replicated, may hold values from -3 to 3
- step_bias: float32 [2, 24], P(None, 'mp'), may hold values from -5 to -2
- decay_log: float32 [2, 24], P(None, 'mp'), may hold values from 0 to 2.5
- skip_gain: float32 [24], P('mp'), may hold values from 0.5 to 1.5
- gate_gain: float32 [1536], P('mp'), may hold values from 0.5 to 1.5
- proj_out: bfloat16 [1536, 768], P('mp'), may hold values from -0.15625 to 0.15625
- lengths: int32 [16], P('dp'), may hold values from 257 to 1024, as said below
- cotangent: bfloat16 [16384, 768], P('dp', 'mp'), may hold values from -6 to 6
Outputs:
- block_out: bfloat16 [16384, 768], P('dp', 'mp')
- grad_tokens: float32 [16384, 768], P('dp', 'mp')
- grad_norm_gain: float32 [768], P('mp')
- grad_proj_gate: float32 [768, 1536], P(None, 'mp')
- grad_proj_inner: float32 [768, 1536], P(None, 'mp')
- grad_proj_state: float32 [768, 256], replicated
- grad_proj_step: float32 [768, 2, 24], P(None, None, 'mp')
- grad_conv_inner: float32 [4, 1536], P(None, 'mp')
- grad_conv_inner_bias: float32 [1536], P('mp')
- grad_conv_state: float32 [4, 256], replicated
- grad_conv_state_bias: float32 [256], replicated
- grad_step_bias: float32 [2, 24], P(None, 'mp')
- grad_decay_log: float32 [2, 24], P(None, 'mp')
- grad_skip_gain: float32 [24], P('mp')
- grad_gate_gain: float32 [1536], P('mp')
- grad_proj_out: float32 [1536, 768], P('mp')
The draws below stay inside these ranges and needn't reach their ends.
Inputs may be any that keep to these rules, and one draw needn't show every extreme that they name: `lengths`: valid positions of each slot; the first slot is full, each other lies in the upper half of 1024 or of 512.
All inputs are finite; a program needn't handle non-finite values.
Results may differ from the reference program's by a relative error of at most 0.012.
Values may be sent and summed in bfloat16 or wider, within the bound.
No kernel may reach another device: no remote copies, remote signals or barrier semaphores. Data moves between devices by JAX's collectives and lax.ppermute only.
A program may use at most 192 MiB of HBM per device.

```python
import jax
import jax.numpy as jnp
from jax import lax

D = 768
E = 1536
H = 24
P_SIZE = 64
N = 64
K = 4
SEQ_LEN = 1024
SEQS = 16
TOKENS = 16384


def draw_lengths(key, part):
    bucket_key = jax.random.fold_in(key, 11)
    fill_key = jax.random.fold_in(key, 23)
    shift_by = jax.random.randint(bucket_key, (SEQS,), 0, 2)
    bucket = jnp.right_shift(jnp.full((SEQS,), SEQ_LEN, jnp.int32), shift_by.astype(jnp.int32))
    offset = jax.random.randint(fill_key, (SEQS,), 0, SEQ_LEN) % (bucket // 2)
    valid_len = bucket - offset
    return valid_len.at[0].set(SEQ_LEN).astype(jnp.int32)


def level_of(key, extent, cuts, least, top_value):
    def one(dim, shards_of):
        steps = jax.random.uniform(jax.random.fold_in(jax.random.fold_in(key, 6), dim), (shards_of,), jnp.float32, least / len(cuts), top_value / len(cuts))
        return jnp.repeat(jnp.exp(steps), extent[dim] // shards_of).reshape((-1,) + (1,) * (len(extent) - dim - 1))

    loudness = one(*cuts[0])
    for cut in cuts[1:]:
        loudness = loudness * one(*cut)
    return loudness


def normal_values(own_key, dims, spread, limit, split=(), kind=jnp.bfloat16):
    entries = jax.random.normal(own_key, dims, jnp.float32) * spread
    if len(split) > 0:
        entries = level_of(own_key, dims, split, -0.22, 0.18) * entries
    return jnp.clip(entries, min=-limit, max=limit).astype(kind)


def setup_inputs(seed: int = 0) -> dict:
    arg_keys = jax.random.split(jax.random.key(seed), 18)
    return {
        "tokens": normal_values(arg_keys[0], (TOKENS, D), 1.0, 6.0, ((0, 16), (1, 2))),
        "norm_gain": jnp.clip(1.0 + 0.1 * jax.random.normal(arg_keys[1], (D,), jnp.float32), 0.5, 1.5).astype(jnp.bfloat16),
        "proj_gate": normal_values(arg_keys[2], (D, E), D ** -0.5, 0.21875, ((1, 2),)),
        "proj_inner": normal_values(arg_keys[3], (D, E), D ** -0.5, 0.21875, ((1, 2),)),
        "proj_state": normal_values(arg_keys[4], (D, 4 * N), D ** -0.5, 0.21875),
        "proj_step": normal_values(arg_keys[5], (D, 2, H), D ** -0.5, 0.21875, ((2, 2),)),
        "conv_inner": normal_values(arg_keys[6], (K, E), 0.5, 3.0, ((1, 2),), jnp.float32),
        "conv_inner_bias": normal_values(arg_keys[7], (E,), 0.5, 3.0, ((0, 2),), jnp.float32),
        "conv_state": normal_values(arg_keys[8], (K, 4 * N), 0.5, 3.0, (), jnp.float32),
        "conv_state_bias": normal_values(arg_keys[9], (4 * N,), 0.5, 3.0, (), jnp.float32),
        "step_bias": jnp.clip(-5.0 + 3.0 * jax.random.uniform(arg_keys[10], (2, H), jnp.float32) ** level_of(arg_keys[10], (2, H), ((1, 2),), -0.2, 0.2), -5.0, -2.0),
        "decay_log": jnp.clip(2.5 * jax.random.uniform(arg_keys[11], (2, H), jnp.float32) ** level_of(arg_keys[11], (2, H), ((1, 2),), -0.2, 0.2), 0.0, 2.5),
        "skip_gain": jnp.clip(0.5 + 1.0 * jax.random.uniform(arg_keys[12], (H,), jnp.float32) ** level_of(arg_keys[12], (H,), ((0, 2),), -0.2, 0.2), 0.5, 1.5),
        "gate_gain": jnp.clip(1.0 + 0.1 * jax.random.normal(arg_keys[13], (E,), jnp.float32), 0.5, 1.5),
        "proj_out": normal_values(arg_keys[14], (E, D), E ** -0.5, 0.15625, ((0, 2),)),
        "lengths": draw_lengths(jax.random.fold_in(arg_keys[17], 71), 0),
        "cotangent": normal_values(arg_keys[16], (TOKENS, D), 1.0, 6.0, ((0, 16), (1, 2))),
    }


EPSILON = 1e-05

@jax.custom_vjp
def low(v):
    return lax.optimization_barrier(v.astype(jnp.bfloat16)).astype(jnp.float32)

@jax.custom_vjp
def low_back(v):
    return v

def low_keep(v):
    return (low(v), None)

def low_pass(kept, grad):
    return (grad,)

def back_keep(v):
    return (v, None)

def back_low(kept, grad):
    return (low(grad),)
low.defvjp(low_keep, low_pass)
low_back.defvjp(back_keep, back_low)

def causal_conv(values, kernel, offset):
    tap_count = kernel.shape[0]
    seq_len = values.shape[0]
    padded = jnp.pad(values, ((tap_count - 1, 0), (0, 0)))
    result = jnp.zeros_like(values) + offset[None, :]
    for tap_idx in range(tap_count):
        result = result + kernel[tap_idx][None, :] * padded[tap_idx:tap_idx + seq_len]
    return result

def block_forward(params, tokens_seq, mask_seq):
    norm_gain, proj_gate, proj_inner, proj_state, proj_step, conv_inner, conv_inner_bias, conv_state, conv_state_bias, step_bias, decay_log, skip_gain, gate_gain, proj_out = params
    highest = lax.Precision.HIGHEST
    seq_len = tokens_seq.shape[0]
    inverse_rms = lax.rsqrt(lax.optimization_barrier(jnp.mean(tokens_seq * tokens_seq, axis=-1, keepdims=True)) + EPSILON)
    normed = low(tokens_seq * inverse_rms * norm_gain)
    gate_pre = low_back(jnp.dot(normed, proj_gate, precision=highest))
    inner_pre = low_back(jnp.dot(normed, proj_inner, precision=highest))
    step_pre = low_back(jnp.dot(normed, proj_step.reshape(D, 2 * H), precision=highest)).reshape(seq_len, 2, H)
    state_pre = low_back(jnp.dot(normed, proj_state, precision=highest))
    inner_act = jax.nn.silu(causal_conv(inner_pre, conv_inner, conv_inner_bias))
    state_act = low(jax.nn.silu(causal_conv(state_pre, conv_state, conv_state_bias)))
    step_size = jax.nn.softplus(step_pre + step_bias)
    decay_rate = -jnp.exp(decay_log) * step_size
    cumulative = jnp.cumsum(decay_rate, axis=0)
    exclusive = cumulative - decay_rate
    position = jnp.arange(seq_len)
    is_lower = (position[None, :] < position[:, None])[None]
    is_upper = (position[None, :] > position[:, None])[None]
    fwd_in = state_act[:, 0:N]
    fwd_out = state_act[:, N:2 * N]
    back_in = state_act[:, 2 * N:3 * N]
    back_out = state_act[:, 3 * N:4 * N]
    inner_heads = inner_act.reshape(seq_len, H, P_SIZE)
    xd_fwd = low(inner_heads * (step_size[:, 0, :] * mask_seq[:, None])[:, :, None])
    xd_back = low(inner_heads * (step_size[:, 1, :] * mask_seq[:, None])[:, :, None])
    scores_fwd = jnp.dot(fwd_out, fwd_in.T, precision=highest)
    scores_back = jnp.dot(back_out, back_in.T, precision=highest)
    cum_fwd = cumulative[:, 0, :].T
    excl_back = exclusive[:, 1, :].T
    decay_fwd = jnp.where(is_lower, jnp.exp(jnp.where(is_lower, cum_fwd[:, :, None] - cum_fwd[:, None, :], 0.0)), 0.0)
    decay_back = jnp.where(is_upper, jnp.exp(jnp.where(is_upper, excl_back[:, None, :] - excl_back[:, :, None], 0.0)), 0.0)
    weights_fwd = low(scores_fwd[None] * decay_fwd)
    weights_back = low(scores_back[None] * decay_back)
    ssd_out = low_back(jnp.einsum('hts,shp->thp', weights_fwd, xd_fwd, precision=highest) + jnp.einsum('hts,shp->thp', weights_back, xd_back, precision=highest))
    y_heads = ssd_out + skip_gain[None, :, None] * inner_heads
    gated = y_heads.reshape(seq_len, E) * jax.nn.silu(gate_pre)
    gate_inv = lax.rsqrt(lax.optimization_barrier(jnp.mean(gated * gated, axis=-1, keepdims=True)) + EPSILON)
    gate_normed = low(gated * gate_inv * gate_gain)
    branch = jnp.dot(gate_normed, proj_out, precision=highest)
    return tokens_seq + mask_seq[:, None] * branch

def reference(tokens, norm_gain, proj_gate, proj_inner, proj_state, proj_step, conv_inner, conv_inner_bias, conv_state, conv_state_bias, step_bias, decay_log, skip_gain, gate_gain, proj_out, lengths, cotangent):
    params = tuple((item.astype(jnp.float32) for item in (norm_gain, proj_gate, proj_inner, proj_state, proj_step, conv_inner, conv_inner_bias, conv_state, conv_state_bias, step_bias, decay_log, skip_gain, gate_gain, proj_out)))
    position = jnp.arange(SEQ_LEN)
    seq_masks = (position[None, :] < lengths[:, None]).astype(jnp.float32)
    token_seqs = tokens.astype(jnp.float32).reshape(SEQS, SEQ_LEN, D)
    cotangent_seqs = cotangent.astype(jnp.float32).reshape(SEQS, SEQ_LEN, D)

    def one_sequence(sums_so_far, seq_items):
        tokens_seq, cotangent_seq, mask_seq = seq_items
        forward_fn = lambda weight_set, inputs_seq: block_forward(weight_set, inputs_seq, mask_seq)
        out_seq, pull_back = jax.vjp(forward_fn, params, tokens_seq)
        grad_params, grad_seq = pull_back(cotangent_seq)
        sums_so_far = jax.tree.map(lambda first, second: first + second, sums_so_far, grad_params)
        return (sums_so_far, (out_seq.astype(jnp.bfloat16), grad_seq))
    zero_sums = jax.tree.map(jnp.zeros_like, params)
    totals, (out_seqs, grad_seqs) = lax.scan(one_sequence, zero_sums, (token_seqs, cotangent_seqs, seq_masks))
    return (out_seqs.reshape(TOKENS, D), grad_seqs.reshape(TOKENS, D), totals[0], totals[1], totals[2], totals[3], totals[4], totals[5], totals[6], totals[7], totals[8], totals[9], totals[10], totals[11], totals[12], totals[13])
```

```python
from functools import partial

import jax
import jax.numpy as jnp
from jax import lax
from jax.experimental import pallas as pl
from jax.experimental.pallas import tpu as pltpu
from jax.sharding import PartitionSpec as P

EPSILON = 1e-05
CHUNK = 128
BLOCK = 256
LANES = 128
F32 = jnp.float32
BF16 = jnp.bfloat16
HIGHEST = lax.Precision.HIGHEST
VMEM_LIMIT = 56 * 1024 * 1024


def mm(a, b):
    return jnp.dot(a, b, preferred_element_type=F32)


def mm_nt(a, b):
    return lax.dot_general(a, b, (((1,), (1,)), ((), ())), preferred_element_type=F32)


def mm_tn(a, b):
    return lax.dot_general(a, b, (((0,), (0,)), ((), ())), preferred_element_type=F32)


def split_two(v):
    hi = v.astype(BF16)
    return hi, (v - hi.astype(F32)).astype(BF16)


def expand(v, spread):
    hi, lo = split_two(v)
    return mm(jnp.concatenate([hi, lo], axis=1), spread)


def row_mask(block, rows, length):
    pos = block * rows + lax.broadcasted_iota(jnp.int32, (rows, 1), 0)
    return (pos < length).astype(F32)


def to_row(col_a, col_b):
    rows = col_a.shape[0]
    lane = lax.broadcasted_iota(jnp.int32, (rows, LANES), 1)
    tile = jnp.where(lane == 0, col_a, jnp.where(lane == 1, col_b, 0.0))
    return jnp.transpose(tile)[0:8, :]


def sigmoid(v):
    return 1.0 / (1.0 + jnp.exp(-v))


def project_kernel(
    length, own, oth, gain, weights, conv, head_par, spread,
    normed_ref, gate_ref, pre_ref, slope_ref, hs_ref, act_ref, sact_ref, xd_ref, hf_ref, sb_ref,
    ext, carry, *, heads, width, state_width,
):
    i = pl.program_id(0)

    @pl.when(i == 0)
    def _():
        ext[0:8, :] = jnp.zeros((8, ext.shape[1]), F32)
        carry[...] = jnp.zeros_like(carry)

    x = jnp.concatenate([own[...], oth[...]], axis=1).astype(F32)
    inv = lax.rsqrt(jnp.mean(x * x, axis=-1, keepdims=True) + EPSILON)
    normed = (x * inv * gain[...]).astype(BF16)
    normed_ref[...] = normed
    conv_width = width + state_width
    gate_ref[...] = mm(normed, weights[:, 0:width])
    pre = mm(normed, weights[:, width : width + conv_width])
    step_pre = mm(normed, weights[:, width + conv_width :])
    pre_ref[...] = pre.astype(BF16)
    ext[8 : 8 + BLOCK, :] = pre
    c = conv[4:5, :] + conv[3:4, :] * pre
    for j in range(3):
        c = c + conv[j : j + 1, :] * ext[5 + j : 5 + j + BLOCK, :]
    sg = sigmoid(c)
    both = c * sg
    slope_ref[...] = (sg * (1.0 + c * (1.0 - sg))).astype(BF16)
    ext[0:8, :] = ext[BLOCK : BLOCK + 8, :]
    act = both[:, :width]
    act_ref[...] = act
    sact = both[:, width:].astype(BF16)
    sact_ref[...] = sact

    z = step_pre + head_par[0:1, :]
    dt = jnp.maximum(z, 0.0) + jnp.log1p(jnp.exp(-jnp.abs(z)))
    rate = head_par[1:2, :] * dt
    dtm = dt * row_mask(i, BLOCK, length[0])
    wide = expand(dtm, spread[...])
    xd_ref[:, 0:width] = (act * wide[:, :width]).astype(BF16)
    xd_ref[:, width:] = (act * wide[:, width:]).astype(BF16)
    hs_ref[:, 0:LANES] = z
    hs_ref[:, LANES : 2 * LANES] = dt
    n = state_width // 4
    tri_r = lax.broadcasted_iota(jnp.int32, (CHUNK, CHUNK), 0)
    tri_c = lax.broadcasted_iota(jnp.int32, (CHUNK, CHUNK), 1)
    tri = (tri_c <= tri_r).astype(F32)
    is_fwd = lax.broadcasted_iota(jnp.int32, (CHUNK, LANES), 1) < heads
    for c_idx in range(BLOCK // CHUNK):
        rows = slice(c_idx * CHUNK, (c_idx + 1) * CHUNK)
        rate_c = rate[rows]
        cum = jnp.dot(tri, rate_c, precision=HIGHEST, preferred_element_type=F32)
        tot = cum[CHUNK - 1 : CHUNK, :]
        cumx = jnp.where(is_fwd, cum, cum - rate_c)
        hs_ref[rows, 2 * LANES : 3 * LANES] = cumx
        hs_ref[rows, 3 * LANES :] = jnp.broadcast_to(tot, (CHUNK, LANES))
        to_edge = jnp.exp(jnp.where(is_fwd, tot - cumx, cumx))
        coef = expand(dtm[rows] * to_edge, spread[...])
        act_c = act[rows]
        sact_c = sact[rows]
        hf_ref[c_idx] = carry[...].astype(BF16)
        keep = expand(jnp.broadcast_to(jnp.exp(tot), (8, LANES)), spread[:, 0:width])[0:1]
        carry[...] = carry[...] * keep + mm_tn(
            sact_c[:, 0:n], (act_c * coef[:, :width]).astype(BF16)
        )
        sb_ref[c_idx] = mm_tn(
            sact_c[:, 2 * n : 3 * n], (act_c * coef[:, width:]).astype(BF16)
        )


def pair_tiles(pair):
    lane = lax.broadcasted_iota(jnp.int32, pair.shape, 1)
    half = pair.shape[1] // 2
    zero = jnp.zeros_like(pair)
    return jnp.concatenate(
        [jnp.where(lane < half, pair, zero), jnp.where(lane < half, zero, pair)], axis=0
    )


def forward_kernel(
    length, act, sact, hs, xd, hf, sb, gate, cown, coth, po, gg, skip, spread,
    y_ref, ssdf_ref, dgn_ref, gz_ref, sums_ref, hb_ref, carry, *, heads, width, state_width, blocks,
):
    i = pl.program_id(0)
    blk = blocks - 1 - i

    @pl.when(i == 0)
    def _():
        carry[...] = jnp.zeros_like(carry)

    n = state_width // 4
    r = lax.broadcasted_iota(jnp.int32, (CHUNK, CHUNK), 0)
    c = lax.broadcasted_iota(jnp.int32, (CHUNK, CHUNK), 1)
    lower = c < r
    upper = c > r
    is_fwd = lax.broadcasted_iota(jnp.int32, (CHUNK, LANES), 1) < heads
    for c_idx in reversed(range(BLOCK // CHUNK)):
        rows = slice(c_idx * CHUNK, (c_idx + 1) * CHUNK)
        cumx = hs[rows, 2 * LANES : 3 * LANES]
        tot = hs[rows, 3 * LANES :]
        cum_t = jnp.transpose(cumx)
        from_edge = expand(jnp.exp(jnp.where(is_fwd, cumx, tot - cumx)), spread[...])
        sact_c = sact[rows, :]
        b_f, c_f = sact_c[:, 0:n], sact_c[:, n : 2 * n]
        b_b, c_b = sact_c[:, 2 * n : 3 * n], sact_c[:, 3 * n :]
        s_f = jnp.where(lower, mm_nt(c_f, b_f), 0.0)
        s_b = jnp.where(upper, mm_nt(c_b, b_b), 0.0)
        hb = carry[...].astype(BF16)
        hb_ref[c_idx] = hb
        in_f = mm(c_f, hf[c_idx])
        in_b = mm(c_b, hb)
        keep = expand(jnp.exp(tot[0:8]), spread[:, width:])[0:1]
        carry[...] = carry[...] * keep + sb[c_idx]
        for p in range(heads // 2):
            lanes = slice(p * LANES, (p + 1) * LANES)
            lanes_b = slice(width + p * LANES, width + (p + 1) * LANES)
            w_f, w_b = [], []
            for h in (2 * p, 2 * p + 1):
                arg = jnp.where(
                    lower,
                    cumx[:, h : h + 1] - cum_t[h : h + 1, :],
                    cum_t[heads + h : heads + h + 1, :] - cumx[:, heads + h : heads + h + 1],
                )
                damp = jnp.exp(arg)
                w_f.append((s_f * damp).astype(BF16))
                w_b.append((s_b * damp).astype(BF16))
            out_f = mm(jnp.concatenate(w_f, axis=1), pair_tiles(xd[rows, lanes]))
            out_b = mm(jnp.concatenate(w_b, axis=1), pair_tiles(xd[rows, lanes_b]))
            out_f = out_f + from_edge[:, lanes] * in_f[:, lanes]
            out_b = out_b + from_edge[:, lanes_b] * in_b[:, lanes]
            ssdf_ref[rows, lanes] = out_f
            y_ref[rows, lanes] = out_f + out_b + skip[:, lanes] * act[rows, lanes]
    gp = gate[...]
    gated = y_ref[...] * (gp * sigmoid(gp))
    mask = row_mask(blk, BLOCK, length[0])
    cot = jnp.concatenate([cown[...], coth[...]], axis=1)
    d_branch = (cot.astype(F32) * mask).astype(BF16)
    dgn = mm_nt(d_branch, po[...])
    dgn_ref[...] = dgn
    scaled = gated * gg[...]
    gz_ref[...] = scaled.astype(BF16)
    sums_ref[...] = to_row(
        jnp.sum(gated * gated, axis=1, keepdims=True), jnp.sum(dgn * scaled, axis=1, keepdims=True)
    )


def gate_back_kernel(
    length, sums, gate, y, ssdf, act, dgn, cown, coth, hs, sact, hf, hb, gg, skip, spread, gather,
    g_ref, dgp_ref, dbr_ref, dc_ref, gb_ref, gf_ref, rd_ref, rows_ref, small_ref, carry,
    *, heads, width, state_width, inner_width,
):
    i = pl.program_id(0)

    @pl.when(i == 0)
    def _():
        carry[...] = jnp.zeros_like(carry)
        small_ref[...] = jnp.zeros_like(small_ref)

    cols = jnp.transpose(sums[...])
    gate_inv = lax.rsqrt(cols[:, 0:1] / inner_width + EPSILON)
    gate_dot = cols[:, 1:2] / inner_width
    gp = gate[...]
    sg = sigmoid(gp)
    act_gate = gp * sg
    yv = y[...]
    gated = yv * act_gate
    dg = dgn[...]
    small_ref[0:1, :] += jnp.sum(dg * gated * gate_inv, axis=0, keepdims=True)
    d_gated = gate_inv * (dg * gg[...]) - gated * (gate_inv * gate_inv * gate_inv * gate_dot)
    d_gp = d_gated * yv * (sg * (1.0 + gp * (1.0 - sg)))
    dgp_ref[...] = d_gp.astype(BF16)
    rd = jnp.sum(d_gp * gp, axis=1, keepdims=True)
    rd_ref[...] = to_row(rd, jnp.zeros_like(rd))
    d_y = d_gated * act_gate
    g_low = d_y.astype(BF16)
    g_ref[...] = g_low
    small_ref[1:2, :] += jnp.sum(d_y * act[...], axis=0, keepdims=True)
    mask = row_mask(i, BLOCK, length[0])
    cot = jnp.concatenate([cown[...], coth[...]], axis=1)
    dbr_ref[...] = (cot.astype(F32) * (mask * gate_inv)).astype(BF16)
    n = state_width // 4
    is_fwd = lax.broadcasted_iota(jnp.int32, (CHUNK, LANES), 1) < heads
    for c_idx in range(BLOCK // CHUNK):
        rows = slice(c_idx * CHUNK, (c_idx + 1) * CHUNK)
        cumx = hs[rows, 2 * LANES : 3 * LANES]
        tot = hs[rows, 3 * LANES :]
        from_edge = expand(jnp.exp(jnp.where(is_fwd, cumx, tot - cumx)), spread[...])
        dy_c = d_y[rows]
        dyf = (dy_c * from_edge[:, :width]).astype(BF16)
        dyb = (dy_c * from_edge[:, width:]).astype(BF16)
        dc_ref[rows, 0:n] = mm_nt(dyf, hf[c_idx])
        dc_ref[rows, n : 2 * n] = mm_nt(dyb, hb[c_idx])
        gv = g_low[rows].astype(F32)
        sf = ssdf[rows]
        back_inter = from_edge[:, width:] * mm(sact[rows, 3 * n :], hb[c_idx])
        back_intra = yv[rows] - sf - skip[...] * act[rows] - back_inter
        hi, lo = split_two(jnp.concatenate([gv * sf, -(gv * back_intra)], axis=1))
        rows_ref[rows, 0:LANES] = mm(hi, gather[...]) + mm(lo, gather[...])
        rows_ref[rows, LANES:] = mm((gv * back_inter).astype(BF16), gather[width:, :])
        gb_ref[c_idx] = carry[...].astype(BF16)
        keep = expand(jnp.exp(tot[0:8]), spread[:, width:])[0:1]
        carry[...] = carry[...] * keep + mm_tn(sact[rows, 3 * n :], dyb)
        gf_ref[c_idx] = mm_tn(sact[rows, n : 2 * n], dyf)


def back_kernel(
    length, g, act, sact, hs, xd, sums, hf, hb, gb, gf, dc, pre, slope, conv, head_par, skip, spread, gather,
    rest_ref, rd_ref, gconv_ref, ghead_ref, ext, carry,
    *, heads, width, state_width, blocks,
):
    i = pl.program_id(0)
    blk = blocks - 1 - i
    per = BLOCK // CHUNK

    @pl.when(i == 0)
    def _():
        ext[BLOCK:, :] = jnp.zeros((8, ext.shape[1]), F32)
        carry[...] = jnp.zeros_like(carry)
        gconv_ref[...] = jnp.zeros_like(gconv_ref)
        ghead_ref[...] = jnp.zeros_like(ghead_ref)

    n = state_width // 4
    conv_width = width + state_width
    r = lax.broadcasted_iota(jnp.int32, (CHUNK, CHUNK), 0)
    c = lax.broadcasted_iota(jnp.int32, (CHUNK, CHUNK), 1)
    later = c > r
    earlier = c < r
    rev = (c >= r).astype(F32)
    tri = (c <= r).astype(F32)
    is_fwd = lax.broadcasted_iota(jnp.int32, (CHUNK, LANES), 1) < heads
    mask = row_mask(blk, BLOCK, length[0])
    for c_idx in reversed(range(per)):
        rows = slice(c_idx * CHUNK, (c_idx + 1) * CHUNK)
        z = hs[rows, 0:LANES]
        dt = hs[rows, LANES : 2 * LANES]
        cumx = hs[rows, 2 * LANES : 3 * LANES]
        tot = hs[rows, 3 * LANES :]
        cum_t = jnp.transpose(cumx)
        mask_c = mask[rows]
        to_edge = expand(jnp.exp(jnp.where(is_fwd, tot - cumx, cumx)), spread[...])
        dtm = expand(dt * mask_c, spread[...])
        sact_c = sact[rows, :]
        b_f, c_f = sact_c[:, 0:n], sact_c[:, n : 2 * n]
        b_b, c_b = sact_c[:, 2 * n : 3 * n], sact_c[:, 3 * n :]
        s_f = jnp.where(later, mm_nt(b_f, c_f), 0.0)
        s_b = jnp.where(earlier, mm_nt(b_b, c_b), 0.0)
        grad_f = carry[...]
        grad_f_low = grad_f.astype(BF16)
        grad_b_low = gb[c_idx]
        keep = expand(jnp.exp(tot[0:8]), spread[...])[0:1]
        keep_f = keep[:, :width]
        edge_f = keep_f * jnp.sum(grad_f * hf[c_idx].astype(F32), axis=0, keepdims=True)
        edge_b = keep[:, width:] * jnp.sum(
            hb[c_idx].astype(F32) * grad_b_low.astype(F32), axis=0, keepdims=True
        )
        carry[...] = grad_f * keep_f + gf[c_idx]
        in_f = mm(b_f, grad_f_low)
        in_b = mm(b_b, grad_b_low)
        d_scores = jnp.zeros((CHUNK, CHUNK), F32)
        direct, cum_hi, cum_lo, xs_f, xs_b = [], [], [], [], []
        direct_b, cum_hi_b, cum_lo_b, ahead = [], [], [], []
        for p in range(heads // 2):
            lanes = slice(p * LANES, (p + 1) * LANES)
            lanes_b = slice(width + p * LANES, width + (p + 1) * LANES)
            g_pair = g[rows, lanes]
            xf_pair = xd[rows, lanes]
            xb_pair = xd[rows, lanes_b]
            dw_f = mm_nt(pair_tiles(xf_pair), g_pair)
            dw_b = mm_nt(pair_tiles(xb_pair), g_pair)
            w_f, w_b = [], []
            for q, h in enumerate((2 * p, 2 * p + 1)):
                arg = jnp.where(
                    later,
                    cum_t[h : h + 1, :] - cumx[:, h : h + 1],
                    cumx[:, heads + h : heads + h + 1] - cum_t[heads + h : heads + h + 1, :],
                )
                damp = jnp.exp(arg)
                w_f.append((s_f * damp).astype(BF16))
                w_b.append((s_b * damp).astype(BF16))
                part = slice(q * CHUNK, (q + 1) * CHUNK)
                d_scores = d_scores + jnp.where(later, dw_f[part], dw_b[part]) * damp
            g_tiles = pair_tiles(g_pair)
            edge_pf = to_edge[:, lanes]
            edge_pb = to_edge[:, lanes_b]
            intra_f = mm(jnp.concatenate(w_f, axis=1), g_tiles)
            inter_f = edge_pf * in_f[:, lanes]
            dx_f = intra_f + inter_f
            dx_b = mm(jnp.concatenate(w_b, axis=1), g_tiles) + edge_pb * in_b[:, lanes]
            xf = xf_pair.astype(F32)
            xb = xb_pair.astype(F32)
            xs_f.append((xf * edge_pf).astype(BF16))
            xs_b.append((xb * edge_pb).astype(BF16))
            act_p = act[rows, lanes]
            gv = g_pair.astype(F32)
            sk = skip[:, lanes]
            ahead.append((xf * inter_f).astype(BF16))
            hi, lo = split_two(-(xf * intra_f))
            cum_hi.append(hi)
            cum_lo.append(lo)
            hi, lo = split_two(xb * dx_b)
            cum_hi_b.append(hi)
            cum_lo_b.append(lo)
            direct.append((act_p * dx_f).astype(BF16))
            direct_b.append((act_p * dx_b).astype(BF16))
            d_inner = sk * gv + dtm[:, lanes] * dx_f + dtm[:, lanes_b] * dx_b
            ext[rows, lanes] = d_inner * slope[rows, lanes].astype(F32)
        low_f = jnp.where(later, d_scores, 0.0).astype(BF16)
        low_b = jnp.where(earlier, d_scores, 0.0).astype(BF16)
        d_bf = mm(low_f, c_f) + mm_nt(jnp.concatenate(xs_f, axis=1), grad_f_low)
        d_cf = mm_tn(low_f, b_f) + dc[rows, 0:n]
        d_bb = mm(low_b, c_b) + mm_nt(jnp.concatenate(xs_b, axis=1), grad_b_low)
        d_cb = mm_tn(low_b, b_b) + dc[rows, n : 2 * n]
        d_state = jnp.concatenate([d_bf, d_cf, d_bb, d_cb], axis=1)
        ext[rows, width:] = d_state * slope[rows, width:].astype(F32)
        gat = gather[...]
        d_direct = mm(jnp.concatenate(direct + direct_b, axis=1), gat)
        d_cum = mm(jnp.concatenate(cum_hi + cum_hi_b, axis=1), gat) + mm(
            jnp.concatenate(cum_lo + cum_lo_b, axis=1), gat
        )
        e_hi, e_lo = split_two(
            jnp.broadcast_to(jnp.concatenate([edge_f, edge_b], axis=1), (8, 2 * width))
        )
        edge = (mm(e_hi, gat) + mm(e_lo, gat))[0:1]
        d_cum = d_cum + sums[rows, 0:LANES]
        d_run = mm(jnp.concatenate(ahead, axis=1), gat[:width]) + sums[rows, LANES:]
        back_run = jnp.dot(rev, d_cum, precision=HIGHEST, preferred_element_type=F32)
        run = jnp.dot(tri, d_run, precision=HIGHEST, preferred_element_type=F32)
        d_rate = jnp.where(is_fwd, back_run + run - d_run, back_run - d_cum + run) + edge
        neg = head_par[1:2, :]
        d_step = neg * d_rate + mask_c * d_direct
        d_z = d_step * sigmoid(z)
        ghead_ref[0:1, :] += jnp.sum(d_rate * (neg * dt), axis=0, keepdims=True)
        ghead_ref[1:2, :] += jnp.sum(d_z, axis=0, keepdims=True)
        rest_ref[rows, conv_width:] = d_z.astype(BF16)
        z_pre = z - head_par[0:1, :]
        rd_ref[rows, :] = jnp.sum(d_z * z_pre, axis=1, keepdims=True) + jnp.zeros((CHUNK, LANES), F32)

    prev = pre[...].astype(F32)
    acc = conv[3:4, :] * ext[0:BLOCK, :]
    gconv_ref[4:5, :] += jnp.sum(ext[0:BLOCK, :], axis=0, keepdims=True)
    gconv_ref[3:4, :] += jnp.sum(ext[0:BLOCK, :] * prev, axis=0, keepdims=True)
    for j in range(3):
        moved = ext[3 - j : 3 - j + BLOCK, :]
        acc = acc + conv[j : j + 1, :] * moved
        gconv_ref[j : j + 1, :] += jnp.sum(moved * prev, axis=0, keepdims=True)
    rest_ref[:, 0:conv_width] = acc.astype(BF16)
    rd_ref[...] += jnp.sum(acc * prev, axis=1, keepdims=True)
    ext[BLOCK:, :] = ext[0:8, :]


def rows_of(cols, order=None):
    if order is None:
        return pl.BlockSpec((BLOCK, cols), lambda i, *_: (i, 0))
    return pl.BlockSpec((BLOCK, cols), lambda i, *_: (order - 1 - i, 0))


def lanes_of(order=None):
    if order is None:
        return pl.BlockSpec((8, BLOCK), lambda i, *_: (0, i))
    return pl.BlockSpec((8, BLOCK), lambda i, *_: (0, order - 1 - i))


def states_of(per, n, width, order=None):
    if order is None:
        return pl.BlockSpec((per, n, width), lambda i, *_: (i, 0, 0))
    return pl.BlockSpec((per, n, width), lambda i, *_: (order - 1 - i, 0, 0))


def fixed(*shape):
    return pl.BlockSpec(shape, lambda i, *_: (0,) * len(shape))


def call(kernel, blocks, in_specs, out_specs, out_shape, scratch, name):
    return pl.pallas_call(
        kernel,
        out_shape=out_shape,
        grid_spec=pltpu.PrefetchScalarGridSpec(
            num_scalar_prefetch=1,
            grid=(blocks,),
            in_specs=in_specs,
            out_specs=out_specs,
            scratch_shapes=scratch,
        ),
        compiler_params=pltpu.CompilerParams(
            dimension_semantics=("arbitrary",), vmem_limit_bytes=VMEM_LIMIT
        ),
        name=name,
    )


def swap_mp(x):
    return lax.ppermute(x, "mp", [(0, 1), (1, 0)])


def dp_bits():
    size = lax.axis_size("dp")
    index = lax.axis_index("dp")
    out = []
    step = 1
    while step < size:
        out.append(((index // step) % 2, [(i, i ^ step) for i in range(size)]))
        step *= 2
    return out


def reduce_scatter(x):
    for bit, perm in dp_bits():
        half = x.shape[0] // 2
        mine = lax.dynamic_slice_in_dim(x, bit * half, half, 0)
        other = lax.dynamic_slice_in_dim(x, (1 - bit) * half, half, 0)
        got = lax.ppermute(other, "dp", perm)
        x = (mine.astype(F32) + got.astype(F32)).astype(x.dtype)
    return x


def gather_back(x):
    for bit, perm in reversed(dp_bits()):
        got = lax.ppermute(x, "dp", perm)
        x = jnp.where(bit == 0, jnp.concatenate([x, got]), jnp.concatenate([got, x]))
    return x


def body(
    tokens,
    norm_gain,
    proj_gate,
    proj_inner,
    proj_state,
    proj_step,
    conv_inner,
    conv_inner_bias,
    conv_state,
    conv_state_bias,
    step_bias,
    decay_log,
    skip_gain,
    gate_gain,
    proj_out,
    lengths,
    cotangent,
):
    rows, width_own = tokens.shape
    model = 2 * width_own
    heads = skip_gain.shape[0]
    width = proj_inner.shape[1]
    head_dim = width // heads
    state_width = proj_state.shape[1]
    n = state_width // 4
    conv_width = width + state_width
    inner_width = width * lax.axis_size("mp")
    blocks = rows // BLOCK
    per = BLOCK // CHUNK
    chunks = rows // CHUNK
    rank = lax.axis_index("mp")
    shape = jax.ShapeDtypeStruct

    oth_tokens = swap_mp(tokens)
    oth_gain = swap_mp(norm_gain.reshape(1, width_own))
    oth_cot = swap_mp(cotangent)

    def own_first(x, axis):
        half = x.shape[axis] // 2
        a = lax.slice_in_dim(x, 0, half, axis=axis)
        b = lax.slice_in_dim(x, half, 2 * half, axis=axis)
        return jnp.where(rank == 0, x, jnp.concatenate([b, a], axis=axis))

    step_weight = proj_step.reshape(model, 2 * heads)
    step_weight = jnp.pad(step_weight, ((0, 0), (0, LANES - 2 * heads)))
    weights = own_first(
        jnp.concatenate([proj_gate, proj_inner, proj_state, step_weight], axis=1), 0
    )
    po = own_first(proj_out, 1)
    gain = jnp.concatenate([norm_gain.reshape(1, width_own), oth_gain], axis=1).astype(F32)
    conv = jnp.concatenate(
        [
            jnp.concatenate([conv_inner, conv_state], axis=1),
            jnp.concatenate([conv_inner_bias, conv_state_bias])[None],
            jnp.zeros((3, conv_width), F32),
        ]
    )
    head_par = jnp.stack([step_bias.reshape(-1), -jnp.exp(decay_log.reshape(-1))])
    head_par = jnp.pad(head_par, ((0, 6), (0, LANES - 2 * heads)))
    lane_head = lax.broadcasted_iota(jnp.int32, (2 * LANES, 2 * width), 1) // head_dim
    lane_row = lax.broadcasted_iota(jnp.int32, (2 * LANES, 2 * width), 0) % LANES
    spread = (lane_head == lane_row).astype(BF16)
    gather_head = lax.broadcasted_iota(jnp.int32, (2 * width, LANES), 0) // head_dim
    gather_lane = lax.broadcasted_iota(jnp.int32, (2 * width, LANES), 1)
    gather = (gather_head == gather_lane).astype(BF16)
    skip = jnp.repeat(skip_gain, head_dim)[None]
    gg = gate_gain[None]

    sizes = dict(heads=heads, width=width, state_width=state_width)
    normed, gate_pre, pre, slope, hs, act, sact, xd, hf, sb = call(
        partial(project_kernel, **sizes),
        blocks,
        [
            rows_of(width_own),
            rows_of(width_own),
            fixed(1, model),
            fixed(*weights.shape),
            fixed(8, conv_width),
            fixed(8, LANES),
            fixed(*spread.shape),
        ],
        [
            rows_of(model),
            rows_of(width),
            rows_of(conv_width),
            rows_of(conv_width),
            rows_of(4 * LANES),
            rows_of(width),
            rows_of(state_width),
            rows_of(2 * width),
            states_of(per, n, width),
            states_of(per, n, width),
        ],
        [
            shape((rows, model), BF16),
            shape((rows, width), F32),
            shape((rows, conv_width), BF16),
            shape((rows, conv_width), BF16),
            shape((rows, 4 * LANES), F32),
            shape((rows, width), F32),
            shape((rows, state_width), BF16),
            shape((rows, 2 * width), BF16),
            shape((chunks, n, width), BF16),
            shape((chunks, n, width), F32),
        ],
        [pltpu.VMEM((BLOCK + 8, conv_width), F32), pltpu.VMEM((n, width), F32)],
        "project",
    )(lengths, tokens, oth_tokens, gain, weights, conv, head_par, spread)

    y, ssdf, dgn, gz, sums, hb = call(
        partial(forward_kernel, blocks=blocks, **sizes),
        blocks,
        [
            rows_of(width, blocks),
            rows_of(state_width, blocks),
            rows_of(4 * LANES, blocks),
            rows_of(2 * width, blocks),
            states_of(per, n, width, blocks),
            states_of(per, n, width, blocks),
            rows_of(width, blocks),
            rows_of(width_own, blocks),
            rows_of(width_own, blocks),
            fixed(*po.shape),
            fixed(1, width),
            fixed(1, width),
            fixed(*spread.shape),
        ],
        [
            rows_of(width, blocks),
            rows_of(width, blocks),
            rows_of(width, blocks),
            rows_of(width, blocks),
            lanes_of(blocks),
            states_of(per, n, width, blocks),
        ],
        [
            shape((rows, width), F32),
            shape((rows, width), F32),
            shape((rows, width), F32),
            shape((rows, width), BF16),
            shape((8, rows), F32),
            shape((chunks, n, width), BF16),
        ],
        [pltpu.VMEM((n, width), F32)],
        "mix",
    )(lengths, act, sact, hs, xd, hf, sb, gate_pre, cotangent, oth_cot, po, gg, skip, spread)

    sums = sums + swap_mp(sums)
    branch_oth = jnp.dot(gz, po[:, width_own:], preferred_element_type=F32).astype(BF16)
    branch_got = swap_mp(branch_oth)
    branch_own = jnp.dot(gz, po[:, :width_own], preferred_element_type=F32)

    g, dgp, dbr, dc, gb, gf, rd_gate, row_sums, small = call(
        partial(gate_back_kernel, inner_width=inner_width, **sizes),
        blocks,
        [
            lanes_of(),
            rows_of(width),
            rows_of(width),
            rows_of(width),
            rows_of(width),
            rows_of(width),
            rows_of(width_own),
            rows_of(width_own),
            rows_of(4 * LANES),
            rows_of(state_width),
            states_of(per, n, width),
            states_of(per, n, width),
            fixed(1, width),
            fixed(1, width),
            fixed(*spread.shape),
            fixed(*gather.shape),
        ],
        [
            rows_of(width),
            rows_of(width),
            rows_of(model),
            rows_of(2 * n),
            states_of(per, n, width),
            states_of(per, n, width),
            lanes_of(),
            rows_of(2 * LANES),
            fixed(8, width),
        ],
        [
            shape((rows, width), BF16),
            shape((rows, width), BF16),
            shape((rows, model), BF16),
            shape((rows, 2 * n), F32),
            shape((chunks, n, width), BF16),
            shape((chunks, n, width), F32),
            shape((8, rows), F32),
            shape((rows, 2 * LANES), F32),
            shape((8, width), F32),
        ],
        [pltpu.VMEM((n, width), F32)],
        "gate_back",
    )(lengths, sums, gate_pre, y, ssdf, act, dgn, cotangent, oth_cot, hs, sact, hf, hb, gg, skip, spread, gather)

    grad_out = mm_tn(gz, dbr)
    grad_gate = mm_tn(normed, dgp)

    rest, rd_rest, gconv, ghead = call(
        partial(back_kernel, blocks=blocks, **sizes),
        blocks,
        [
            rows_of(width, blocks),
            rows_of(width, blocks),
            rows_of(state_width, blocks),
            rows_of(4 * LANES, blocks),
            rows_of(2 * width, blocks),
            rows_of(2 * LANES, blocks),
            states_of(per, n, width, blocks),
            states_of(per, n, width, blocks),
            states_of(per, n, width, blocks),
            states_of(per, n, width, blocks),
            rows_of(2 * n, blocks),
            rows_of(conv_width, blocks),
            rows_of(conv_width, blocks),
            fixed(8, conv_width),
            fixed(8, LANES),
            fixed(1, width),
            fixed(*spread.shape),
            fixed(*gather.shape),
        ],
        [
            rows_of(conv_width + LANES, blocks),
            rows_of(LANES, blocks),
            fixed(8, conv_width),
            fixed(8, LANES),
        ],
        [
            shape((rows, conv_width + LANES), BF16),
            shape((rows, LANES), F32),
            shape((8, conv_width), F32),
            shape((8, LANES), F32),
        ],
        [pltpu.VMEM((BLOCK + 8, conv_width), F32), pltpu.VMEM((n, width), F32)],
        "mix_back",
    )(lengths, g, act, sact, hs, xd, row_sums, hf, hb, gb, gf, dc, pre, slope, conv, head_par, skip, spread, gather)

    w_gate = weights[:, :width]
    w_rest = weights[:, width:]
    dn_oth = mm_nt(dgp, w_gate[width_own:]) + mm_nt(rest, w_rest[width_own:])
    dn_got = swap_mp(dn_oth.astype(BF16))
    rd_part = rd_gate[0] + rd_rest[:, 0]
    rd_full = rd_part + swap_mp(rd_part.reshape(8, rows // 8)).reshape(rows)
    dn_own = mm_nt(dgp, w_gate[:width_own]) + mm_nt(rest, w_rest[:width_own])
    grad_inner = mm_tn(normed, rest[:, :width])
    grad_rest_t = mm_tn(rest[:, width:], normed)

    normed_f = normed.astype(F32)
    dn_all = jnp.concatenate([dn_own, dn_oth], axis=1)
    grad_gain = jnp.sum(dn_all * normed_f, axis=0) / gain[0]
    grad_gain = own_first(grad_gain, 0)

    early = jnp.concatenate([grad_out, own_first(grad_gate, 0)]).astype(BF16)
    state_small = jnp.concatenate(
        [gconv[:5, width:].reshape(-1), jnp.zeros((2 * model - 5 * state_width,), F32), grad_gain]
    ).reshape(3, model)
    skip_sum = jnp.sum(small[1].reshape(heads, head_dim), axis=1)
    misc = jnp.concatenate(
        [ghead[0, : 2 * heads], ghead[1, : 2 * heads], skip_sum, jnp.zeros((model - 5 * heads,), F32)]
    )[None]
    both_rows = state_width + 3
    grad_rest_t = own_first(grad_rest_t, 1)
    late = jnp.concatenate(
        [
            grad_rest_t[:state_width],
            state_small,
            own_first(grad_inner, 0),
            grad_rest_t[state_width : state_width + 2 * heads],
            gconv[:5, :width],
            small[0:1],
            misc,
        ]
    ).astype(BF16)
    used = late.shape[0]
    unit = 8 * lax.axis_size("dp")
    late = jnp.pad(late, ((0, -used % unit), (0, 0)))

    early = gather_back(reduce_scatter(early))
    part = reduce_scatter(late)
    shard = part.shape[0]
    part_rows = lax.axis_index("dp") * 0
    for level, (bit, _) in enumerate(dp_bits()):
        part_rows = part_rows + bit * (late.shape[0] >> (level + 1))
    shared = (part_rows + lax.broadcasted_iota(jnp.int32, (shard, 1), 0)) < both_rows
    part_f = part.astype(F32)
    part = jnp.where(shared, part_f + swap_mp(part).astype(F32), part_f).astype(BF16)
    late = gather_back(part).astype(F32)

    grad_proj_out = own_first(early[:width].astype(F32), 1)
    grad_proj_gate = early[width:].astype(F32)
    at = 0
    grad_proj_state = late[:state_width].T
    at = state_width
    conv_state_all = late[at : at + 2].reshape(-1)[: 5 * state_width].reshape(5, state_width)
    grad_norm_gain = lax.dynamic_slice_in_dim(late[at + 2], rank * width_own, width_own, 0)
    at += 3
    grad_proj_inner = late[at : at + model]
    at += model
    grad_proj_step = late[at : at + 2 * heads].T.reshape(model, 2, heads)
    at += 2 * heads
    conv_inner_all = late[at : at + 5]
    grad_gate_gain = late[at + 5]
    misc = late[at + 6]
    grad_decay_log = misc[: 2 * heads].reshape(2, heads)
    grad_step_bias = misc[2 * heads : 4 * heads].reshape(2, heads)
    grad_skip = misc[4 * heads : 5 * heads]

    seq_mask = (jnp.arange(rows) < lengths[0]).astype(F32)[:, None]
    gate_inv = lax.rsqrt(sums[0] / inner_width + EPSILON)[:, None]
    tokens_f = tokens.astype(F32)
    block_out = (
        tokens_f + seq_mask * gate_inv * (branch_own + branch_got.astype(F32))
    ).astype(BF16)
    oth_f = oth_tokens.astype(F32)
    square = jnp.sum(tokens_f * tokens_f, axis=1, keepdims=True) + jnp.sum(
        oth_f * oth_f, axis=1, keepdims=True
    )
    inv = lax.rsqrt(square / model + EPSILON)
    grad_full = dn_own + dn_got.astype(F32)
    grad_tokens = (
        cotangent.astype(F32)
        + inv * (grad_full * gain[:, :width_own])
        - tokens_f * (inv * inv * (rd_full[:, None] / model))
    )
    return (
        block_out,
        grad_tokens,
        grad_norm_gain,
        grad_proj_gate,
        grad_proj_inner,
        grad_proj_state,
        grad_proj_step,
        conv_inner_all[:4],
        conv_inner_all[4],
        conv_state_all[:4],
        conv_state_all[4],
        grad_step_bias,
        grad_decay_log,
        grad_skip,
        grad_gate_gain,
        grad_proj_out,
    )


def solution(mesh):
    in_specs = (
        P("dp", "mp"),
        P("mp"),
        P(None, "mp"),
        P(None, "mp"),
        P(),
        P(None, None, "mp"),
        P(None, "mp"),
        P("mp"),
        P(),
        P(),
        P(None, "mp"),
        P(None, "mp"),
        P("mp"),
        P("mp"),
        P("mp", None),
        P("dp"),
        P("dp", "mp"),
    )
    out_specs = (
        P("dp", "mp"),
        P("dp", "mp"),
        P("mp"),
        P(None, "mp"),
        P(None, "mp"),
        P(),
        P(None, None, "mp"),
        P(None, "mp"),
        P("mp"),
        P(),
        P(),
        P(None, "mp"),
        P(None, "mp"),
        P("mp"),
        P("mp"),
        P("mp", None),
    )
    return jax.shard_map(body, mesh=mesh, in_specs=in_specs, out_specs=out_specs, check_vma=False)
```

```python
from functools import partial

import jax
import jax.numpy as jnp
from jax import lax
from jax.experimental import pallas as pl
from jax.experimental.pallas import tpu as pltpu
from jax.sharding import PartitionSpec as P

EPSILON = 1e-05
CHUNK = 128
BLOCK = 256
LANES = 128
F32 = jnp.float32
BF16 = jnp.bfloat16
HIGHEST = lax.Precision.HIGHEST
VMEM_LIMIT = 28 * 1024 * 1024
SHARDS = 16
LATE_ROWS = 72


def mm(a, b):
    return jnp.dot(a, b, preferred_element_type=F32)


def mm_nt(a, b):
    return lax.dot_general(a, b, (((1,), (1,)), ((), ())), preferred_element_type=F32)


def mm_tn(a, b):
    return lax.dot_general(a, b, (((0,), (0,)), ((), ())), preferred_element_type=F32)


def split_two(v):
    hi = v.astype(BF16)
    return hi, (v - hi.astype(F32)).astype(BF16)


def expand(v, spread):
    hi, lo = split_two(v)
    return mm(jnp.concatenate([hi, lo], axis=1), spread)


def row_mask(block, rows, length):
    pos = block * rows + lax.broadcasted_iota(jnp.int32, (rows, 1), 0)
    return (pos < length).astype(F32)


def to_row(col_a, col_b):
    rows = col_a.shape[0]
    lane = lax.broadcasted_iota(jnp.int32, (rows, LANES), 1)
    tile = jnp.where(lane == 0, col_a, jnp.where(lane == 1, col_b, 0.0))
    return jnp.transpose(tile)[0:8, :]


def sigmoid(v):
    return 0.5 * jnp.tanh(0.5 * v) + 0.5


def natural(rank, own, oth):
    return jnp.where(
        rank == 0, jnp.concatenate([own, oth], axis=1), jnp.concatenate([oth, own], axis=1)
    )


def eight(row):
    return jnp.broadcast_to(row, (8, row.shape[1]))


def project_kernel(
    i, scalars, own, oth, gain, w_gate, w_inner, w_state, w_step, conv, head_par, spread,
    normed_ref, gate_ref, pre_ref, slope_ref, hs_ref, act_ref, sact_ref, xd_ref, hf_ref, sb_ref,
    ext, carry, *, heads, width, state_width,
):
    @pl.when(i == 0)
    def _():
        ext[0:8, :] = jnp.zeros((8, ext.shape[1]), F32)
        carry[...] = jnp.zeros_like(carry)

    x = natural(scalars[1], own[...], oth[...]).astype(F32)
    inv = lax.rsqrt(jnp.mean(x * x, axis=-1, keepdims=True) + EPSILON)
    normed = (x * inv * gain[...]).astype(BF16)
    normed_ref[...] = normed
    step_pre = mm(normed, w_step[...])
    z = step_pre + head_par[0:1, :]
    dt = jnp.maximum(z, 0.0) + jnp.log1p(jnp.exp(-jnp.abs(z)))
    rate = head_par[1:2, :] * dt
    dtm = dt * row_mask(i, BLOCK, scalars[0])
    hs_ref[:, 0:LANES] = z
    hs_ref[:, LANES : 2 * LANES] = dt
    tri_r = lax.broadcasted_iota(jnp.int32, (CHUNK, CHUNK), 0)
    tri_c = lax.broadcasted_iota(jnp.int32, (CHUNK, CHUNK), 1)
    tri = (tri_c <= tri_r).astype(F32)
    is_fwd = lax.broadcasted_iota(jnp.int32, (CHUNK, LANES), 1) < heads
    per = BLOCK // CHUNK
    to_spread = [dtm]
    keeps = []
    for c_idx in range(per):
        rows = slice(c_idx * CHUNK, (c_idx + 1) * CHUNK)
        rate_c = rate[rows]
        cum = jnp.dot(tri, rate_c, precision=HIGHEST, preferred_element_type=F32)
        tot = cum[CHUNK - 1 : CHUNK, :]
        cumx = jnp.where(is_fwd, cum, cum - rate_c)
        hs_ref[rows, 2 * LANES : 3 * LANES] = cumx
        hs_ref[rows, 3 * LANES :] = jnp.broadcast_to(tot, (CHUNK, LANES))
        to_spread.append(dtm[rows] * jnp.exp(jnp.where(is_fwd, tot - cumx, cumx)))
        keeps.append(eight(jnp.exp(tot)))
    wide = expand(jnp.concatenate(to_spread + keeps, axis=0), spread[...])

    ext[8 : 8 + BLOCK, 0:width] = mm(normed, w_inner[...])
    ext[8 : 8 + BLOCK, width:] = mm(normed, w_state[...])
    gate_ref[...] = mm(normed, w_gate[...])
    pre = ext[8 : 8 + BLOCK, :]
    pre_ref[...] = pre.astype(BF16)
    c = conv[4:5, :] + conv[3:4, :] * pre
    for j in range(3):
        c = c + conv[j : j + 1, :] * ext[5 + j : 5 + j + BLOCK, :]
    sg = sigmoid(c)
    both = c * sg
    slope_ref[...] = (sg * (1.0 + c * (1.0 - sg))).astype(BF16)
    ext[0:8, :] = ext[BLOCK : BLOCK + 8, :]
    act = both[:, :width]
    act_ref[...] = act
    sact = both[:, width:].astype(BF16)
    sact_ref[...] = sact
    xd_ref[:, 0:width] = (act * wide[0:BLOCK, :width]).astype(BF16)
    xd_ref[:, width:] = (act * wide[0:BLOCK, width:]).astype(BF16)
    n = state_width // 4
    for c_idx in range(per):
        rows = slice(c_idx * CHUNK, (c_idx + 1) * CHUNK)
        coef = wide[BLOCK + c_idx * CHUNK : BLOCK + (c_idx + 1) * CHUNK]
        keep = wide[2 * BLOCK + 8 * c_idx : 2 * BLOCK + 8 * c_idx + 1, :width]
        hf_ref[c_idx] = carry[...].astype(BF16)
        carry[...] = carry[...] * keep + mm_tn(
            sact[rows, 0:n], (act[rows] * coef[:, :width]).astype(BF16)
        )
        sb_ref[c_idx] = mm_tn(
            sact[rows, 2 * n : 3 * n], (act[rows] * coef[:, width:]).astype(BF16)
        )


def pair_tiles(pair):
    lane = lax.broadcasted_iota(jnp.int32, (1, pair.shape[1]), 1)
    first = (lane < pair.shape[1] // 2).astype(F32)
    keep_a, keep_b = first.astype(BF16), (1.0 - first).astype(BF16)
    return jnp.concatenate([pair * keep_a, pair * keep_b], axis=0)


def mix_kernel(
    i, scalars, act, sact, hs, xd, hf, sb, head_par, spread, y_ref, hb_ref, carry,
    *, heads, width, state_width,
):
    @pl.when(i == 0)
    def _():
        carry[...] = jnp.zeros_like(carry)

    n = state_width // 4
    per = BLOCK // CHUNK
    r = lax.broadcasted_iota(jnp.int32, (CHUNK, CHUNK), 0)
    c = lax.broadcasted_iota(jnp.int32, (CHUNK, CHUNK), 1)
    lower = c < r
    upper = c > r
    is_fwd = lax.broadcasted_iota(jnp.int32, (BLOCK, LANES), 1) < heads
    cum_all = hs[:, 2 * LANES : 3 * LANES]
    tot_all = hs[:, 3 * LANES :]
    wide = expand(
        jnp.concatenate(
            [jnp.exp(jnp.where(is_fwd, cum_all, tot_all - cum_all))]
            + [jnp.exp(tot_all[k * CHUNK : k * CHUNK + 8]) for k in range(per)]
            + [eight(head_par[2:3, :])],
            axis=0,
        ),
        spread[...],
    )
    skip = wide[BLOCK + 8 * per : BLOCK + 8 * per + 1]
    for c_idx in reversed(range(per)):
        rows = slice(c_idx * CHUNK, (c_idx + 1) * CHUNK)
        cumx = cum_all[rows]
        cum_t = jnp.transpose(cumx)
        sact_c = sact[rows, :]
        b_f, c_f = sact_c[:, 0:n], sact_c[:, n : 2 * n]
        b_b, c_b = sact_c[:, 2 * n : 3 * n], sact_c[:, 3 * n :]
        s_f = jnp.where(lower, mm_nt(c_f, b_f), 0.0)
        s_b = jnp.where(upper, mm_nt(c_b, b_b), 0.0)
        hb = carry[...].astype(BF16)
        hb_ref[c_idx] = hb
        in_f = mm(c_f, hf[c_idx])
        in_b = mm(c_b, hb)
        keep = wide[BLOCK + 8 * c_idx : BLOCK + 8 * c_idx + 1, width:]
        carry[...] = carry[...] * keep + sb[c_idx]
        for p in range(heads // 2):
            lanes = slice(p * LANES, (p + 1) * LANES)
            lanes_b = slice(width + p * LANES, width + (p + 1) * LANES)
            w_f, w_b = [], []
            for h in (2 * p, 2 * p + 1):
                arg = jnp.where(
                    lower,
                    cumx[:, h : h + 1] - cum_t[h : h + 1, :],
                    cum_t[heads + h : heads + h + 1, :] - cumx[:, heads + h : heads + h + 1],
                )
                damp = jnp.exp(arg)
                w_f.append((s_f * damp).astype(BF16))
                w_b.append((s_b * damp).astype(BF16))
            out = mm(
                jnp.concatenate(w_f + w_b, axis=1),
                jnp.concatenate([pair_tiles(xd[rows, lanes]), pair_tiles(xd[rows, lanes_b])], axis=0),
            )
            y_ref[rows, lanes] = (
                out
                + wide[rows, lanes] * in_f[:, lanes]
                + wide[rows, lanes_b] * in_b[:, lanes]
                + skip[:, lanes] * act[rows, lanes]
            )


def gate_kernel(i, scalars, y, gate, cown, coth, po, gg, dgn_ref, gz_ref, sums_ref):
    gp = gate[...]
    gated = y[...] * (gp * sigmoid(gp))
    mask = row_mask(i, BLOCK, scalars[0])
    cot = natural(scalars[1], cown[...], coth[...])
    dgn = mm_nt((cot.astype(F32) * mask).astype(BF16), po[...])
    dgn_ref[...] = dgn
    scaled = gated * gg[...]
    gz_ref[...] = scaled.astype(BF16)
    sums_ref[...] = to_row(
        jnp.sum(gated * gated, axis=1, keepdims=True), jnp.sum(dgn * scaled, axis=1, keepdims=True)
    )


def gate_back_kernel(
    i, scalars, sums, gate, y, act, dgn, cown, coth, hs, sact, hf, hb, gg, spread, gather,
    g_ref, dgp_ref, dbr_ref, dc_ref, gb_ref, gf_ref, rd_ref, rows_ref, small_ref, carry, prod,
    *, heads, width, state_width, inner_width,
):
    @pl.when(i == 0)
    def _():
        carry[...] = jnp.zeros_like(carry)
        small_ref[...] = jnp.zeros_like(small_ref)

    per = BLOCK // CHUNK
    is_fwd = lax.broadcasted_iota(jnp.int32, (BLOCK, LANES), 1) < heads
    cum_all = hs[:, 2 * LANES : 3 * LANES]
    tot_all = hs[:, 3 * LANES :]
    wide = expand(
        jnp.concatenate(
            [jnp.exp(jnp.where(is_fwd, cum_all, tot_all - cum_all))]
            + [jnp.exp(tot_all[k * CHUNK : k * CHUNK + 8]) for k in range(per)],
            axis=0,
        ),
        spread[...],
    )
    cols = jnp.transpose(sums[...])
    gate_inv = lax.rsqrt(cols[:, 0:1] / inner_width + EPSILON)
    gate_dot = cols[:, 1:2] / inner_width
    gp = gate[...]
    sg = sigmoid(gp)
    act_gate = gp * sg
    yv = y[...]
    gated = yv * act_gate
    dg = dgn[...]
    small_ref[0:1, :] += jnp.sum(dg * gated * gate_inv, axis=0, keepdims=True)
    d_gated = gate_inv * (dg * gg[...]) - gated * (gate_inv * gate_inv * gate_inv * gate_dot)
    d_gp = d_gated * yv * (sg * (1.0 + gp * (1.0 - sg)))
    dgp_ref[...] = d_gp.astype(BF16)
    rd = jnp.sum(d_gp * gp, axis=1, keepdims=True)
    rd_ref[...] = to_row(rd, jnp.zeros_like(rd))
    d_y = d_gated * act_gate
    g_ref[...] = d_y.astype(BF16)
    small_ref[1:2, :] += jnp.sum(d_y * act[...], axis=0, keepdims=True)
    mask = row_mask(i, BLOCK, scalars[0])
    cot = natural(scalars[1], cown[...], coth[...])
    dbr_ref[...] = (cot.astype(F32) * (mask * gate_inv)).astype(BF16)
    n = state_width // 4
    for c_idx in range(per):
        rows = slice(c_idx * CHUNK, (c_idx + 1) * CHUNK)
        dy_c = d_y[rows]
        dyf = dy_c * wide[rows, :width]
        dyb = dy_c * wide[rows, width:]
        prod[rows, 0:width] = (dyf * mm(sact[rows, n : 2 * n], hf[c_idx])).astype(BF16)
        prod[rows, width:] = (dyb * mm(sact[rows, 3 * n :], hb[c_idx])).astype(BF16)
        dyf = dyf.astype(BF16)
        dyb = dyb.astype(BF16)
        dc_ref[rows, 0:n] = mm_nt(dyf, hf[c_idx])
        dc_ref[rows, n : 2 * n] = mm_nt(dyb, hb[c_idx])
        gb_ref[c_idx] = carry[...].astype(BF16)
        keep = wide[BLOCK + 8 * c_idx : BLOCK + 8 * c_idx + 1, width:]
        carry[...] = carry[...] * keep + mm_tn(sact[rows, 3 * n :], dyb)
        gf_ref[c_idx] = mm_tn(sact[rows, n : 2 * n], dyf)
    rows_ref[...] = mm(prod[...], gather[...])


def back_kernel(
    i, scalars, g, act, sact, hs, xd, row_in, hf, hb, gb, gf, dc, pre, slope, conv, head_par, spread, gather,
    ext_in, carry_in, gconv_in, ghead_in, _rest, _rd, rest_ref, rd_ref, gconv_ref, ghead_ref, ext_out,
    carry, ext, stack, xs, rsum,
    *, heads, width, state_width, top,
):
    blk = top - i
    per = BLOCK // CHUNK

    @pl.when(i == 0)
    def _():
        ext[BLOCK:, :] = ext_in[...]
        carry[...] = carry_in[...]
        gconv_ref[...] = gconv_in[...]
        ghead_ref[...] = ghead_in[...]
        stack[3 * CHUNK : 4 * CHUNK, width:] = jnp.zeros((CHUNK, width), BF16)
        rsum[...] = jnp.zeros_like(rsum)

    n = state_width // 4
    conv_width = width + state_width
    r = lax.broadcasted_iota(jnp.int32, (CHUNK, CHUNK), 0)
    c = lax.broadcasted_iota(jnp.int32, (CHUNK, CHUNK), 1)
    later = c > r
    earlier = c < r
    rev = (c >= r).astype(F32)
    tri = (c <= r).astype(F32)
    is_fwd_all = lax.broadcasted_iota(jnp.int32, (BLOCK, LANES), 1) < heads
    is_fwd = lax.broadcasted_iota(jnp.int32, (CHUNK, LANES), 1) < heads
    mask = row_mask(blk, BLOCK, scalars[0])
    dt_all = hs[:, LANES : 2 * LANES]
    cum_all = hs[:, 2 * LANES : 3 * LANES]
    tot_all = hs[:, 3 * LANES :]
    wide = expand(
        jnp.concatenate(
            [jnp.exp(jnp.where(is_fwd_all, tot_all - cum_all, cum_all)), dt_all * mask]
            + [jnp.exp(tot_all[k * CHUNK : k * CHUNK + 8]) for k in range(per)]
            + [eight(head_par[2:3, :])],
            axis=0,
        ),
        spread[...],
    )
    skip = wide[2 * BLOCK + 8 * per : 2 * BLOCK + 8 * per + 1]
    rd_parts = []
    for c_idx in reversed(range(per)):
        rows = slice(c_idx * CHUNK, (c_idx + 1) * CHUNK)
        rows_dt = slice(BLOCK + c_idx * CHUNK, BLOCK + (c_idx + 1) * CHUNK)
        z = hs[rows, 0:LANES]
        dt = dt_all[rows]
        cumx = cum_all[rows]
        cum_t = jnp.transpose(cumx)
        sact_c = sact[rows, :]
        b_f, c_f = sact_c[:, 0:n], sact_c[:, n : 2 * n]
        b_b, c_b = sact_c[:, 2 * n : 3 * n], sact_c[:, 3 * n :]
        s_f = jnp.where(later, mm_nt(b_f, c_f), 0.0)
        s_b = jnp.where(earlier, mm_nt(b_b, c_b), 0.0)
        grad_f = carry[...]
        grad_f_low = grad_f.astype(BF16)
        grad_b_low = gb[c_idx]
        keep = wide[2 * BLOCK + 8 * c_idx : 2 * BLOCK + 8 * c_idx + 1]
        keep_f = keep[:, :width]
        edge_f = keep_f * jnp.sum(grad_f * hf[c_idx].astype(F32), axis=0, keepdims=True)
        edge_b = keep[:, width:] * jnp.sum(
            hb[c_idx].astype(F32) * grad_b_low.astype(F32), axis=0, keepdims=True
        )
        e_hi, e_lo = split_two(eight(jnp.concatenate([edge_f, edge_b], axis=1)))
        stack[4 * CHUNK :, :] = jnp.concatenate([e_hi, e_lo], axis=0)
        carry[...] = grad_f * keep_f + gf[c_idx]
        in_f = mm(b_f, grad_f_low)
        in_b = mm(b_b, grad_b_low)
        d_scores = jnp.zeros((CHUNK, CHUNK), F32)
        for p in range(heads // 2):
            lanes = slice(p * LANES, (p + 1) * LANES)
            lanes_b = slice(width + p * LANES, width + (p + 1) * LANES)
            g_pair = g[rows, lanes]
            xf_pair = xd[rows, lanes]
            xb_pair = xd[rows, lanes_b]
            dw = mm_nt(
                jnp.concatenate([pair_tiles(xf_pair), pair_tiles(xb_pair)], axis=0), g_pair
            )
            w_f, w_b = [], []
            for q, h in enumerate((2 * p, 2 * p + 1)):
                arg = jnp.where(
                    later,
                    cum_t[h : h + 1, :] - cumx[:, h : h + 1],
                    cumx[:, heads + h : heads + h + 1] - cum_t[heads + h : heads + h + 1, :],
                )
                damp = jnp.exp(arg)
                low_f = (s_f * damp).astype(BF16)
                low_b = (s_b * damp).astype(BF16)
                w_f.append(low_f)
                w_b.append(low_b)
                dw_f = dw[q * CHUNK : (q + 1) * CHUNK]
                dw_b = dw[(2 + q) * CHUNK : (3 + q) * CHUNK]
                d_scores = d_scores + jnp.where(later, dw_f, dw_b) * damp
                rsum[h : h + 1, :] = jnp.sum(dw_f * low_f.astype(F32), axis=0, keepdims=True)
                rsum[heads + h : heads + h + 1, :] = -jnp.sum(
                    dw_b * low_b.astype(F32), axis=0, keepdims=True
                )
            dx = mm(
                jnp.concatenate(
                    [jnp.concatenate(w_f, axis=1), jnp.concatenate(w_b, axis=1)], axis=0
                ),
                pair_tiles(g_pair),
            )
            edge_pf = wide[rows, lanes]
            edge_pb = wide[rows, lanes_b]
            intra_f = dx[:CHUNK]
            inter_f = edge_pf * in_f[:, lanes]
            dx_f = intra_f + inter_f
            dx_b = dx[CHUNK:] + edge_pb * in_b[:, lanes]
            xf = xf_pair.astype(F32)
            xb = xb_pair.astype(F32)
            xs[:, lanes] = (xf * edge_pf).astype(BF16)
            xs[:, lanes_b] = (xb * edge_pb).astype(BF16)
            act_p = act[rows, lanes]
            hi, lo = split_two(-(xf * intra_f))
            stack[0:CHUNK, lanes] = hi
            stack[CHUNK : 2 * CHUNK, lanes] = lo
            hi, lo = split_two(xb * dx_b)
            stack[0:CHUNK, lanes_b] = hi
            stack[CHUNK : 2 * CHUNK, lanes_b] = lo
            stack[2 * CHUNK : 3 * CHUNK, lanes] = (act_p * dx_f).astype(BF16)
            stack[2 * CHUNK : 3 * CHUNK, lanes_b] = (act_p * dx_b).astype(BF16)
            stack[3 * CHUNK : 4 * CHUNK, lanes] = (xf * inter_f).astype(BF16)
            d_inner = (
                skip[:, lanes] * g_pair.astype(F32)
                + wide[rows_dt, lanes] * dx_f
                + wide[rows_dt, lanes_b] * dx_b
            )
            ext[rows, lanes] = d_inner * slope[rows, lanes].astype(F32)
        low_f = jnp.where(later, d_scores, 0.0).astype(BF16)
        low_b = jnp.where(earlier, d_scores, 0.0).astype(BF16)
        d_bf = mm(low_f, c_f) + mm_nt(xs[:, :width], grad_f_low)
        d_cf = mm_tn(low_f, b_f) + dc[rows, 0:n]
        d_bb = mm(low_b, c_b) + mm_nt(xs[:, width:], grad_b_low)
        d_cb = mm_tn(low_b, b_b) + dc[rows, n : 2 * n]
        d_state = jnp.concatenate([d_bf, d_cf, d_bb, d_cb], axis=1)
        ext[rows, width:] = d_state * slope[rows, width:].astype(F32)
        head_sums = mm(stack[...], gather[...])
        rin = row_in[rows, :]
        d_cum = (
            head_sums[0:CHUNK]
            + head_sums[CHUNK : 2 * CHUNK]
            + jnp.transpose(rsum[...])
            + jnp.where(is_fwd, rin, 0.0)
        )
        d_run = head_sums[3 * CHUNK : 4 * CHUNK] + jnp.where(is_fwd, 0.0, rin)
        edge = head_sums[4 * CHUNK : 4 * CHUNK + 1] + head_sums[4 * CHUNK + 8 : 4 * CHUNK + 9]
        back_run = jnp.dot(rev, d_cum, precision=HIGHEST, preferred_element_type=F32)
        run = jnp.dot(tri, d_run, precision=HIGHEST, preferred_element_type=F32)
        d_rate = jnp.where(is_fwd, back_run + run - d_run, back_run - d_cum + run) + edge
        neg = head_par[1:2, :]
        d_step = neg * d_rate + mask[rows] * head_sums[2 * CHUNK : 3 * CHUNK]
        d_z = d_step / (1.0 + jnp.exp(-z))
        ghead_ref[0:1, :] += jnp.sum(d_rate * (neg * dt), axis=0, keepdims=True)
        ghead_ref[1:2, :] += jnp.sum(d_z, axis=0, keepdims=True)
        rest_ref[rows, conv_width:] = d_z.astype(BF16)
        rd_parts.append(jnp.sum(d_z * (z - head_par[0:1, :]), axis=1, keepdims=True))

    prev = pre[...].astype(F32)
    moved = ext[0:BLOCK, :]
    acc = conv[3:4, :] * moved
    gconv_ref[4:5, :] += jnp.sum(moved, axis=0, keepdims=True)
    gconv_ref[3:4, :] += jnp.sum(moved * prev, axis=0, keepdims=True)
    for j in range(3):
        moved = ext[3 - j : 3 - j + BLOCK, :]
        acc = acc + conv[j : j + 1, :] * moved
        gconv_ref[j : j + 1, :] += jnp.sum(moved * prev, axis=0, keepdims=True)
    rest_ref[:, 0:conv_width] = acc.astype(BF16)
    rd = jnp.sum(acc * prev, axis=1, keepdims=True) + jnp.concatenate(rd_parts[::-1], axis=0)
    rd_ref[...] = to_row(rd, jnp.zeros_like(rd))
    ext[BLOCK:, :] = ext[0:8, :]
    ext_out[...] = ext[0:8, :]


def home_of(r, me, order):
    j = me % SHARDS
    levels = len(order)
    for p, bit in enumerate(order):
        if (r >> (levels - 1 - p)) & 1:
            j = jnp.bitwise_xor(j, 1 << bit)
    return j


def pack_early_kernel(
    scalars, grad_out, grad_gate, w_gate, keep_ref, send_ref, gain_ref, *, order
):
    hi, lo = split_two(grad_gate[...].astype(F32) * w_gate[...].astype(F32))
    ones = jnp.ones((8, hi.shape[1]), BF16)
    gain_ref[...] = mm_nt(ones, hi) + mm_nt(ones, lo)
    part = grad_out.shape[0] // SHARDS
    for r in range(SHARDS):
        j = home_of(r, scalars[2], order)
        out = keep_ref if r < SHARDS // 2 else send_ref
        at = (r % (SHARDS // 2)) * 2 * part
        src = pl.ds(pl.multiple_of(j * part, part), part)
        out[at : at + part, :] = grad_out[src, :]
        out[at + part : at + 2 * part, :] = grad_gate[src, :]


def unpack_early_kernel(scalars, first, second, out_ref, gate_ref, *, order):
    part = out_ref.shape[0] // SHARDS
    for r in range(SHARDS):
        j = home_of(r, scalars[2], order)
        src = first if r < SHARDS // 2 else second
        at = (r % (SHARDS // 2)) * 2 * part
        dst = pl.ds(pl.multiple_of(j * part, part), part)
        out_ref[dst, :] = src[at : at + part, :].astype(F32)
        gate_ref[dst, :] = src[at + part : at + 2 * part, :].astype(F32)


def pack_late_kernel(
    scalars, inner, state, w_inner, w_state_t, gain, gain_part, gconv, ghead, small,
    keep_ref, send_ref, misc, *, order, heads, state_width,
):
    model, width = w_inner.shape
    hi, lo = split_two(inner[...].astype(F32) * w_inner[...].astype(F32))
    ones = jnp.ones((8, hi.shape[1]), BF16)
    gain_row = (mm_nt(ones, hi) + mm_nt(ones, lo) + gain_part[...])[0:1]
    gain_row += jnp.sum(state[...].astype(F32) * w_state_t[...].astype(F32), axis=0, keepdims=True)
    gain_row = gain_row / gain[...]
    step = state[state_width:, :].astype(F32)
    misc[...] = jnp.zeros_like(misc)

    def put_single(k, row):
        at = (k // 2) * 8 + k % 2
        misc[at : at + 1, :] = row

    for k in range(2 * heads):
        put_single(k, step[k : k + 1, :])
    at = 2 * heads
    for k in range(5):
        put_single(at + k, gconv[k : k + 1, 0:width])
    put_single(at + 5, small[0:1, :])
    put_single(at + 6, small[1:2, :])
    at = ((at + 7) // 2) * 8 + (at + 7) % 2
    misc[at : at + 1, 0:LANES] = ghead[0:1, :]
    misc[at : at + 1, LANES : 2 * LANES] = ghead[1:2, :]
    fit = model // state_width
    for k in range(5):
        at = (k // fit) * 8 + 4
        lanes = slice((k % fit) * state_width, (k % fit + 1) * state_width)
        misc[at : at + 1, lanes] = gconv[k : k + 1, width:]
    at = (-(-5 // fit)) * 8 + 4
    misc[at : at + 1, :] = gain_row
    part = model // SHARDS
    part_s = state_width // SHARDS
    rows = part + part_s + 8
    for r in range(SHARDS):
        j = home_of(r, scalars[2], order)
        out = keep_ref if r < SHARDS // 2 else send_ref
        at = (r % (SHARDS // 2)) * rows
        out[at : at + part, :] = inner[pl.ds(pl.multiple_of(j * part, part), part), :]
        out[at + part : at + part + part_s, :] = state[
            pl.ds(pl.multiple_of(j * part_s, part_s), part_s), :
        ]
        out[at + part + part_s : at + rows, :] = misc[
            pl.ds(pl.multiple_of(j * 8, 8), 8), :
        ].astype(BF16)


def unpack_late_kernel(
    scalars, first, second, inner_ref, state_ref, step_ref, convi_ref, singles_ref, convs_ref,
    state, misc, *, order, heads,
):
    model = inner_ref.shape[0]
    state_width = state_ref.shape[1]
    part = model // SHARDS
    part_s = state_width // SHARDS
    rows = part + part_s + 8
    for r in range(SHARDS):
        j = home_of(r, scalars[2], order)
        src = first if r < SHARDS // 2 else second
        at = (r % (SHARDS // 2)) * rows
        inner_ref[pl.ds(pl.multiple_of(j * part, part), part), :] = src[at : at + part, :].astype(F32)
        state[pl.ds(pl.multiple_of(j * part_s, part_s), part_s), :] = src[
            at + part : at + part + part_s, :
        ].astype(F32)
        misc[pl.ds(pl.multiple_of(j * 8, 8), 8), :] = src[at + part + part_s : at + rows, :].astype(F32)
    state_ref[...] = jnp.transpose(state[...])

    def single(k):
        at = (k // 2) * 8 + k % 2
        return misc[at : at + 1, :]

    for h in range(heads):
        for d in range(2):
            step_ref[h, d : d + 1, :] = single(d * heads + h)
    at = 2 * heads
    for k in range(4):
        convi_ref[k : k + 1, :] = single(at + k)
    singles_ref[0:1, :] = single(at + 4)
    singles_ref[1:2, :] = single(at + 5)
    singles_ref[2:3, :] = single(at + 6)
    singles_ref[3:4, :] = single(at + 7)
    fit = model // state_width
    at = (-(-5 // fit)) * 8 + 4
    singles_ref[4:5, :] = misc[at : at + 1, :]
    singles_ref[5:8, :] = jnp.zeros((3, model), F32)
    for k in range(5):
        at = (k // fit) * 8 + 4
        lanes = slice((k % fit) * state_width, (k % fit + 1) * state_width)
        if k < 4:
            convs_ref[k : k + 1, :] = misc[at : at + 1, lanes]
        else:
            singles_ref[5:6, 0:state_width] = misc[at : at + 1, lanes]


def place(i, top):
    return i if top is None else top - i


def rows_of(top=None):
    return lambda ref, i: ref.at[pl.ds(pl.multiple_of(place(i, top) * BLOCK, BLOCK), BLOCK)]


def lanes_of(top=None):
    return lambda ref, i: ref.at[:, pl.ds(pl.multiple_of(place(i, top) * BLOCK, BLOCK), BLOCK)]


def states_of(top=None):
    per = BLOCK // CHUNK
    return lambda ref, i: ref.at[pl.ds(place(i, top) * per, per)]


def fixed(ref, i):
    return ref


def call(kernel, blocks, ins, out_views, out_shape, scratch, name, us, aliases=None):
    views = [view for _, view in ins[1:]] + out_views
    arrays = [ins[0]] + [
        pltpu.with_memory_space_constraint(x, pltpu.VMEM) if view is not fixed else x
        for x, view in ins[1:]
    ]

    def looped(scalars, *refs):
        def step(i, _):
            blocks_of = [view(ref, i) for view, ref in zip(views, refs)]
            kernel(i, scalars, *blocks_of, *refs[len(views) :])
            return 0

        lax.fori_loop(0, blocks, step, 0)

    vmem = pl.BlockSpec(memory_space=pltpu.VMEM)
    return pl.pallas_call(
        looped,
        out_shape=[pltpu.VMEM(o.shape, o.dtype) for o in out_shape],
        in_specs=[pl.BlockSpec(memory_space=pltpu.SMEM)] + [vmem] * (len(arrays) - 1),
        out_specs=[vmem] * len(out_shape),
        scratch_shapes=scratch,
        compiler_params=pltpu.CompilerParams(vmem_limit_bytes=VMEM_LIMIT),
        cost_estimate=pl.CostEstimate(
            flops=int(us * 5e8), transcendentals=0, bytes_accessed=int(us * 3e6)
        ),
        name=name,
        input_output_aliases=aliases or {},
    )(*arrays)


def whole(kernel, args, out_shape, scratch, name, us, in_vmem=True):
    vmem = pl.BlockSpec(memory_space=pltpu.VMEM)
    return pl.pallas_call(
        kernel,
        out_shape=[pltpu.VMEM(o.shape, o.dtype) if in_vmem else o for o in out_shape],
        in_specs=[pl.BlockSpec(memory_space=pltpu.SMEM)] + [vmem] * (len(args) - 1),
        out_specs=[vmem] * len(out_shape),
        scratch_shapes=scratch,
        compiler_params=pltpu.CompilerParams(vmem_limit_bytes=VMEM_LIMIT),
        cost_estimate=pl.CostEstimate(
            flops=int(us * 5e8), transcendentals=0, bytes_accessed=int(us * 3e6)
        ),
        name=name,
    )(*args)


def swap_mp(x):
    return lax.ppermute(x, "mp", [(0, 1), (1, 0)])


def swap_dp(x, bit):
    size = lax.axis_size("dp")
    return lax.ppermute(x, "dp", [(i, i ^ (1 << bit)) for i in range(size)])


def add_low(a, b):
    return (a.astype(F32) + b.astype(F32)).astype(BF16)


def after(x, *others):
    return lax.optimization_barrier((x, *others))[0]


def body(
    tokens,
    norm_gain,
    proj_gate,
    proj_inner,
    proj_state,
    proj_step,
    conv_inner,
    conv_inner_bias,
    conv_state,
    conv_state_bias,
    step_bias,
    decay_log,
    skip_gain,
    gate_gain,
    proj_out,
    lengths,
    cotangent,
):
    rows, width_own = tokens.shape
    model = 2 * width_own
    heads = skip_gain.shape[0]
    width = proj_inner.shape[1]
    head_dim = width // heads
    state_width = proj_state.shape[1]
    n = state_width // 4
    conv_width = width + state_width
    inner_width = width * lax.axis_size("mp")
    blocks = rows // BLOCK
    per = BLOCK // CHUNK
    chunks = rows // CHUNK
    rank = lax.axis_index("mp")
    shape = jax.ShapeDtypeStruct

    oth_tokens = swap_mp(tokens)
    oth_gain = swap_mp(norm_gain.reshape(1, width_own))
    oth_cot = swap_mp(after(cotangent, oth_tokens))

    scalars = jnp.stack([lengths[0], rank, lax.axis_index("dp")]).astype(jnp.int32)
    step_weight = proj_step.reshape(model, 2 * heads)
    step_weight = jnp.pad(step_weight, ((0, 0), (0, LANES - 2 * heads)))
    w_state_t = jnp.concatenate([proj_state, step_weight], axis=1).T
    own_gain = norm_gain.reshape(1, width_own)
    gain = natural(rank, own_gain, oth_gain).astype(F32)
    conv = jnp.concatenate(
        [
            jnp.concatenate([conv_inner, conv_state], axis=1),
            jnp.concatenate([conv_inner_bias, conv_state_bias])[None],
            jnp.zeros((3, conv_width), F32),
        ]
    )
    head_par = jnp.stack(
        [
            step_bias.reshape(-1),
            -jnp.exp(decay_log.reshape(-1)),
            jnp.pad(skip_gain, (0, heads)),
        ]
    )
    head_par = jnp.pad(head_par, ((0, 5), (0, LANES - 2 * heads)))
    lane_head = lax.broadcasted_iota(jnp.int32, (2 * LANES, 2 * width), 1) // head_dim
    lane_row = lax.broadcasted_iota(jnp.int32, (2 * LANES, 2 * width), 0) % LANES
    spread = (lane_head == lane_row).astype(BF16)
    gather_head = lax.broadcasted_iota(jnp.int32, (2 * width, LANES), 0) // head_dim
    gather_lane = lax.broadcasted_iota(jnp.int32, (2 * width, LANES), 1)
    gather = (gather_head == gather_lane).astype(BF16)
    gg = gate_gain[None]

    sizes = dict(heads=heads, width=width, state_width=state_width)
    low = lambda *dims: shape(dims, BF16)
    full = lambda *dims: shape(dims, F32)
    up, states, top = rows_of(), states_of(), blocks - 1
    down, states_down = rows_of(top), states_of(top)
    normed, gate_pre, pre, slope, hs, act, sact, xd, hf, sb = call(
        partial(project_kernel, **sizes),
        blocks,
        [
            scalars,
            (tokens, up),
            (oth_tokens, up),
            (gain, fixed),
            (proj_gate, fixed),
            (proj_inner, fixed),
            (proj_state, fixed),
            (step_weight, fixed),
            (conv, fixed),
            (head_par, fixed),
            (spread, fixed),
        ],
        [up, up, up, up, up, up, up, up, states, states],
        [
            low(rows, model),
            full(rows, width),
            low(rows, conv_width),
            low(rows, conv_width),
            full(rows, 4 * LANES),
            full(rows, width),
            low(rows, state_width),
            low(rows, 2 * width),
            low(chunks, n, width),
            full(chunks, n, width),
        ],
        [pltpu.VMEM((BLOCK + 8, conv_width), F32), pltpu.VMEM((n, width), F32)],
        "project",
        12,
    )

    y, hb = call(
        partial(mix_kernel, **sizes),
        blocks,
        [
            scalars,
            (act, down),
            (sact, down),
            (hs, down),
            (xd, down),
            (hf, states_down),
            (sb, states_down),
            (head_par, fixed),
            (spread, fixed),
        ],
        [down, states_down],
        [full(rows, width), low(chunks, n, width)],
        [pltpu.VMEM((n, width), F32)],
        "mix",
        7,
    )

    dgn, gz, sums = call(
        gate_kernel,
        blocks,
        [
            scalars,
            (y, up),
            (gate_pre, up),
            (cotangent, up),
            (oth_cot, up),
            (proj_out, fixed),
            (gg, fixed),
        ],
        [up, up, lanes_of()],
        [full(rows, width), low(rows, width), full(8, rows)],
        [],
        "gate",
        3,
    )

    oth_sums = swap_mp(sums)
    own_at, oth_at = rank * width_own, (1 - rank) * width_own
    po_own = lax.dynamic_slice_in_dim(proj_out, own_at, width_own, 1)
    po_oth = lax.dynamic_slice_in_dim(proj_out, oth_at, width_own, 1)
    branch_oth = mm(gz, po_oth).astype(BF16)
    sums = sums + oth_sums
    branch_got = swap_mp(after(branch_oth, sums))

    g, dgp, dbr, dc, gb, gf, rd_gate, row_sums, small = call(
        partial(gate_back_kernel, inner_width=inner_width, **sizes),
        blocks,
        [
            scalars,
            (sums, lanes_of()),
            (gate_pre, up),
            (y, up),
            (act, up),
            (dgn, up),
            (cotangent, up),
            (oth_cot, up),
            (hs, up),
            (sact, up),
            (hf, states),
            (hb, states),
            (gg, fixed),
            (spread, fixed),
            (gather, fixed),
        ],
        [up, up, up, up, states, states, lanes_of(), up, fixed],
        [
            low(rows, width),
            low(rows, width),
            low(rows, model),
            full(rows, 2 * n),
            low(chunks, n, width),
            full(chunks, n, width),
            full(8, rows),
            full(rows, LANES),
            full(8, width),
        ],
        [pltpu.VMEM((n, width), F32), pltpu.VMEM((BLOCK, 2 * width), BF16)],
        "gate_back",
        8,
    )

    def back_part(first, count, g, state):
        here, states_here = rows_of(first), states_of(first)
        ins = [
            scalars,
            (g, here),
            (act, here),
            (sact, here),
            (hs, here),
            (xd, here),
            (row_sums, here),
            (hf, states_here),
            (hb, states_here),
            (gb, states_here),
            (gf, states_here),
            (dc, here),
            (pre, here),
            (slope, here),
            (conv, fixed),
            (head_par, fixed),
            (spread, fixed),
            (gather, fixed),
            *[(x, fixed) for x in state[:4]],
            (state[4], here),
            (state[5], lanes_of(first)),
        ]
        return call(
            partial(back_kernel, top=first, **sizes),
            count,
            ins,
            [here, lanes_of(first), fixed, fixed, fixed, fixed],
            [
                low(rows, conv_width + LANES),
                full(8, rows),
                full(8, conv_width),
                full(8, LANES),
                full(8, conv_width),
                full(n, width),
            ],
            [
                pltpu.VMEM((BLOCK + 8, conv_width), F32),
                pltpu.VMEM((4 * CHUNK + 16, 2 * width), BF16),
                pltpu.VMEM((CHUNK, 2 * width), BF16),
                pltpu.VMEM((LANES, CHUNK), F32),
            ],
            "mix_back",
            6 * count,
            aliases={len(ins) - 2: 0, len(ins) - 1: 1},
        )

    order_a, order_b = (0, 2, 3, 1), (0, 1, 2, 3)
    grad_out = mm_tn(gz, dbr).astype(BF16)
    grad_gate = mm_tn(normed, dgp).astype(BF16)
    keep, send, gain_part = whole(
        partial(pack_early_kernel, order=order_a),
        (scalars, grad_out, grad_gate, proj_gate),
        [low(width, model), low(width, model), full(8, model)],
        [],
        "pack_early",
        3,
    )

    def halve(keep, send, bit):
        got = swap_dp(send, bit)
        h = keep.shape[0] // 2
        return add_low(keep[:h], got[:h]), add_low(keep[h:], got[h:])

    def finish(keep, send, bit):
        x = add_low(keep, swap_dp(send, bit))
        extra = SHARDS
        while extra < lax.axis_size("dp"):
            x = add_low(x, swap_dp(x, extra.bit_length() - 1))
            extra *= 2
        return x

    zeros = (
        jnp.zeros((8, conv_width), F32),
        jnp.zeros((n, width), F32),
        jnp.zeros((8, conv_width), F32),
        jnp.zeros((8, LANES), F32),
    )
    keep, send = halve(keep, send, order_a[0])
    half = blocks // 2
    blank = (jnp.zeros((rows, conv_width + LANES), BF16), jnp.zeros((8, rows), F32))
    g = after(g, send)
    got = swap_dp(send, order_a[1])
    rest, rd_rest, gconv, ghead, ext_carry, carry = back_part(top, half, g, zeros + blank)
    h = keep.shape[0] // 2
    got, carry = lax.optimization_barrier((got, carry))
    keep, send = add_low(keep[:h], got[:h]), add_low(keep[h:], got[h:])
    carry = after(carry, send)
    got = swap_dp(send, order_a[2])
    rest, rd_rest, gconv, ghead, _, _ = back_part(
        top - half, blocks - half, g, (ext_carry, carry, gconv, ghead, rest, rd_rest)
    )
    h = keep.shape[0] // 2
    got, rest = lax.optimization_barrier((got, rest))
    keep, send = add_low(keep[:h], got[:h]), add_low(keep[h:], got[h:])
    x = finish(keep, send, order_a[3])

    grad_inner = mm_tn(normed, rest[:, :width]).astype(BF16)
    grad_state = mm_tn(rest[:, width:], normed).astype(BF16)
    keep, send = whole(
        partial(pack_late_kernel, order=order_b, heads=heads, state_width=state_width),
        (
            scalars, grad_inner, grad_state, proj_inner, w_state_t, gain, gain_part, gconv, ghead, small
        ),
        [low(LATE_ROWS * SHARDS // 2, model), low(LATE_ROWS * SHARDS // 2, model)],
        [pltpu.VMEM((8 * SHARDS, model), F32)],
        "pack_late",
        3,
    )

    keep, send = halve(keep, send, order_b[0])
    rest = after(rest, send)
    rows_at = lambda w, at: lax.dynamic_slice_in_dim(w, at, width_own, 0)

    def project_back(at):
        return (
            mm_nt(dgp, rows_at(proj_gate, at))
            + mm_nt(rest[:, :width], rows_at(proj_inner, at))
            + mm_nt(rest[:, width:conv_width], rows_at(proj_state, at))
            + mm_nt(rest[:, conv_width:], rows_at(step_weight, at))
        )

    dn_oth = project_back(oth_at).astype(BF16)
    rd_part = rd_gate[0] + rd_rest[0]
    oth_rd = swap_mp(rd_part.reshape(8, rows // 8)).reshape(rows)
    dn_got = swap_mp(dn_oth)
    dn_own = project_back(own_at)

    keep, send = halve(keep, send, order_b[1])
    keep, send = halve(keep, send, order_b[2])
    z = finish(keep, send, order_b[3])
    part = model // SHARDS
    tail = z[part:]
    tail_row = lax.broadcasted_iota(jnp.int32, (LATE_ROWS - part, 1), 0)
    alone = (tail_row >= LATE_ROWS - part - 8) & (tail_row < LATE_ROWS - part - 4)
    tail_f = tail.astype(F32)
    tail = jnp.where(alone, tail_f, tail_f + swap_mp(tail).astype(F32)).astype(BF16)
    z = jnp.concatenate([z[:part], tail])

    for bit in reversed(order_a[1:]):
        x = jnp.concatenate([x, swap_dp(x, bit)])
    grad_proj_out, grad_proj_gate = whole(
        partial(unpack_early_kernel, order=order_a),
        (scalars, x, swap_dp(x, order_a[0])),
        [full(width, model), full(model, width)],
        [],
        "unpack_early",
        4,
        in_vmem=False,
    )
    for bit in reversed(order_b[1:]):
        z = jnp.concatenate([z, swap_dp(z, bit)])
    grad_proj_inner, grad_proj_state, step, grad_conv_inner, singles, grad_conv_state = whole(
        partial(unpack_late_kernel, order=order_b, heads=heads),
        (scalars, z, swap_dp(z, order_b[0])),
        [
            full(model, width),
            full(model, state_width),
            full(heads, 2, model),
            full(4, width),
            full(8, model),
            full(4, state_width),
        ],
        [pltpu.VMEM((state_width, model), F32), pltpu.VMEM((8 * SHARDS, model), F32)],
        "unpack_late",
        4,
        in_vmem=False,
    )
    grad_norm_gain = lax.dynamic_slice_in_dim(singles[4], own_at, width_own, 0)
    grad_skip = jnp.sum(singles[2].reshape(heads, head_dim), axis=1)
    grad_decay_log = singles[3, : 2 * heads].reshape(2, heads)
    grad_step_bias = singles[3, LANES : LANES + 2 * heads].reshape(2, heads)

    seq_mask = (jnp.arange(rows) < lengths[0]).astype(F32)[:, None]
    gate_inv = lax.rsqrt(sums[0] / inner_width + EPSILON)[:, None]
    tokens_f = tokens.astype(F32)
    branch_own = mm(gz, po_own)
    block_out = (tokens_f + seq_mask * gate_inv * (branch_own + branch_got.astype(F32))).astype(BF16)
    oth_f = oth_tokens.astype(F32)
    square = jnp.sum(tokens_f * tokens_f, axis=1, keepdims=True) + jnp.sum(
        oth_f * oth_f, axis=1, keepdims=True
    )
    inv = lax.rsqrt(square / model + EPSILON)
    grad_full = dn_own + dn_got.astype(F32)
    grad_tokens = (
        cotangent.astype(F32)
        + inv * (grad_full * norm_gain.astype(F32)[None])
        - tokens_f * (inv * inv * ((rd_part + oth_rd)[:, None] / model))
    )
    return (
        block_out,
        grad_tokens,
        grad_norm_gain,
        grad_proj_gate,
        grad_proj_inner,
        grad_proj_state,
        step.transpose(2, 1, 0),
        grad_conv_inner,
        singles[0],
        grad_conv_state,
        singles[5, :state_width],
        grad_step_bias,
        grad_decay_log,
        grad_skip,
        singles[1],
        grad_proj_out,
    )


def solution(mesh):
    in_specs = (
        P("dp", "mp"),
        P("mp"),
        P(None, "mp"),
        P(None, "mp"),
        P(),
        P(None, None, "mp"),
        P(None, "mp"),
        P("mp"),
        P(),
        P(),
        P(None, "mp"),
        P(None, "mp"),
        P("mp"),
        P("mp"),
        P("mp", None),
        P("dp"),
        P("dp", "mp"),
    )
    out_specs = (
        P("dp", "mp"),
        P("dp", "mp"),
        P("mp"),
        P(None, "mp"),
        P(None, "mp"),
        P(),
        P(None, None, "mp"),
        P(None, "mp"),
        P("mp"),
        P(),
        P(),
        P(None, "mp"),
        P(None, "mp"),
        P("mp"),
        P("mp"),
        P("mp", None),
    )
    return jax.shard_map(body, mesh=mesh, in_specs=in_specs, out_specs=out_specs, check_vma=False)
```

```python
from functools import partial

import jax
import jax.numpy as jnp
from jax import lax
from jax.experimental import pallas as pl
from jax.experimental.pallas import tpu as pltpu
from jax.sharding import PartitionSpec as P

EPSILON = 1e-05
CHUNK = 128
PROJECT_BLOCK, MIX_BLOCK, GATE_BLOCK, BACK_BLOCK = 256, 256, 256, 128
LANES = 128
F32 = jnp.float32
BF16 = jnp.bfloat16
HIGHEST = lax.Precision.HIGHEST
VMEM_LIMIT = 12 * 1024 * 1024
SHARDS = 16
LOG2_E = 1.4426950408889634
LATE_ROWS = 72


def mm(a, b):
    return jnp.dot(a, b, preferred_element_type=F32)


def mm_nt(a, b):
    return lax.dot_general(a, b, (((1,), (1,)), ((), ())), preferred_element_type=F32)


def mm_tn(a, b):
    return lax.dot_general(a, b, (((0,), (0,)), ((), ())), preferred_element_type=F32)


def split_two(v):
    hi = v.astype(BF16)
    return hi, (v - hi.astype(F32)).astype(BF16)


def expand(v, spread):
    hi, lo = split_two(v)
    return mm(jnp.concatenate([hi, lo], axis=1), spread)


def row_mask(block, rows, length):
    pos = block * rows + lax.broadcasted_iota(jnp.int32, (rows, 1), 0)
    return (pos < length).astype(F32)


def to_row(col_a, col_b):
    rows = col_a.shape[0]
    lane = lax.broadcasted_iota(jnp.int32, (rows, LANES), 1)
    tile = jnp.where(lane == 0, col_a, jnp.where(lane == 1, col_b, 0.0))
    return jnp.transpose(tile)[0:8, :]


def sigmoid(v):
    return 0.5 * jnp.tanh(0.5 * v) + 0.5


def natural(rank, own, oth):
    return jnp.where(
        rank == 0, jnp.concatenate([own, oth], axis=1), jnp.concatenate([oth, own], axis=1)
    )


def eight(row):
    return jnp.broadcast_to(row, (8, row.shape[1]))


def stage_kernel(w_state, w_step, *refs, count, head_dim):
    sources, outs, sems = refs[:count], refs[count:-1], refs[-1]
    spread, gather, w_state_t = outs[count:]
    copies = [
        pltpu.make_async_copy(src, dst, sems.at[k]) for k, (src, dst) in enumerate(zip(sources, outs))
    ]
    for copy in copies:
        copy.start()
    state_width = w_state.shape[1]
    w_state_t[:state_width, :] = jnp.transpose(w_state[...].astype(F32)).astype(BF16)
    w_state_t[state_width:, :] = jnp.transpose(w_step[...].astype(F32)).astype(BF16)
    head = lax.broadcasted_iota(jnp.int32, spread.shape, 1) // head_dim
    row = lax.broadcasted_iota(jnp.int32, spread.shape, 0) % LANES
    spread[...] = jnp.where(head == row, 1.0, 0.0).astype(BF16)
    head = lax.broadcasted_iota(jnp.int32, gather.shape, 0) // head_dim
    lane = lax.broadcasted_iota(jnp.int32, gather.shape, 1)
    gather[...] = jnp.where(head == lane, 1.0, 0.0).astype(BF16)
    for copy in copies:
        copy.wait()


def project_kernel(
    i, scalars, own, oth, gain, w_gate, w_inner, w_state, w_step, conv, head_par, spread,
    normed_ref, gate_ref, pre_ref, slope_ref, hs_ref, act_ref, sact_ref, xd_ref, hf_ref, sb_ref,
    ext, carry, *, heads, width, state_width, block,
):
    @pl.when(i == 0)
    def _():
        ext[0:8, :] = jnp.zeros((8, ext.shape[1]), F32)
        carry[...] = jnp.zeros_like(carry)

    x = natural(scalars[1], own[...], oth[...]).astype(F32)
    inv = lax.rsqrt(jnp.mean(x * x, axis=-1, keepdims=True) + EPSILON)
    normed = (x * inv * gain[...]).astype(BF16)
    normed_ref[...] = normed
    step_pre = mm(normed, w_step[...])
    z = step_pre + head_par[0:1, :]
    dt = jnp.maximum(z, 0.0) + jnp.log1p(jnp.exp(-jnp.abs(z)))
    rate = head_par[1:2, :] * dt
    dtm = dt * row_mask(i, block, scalars[0])
    hs_ref[:, 0:LANES] = z
    hs_ref[:, LANES : 2 * LANES] = dt
    tri_r = lax.broadcasted_iota(jnp.int32, (CHUNK, CHUNK), 0)
    tri_c = lax.broadcasted_iota(jnp.int32, (CHUNK, CHUNK), 1)
    tri = (tri_c <= tri_r).astype(F32)
    is_fwd = lax.broadcasted_iota(jnp.int32, (CHUNK, LANES), 1) < heads
    per = block // CHUNK
    to_spread = [dtm]
    keeps = []
    for c_idx in range(per):
        rows = slice(c_idx * CHUNK, (c_idx + 1) * CHUNK)
        rate_c = rate[rows]
        cum = jnp.dot(tri, rate_c, precision=HIGHEST, preferred_element_type=F32)
        tot = cum[CHUNK - 1 : CHUNK, :]
        cumx = jnp.where(is_fwd, cum, cum - rate_c)
        hs_ref[rows, 2 * LANES : 3 * LANES] = cumx
        hs_ref[rows, 3 * LANES :] = jnp.broadcast_to(tot, (CHUNK, LANES))
        to_spread.append(dtm[rows] * jnp.exp(jnp.where(is_fwd, tot - cumx, cumx)))
        keeps.append(eight(jnp.exp(tot)))
    wide = expand(jnp.concatenate(to_spread + keeps, axis=0), spread[...])

    ext[8 : 8 + block, 0:width] = mm(normed, w_inner[...])
    ext[8 : 8 + block, width:] = mm(normed, w_state[...])
    gate_ref[...] = mm(normed, w_gate[...])
    whole_ext = ext[...]
    pre = whole_ext[8:]
    pre_ref[...] = pre.astype(BF16)
    c = conv[4:5, :] + conv[3:4, :] * pre
    for j in range(3):
        c = c + conv[j : j + 1, :] * pltpu.roll(whole_ext, 3 - j, 0)[8:]
    sg = sigmoid(c)
    both = c * sg
    slope_ref[...] = (sg * (1.0 + c * (1.0 - sg))).astype(BF16)
    ext[0:8, :] = ext[block : block + 8, :]
    act = both[:, :width]
    act_ref[...] = act
    sact = both[:, width:].astype(BF16)
    sact_ref[...] = sact
    xd_ref[:, 0:width] = (act * wide[0:block, :width]).astype(BF16)
    xd_ref[:, width:] = (act * wide[0:block, width:]).astype(BF16)
    n = state_width // 4
    for c_idx in range(per):
        rows = slice(c_idx * CHUNK, (c_idx + 1) * CHUNK)
        coef = wide[block + c_idx * CHUNK : block + (c_idx + 1) * CHUNK]
        keep = wide[2 * block + 8 * c_idx : 2 * block + 8 * c_idx + 1, :width]
        hf_ref[c_idx] = carry[...].astype(BF16)
        carry[...] = carry[...] * keep + mm_tn(
            sact[rows, 0:n], (act[rows] * coef[:, :width]).astype(BF16)
        )
        sb_ref[c_idx] = mm_tn(
            sact[rows, 2 * n : 3 * n], (act[rows] * coef[:, width:]).astype(BF16)
        )


def pair_tiles(pair):
    lane = lax.broadcasted_iota(jnp.int32, (1, pair.shape[1]), 1)
    first = (lane < pair.shape[1] // 2).astype(F32)
    keep_a, keep_b = first.astype(BF16), (1.0 - first).astype(BF16)
    return jnp.concatenate([pair * keep_a, pair * keep_b], axis=0)


def mix_kernel(
    i, scalars, act, sact, hs, xd, hf, sb, head_par, spread, y_ref, hb_ref, carry,
    *, heads, width, state_width, block,
):
    @pl.when(i == 0)
    def _():
        carry[...] = jnp.zeros_like(carry)

    n = state_width // 4
    per = block // CHUNK
    r = lax.broadcasted_iota(jnp.int32, (CHUNK, CHUNK), 0)
    c = lax.broadcasted_iota(jnp.int32, (CHUNK, CHUNK), 1)
    lower = c < r
    upper = c > r
    is_fwd = lax.broadcasted_iota(jnp.int32, (block, LANES), 1) < heads
    cum_all = hs[:, 2 * LANES : 3 * LANES]
    tot_all = hs[:, 3 * LANES :]
    wide = expand(
        jnp.concatenate(
            [jnp.exp(jnp.where(is_fwd, cum_all, tot_all - cum_all))]
            + [jnp.exp(tot_all[k * CHUNK : k * CHUNK + 8]) for k in range(per)]
            + [eight(head_par[2:3, :])],
            axis=0,
        ),
        spread[...],
    )
    skip = wide[block + 8 * per : block + 8 * per + 1]
    for c_idx in reversed(range(per)):
        rows = slice(c_idx * CHUNK, (c_idx + 1) * CHUNK)
        cumx = cum_all[rows] * LOG2_E
        cum_t = jnp.transpose(cumx)
        sact_c = sact[rows, :]
        b_f, c_f = sact_c[:, 0:n], sact_c[:, n : 2 * n]
        b_b, c_b = sact_c[:, 2 * n : 3 * n], sact_c[:, 3 * n :]
        s_f = jnp.where(lower, mm_nt(c_f, b_f), 0.0)
        s_b = jnp.where(upper, mm_nt(c_b, b_b), 0.0)
        hb = carry[...].astype(BF16)
        hb_ref[c_idx] = hb
        in_f = mm(c_f, hf[c_idx])
        in_b = mm(c_b, hb)
        keep = wide[block + 8 * c_idx : block + 8 * c_idx + 1, width:]
        carry[...] = carry[...] * keep + sb[c_idx]
        for p in range(heads // 2):
            lanes = slice(p * LANES, (p + 1) * LANES)
            lanes_b = slice(width + p * LANES, width + (p + 1) * LANES)
            w_f, w_b = [], []
            for h in (2 * p, 2 * p + 1):
                damp = jnp.exp2(
                    jnp.minimum(
                        cumx[:, h : h + 1] - cum_t[h : h + 1, :],
                        cum_t[heads + h : heads + h + 1, :] - cumx[:, heads + h : heads + h + 1],
                    )
                )
                w_f.append((s_f * damp).astype(BF16))
                w_b.append((s_b * damp).astype(BF16))
            out = mm(
                jnp.concatenate(w_f + w_b, axis=1),
                jnp.concatenate([pair_tiles(xd[rows, lanes]), pair_tiles(xd[rows, lanes_b])], axis=0),
            )
            y_ref[rows, lanes] = (
                out
                + wide[rows, lanes] * in_f[:, lanes]
                + wide[rows, lanes_b] * in_b[:, lanes]
                + skip[:, lanes] * act[rows, lanes]
            )


def gate_kernel(i, scalars, y, gate, cown, coth, po, gg, dgn_ref, gz_ref, sums_ref, *, block):
    gp = gate[...]
    gated = y[...] * (gp * sigmoid(gp))
    mask = row_mask(i, block, scalars[0])
    cot = natural(scalars[1], cown[...], coth[...])
    dgn = mm_nt((cot.astype(F32) * mask).astype(BF16), po[...])
    dgn_ref[...] = dgn
    scaled = gated * gg[...]
    gz_ref[...] = scaled.astype(BF16)
    sums_ref[...] = to_row(
        jnp.sum(gated * gated, axis=1, keepdims=True), jnp.sum(dgn * scaled, axis=1, keepdims=True)
    )


def gate_back_kernel(
    i, scalars, sums, gate, y, act, dgn, cown, coth, hs, sact, hf, hb, gg, spread, gather,
    g_ref, dgp_ref, dbr_ref, dc_ref, gb_ref, gf_ref, rd_ref, rows_ref, small_ref, carry, prod,
    *, heads, width, state_width, block, inner_width,
):
    @pl.when(i == 0)
    def _():
        carry[...] = jnp.zeros_like(carry)
        small_ref[...] = jnp.zeros_like(small_ref)

    per = block // CHUNK
    is_fwd = lax.broadcasted_iota(jnp.int32, (block, LANES), 1) < heads
    cum_all = hs[:, 2 * LANES : 3 * LANES]
    tot_all = hs[:, 3 * LANES :]
    wide = expand(
        jnp.concatenate(
            [jnp.exp(jnp.where(is_fwd, cum_all, tot_all - cum_all))]
            + [jnp.exp(tot_all[k * CHUNK : k * CHUNK + 8]) for k in range(per)],
            axis=0,
        ),
        spread[...],
    )
    cols = jnp.transpose(sums[...])
    gate_inv = lax.rsqrt(cols[:, 0:1] / inner_width + EPSILON)
    gate_dot = cols[:, 1:2] / inner_width
    gp = gate[...]
    sg = sigmoid(gp)
    act_gate = gp * sg
    yv = y[...]
    gated = yv * act_gate
    dg = dgn[...]
    small_ref[0:1, :] += jnp.sum(dg * gated * gate_inv, axis=0, keepdims=True)
    d_gated = gate_inv * (dg * gg[...]) - gated * (gate_inv * gate_inv * gate_inv * gate_dot)
    d_gp = d_gated * yv * (sg * (1.0 + gp * (1.0 - sg)))
    dgp_ref[...] = d_gp.astype(BF16)
    rd = jnp.sum(d_gp * gp, axis=1, keepdims=True)
    rd_ref[...] = to_row(rd, jnp.zeros_like(rd))
    d_y = d_gated * act_gate
    g_ref[...] = d_y.astype(BF16)
    small_ref[1:2, :] += jnp.sum(d_y * act[...], axis=0, keepdims=True)
    mask = row_mask(i, block, scalars[0])
    cot = natural(scalars[1], cown[...], coth[...])
    dbr_ref[...] = (cot.astype(F32) * (mask * gate_inv)).astype(BF16)
    n = state_width // 4
    for c_idx in range(per):
        rows = slice(c_idx * CHUNK, (c_idx + 1) * CHUNK)
        dy_c = d_y[rows]
        dyf = dy_c * wide[rows, :width]
        dyb = dy_c * wide[rows, width:]
        prod[rows, 0:width] = (dyf * mm(sact[rows, n : 2 * n], hf[c_idx])).astype(BF16)
        prod[rows, width:] = (dyb * mm(sact[rows, 3 * n :], hb[c_idx])).astype(BF16)
        dyf = dyf.astype(BF16)
        dyb = dyb.astype(BF16)
        dc_ref[rows, 0:n] = mm_nt(dyf, hf[c_idx])
        dc_ref[rows, n : 2 * n] = mm_nt(dyb, hb[c_idx])
        gb_ref[c_idx] = carry[...].astype(BF16)
        keep = wide[block + 8 * c_idx : block + 8 * c_idx + 1, width:]
        carry[...] = carry[...] * keep + mm_tn(sact[rows, 3 * n :], dyb)
        gf_ref[c_idx] = mm_tn(sact[rows, n : 2 * n], dyf)
    rows_ref[...] = mm(prod[...], gather[...])


def back_kernel(
    i, scalars, g, act, sact, hs, xd, row_in, hf, hb, gb, gf, dc, pre, slope, conv, head_par, spread, gather,
    ext_in, carry_in, gconv_in, ghead_in, _rest, _rd, rest_ref, rd_ref, gconv_ref, ghead_ref, ext_out,
    carry, ext, stack, xs, rsum,
    *, heads, width, state_width, block, top,
):
    blk = top - i
    per = block // CHUNK

    @pl.when(i == 0)
    def _():
        ext[block:, :] = ext_in[...]
        carry[...] = carry_in[...]
        gconv_ref[...] = gconv_in[...]
        ghead_ref[...] = ghead_in[...]
        stack[3 * CHUNK : 4 * CHUNK, width:] = jnp.zeros((CHUNK, width), BF16)
        rsum[...] = jnp.zeros_like(rsum)

    n = state_width // 4
    conv_width = width + state_width
    r = lax.broadcasted_iota(jnp.int32, (CHUNK, CHUNK), 0)
    c = lax.broadcasted_iota(jnp.int32, (CHUNK, CHUNK), 1)
    later = c > r
    earlier = c < r
    rev = (c >= r).astype(F32)
    tri = (c <= r).astype(F32)
    is_fwd_all = lax.broadcasted_iota(jnp.int32, (block, LANES), 1) < heads
    is_fwd = lax.broadcasted_iota(jnp.int32, (CHUNK, LANES), 1) < heads
    mask = row_mask(blk, block, scalars[0])
    dt_all = hs[:, LANES : 2 * LANES]
    cum_all = hs[:, 2 * LANES : 3 * LANES]
    tot_all = hs[:, 3 * LANES :]
    wide = expand(
        jnp.concatenate(
            [jnp.exp(jnp.where(is_fwd_all, tot_all - cum_all, cum_all)), dt_all * mask]
            + [jnp.exp(tot_all[k * CHUNK : k * CHUNK + 8]) for k in range(per)]
            + [eight(head_par[2:3, :])],
            axis=0,
        ),
        spread[...],
    )
    skip = wide[2 * block + 8 * per : 2 * block + 8 * per + 1]
    rd_parts = []
    for c_idx in reversed(range(per)):
        rows = slice(c_idx * CHUNK, (c_idx + 1) * CHUNK)
        rows_dt = slice(block + c_idx * CHUNK, block + (c_idx + 1) * CHUNK)
        z = hs[rows, 0:LANES]
        dt = dt_all[rows]
        cumx = cum_all[rows] * LOG2_E
        cum_t = jnp.transpose(cumx)
        sact_c = sact[rows, :]
        b_f, c_f = sact_c[:, 0:n], sact_c[:, n : 2 * n]
        b_b, c_b = sact_c[:, 2 * n : 3 * n], sact_c[:, 3 * n :]
        s_f = jnp.where(later, mm_nt(b_f, c_f), 0.0)
        s_b = jnp.where(earlier, mm_nt(b_b, c_b), 0.0)
        grad_f = carry[...]
        grad_f_low = grad_f.astype(BF16)
        grad_b_low = gb[c_idx]
        keep = wide[2 * block + 8 * c_idx : 2 * block + 8 * c_idx + 1]
        keep_f = keep[:, :width]
        edge_f = keep_f * jnp.sum(grad_f * hf[c_idx].astype(F32), axis=0, keepdims=True)
        edge_b = keep[:, width:] * jnp.sum(
            hb[c_idx].astype(F32) * grad_b_low.astype(F32), axis=0, keepdims=True
        )
        e_hi, e_lo = split_two(eight(jnp.concatenate([edge_f, edge_b], axis=1)))
        stack[4 * CHUNK :, :] = jnp.concatenate([e_hi, e_lo], axis=0)
        carry[...] = grad_f * keep_f + gf[c_idx]
        in_f = mm(b_f, grad_f_low)
        in_b = mm(b_b, grad_b_low)
        d_scores = jnp.zeros((CHUNK, CHUNK), F32)
        for p in range(heads // 2):
            lanes = slice(p * LANES, (p + 1) * LANES)
            lanes_b = slice(width + p * LANES, width + (p + 1) * LANES)
            g_pair = g[rows, lanes]
            xf_pair = xd[rows, lanes]
            xb_pair = xd[rows, lanes_b]
            dw = mm_nt(
                jnp.concatenate([pair_tiles(xf_pair), pair_tiles(xb_pair)], axis=0), g_pair
            )
            w_f, w_b = [], []
            for q, h in enumerate((2 * p, 2 * p + 1)):
                damp = jnp.exp2(
                    jnp.minimum(
                        cum_t[h : h + 1, :] - cumx[:, h : h + 1],
                        cumx[:, heads + h : heads + h + 1] - cum_t[heads + h : heads + h + 1, :],
                    )
                )
                low_f = (s_f * damp).astype(BF16)
                low_b = (s_b * damp).astype(BF16)
                w_f.append(low_f)
                w_b.append(low_b)
                dw_f = dw[q * CHUNK : (q + 1) * CHUNK]
                dw_b = dw[(2 + q) * CHUNK : (3 + q) * CHUNK]
                d_scores = d_scores + jnp.where(later, dw_f, dw_b) * damp
                rsum[h : h + 1, :] = jnp.sum(dw_f * low_f.astype(F32), axis=0, keepdims=True)
                rsum[heads + h : heads + h + 1, :] = -jnp.sum(
                    dw_b * low_b.astype(F32), axis=0, keepdims=True
                )
            dx = mm(
                jnp.concatenate(
                    [jnp.concatenate(w_f, axis=1), jnp.concatenate(w_b, axis=1)], axis=0
                ),
                pair_tiles(g_pair),
            )
            edge_pf = wide[rows, lanes]
            edge_pb = wide[rows, lanes_b]
            intra_f = dx[:CHUNK]
            inter_f = edge_pf * in_f[:, lanes]
            dx_f = intra_f + inter_f
            dx_b = dx[CHUNK:] + edge_pb * in_b[:, lanes]
            xf = xf_pair.astype(F32)
            xb = xb_pair.astype(F32)
            xs[:, lanes] = (xf * edge_pf).astype(BF16)
            xs[:, lanes_b] = (xb * edge_pb).astype(BF16)
            act_p = act[rows, lanes]
            hi, lo = split_two(-(xf * intra_f))
            stack[0:CHUNK, lanes] = hi
            stack[CHUNK : 2 * CHUNK, lanes] = lo
            hi, lo = split_two(xb * dx_b)
            stack[0:CHUNK, lanes_b] = hi
            stack[CHUNK : 2 * CHUNK, lanes_b] = lo
            stack[2 * CHUNK : 3 * CHUNK, lanes] = (act_p * dx_f).astype(BF16)
            stack[2 * CHUNK : 3 * CHUNK, lanes_b] = (act_p * dx_b).astype(BF16)
            stack[3 * CHUNK : 4 * CHUNK, lanes] = (xf * inter_f).astype(BF16)
            d_inner = (
                skip[:, lanes] * g_pair.astype(F32)
                + wide[rows_dt, lanes] * dx_f
                + wide[rows_dt, lanes_b] * dx_b
            )
            ext[rows, lanes] = d_inner * slope[rows, lanes].astype(F32)
        low_f = jnp.where(later, d_scores, 0.0).astype(BF16)
        low_b = jnp.where(earlier, d_scores, 0.0).astype(BF16)
        d_bf = mm(low_f, c_f) + mm_nt(xs[:, :width], grad_f_low)
        d_cf = mm_tn(low_f, b_f) + dc[rows, 0:n]
        d_bb = mm(low_b, c_b) + mm_nt(xs[:, width:], grad_b_low)
        d_cb = mm_tn(low_b, b_b) + dc[rows, n : 2 * n]
        d_state = jnp.concatenate([d_bf, d_cf, d_bb, d_cb], axis=1)
        ext[rows, width:] = d_state * slope[rows, width:].astype(F32)
        head_sums = mm(stack[...], gather[...])
        rin = row_in[rows, :]
        d_cum = (
            head_sums[0:CHUNK]
            + head_sums[CHUNK : 2 * CHUNK]
            + jnp.transpose(rsum[...])
            + jnp.where(is_fwd, rin, 0.0)
        )
        d_run = head_sums[3 * CHUNK : 4 * CHUNK] + jnp.where(is_fwd, 0.0, rin)
        edge = head_sums[4 * CHUNK : 4 * CHUNK + 1] + head_sums[4 * CHUNK + 8 : 4 * CHUNK + 9]
        back_run = jnp.dot(rev, d_cum, precision=HIGHEST, preferred_element_type=F32)
        run = jnp.dot(tri, d_run, precision=HIGHEST, preferred_element_type=F32)
        d_rate = jnp.where(is_fwd, back_run + run - d_run, back_run - d_cum + run) + edge
        neg = head_par[1:2, :]
        d_step = neg * d_rate + mask[rows] * head_sums[2 * CHUNK : 3 * CHUNK]
        d_z = d_step / (1.0 + jnp.exp(-z))
        ghead_ref[0:1, :] += jnp.sum(d_rate * (neg * dt), axis=0, keepdims=True)
        ghead_ref[1:2, :] += jnp.sum(d_z, axis=0, keepdims=True)
        rest_ref[rows, conv_width:] = d_z.astype(BF16)
        rd_parts.append(jnp.sum(d_z * (z - head_par[0:1, :]), axis=1, keepdims=True))

    prev = pre[...].astype(F32)
    whole_ext = ext[...]
    moved = whole_ext[:block]
    acc = conv[3:4, :] * moved
    gconv_ref[4:5, :] += jnp.sum(moved, axis=0, keepdims=True)
    gconv_ref[3:4, :] += jnp.sum(moved * prev, axis=0, keepdims=True)
    for j in range(3):
        moved = pltpu.roll(whole_ext, block + 8 - (3 - j), 0)[:block]
        acc = acc + conv[j : j + 1, :] * moved
        gconv_ref[j : j + 1, :] += jnp.sum(moved * prev, axis=0, keepdims=True)
    rest_ref[:, 0:conv_width] = acc.astype(BF16)
    rd = jnp.sum(acc * prev, axis=1, keepdims=True) + jnp.concatenate(rd_parts[::-1], axis=0)
    rd_ref[...] = to_row(rd, jnp.zeros_like(rd))
    ext[block:, :] = ext[0:8, :]
    ext_out[...] = ext[0:8, :]


def columns_of(scalars, other, size):
    rank = scalars[1]
    return pl.ds(pl.multiple_of((1 - rank if other else rank) * size, LANES), size)


def branch_kernel(scalars, gz, po, out_ref, *, other):
    cols = columns_of(scalars, other, out_ref.shape[1])
    out_ref[...] = mm(gz[...], po[:, cols]).astype(out_ref.dtype)


def back_project_kernel(
    scalars, dgp, rest, w_gate, w_inner, w_state, w_step, out_ref, *, other
):
    at = columns_of(scalars, other, out_ref.shape[1])
    a = w_inner.shape[1]
    b = a + w_state.shape[1]
    out_ref[...] = (
        mm_nt(dgp[...], w_gate[at, :])
        + mm_nt(rest[:, 0:a], w_inner[at, :])
        + mm_nt(rest[:, a:b], w_state[at, :])
        + mm_nt(rest[:, b:], w_step[at, :])
    ).astype(out_ref.dtype)


def home_of(r, me, order):
    j = me % SHARDS
    levels = len(order)
    for p, bit in enumerate(order):
        if (r >> (levels - 1 - p)) & 1:
            j = jnp.bitwise_xor(j, 1 << bit)
    return j


def pack_early_kernel(
    scalars, grad_out, grad_gate, w_gate, keep_ref, send_ref, gain_ref, *, order
):
    hi, lo = split_two(grad_gate[...].astype(F32) * w_gate[...].astype(F32))
    ones = jnp.ones((8, hi.shape[1]), BF16)
    gain_ref[...] = mm_nt(ones, hi) + mm_nt(ones, lo)
    part = grad_out.shape[0] // SHARDS
    for r in range(SHARDS):
        j = home_of(r, scalars[2], order)
        out = keep_ref if r < SHARDS // 2 else send_ref
        at = (r % (SHARDS // 2)) * 2 * part
        src = pl.ds(pl.multiple_of(j * part, part), part)
        out[at : at + part, :] = grad_out[src, :]
        out[at + part : at + 2 * part, :] = grad_gate[src, :]


def unpack_early_kernel(scalars, first, second, out_ref, gate_ref, *, order):
    part = out_ref.shape[0] // SHARDS
    for r in range(SHARDS):
        j = home_of(r, scalars[2], order)
        src = first if r < SHARDS // 2 else second
        at = (r % (SHARDS // 2)) * 2 * part
        dst = pl.ds(pl.multiple_of(j * part, part), part)
        out_ref[dst, :] = src[at : at + part, :].astype(F32)
        gate_ref[dst, :] = src[at + part : at + 2 * part, :].astype(F32)


def pack_late_kernel(
    scalars, inner, state, w_inner, w_state_t, gain, gain_part, gconv, ghead, small,
    keep_ref, send_ref, misc, *, order, heads, state_width,
):
    model, width = w_inner.shape
    hi, lo = split_two(inner[...].astype(F32) * w_inner[...].astype(F32))
    ones = jnp.ones((8, hi.shape[1]), BF16)
    gain_row = (mm_nt(ones, hi) + mm_nt(ones, lo) + gain_part[...])[0:1]
    gain_row += jnp.sum(state[...].astype(F32) * w_state_t[...].astype(F32), axis=0, keepdims=True)
    gain_row = gain_row / gain[...]
    step = state[state_width:, :].astype(F32)
    misc[...] = jnp.zeros_like(misc)

    def put_single(k, row):
        at = (k // 2) * 8 + k % 2
        misc[at : at + 1, :] = row

    for k in range(2 * heads):
        put_single(k, step[k : k + 1, :])
    at = 2 * heads
    for k in range(5):
        put_single(at + k, gconv[k : k + 1, 0:width])
    put_single(at + 5, small[0:1, :])
    put_single(at + 6, small[1:2, :])
    at = ((at + 7) // 2) * 8 + (at + 7) % 2
    misc[at : at + 1, 0:LANES] = ghead[0:1, :]
    misc[at : at + 1, LANES : 2 * LANES] = ghead[1:2, :]
    fit = model // state_width
    for k in range(5):
        at = (k // fit) * 8 + 4
        lanes = slice((k % fit) * state_width, (k % fit + 1) * state_width)
        misc[at : at + 1, lanes] = gconv[k : k + 1, width:]
    at = (-(-5 // fit)) * 8 + 4
    misc[at : at + 1, :] = gain_row
    part = model // SHARDS
    part_s = state_width // SHARDS
    rows = part + part_s + 8
    for r in range(SHARDS):
        j = home_of(r, scalars[2], order)
        out = keep_ref if r < SHARDS // 2 else send_ref
        at = (r % (SHARDS // 2)) * rows
        out[at : at + part, :] = inner[pl.ds(pl.multiple_of(j * part, part), part), :]
        out[at + part : at + part + part_s, :] = state[
            pl.ds(pl.multiple_of(j * part_s, part_s), part_s), :
        ]
        out[at + part + part_s : at + rows, :] = misc[
            pl.ds(pl.multiple_of(j * 8, 8), 8), :
        ].astype(BF16)


def unpack_late_kernel(
    scalars, first, second, inner_ref, state_ref, step_ref, convi_ref, singles_ref, convs_ref,
    state, misc, *, order, heads,
):
    model = inner_ref.shape[0]
    state_width = state_ref.shape[1]
    part = model // SHARDS
    part_s = state_width // SHARDS
    rows = part + part_s + 8
    for r in range(SHARDS):
        j = home_of(r, scalars[2], order)
        src = first if r < SHARDS // 2 else second
        at = (r % (SHARDS // 2)) * rows
        inner_ref[pl.ds(pl.multiple_of(j * part, part), part), :] = src[at : at + part, :].astype(F32)
        state[pl.ds(pl.multiple_of(j * part_s, part_s), part_s), :] = src[
            at + part : at + part + part_s, :
        ].astype(F32)
        misc[pl.ds(pl.multiple_of(j * 8, 8), 8), :] = src[at + part + part_s : at + rows, :].astype(F32)
    state_ref[...] = jnp.transpose(state[...])

    def single(k):
        at = (k // 2) * 8 + k % 2
        return misc[at : at + 1, :]

    for h in range(heads):
        for d in range(2):
            step_ref[h, d : d + 1, :] = single(d * heads + h)
    at = 2 * heads
    for k in range(4):
        convi_ref[k : k + 1, :] = single(at + k)
    singles_ref[0:1, :] = single(at + 4)
    singles_ref[1:2, :] = single(at + 5)
    singles_ref[2:3, :] = single(at + 6)
    singles_ref[3:4, :] = single(at + 7)
    fit = model // state_width
    at = (-(-5 // fit)) * 8 + 4
    singles_ref[4:5, :] = misc[at : at + 1, :]
    singles_ref[5:8, :] = jnp.zeros((3, model), F32)
    for k in range(5):
        at = (k // fit) * 8 + 4
        lanes = slice((k % fit) * state_width, (k % fit + 1) * state_width)
        if k < 4:
            convs_ref[k : k + 1, :] = misc[at : at + 1, lanes]
        else:
            singles_ref[5:6, 0:state_width] = misc[at : at + 1, lanes]


def place(i, top):
    return i if top is None else top - i


def rows_of(block, top=None):
    return lambda ref, i: ref.at[pl.ds(pl.multiple_of(place(i, top) * block, block), block)]


def lanes_of(block, top=None):
    return lambda ref, i: ref.at[:, pl.ds(pl.multiple_of(place(i, top) * block, block), block)]


def states_of(block, top=None):
    per = block // CHUNK
    return lambda ref, i: ref.at[pl.ds(place(i, top) * per, per)]


def fixed(ref, i):
    return ref


def call(kernel, blocks, ins, out_views, out_shape, scratch, name, us, aliases=None):
    views = [view for _, view in ins[1:]] + out_views
    arrays = [ins[0]] + [
        pltpu.with_memory_space_constraint(x, pltpu.VMEM) if view is not fixed else x
        for x, view in ins[1:]
    ]

    def looped(scalars, *refs):
        def step(i, _):
            blocks_of = [view(ref, i) for view, ref in zip(views, refs)]
            kernel(i, scalars, *blocks_of, *refs[len(views) :])
            return 0

        lax.fori_loop(0, blocks, step, 0)

    vmem = pl.BlockSpec(memory_space=pltpu.VMEM)
    return pl.pallas_call(
        looped,
        out_shape=[pltpu.VMEM(o.shape, o.dtype) for o in out_shape],
        in_specs=[pl.BlockSpec(memory_space=pltpu.SMEM)] + [vmem] * (len(arrays) - 1),
        out_specs=[vmem] * len(out_shape),
        scratch_shapes=scratch,
        compiler_params=pltpu.CompilerParams(vmem_limit_bytes=VMEM_LIMIT),
        cost_estimate=pl.CostEstimate(
            flops=int(us * 5e8), transcendentals=0, bytes_accessed=int(us * 3e6)
        ),
        name=name,
        input_output_aliases=aliases or {},
    )(*arrays)


def whole(kernel, args, out_shape, scratch, name, us, in_vmem=True):
    vmem = pl.BlockSpec(memory_space=pltpu.VMEM)
    return pl.pallas_call(
        kernel,
        out_shape=[pltpu.VMEM(o.shape, o.dtype) if in_vmem else o for o in out_shape],
        in_specs=[pl.BlockSpec(memory_space=pltpu.SMEM)] + [vmem] * (len(args) - 1),
        out_specs=[vmem] * len(out_shape),
        scratch_shapes=scratch,
        compiler_params=pltpu.CompilerParams(vmem_limit_bytes=VMEM_LIMIT),
        cost_estimate=pl.CostEstimate(
            flops=int(us * 5e8), transcendentals=0, bytes_accessed=int(us * 3e6)
        ),
        name=name,
    )(*args)


def swap_mp(x):
    return lax.ppermute(x, "mp", [(0, 1), (1, 0)])


def swap_dp(x, bit):
    size = lax.axis_size("dp")
    return lax.ppermute(x, "dp", [(i, i ^ (1 << bit)) for i in range(size)])


def add_low(a, b):
    return (a.astype(F32) + b.astype(F32)).astype(BF16)


def after(x, *others):
    return lax.optimization_barrier((x, *others))[0]


def body(
    tokens,
    norm_gain,
    proj_gate,
    proj_inner,
    proj_state,
    proj_step,
    conv_inner,
    conv_inner_bias,
    conv_state,
    conv_state_bias,
    step_bias,
    decay_log,
    skip_gain,
    gate_gain,
    proj_out,
    lengths,
    cotangent,
):
    rows, width_own = tokens.shape
    model = 2 * width_own
    heads = skip_gain.shape[0]
    width = proj_inner.shape[1]
    head_dim = width // heads
    state_width = proj_state.shape[1]
    n = state_width // 4
    conv_width = width + state_width
    inner_width = width * lax.axis_size("mp")
    chunks = rows // CHUNK
    rank = lax.axis_index("mp")
    shape = jax.ShapeDtypeStruct

    oth_tokens = swap_mp(tokens)
    oth_gain = swap_mp(norm_gain.reshape(1, width_own))
    oth_cot = swap_mp(after(cotangent, oth_tokens))

    scalars = jnp.stack([lengths[0], rank, lax.axis_index("dp")]).astype(jnp.int32)
    step_weight = proj_step.reshape(model, 2 * heads)
    step_weight = jnp.pad(step_weight, ((0, 0), (0, LANES - 2 * heads)))
    own_gain = norm_gain.reshape(1, width_own)
    gain = natural(rank, own_gain, oth_gain).astype(F32)
    conv = jnp.concatenate(
        [
            jnp.concatenate([conv_inner, conv_state], axis=1),
            jnp.concatenate([conv_inner_bias, conv_state_bias])[None],
            jnp.zeros((3, conv_width), F32),
        ]
    )
    head_par = jnp.stack(
        [
            step_bias.reshape(-1),
            -jnp.exp(decay_log.reshape(-1)),
            jnp.pad(skip_gain, (0, heads)),
        ]
    )
    head_par = jnp.pad(head_par, ((0, 5), (0, LANES - 2 * heads)))
    staged = (tokens, cotangent, proj_gate, proj_inner, proj_state, proj_out)
    hbm = pl.BlockSpec(memory_space=pl.ANY)
    vmem = pl.BlockSpec(memory_space=pltpu.VMEM)
    tokens_v, cot_v, gate_v, inner_v, state_v, out_v, spread, gather, w_state_t = pl.pallas_call(
        partial(stage_kernel, count=len(staged), head_dim=head_dim),
        out_shape=[pltpu.VMEM(x.shape, x.dtype) for x in staged]
        + [
            pltpu.VMEM((2 * LANES, 2 * width), BF16),
            pltpu.VMEM((2 * width, LANES), BF16),
            pltpu.VMEM((state_width + LANES, model), BF16),
        ],
        in_specs=[vmem, vmem] + [hbm] * len(staged),
        out_specs=[vmem] * (len(staged) + 3),
        scratch_shapes=[pltpu.SemaphoreType.DMA((len(staged),))],
        compiler_params=pltpu.CompilerParams(vmem_limit_bytes=VMEM_LIMIT),
        name="stage",
    )(proj_state, step_weight, *staged)
    gg = gate_gain[None]

    sizes = dict(heads=heads, width=width, state_width=state_width)
    low = lambda *dims: shape(dims, BF16)
    full = lambda *dims: shape(dims, F32)
    block = PROJECT_BLOCK
    up, states = rows_of(block), states_of(block)
    normed, gate_pre, pre, slope, hs, act, sact, xd, hf, sb = call(
        partial(project_kernel, block=block, **sizes),
        rows // block,
        [
            scalars,
            (tokens_v, up),
            (oth_tokens, up),
            (gain, fixed),
            (gate_v, fixed),
            (inner_v, fixed),
            (state_v, fixed),
            (step_weight, fixed),
            (conv, fixed),
            (head_par, fixed),
            (spread, fixed),
        ],
        [up, up, up, up, up, up, up, up, states, states],
        [
            low(rows, model),
            full(rows, width),
            low(rows, conv_width),
            low(rows, conv_width),
            full(rows, 4 * LANES),
            full(rows, width),
            low(rows, state_width),
            low(rows, 2 * width),
            low(chunks, n, width),
            full(chunks, n, width),
        ],
        [pltpu.VMEM((block + 8, conv_width), F32), pltpu.VMEM((n, width), F32)],
        "project",
        12,
    )

    block = MIX_BLOCK
    top = rows // block - 1
    down, states_down = rows_of(block, top), states_of(block, top)
    y, hb = call(
        partial(mix_kernel, block=block, **sizes),
        rows // block,
        [
            scalars,
            (act, down),
            (sact, down),
            (hs, down),
            (xd, down),
            (hf, states_down),
            (sb, states_down),
            (head_par, fixed),
            (spread, fixed),
        ],
        [down, states_down],
        [full(rows, width), low(chunks, n, width)],
        [pltpu.VMEM((n, width), F32)],
        "mix",
        7,
    )

    block = GATE_BLOCK
    up, states, up_lanes = rows_of(block), states_of(block), lanes_of(block)
    dgn, gz, sums = call(
        partial(gate_kernel, block=block),
        rows // block,
        [
            scalars,
            (y, up),
            (gate_pre, up),
            (cot_v, up),
            (oth_cot, up),
            (out_v, fixed),
            (gg, fixed),
        ],
        [up, up, up_lanes],
        [full(rows, width), low(rows, width), full(8, rows)],
        [],
        "gate",
        3,
    )

    oth_sums = swap_mp(sums)
    branch_oth = whole(
        partial(branch_kernel, other=True), (scalars, gz, out_v), [low(rows, width_own)], [], "branch_oth", 3
    )[0]
    sums = sums + oth_sums
    branch_got = swap_mp(after(branch_oth, sums))
    sums_in = after(sums, branch_oth)

    g, dgp, dbr, dc, gb, gf, rd_gate, row_sums, small = call(
        partial(gate_back_kernel, block=block, inner_width=inner_width, **sizes),
        rows // block,
        [
            scalars,
            (sums_in, up_lanes),
            (gate_pre, up),
            (y, up),
            (act, up),
            (dgn, up),
            (cot_v, up),
            (oth_cot, up),
            (hs, up),
            (sact, up),
            (hf, states),
            (hb, states),
            (gg, fixed),
            (spread, fixed),
            (gather, fixed),
        ],
        [up, up, up, up, states, states, up_lanes, up, fixed],
        [
            low(rows, width),
            low(rows, width),
            low(rows, model),
            full(rows, 2 * n),
            low(chunks, n, width),
            full(chunks, n, width),
            full(8, rows),
            full(rows, LANES),
            full(8, width),
        ],
        [pltpu.VMEM((n, width), F32), pltpu.VMEM((block, 2 * width), BF16)],
        "gate_back",
        8,
    )

    def back_part(first, count, g, state):
        block = BACK_BLOCK
        here, states_here, here_lanes = rows_of(block, first), states_of(block, first), lanes_of(block, first)
        ins = [
            scalars,
            (g, here),
            (act, here),
            (sact, here),
            (hs, here),
            (xd, here),
            (row_sums, here),
            (hf, states_here),
            (hb, states_here),
            (gb, states_here),
            (gf, states_here),
            (dc, here),
            (pre, here),
            (slope, here),
            (conv, fixed),
            (head_par, fixed),
            (spread, fixed),
            (gather, fixed),
            *[(x, fixed) for x in state[:4]],
            (state[4], here),
            (state[5], here_lanes),
        ]
        return call(
            partial(back_kernel, block=block, top=first, **sizes),
            count,
            ins,
            [here, here_lanes, fixed, fixed, fixed, fixed],
            [
                low(rows, conv_width + LANES),
                full(8, rows),
                full(8, conv_width),
                full(8, LANES),
                full(8, conv_width),
                full(n, width),
            ],
            [
                pltpu.VMEM((block + 8, conv_width), F32),
                pltpu.VMEM((4 * CHUNK + 16, 2 * width), BF16),
                pltpu.VMEM((CHUNK, 2 * width), BF16),
                pltpu.VMEM((LANES, CHUNK), F32),
            ],
            "mix_back",
            3 * count,
            aliases={len(ins) - 2: 0, len(ins) - 1: 1},
        )

    order_a, order_b = (0, 2, 1, 3), (0, 1, 2, 3)
    grad_out = mm_tn(gz, dbr).astype(BF16)
    grad_gate = mm_tn(normed, dgp).astype(BF16)
    keep, send, gain_part = whole(
        partial(pack_early_kernel, order=order_a),
        (scalars, grad_out, grad_gate, proj_gate),
        [low(width, model), low(width, model), full(8, model)],
        [],
        "pack_early",
        3,
    )

    def halve(keep, send, bit):
        got = swap_dp(send, bit)
        h = keep.shape[0] // 2
        return add_low(keep[:h], got[:h]), add_low(keep[h:], got[h:])

    def finish(keep, send, bit):
        return rest_of_dp(add_low(keep, swap_dp(send, bit)))

    def rest_of_dp(x):
        extra = SHARDS
        while extra < lax.axis_size("dp"):
            x = add_low(x, swap_dp(x, extra.bit_length() - 1))
            extra *= 2
        return x

    zeros = (
        jnp.zeros((8, conv_width), F32),
        jnp.zeros((n, width), F32),
        jnp.zeros((8, conv_width), F32),
        jnp.zeros((8, LANES), F32),
    )
    keep, send = halve(keep, send, order_a[0])
    state = (
        *zeros,
        jnp.zeros((rows, conv_width + LANES), BF16),
        jnp.zeros((8, rows), F32),
    )
    parts = 4
    count = rows // BACK_BLOCK // parts
    g = after(g, send)
    sent, x = swap_dp(send, order_a[1]), None
    for k in range(parts):
        outs = back_part((parts - k) * count - 1, count, g, state)
        rest, rd_rest, gconv, ghead, ext_carry, carry = outs
        if k > 0:
            sent, carry = lax.optimization_barrier((sent, carry))
            h = keep.shape[0] // 2
            if k < 3:
                keep, send = add_low(keep[:h], sent[:h]), add_low(keep[h:], sent[h:])
                carry = after(carry, send)
                sent = swap_dp(send, order_a[k + 1])
            else:
                x = rest_of_dp(add_low(keep, sent))
        state = (ext_carry, carry, gconv, ghead, rest, rd_rest)

    grad_inner = mm_tn(normed, rest[:, :width]).astype(BF16)
    grad_state = mm_tn(rest[:, width:], normed).astype(BF16)
    keep, send = whole(
        partial(pack_late_kernel, order=order_b, heads=heads, state_width=state_width),
        (
            scalars, grad_inner, grad_state, proj_inner, w_state_t, gain, gain_part, gconv, ghead, small
        ),
        [low(LATE_ROWS * SHARDS // 2, model), low(LATE_ROWS * SHARDS // 2, model)],
        [pltpu.VMEM((8 * SHARDS, model), F32)],
        "pack_late",
        3,
    )

    keep, send = halve(keep, send, order_b[0])
    rest, gz_late, tokens_late, oth_late = lax.optimization_barrier((rest, gz, tokens, oth_tokens, send))[:4]
    back_args = (scalars, dgp, rest, gate_v, inner_v, state_v, step_weight)

    def halve_with(keep, send, bit, *work):
        got = after(swap_dp(send, bit), *work)
        h = keep.shape[0] // 2
        return add_low(keep[:h], got[:h]), add_low(keep[h:], got[h:])

    dn_oth = whole(
        partial(back_project_kernel, other=True), back_args, [low(rows, width_own)], [], "back_oth", 4
    )[0]
    rd_part = rd_gate[0] + rd_rest[0]
    sent = swap_dp(x, order_a[3])
    x = jnp.concatenate([x, sent])
    keep, send = halve_with(keep, send, order_b[1], dn_oth, rd_part, x)
    dn_got = swap_mp(dn_oth)
    oth_rd = swap_mp(rd_part.reshape(8, rows // 8)).reshape(rows)
    dn_own = whole(
        partial(back_project_kernel, other=False), back_args, [full(rows, width_own)], [], "back_own", 4
    )[0]
    x = after(x, send)
    sent = swap_dp(x, order_a[2])
    keep, send = halve_with(keep, send, order_b[2], dn_own)

    seq_mask = (jnp.arange(rows) < lengths[0]).astype(F32)[:, None]
    gate_inv = lax.rsqrt(sums[0] / inner_width + EPSILON)[:, None]
    tokens_f = tokens_late.astype(F32)
    branch_own = whole(
        partial(branch_kernel, other=False), (scalars, gz_late, out_v), [full(rows, width_own)], [], "branch_own", 3
    )[0]
    block_out = (tokens_f + seq_mask * gate_inv * (branch_own + branch_got.astype(F32))).astype(BF16)
    x = jnp.concatenate([x, sent])
    z = rest_of_dp(add_low(keep, after(swap_dp(send, order_b[3]), block_out, x)))
    part = model // SHARDS
    tail = z[part:]
    tail_row = lax.broadcasted_iota(jnp.int32, (LATE_ROWS - part, 1), 0)
    alone = (tail_row >= LATE_ROWS - part - 8) & (tail_row < LATE_ROWS - part - 4)
    tail_f = tail.astype(F32)
    tail = jnp.where(alone, tail_f, tail_f + swap_mp(tail).astype(F32)).astype(BF16)
    z = jnp.concatenate([z[:part], tail])
    z = after(z, dn_got)

    oth_f = oth_late.astype(F32)
    square = jnp.sum(tokens_f * tokens_f, axis=1, keepdims=True) + jnp.sum(
        oth_f * oth_f, axis=1, keepdims=True
    )
    inv = lax.rsqrt(square / model + EPSILON)
    grad_full = dn_own + dn_got.astype(F32)
    grad_tokens = (
        cotangent.astype(F32)
        + inv * (grad_full * norm_gain.astype(F32)[None])
        - tokens_f * (inv * inv * ((rd_part + oth_rd)[:, None] / model))
    )

    z = jnp.concatenate([z, swap_dp(z, order_b[3])])
    z = jnp.concatenate([z, after(swap_dp(z, order_b[2]), grad_tokens)])
    x = after(x, z)
    x = jnp.concatenate([x, swap_dp(x, order_a[1])])
    grad_proj_out, grad_proj_gate = whole(
        partial(unpack_early_kernel, order=order_a),
        (scalars, x, swap_dp(x, order_a[0])),
        [full(width, model), full(model, width)],
        [],
        "unpack_early",
        4,
        in_vmem=False,
    )
    z = jnp.concatenate([z, swap_dp(z, order_b[1])])
    grad_proj_inner, grad_proj_state, step, grad_conv_inner, singles, grad_conv_state = whole(
        partial(unpack_late_kernel, order=order_b, heads=heads),
        (scalars, z, swap_dp(z, order_b[0])),
        [
            full(model, width),
            full(model, state_width),
            full(heads, 2, model),
            full(4, width),
            full(8, model),
            full(4, state_width),
        ],
        [pltpu.VMEM((state_width, model), F32), pltpu.VMEM((8 * SHARDS, model), F32)],
        "unpack_late",
        4,
        in_vmem=False,
    )
    grad_norm_gain = lax.dynamic_slice_in_dim(singles[4], rank * width_own, width_own, 0)
    grad_skip = jnp.sum(singles[2].reshape(heads, head_dim), axis=1)
    grad_decay_log = singles[3, : 2 * heads].reshape(2, heads)
    grad_step_bias = singles[3, LANES : LANES + 2 * heads].reshape(2, heads)

    return (
        block_out,
        grad_tokens,
        grad_norm_gain,
        grad_proj_gate,
        grad_proj_inner,
        grad_proj_state,
        step.transpose(2, 1, 0),
        grad_conv_inner,
        singles[0],
        grad_conv_state,
        singles[5, :state_width],
        grad_step_bias,
        grad_decay_log,
        grad_skip,
        singles[1],
        grad_proj_out,
    )


def solution(mesh):
    in_specs = (
        P("dp", "mp"),
        P("mp"),
        P(None, "mp"),
        P(None, "mp"),
        P(),
        P(None, None, "mp"),
        P(None, "mp"),
        P("mp"),
        P(),
        P(),
        P(None, "mp"),
        P(None, "mp"),
        P("mp"),
        P("mp"),
        P("mp", None),
        P("dp"),
        P("dp", "mp"),
    )
    out_specs = (
        P("dp", "mp"),
        P("dp", "mp"),
        P("mp"),
        P(None, "mp"),
        P(None, "mp"),
        P(),
        P(None, None, "mp"),
        P(None, "mp"),
        P("mp"),
        P(),
        P(),
        P(None, "mp"),
        P(None, "mp"),
        P("mp"),
        P("mp"),
        P("mp", None),
    )
    return jax.shard_map(body, mesh=mesh, in_specs=in_specs, out_specs=out_specs, check_vma=False)
```

```python
from functools import partial

import jax
import jax.numpy as jnp
from jax import lax
from jax.experimental import pallas as pl
from jax.experimental.pallas import tpu as pltpu
from jax.sharding import PartitionSpec as P

EPSILON = 1e-05
CHUNK = 128
PROJECT_BLOCK, MIX_BLOCK, GATE_BLOCK, BACK_BLOCK = 256, 256, 256, 128
LANES = 128
F32 = jnp.float32
BF16 = jnp.bfloat16
HIGHEST = lax.Precision.HIGHEST
VMEM_LIMIT = 12 * 1024 * 1024
SHARDS = 16
LOG2_E = 1.4426950408889634
LATE_ROWS = 72


def mm(a, b):
    return jnp.dot(a, b, preferred_element_type=F32)


def mm_nt(a, b):
    return lax.dot_general(a, b, (((1,), (1,)), ((), ())), preferred_element_type=F32)


def mm_tn(a, b):
    return lax.dot_general(a, b, (((0,), (0,)), ((), ())), preferred_element_type=F32)


def split_two(v):
    hi = v.astype(BF16)
    return hi, (v - hi.astype(F32)).astype(BF16)


def expand(v, spread):
    hi, lo = split_two(v)
    return mm(jnp.concatenate([hi, lo], axis=1), spread)


def row_mask(block, rows, length):
    pos = block * rows + lax.broadcasted_iota(jnp.int32, (rows, 1), 0)
    return (pos < length).astype(F32)


def to_row(col_a, col_b):
    rows = col_a.shape[0]
    lane = lax.broadcasted_iota(jnp.int32, (rows, LANES), 1)
    tile = jnp.where(lane == 0, col_a, jnp.where(lane == 1, col_b, 0.0))
    return jnp.transpose(tile)[0:8, :]


def sigmoid(v):
    return 0.5 * jnp.tanh(0.5 * v) + 0.5


def natural(rank, own, oth):
    return jnp.where(
        rank == 0, jnp.concatenate([own, oth], axis=1), jnp.concatenate([oth, own], axis=1)
    )


def eight(row):
    return jnp.broadcast_to(row, (8, row.shape[1]))


def stage_kernel(w_state, w_step, *refs, count, head_dim):
    sources, outs, sems = refs[:count], refs[count:-1], refs[-1]
    spread, gather, w_state_t = outs[count:]
    copies = [
        pltpu.make_async_copy(src, dst, sems.at[k]) for k, (src, dst) in enumerate(zip(sources, outs))
    ]
    for copy in copies:
        copy.start()
    state_width = w_state.shape[1]
    w_state_t[:state_width, :] = jnp.transpose(w_state[...].astype(F32)).astype(BF16)
    w_state_t[state_width:, :] = jnp.transpose(w_step[...].astype(F32)).astype(BF16)
    head = lax.broadcasted_iota(jnp.int32, spread.shape, 1) // head_dim
    row = lax.broadcasted_iota(jnp.int32, spread.shape, 0) % LANES
    spread[...] = jnp.where(head == row, 1.0, 0.0).astype(BF16)
    head = lax.broadcasted_iota(jnp.int32, gather.shape, 0) // head_dim
    lane = lax.broadcasted_iota(jnp.int32, gather.shape, 1)
    gather[...] = jnp.where(head == lane, 1.0, 0.0).astype(BF16)
    for copy in copies:
        copy.wait()


def project_kernel(
    i, scalars, own, oth, gain, w_gate, w_inner, w_state, w_step, conv, head_par, spread,
    normed_ref, gate_ref, pre_ref, slope_ref, hs_ref, act_ref, sact_ref, xd_ref, hf_ref, sb_ref,
    ext, carry, *, heads, width, state_width, block,
):
    @pl.when(i == 0)
    def _():
        ext[0:8, :] = jnp.zeros((8, ext.shape[1]), F32)
        carry[...] = jnp.zeros_like(carry)

    x = natural(scalars[1], own[...], oth[...]).astype(F32)
    inv = lax.rsqrt(jnp.mean(x * x, axis=-1, keepdims=True) + EPSILON)
    normed = (x * inv * gain[...]).astype(BF16)
    normed_ref[...] = normed
    step_pre = mm(normed, w_step[...])
    z = step_pre + head_par[0:1, :]
    dt = jnp.maximum(z, 0.0) + jnp.log1p(jnp.exp(-jnp.abs(z)))
    rate = head_par[1:2, :] * dt
    dtm = dt * row_mask(i, block, scalars[0])
    hs_ref[:, 0:LANES] = z
    hs_ref[:, LANES : 2 * LANES] = dt
    tri_r = lax.broadcasted_iota(jnp.int32, (CHUNK, CHUNK), 0)
    tri_c = lax.broadcasted_iota(jnp.int32, (CHUNK, CHUNK), 1)
    tri = (tri_c <= tri_r).astype(F32)
    is_fwd = lax.broadcasted_iota(jnp.int32, (CHUNK, LANES), 1) < heads
    per = block // CHUNK
    to_spread = [dtm]
    keeps = []
    for c_idx in range(per):
        rows = slice(c_idx * CHUNK, (c_idx + 1) * CHUNK)
        rate_c = rate[rows]
        cum = jnp.dot(tri, rate_c, precision=HIGHEST, preferred_element_type=F32)
        tot = cum[CHUNK - 1 : CHUNK, :]
        cumx = jnp.where(is_fwd, cum, cum - rate_c)
        hs_ref[rows, 2 * LANES : 3 * LANES] = cumx
        hs_ref[rows, 3 * LANES :] = jnp.broadcast_to(tot, (CHUNK, LANES))
        to_spread.append(dtm[rows] * jnp.exp(jnp.where(is_fwd, tot - cumx, cumx)))
        keeps.append(eight(jnp.exp(tot)))
    wide = expand(jnp.concatenate(to_spread + keeps, axis=0), spread[...])

    ext[8 : 8 + block, 0:width] = mm(normed, w_inner[...])
    ext[8 : 8 + block, width:] = mm(normed, w_state[...])
    gate_ref[...] = mm(normed, w_gate[...])
    whole_ext = ext[...]
    pre = whole_ext[8:]
    pre_ref[...] = pre.astype(BF16)
    c = conv[4:5, :] + conv[3:4, :] * pre
    for j in range(3):
        c = c + conv[j : j + 1, :] * pltpu.roll(whole_ext, 3 - j, 0)[8:]
    sg = sigmoid(c)
    both = c * sg
    slope_ref[...] = (sg * (1.0 + c * (1.0 - sg))).astype(BF16)
    ext[0:8, :] = ext[block : block + 8, :]
    act = both[:, :width]
    act_ref[...] = act
    sact = both[:, width:].astype(BF16)
    sact_ref[...] = sact
    xd_ref[:, 0:width] = (act * wide[0:block, :width]).astype(BF16)
    xd_ref[:, width:] = (act * wide[0:block, width:]).astype(BF16)
    n = state_width // 4
    for c_idx in range(per):
        rows = slice(c_idx * CHUNK, (c_idx + 1) * CHUNK)
        coef = wide[block + c_idx * CHUNK : block + (c_idx + 1) * CHUNK]
        keep = wide[2 * block + 8 * c_idx : 2 * block + 8 * c_idx + 1, :width]
        hf_ref[c_idx] = carry[...].astype(BF16)
        carry[...] = carry[...] * keep + mm_tn(
            sact[rows, 0:n], (act[rows] * coef[:, :width]).astype(BF16)
        )
        sb_ref[c_idx] = mm_tn(
            sact[rows, 2 * n : 3 * n], (act[rows] * coef[:, width:]).astype(BF16)
        )


def pair_tiles(pair):
    lane = lax.broadcasted_iota(jnp.int32, (1, pair.shape[1]), 1)
    first = (lane < pair.shape[1] // 2).astype(F32)
    keep_a, keep_b = first.astype(BF16), (1.0 - first).astype(BF16)
    return jnp.concatenate([pair * keep_a, pair * keep_b], axis=0)


def mix_kernel(
    i, scalars, act, sact, hs, xd, hf, sb, head_par, spread, y_ref, hb_ref, carry,
    *, heads, width, state_width, block,
):
    @pl.when(i == 0)
    def _():
        carry[...] = jnp.zeros_like(carry)

    n = state_width // 4
    per = block // CHUNK
    r = lax.broadcasted_iota(jnp.int32, (CHUNK, CHUNK), 0)
    c = lax.broadcasted_iota(jnp.int32, (CHUNK, CHUNK), 1)
    lower = c < r
    upper = c > r
    is_fwd = lax.broadcasted_iota(jnp.int32, (block, LANES), 1) < heads
    cum_all = hs[:, 2 * LANES : 3 * LANES]
    tot_all = hs[:, 3 * LANES :]
    wide = expand(
        jnp.concatenate(
            [jnp.exp(jnp.where(is_fwd, cum_all, tot_all - cum_all))]
            + [jnp.exp(tot_all[k * CHUNK : k * CHUNK + 8]) for k in range(per)]
            + [eight(head_par[2:3, :])],
            axis=0,
        ),
        spread[...],
    )
    skip = wide[block + 8 * per : block + 8 * per + 1]
    for c_idx in reversed(range(per)):
        rows = slice(c_idx * CHUNK, (c_idx + 1) * CHUNK)
        cumx = cum_all[rows] * LOG2_E
        cum_t = jnp.transpose(cumx)
        sact_c = sact[rows, :]
        b_f, c_f = sact_c[:, 0:n], sact_c[:, n : 2 * n]
        b_b, c_b = sact_c[:, 2 * n : 3 * n], sact_c[:, 3 * n :]
        s_f = jnp.where(lower, mm_nt(c_f, b_f), 0.0)
        s_b = jnp.where(upper, mm_nt(c_b, b_b), 0.0)
        hb = carry[...].astype(BF16)
        hb_ref[c_idx] = hb
        in_f = mm(c_f, hf[c_idx])
        in_b = mm(c_b, hb)
        keep = wide[block + 8 * c_idx : block + 8 * c_idx + 1, width:]
        carry[...] = carry[...] * keep + sb[c_idx]
        for p in range(heads // 2):
            lanes = slice(p * LANES, (p + 1) * LANES)
            lanes_b = slice(width + p * LANES, width + (p + 1) * LANES)
            w_f, w_b = [], []
            for h in (2 * p, 2 * p + 1):
                damp = jnp.exp2(
                    jnp.minimum(
                        cumx[:, h : h + 1] - cum_t[h : h + 1, :],
                        cum_t[heads + h : heads + h + 1, :] - cumx[:, heads + h : heads + h + 1],
                    )
                )
                w_f.append((s_f * damp).astype(BF16))
                w_b.append((s_b * damp).astype(BF16))
            out = mm(
                jnp.concatenate(w_f + w_b, axis=1),
                jnp.concatenate([pair_tiles(xd[rows, lanes]), pair_tiles(xd[rows, lanes_b])], axis=0),
            )
            y_ref[rows, lanes] = (
                out
                + wide[rows, lanes] * in_f[:, lanes]
                + wide[rows, lanes_b] * in_b[:, lanes]
                + skip[:, lanes] * act[rows, lanes]
            )


def gate_kernel(i, scalars, y, gate, cown, coth, po, gg, dgn_ref, gz_ref, sums_ref, *, block):
    gp = gate[...]
    gated = y[...] * (gp * sigmoid(gp))
    mask = row_mask(i, block, scalars[0])
    cot = natural(scalars[1], cown[...], coth[...])
    dgn = mm_nt((cot.astype(F32) * mask).astype(BF16), po[...])
    dgn_ref[...] = dgn
    scaled = gated * gg[...]
    gz_ref[...] = scaled.astype(BF16)
    sums_ref[...] = to_row(
        jnp.sum(gated * gated, axis=1, keepdims=True), jnp.sum(dgn * scaled, axis=1, keepdims=True)
    )


def gate_back_kernel(
    i, scalars, sums, gate, y, act, dgn, cown, coth, hs, sact, hf, hb, gg, spread, gather,
    g_ref, dgp_ref, dbr_ref, dc_ref, gb_ref, gf_ref, rd_ref, rows_ref, small_ref, carry, prod,
    *, heads, width, state_width, block, inner_width,
):
    @pl.when(i == 0)
    def _():
        carry[...] = jnp.zeros_like(carry)
        small_ref[...] = jnp.zeros_like(small_ref)

    per = block // CHUNK
    is_fwd = lax.broadcasted_iota(jnp.int32, (block, LANES), 1) < heads
    cum_all = hs[:, 2 * LANES : 3 * LANES]
    tot_all = hs[:, 3 * LANES :]
    wide = expand(
        jnp.concatenate(
            [jnp.exp(jnp.where(is_fwd, cum_all, tot_all - cum_all))]
            + [jnp.exp(tot_all[k * CHUNK : k * CHUNK + 8]) for k in range(per)],
            axis=0,
        ),
        spread[...],
    )
    cols = jnp.transpose(sums[...])
    gate_inv = lax.rsqrt(cols[:, 0:1] / inner_width + EPSILON)
    gate_dot = cols[:, 1:2] / inner_width
    gp = gate[...]
    sg = sigmoid(gp)
    act_gate = gp * sg
    yv = y[...]
    gated = yv * act_gate
    dg = dgn[...]
    small_ref[0:1, :] += jnp.sum(dg * gated * gate_inv, axis=0, keepdims=True)
    d_gated = gate_inv * (dg * gg[...]) - gated * (gate_inv * gate_inv * gate_inv * gate_dot)
    d_gp = d_gated * yv * (sg * (1.0 + gp * (1.0 - sg)))
    dgp_ref[...] = d_gp.astype(BF16)
    rd = jnp.sum(d_gp * gp, axis=1, keepdims=True)
    rd_ref[...] = to_row(rd, jnp.zeros_like(rd))
    d_y = d_gated * act_gate
    g_ref[...] = d_y.astype(BF16)
    small_ref[1:2, :] += jnp.sum(d_y * act[...], axis=0, keepdims=True)
    mask = row_mask(i, block, scalars[0])
    cot = natural(scalars[1], cown[...], coth[...])
    dbr_ref[...] = (cot.astype(F32) * (mask * gate_inv)).astype(BF16)
    n = state_width // 4
    for c_idx in range(per):
        rows = slice(c_idx * CHUNK, (c_idx + 1) * CHUNK)
        dy_c = d_y[rows]
        dyf = dy_c * wide[rows, :width]
        dyb = dy_c * wide[rows, width:]
        prod[rows, 0:width] = (dyf * mm(sact[rows, n : 2 * n], hf[c_idx])).astype(BF16)
        prod[rows, width:] = (dyb * mm(sact[rows, 3 * n :], hb[c_idx])).astype(BF16)
        dyf = dyf.astype(BF16)
        dyb = dyb.astype(BF16)
        dc_ref[rows, 0:n] = mm_nt(dyf, hf[c_idx])
        dc_ref[rows, n : 2 * n] = mm_nt(dyb, hb[c_idx])
        gb_ref[c_idx] = carry[...].astype(BF16)
        keep = wide[block + 8 * c_idx : block + 8 * c_idx + 1, width:]
        carry[...] = carry[...] * keep + mm_tn(sact[rows, 3 * n :], dyb)
        gf_ref[c_idx] = mm_tn(sact[rows, n : 2 * n], dyf)
    rows_ref[...] = mm(prod[...], gather[...])


def back_kernel(
    i, scalars, g, act, sact, hs, xd, row_in, hf, hb, gb, gf, dc, pre, slope, conv, head_par, spread, gather,
    ext_in, carry_in, gconv_in, ghead_in, _rest, _rd, rest_ref, rd_ref, gconv_ref, ghead_ref, ext_out,
    carry, ext, stack, xs, rsum,
    *, heads, width, state_width, block, top,
):
    blk = top - i
    per = block // CHUNK

    @pl.when(i == 0)
    def _():
        ext[block:, :] = ext_in[...]
        carry[...] = carry_in[...]
        gconv_ref[...] = gconv_in[...]
        ghead_ref[...] = ghead_in[...]
        stack[3 * CHUNK : 4 * CHUNK, width:] = jnp.zeros((CHUNK, width), BF16)
        rsum[...] = jnp.zeros_like(rsum)

    n = state_width // 4
    conv_width = width + state_width
    r = lax.broadcasted_iota(jnp.int32, (CHUNK, CHUNK), 0)
    c = lax.broadcasted_iota(jnp.int32, (CHUNK, CHUNK), 1)
    later = c > r
    earlier = c < r
    rev = (c >= r).astype(F32)
    tri = (c <= r).astype(F32)
    is_fwd_all = lax.broadcasted_iota(jnp.int32, (block, LANES), 1) < heads
    is_fwd = lax.broadcasted_iota(jnp.int32, (CHUNK, LANES), 1) < heads
    mask = row_mask(blk, block, scalars[0])
    dt_all = hs[:, LANES : 2 * LANES]
    cum_all = hs[:, 2 * LANES : 3 * LANES]
    tot_all = hs[:, 3 * LANES :]
    wide = expand(
        jnp.concatenate(
            [jnp.exp(jnp.where(is_fwd_all, tot_all - cum_all, cum_all)), dt_all * mask]
            + [jnp.exp(tot_all[k * CHUNK : k * CHUNK + 8]) for k in range(per)]
            + [eight(head_par[2:3, :])],
            axis=0,
        ),
        spread[...],
    )
    skip = wide[2 * block + 8 * per : 2 * block + 8 * per + 1]
    rd_parts = []
    for c_idx in reversed(range(per)):
        rows = slice(c_idx * CHUNK, (c_idx + 1) * CHUNK)
        rows_dt = slice(block + c_idx * CHUNK, block + (c_idx + 1) * CHUNK)
        z = hs[rows, 0:LANES]
        dt = dt_all[rows]
        cumx = cum_all[rows] * LOG2_E
        cum_t = jnp.transpose(cumx)
        sact_c = sact[rows, :]
        b_f, c_f = sact_c[:, 0:n], sact_c[:, n : 2 * n]
        b_b, c_b = sact_c[:, 2 * n : 3 * n], sact_c[:, 3 * n :]
        s_f = jnp.where(later, mm_nt(b_f, c_f), 0.0)
        s_b = jnp.where(earlier, mm_nt(b_b, c_b), 0.0)
        grad_f = carry[...]
        grad_f_low = grad_f.astype(BF16)
        grad_b_low = gb[c_idx]
        keep = wide[2 * block + 8 * c_idx : 2 * block + 8 * c_idx + 1]
        keep_f = keep[:, :width]
        edge_f = keep_f * jnp.sum(grad_f * hf[c_idx].astype(F32), axis=0, keepdims=True)
        edge_b = keep[:, width:] * jnp.sum(
            hb[c_idx].astype(F32) * grad_b_low.astype(F32), axis=0, keepdims=True
        )
        e_hi, e_lo = split_two(eight(jnp.concatenate([edge_f, edge_b], axis=1)))
        stack[4 * CHUNK :, :] = jnp.concatenate([e_hi, e_lo], axis=0)
        carry[...] = grad_f * keep_f + gf[c_idx]
        in_f = mm(b_f, grad_f_low)
        in_b = mm(b_b, grad_b_low)
        d_scores = jnp.zeros((CHUNK, CHUNK), F32)
        for p in range(heads // 2):
            lanes = slice(p * LANES, (p + 1) * LANES)
            lanes_b = slice(width + p * LANES, width + (p + 1) * LANES)
            g_pair = g[rows, lanes]
            xf_pair = xd[rows, lanes]
            xb_pair = xd[rows, lanes_b]
            dw = mm_nt(
                jnp.concatenate([pair_tiles(xf_pair), pair_tiles(xb_pair)], axis=0), g_pair
            )
            w_f, w_b = [], []
            for q, h in enumerate((2 * p, 2 * p + 1)):
                damp = jnp.exp2(
                    jnp.minimum(
                        cum_t[h : h + 1, :] - cumx[:, h : h + 1],
                        cumx[:, heads + h : heads + h + 1] - cum_t[heads + h : heads + h + 1, :],
                    )
                )
                low_f = (s_f * damp).astype(BF16)
                low_b = (s_b * damp).astype(BF16)
                w_f.append(low_f)
                w_b.append(low_b)
                dw_f = dw[q * CHUNK : (q + 1) * CHUNK]
                dw_b = dw[(2 + q) * CHUNK : (3 + q) * CHUNK]
                d_scores = d_scores + jnp.where(later, dw_f, dw_b) * damp
                rsum[h : h + 1, :] = jnp.sum(dw_f * low_f.astype(F32), axis=0, keepdims=True)
                rsum[heads + h : heads + h + 1, :] = -jnp.sum(
                    dw_b * low_b.astype(F32), axis=0, keepdims=True
                )
            dx = mm(
                jnp.concatenate(
                    [jnp.concatenate(w_f, axis=1), jnp.concatenate(w_b, axis=1)], axis=0
                ),
                pair_tiles(g_pair),
            )
            edge_pf = wide[rows, lanes]
            edge_pb = wide[rows, lanes_b]
            intra_f = dx[:CHUNK]
            inter_f = edge_pf * in_f[:, lanes]
            dx_f = intra_f + inter_f
            dx_b = dx[CHUNK:] + edge_pb * in_b[:, lanes]
            xf = xf_pair.astype(F32)
            xb = xb_pair.astype(F32)
            xs[:, lanes] = (xf * edge_pf).astype(BF16)
            xs[:, lanes_b] = (xb * edge_pb).astype(BF16)
            act_p = act[rows, lanes]
            hi, lo = split_two(-(xf * intra_f))
            stack[0:CHUNK, lanes] = hi
            stack[CHUNK : 2 * CHUNK, lanes] = lo
            hi, lo = split_two(xb * dx_b)
            stack[0:CHUNK, lanes_b] = hi
            stack[CHUNK : 2 * CHUNK, lanes_b] = lo
            stack[2 * CHUNK : 3 * CHUNK, lanes] = (act_p * dx_f).astype(BF16)
            stack[2 * CHUNK : 3 * CHUNK, lanes_b] = (act_p * dx_b).astype(BF16)
            stack[3 * CHUNK : 4 * CHUNK, lanes] = (xf * inter_f).astype(BF16)
            d_inner = (
                skip[:, lanes] * g_pair.astype(F32)
                + wide[rows_dt, lanes] * dx_f
                + wide[rows_dt, lanes_b] * dx_b
            )
            ext[rows, lanes] = d_inner * slope[rows, lanes].astype(F32)
        low_f = jnp.where(later, d_scores, 0.0).astype(BF16)
        low_b = jnp.where(earlier, d_scores, 0.0).astype(BF16)
        d_bf = mm(low_f, c_f) + mm_nt(xs[:, :width], grad_f_low)
        d_cf = mm_tn(low_f, b_f) + dc[rows, 0:n]
        d_bb = mm(low_b, c_b) + mm_nt(xs[:, width:], grad_b_low)
        d_cb = mm_tn(low_b, b_b) + dc[rows, n : 2 * n]
        d_state = jnp.concatenate([d_bf, d_cf, d_bb, d_cb], axis=1)
        ext[rows, width:] = d_state * slope[rows, width:].astype(F32)
        head_sums = mm(stack[...], gather[...])
        rin = row_in[rows, :]
        d_cum = (
            head_sums[0:CHUNK]
            + head_sums[CHUNK : 2 * CHUNK]
            + jnp.transpose(rsum[...])
            + jnp.where(is_fwd, rin, 0.0)
        )
        d_run = head_sums[3 * CHUNK : 4 * CHUNK] + jnp.where(is_fwd, 0.0, rin)
        edge = head_sums[4 * CHUNK : 4 * CHUNK + 1] + head_sums[4 * CHUNK + 8 : 4 * CHUNK + 9]
        back_run = jnp.dot(rev, d_cum, precision=HIGHEST, preferred_element_type=F32)
        run = jnp.dot(tri, d_run, precision=HIGHEST, preferred_element_type=F32)
        d_rate = jnp.where(is_fwd, back_run + run - d_run, back_run - d_cum + run) + edge
        neg = head_par[1:2, :]
        d_step = neg * d_rate + mask[rows] * head_sums[2 * CHUNK : 3 * CHUNK]
        d_z = d_step / (1.0 + jnp.exp(-z))
        ghead_ref[0:1, :] += jnp.sum(d_rate * (neg * dt), axis=0, keepdims=True)
        ghead_ref[1:2, :] += jnp.sum(d_z, axis=0, keepdims=True)
        rest_ref[rows, conv_width:] = d_z.astype(BF16)
        rd_parts.append(jnp.sum(d_z * (z - head_par[0:1, :]), axis=1, keepdims=True))

    prev = pre[...].astype(F32)
    whole_ext = ext[...]
    moved = whole_ext[:block]
    acc = conv[3:4, :] * moved
    gconv_ref[4:5, :] += jnp.sum(moved, axis=0, keepdims=True)
    gconv_ref[3:4, :] += jnp.sum(moved * prev, axis=0, keepdims=True)
    for j in range(3):
        moved = pltpu.roll(whole_ext, block + 8 - (3 - j), 0)[:block]
        acc = acc + conv[j : j + 1, :] * moved
        gconv_ref[j : j + 1, :] += jnp.sum(moved * prev, axis=0, keepdims=True)
    rest_ref[:, 0:conv_width] = acc.astype(BF16)
    rd = jnp.sum(acc * prev, axis=1, keepdims=True) + jnp.concatenate(rd_parts[::-1], axis=0)
    rd_ref[...] = to_row(rd, jnp.zeros_like(rd))
    ext[block:, :] = ext[0:8, :]
    ext_out[...] = ext[0:8, :]


def columns_of(scalars, other, size):
    rank = scalars[1]
    return pl.ds(pl.multiple_of((1 - rank if other else rank) * size, LANES), size)


def branch_kernel(scalars, gz, po, out_ref, *, other):
    cols = columns_of(scalars, other, out_ref.shape[1])
    out_ref[...] = mm(gz[...], po[:, cols]).astype(out_ref.dtype)


def back_project_kernel(
    scalars, dgp, rest, w_gate, w_inner, w_state, w_step, out_ref, *, other
):
    at = columns_of(scalars, other, out_ref.shape[1])
    a = w_inner.shape[1]
    b = a + w_state.shape[1]
    out_ref[...] = (
        mm_nt(dgp[...], w_gate[at, :])
        + mm_nt(rest[:, 0:a], w_inner[at, :])
        + mm_nt(rest[:, a:b], w_state[at, :])
        + mm_nt(rest[:, b:], w_step[at, :])
    ).astype(out_ref.dtype)


def home_of(r, me, order):
    j = me % SHARDS
    levels = len(order)
    for p, bit in enumerate(order):
        if (r >> (levels - 1 - p)) & 1:
            j = jnp.bitwise_xor(j, 1 << bit)
    return j


def pack_early_kernel(
    scalars, grad_out, grad_gate, w_gate, keep_ref, send_ref, gain_ref, *, order
):
    hi, lo = split_two(grad_gate[...].astype(F32) * w_gate[...].astype(F32))
    ones = jnp.ones((8, hi.shape[1]), BF16)
    gain_ref[...] = mm_nt(ones, hi) + mm_nt(ones, lo)
    part = grad_out.shape[0] // SHARDS
    for r in range(SHARDS):
        j = home_of(r, scalars[2], order)
        out = keep_ref if r < SHARDS // 2 else send_ref
        at = (r % (SHARDS // 2)) * 2 * part
        src = pl.ds(pl.multiple_of(j * part, part), part)
        out[at : at + part, :] = grad_out[src, :]
        out[at + part : at + 2 * part, :] = grad_gate[src, :]


def unpack_early_kernel(scalars, first, second, out_ref, gate_ref, *, order):
    part = out_ref.shape[0] // SHARDS
    for r in range(SHARDS):
        j = home_of(r, scalars[2], order)
        src = first if r < SHARDS // 2 else second
        at = (r % (SHARDS // 2)) * 2 * part
        dst = pl.ds(pl.multiple_of(j * part, part), part)
        out_ref[dst, :] = src[at : at + part, :].astype(F32)
        gate_ref[dst, :] = src[at + part : at + 2 * part, :].astype(F32)


def pack_late_kernel(
    scalars, inner, state, w_inner, w_state_t, gain, gain_part, gconv, ghead, small, gather,
    keep_ref, send_ref, misc, *, order, heads, state_width,
):
    model, width = w_inner.shape
    hi, lo = split_two(inner[...].astype(F32) * w_inner[...].astype(F32))
    ones = jnp.ones((8, hi.shape[1]), BF16)
    gain_row = (mm_nt(ones, hi) + mm_nt(ones, lo) + gain_part[...])[0:1]
    gain_row += jnp.sum(state[...].astype(F32) * w_state_t[...].astype(F32), axis=0, keepdims=True)
    gain_row = gain_row / gain[...]
    step = state[state_width:, :].astype(F32)
    misc[...] = jnp.zeros_like(misc)

    def put_single(k, row):
        at = (k // 2) * 8 + k % 2
        misc[at : at + 1, :] = row

    for k in range(2 * heads):
        put_single(k, step[k : k + 1, :])
    at = 2 * heads
    for k in range(5):
        put_single(at + k, gconv[k : k + 1, 0:width])
    put_single(at + 5, small[0:1, :])
    hi, lo = split_two(eight(small[1:2, :]))
    skip = mm(hi, gather[0:width, :]) + mm(lo, gather[0:width, :])
    at = ((at + 6) // 2) * 8 + (at + 6) % 2
    misc[at : at + 1, 2 * LANES : 3 * LANES] = skip[0:1]
    misc[at : at + 1, 0:LANES] = ghead[0:1, :]
    misc[at : at + 1, LANES : 2 * LANES] = ghead[1:2, :]
    fit = model // state_width
    for k in range(5):
        at = (k // fit) * 8 + 4
        lanes = slice((k % fit) * state_width, (k % fit + 1) * state_width)
        misc[at : at + 1, lanes] = gconv[k : k + 1, width:]
    at = (-(-5 // fit)) * 8 + 4
    misc[at : at + 1, :] = gain_row
    part = model // SHARDS
    part_s = state_width // SHARDS
    rows = part + part_s + 8
    for r in range(SHARDS):
        j = home_of(r, scalars[2], order)
        out = keep_ref if r < SHARDS // 2 else send_ref
        at = (r % (SHARDS // 2)) * rows
        out[at : at + part, :] = inner[pl.ds(pl.multiple_of(j * part, part), part), :]
        out[at + part : at + part + part_s, :] = state[
            pl.ds(pl.multiple_of(j * part_s, part_s), part_s), :
        ]
        out[at + part + part_s : at + rows, :] = misc[
            pl.ds(pl.multiple_of(j * 8, 8), 8), :
        ].astype(BF16)


def unpack_late_kernel(
    scalars, first, second, inner_ref, state_ref, step_ref, convi_ref, convi_b_ref, convs_ref, convs_b_ref,
    gg_ref, bias_ref, decay_ref, skip_ref, gain_ref, state, misc, *, order, heads,
):
    model = inner_ref.shape[0]
    state_width = state_ref.shape[1]
    part = model // SHARDS
    part_s = state_width // SHARDS
    rows = part + part_s + 8
    for r in range(SHARDS):
        j = home_of(r, scalars[2], order)
        src = first if r < SHARDS // 2 else second
        at = (r % (SHARDS // 2)) * rows
        inner_ref[pl.ds(pl.multiple_of(j * part, part), part), :] = src[at : at + part, :].astype(F32)
        state[pl.ds(pl.multiple_of(j * part_s, part_s), part_s), :] = src[
            at + part : at + part + part_s, :
        ].astype(F32)
        misc[pl.ds(pl.multiple_of(j * 8, 8), 8), :] = src[at + part + part_s : at + rows, :].astype(F32)
    state_ref[...] = jnp.transpose(state[...])

    def single(k):
        at = (k // 2) * 8 + k % 2
        return misc[at : at + 1, :]

    for h in range(heads):
        for d in range(2):
            step_ref[h, d : d + 1, :] = single(d * heads + h)
    at = 2 * heads
    for k in range(4):
        convi_ref[k : k + 1, :] = single(at + k)
    convi_b_ref[...] = single(at + 4)
    gg_ref[...] = single(at + 5)
    head_row = single(at + 6)
    for d in range(2):
        decay_ref[d : d + 1, :] = head_row[:, d * heads : (d + 1) * heads]
        bias_ref[d : d + 1, :] = head_row[:, LANES + d * heads : LANES + (d + 1) * heads]
    skip_ref[...] = head_row[:, 2 * LANES : 2 * LANES + heads]
    fit = model // state_width
    for k in range(5):
        at = (k // fit) * 8 + 4
        lanes = slice((k % fit) * state_width, (k % fit + 1) * state_width)
        out, row = (convs_ref, k) if k < 4 else (convs_b_ref, 0)
        out[row : row + 1, :] = misc[at : at + 1, lanes]
    at = (-(-5 // fit)) * 8 + 4
    half = model // 2
    gain_ref[...] = jnp.where(
        scalars[1] == 0, misc[at : at + 1, :half], misc[at : at + 1, half:]
    )


def place(i, top):
    return i if top is None else top - i


def rows_of(block, top=None):
    return lambda ref, i: ref.at[pl.ds(pl.multiple_of(place(i, top) * block, block), block)]


def lanes_of(block, top=None):
    return lambda ref, i: ref.at[:, pl.ds(pl.multiple_of(place(i, top) * block, block), block)]


def states_of(block, top=None):
    per = block // CHUNK
    return lambda ref, i: ref.at[pl.ds(place(i, top) * per, per)]


def fixed(ref, i):
    return ref


def call(kernel, blocks, ins, out_views, out_shape, scratch, name, us, aliases=None):
    views = [view for _, view in ins[1:]] + out_views
    arrays = [ins[0]] + [
        pltpu.with_memory_space_constraint(x, pltpu.VMEM) if view is not fixed else x
        for x, view in ins[1:]
    ]

    def looped(scalars, *refs):
        def step(i, _):
            blocks_of = [view(ref, i) for view, ref in zip(views, refs)]
            kernel(i, scalars, *blocks_of, *refs[len(views) :])
            return 0

        lax.fori_loop(0, blocks, step, 0)

    vmem = pl.BlockSpec(memory_space=pltpu.VMEM)
    return pl.pallas_call(
        looped,
        out_shape=[pltpu.VMEM(o.shape, o.dtype) for o in out_shape],
        in_specs=[pl.BlockSpec(memory_space=pltpu.SMEM)] + [vmem] * (len(arrays) - 1),
        out_specs=[vmem] * len(out_shape),
        scratch_shapes=scratch,
        compiler_params=pltpu.CompilerParams(vmem_limit_bytes=VMEM_LIMIT),
        cost_estimate=pl.CostEstimate(
            flops=int(us * 5e8), transcendentals=0, bytes_accessed=int(us * 3e6)
        ),
        name=name,
        input_output_aliases=aliases or {},
    )(*arrays)


def whole(kernel, args, out_shape, scratch, name, us, in_vmem=True):
    vmem = pl.BlockSpec(memory_space=pltpu.VMEM)
    return pl.pallas_call(
        kernel,
        out_shape=[pltpu.VMEM(o.shape, o.dtype) if in_vmem else o for o in out_shape],
        in_specs=[pl.BlockSpec(memory_space=pltpu.SMEM)] + [vmem] * (len(args) - 1),
        out_specs=[vmem] * len(out_shape),
        scratch_shapes=scratch,
        compiler_params=pltpu.CompilerParams(vmem_limit_bytes=VMEM_LIMIT),
        cost_estimate=pl.CostEstimate(
            flops=int(us * 5e8), transcendentals=0, bytes_accessed=int(us * 3e6)
        ),
        name=name,
    )(*args)


def swap_mp(x):
    return lax.ppermute(x, "mp", [(0, 1), (1, 0)])


def swap_dp(x, bit):
    size = lax.axis_size("dp")
    return lax.ppermute(x, "dp", [(i, i ^ (1 << bit)) for i in range(size)])


def add_low(a, b):
    return (a.astype(F32) + b.astype(F32)).astype(BF16)


def after(x, *others):
    return lax.optimization_barrier((x, *others))[0]


def body(
    tokens,
    norm_gain,
    proj_gate,
    proj_inner,
    proj_state,
    proj_step,
    conv_inner,
    conv_inner_bias,
    conv_state,
    conv_state_bias,
    step_bias,
    decay_log,
    skip_gain,
    gate_gain,
    proj_out,
    lengths,
    cotangent,
):
    rows, width_own = tokens.shape
    model = 2 * width_own
    heads = skip_gain.shape[0]
    width = proj_inner.shape[1]
    head_dim = width // heads
    state_width = proj_state.shape[1]
    n = state_width // 4
    conv_width = width + state_width
    inner_width = width * lax.axis_size("mp")
    chunks = rows // CHUNK
    rank = lax.axis_index("mp")
    shape = jax.ShapeDtypeStruct

    oth_tokens = swap_mp(tokens)
    oth_gain = swap_mp(norm_gain.reshape(1, width_own))
    oth_cot = swap_mp(after(cotangent, oth_tokens))

    scalars = jnp.stack([lengths[0], rank, lax.axis_index("dp")]).astype(jnp.int32)
    step_weight = proj_step.reshape(model, 2 * heads)
    step_weight = jnp.pad(step_weight, ((0, 0), (0, LANES - 2 * heads)))
    own_gain = norm_gain.reshape(1, width_own)
    gain = natural(rank, own_gain, oth_gain).astype(F32)
    conv = jnp.concatenate(
        [
            jnp.concatenate([conv_inner, conv_state], axis=1),
            jnp.concatenate([conv_inner_bias, conv_state_bias])[None],
            jnp.zeros((3, conv_width), F32),
        ]
    )
    head_par = jnp.stack(
        [
            step_bias.reshape(-1),
            -jnp.exp(decay_log.reshape(-1)),
            jnp.pad(skip_gain, (0, heads)),
        ]
    )
    head_par = jnp.pad(head_par, ((0, 5), (0, LANES - 2 * heads)))
    staged = (tokens, cotangent, proj_gate, proj_inner, proj_state, proj_out)
    hbm = pl.BlockSpec(memory_space=pl.ANY)
    vmem = pl.BlockSpec(memory_space=pltpu.VMEM)
    tokens_v, cot_v, gate_v, inner_v, state_v, out_v, spread, gather, w_state_t = pl.pallas_call(
        partial(stage_kernel, count=len(staged), head_dim=head_dim),
        out_shape=[pltpu.VMEM(x.shape, x.dtype) for x in staged]
        + [
            pltpu.VMEM((2 * LANES, 2 * width), BF16),
            pltpu.VMEM((2 * width, LANES), BF16),
            pltpu.VMEM((state_width + LANES, model), BF16),
        ],
        in_specs=[vmem, vmem] + [hbm] * len(staged),
        out_specs=[vmem] * (len(staged) + 3),
        scratch_shapes=[pltpu.SemaphoreType.DMA((len(staged),))],
        compiler_params=pltpu.CompilerParams(vmem_limit_bytes=VMEM_LIMIT),
        name="stage",
    )(proj_state, step_weight, *staged)
    gg = gate_gain[None]

    sizes = dict(heads=heads, width=width, state_width=state_width)
    low = lambda *dims: shape(dims, BF16)
    full = lambda *dims: shape(dims, F32)
    block = PROJECT_BLOCK
    up, states = rows_of(block), states_of(block)
    normed, gate_pre, pre, slope, hs, act, sact, xd, hf, sb = call(
        partial(project_kernel, block=block, **sizes),
        rows // block,
        [
            scalars,
            (tokens_v, up),
            (oth_tokens, up),
            (gain, fixed),
            (gate_v, fixed),
            (inner_v, fixed),
            (state_v, fixed),
            (step_weight, fixed),
            (conv, fixed),
            (head_par, fixed),
            (spread, fixed),
        ],
        [up, up, up, up, up, up, up, up, states, states],
        [
            low(rows, model),
            full(rows, width),
            low(rows, conv_width),
            low(rows, conv_width),
            full(rows, 4 * LANES),
            full(rows, width),
            low(rows, state_width),
            low(rows, 2 * width),
            low(chunks, n, width),
            full(chunks, n, width),
        ],
        [pltpu.VMEM((block + 8, conv_width), F32), pltpu.VMEM((n, width), F32)],
        "project",
        12,
    )

    block = MIX_BLOCK
    top = rows // block - 1
    down, states_down = rows_of(block, top), states_of(block, top)
    y, hb = call(
        partial(mix_kernel, block=block, **sizes),
        rows // block,
        [
            scalars,
            (act, down),
            (sact, down),
            (hs, down),
            (xd, down),
            (hf, states_down),
            (sb, states_down),
            (head_par, fixed),
            (spread, fixed),
        ],
        [down, states_down],
        [full(rows, width), low(chunks, n, width)],
        [pltpu.VMEM((n, width), F32)],
        "mix",
        7,
    )

    block = GATE_BLOCK
    up, states, up_lanes = rows_of(block), states_of(block), lanes_of(block)
    dgn, gz, sums = call(
        partial(gate_kernel, block=block),
        rows // block,
        [
            scalars,
            (y, up),
            (gate_pre, up),
            (cot_v, up),
            (oth_cot, up),
            (out_v, fixed),
            (gg, fixed),
        ],
        [up, up, up_lanes],
        [full(rows, width), low(rows, width), full(8, rows)],
        [],
        "gate",
        3,
    )

    oth_sums = swap_mp(sums)
    branch_oth = whole(
        partial(branch_kernel, other=True), (scalars, gz, out_v), [low(rows, width_own)], [], "branch_oth", 3
    )[0]
    sums = sums + oth_sums
    branch_got = swap_mp(after(branch_oth, sums))
    sums_in = after(sums, branch_oth)

    g, dgp, dbr, dc, gb, gf, rd_gate, row_sums, small = call(
        partial(gate_back_kernel, block=block, inner_width=inner_width, **sizes),
        rows // block,
        [
            scalars,
            (sums_in, up_lanes),
            (gate_pre, up),
            (y, up),
            (act, up),
            (dgn, up),
            (cot_v, up),
            (oth_cot, up),
            (hs, up),
            (sact, up),
            (hf, states),
            (hb, states),
            (gg, fixed),
            (spread, fixed),
            (gather, fixed),
        ],
        [up, up, up, up, states, states, up_lanes, up, fixed],
        [
            low(rows, width),
            low(rows, width),
            low(rows, model),
            full(rows, 2 * n),
            low(chunks, n, width),
            full(chunks, n, width),
            full(8, rows),
            full(rows, LANES),
            full(8, width),
        ],
        [pltpu.VMEM((n, width), F32), pltpu.VMEM((block, 2 * width), BF16)],
        "gate_back",
        8,
    )

    def back_part(first, count, g, state):
        block = BACK_BLOCK
        here, states_here, here_lanes = rows_of(block, first), states_of(block, first), lanes_of(block, first)
        ins = [
            scalars,
            (g, here),
            (act, here),
            (sact, here),
            (hs, here),
            (xd, here),
            (row_sums, here),
            (hf, states_here),
            (hb, states_here),
            (gb, states_here),
            (gf, states_here),
            (dc, here),
            (pre, here),
            (slope, here),
            (conv, fixed),
            (head_par, fixed),
            (spread, fixed),
            (gather, fixed),
            *[(x, fixed) for x in state[:4]],
            (state[4], here),
            (state[5], here_lanes),
        ]
        return call(
            partial(back_kernel, block=block, top=first, **sizes),
            count,
            ins,
            [here, here_lanes, fixed, fixed, fixed, fixed],
            [
                low(rows, conv_width + LANES),
                full(8, rows),
                full(8, conv_width),
                full(8, LANES),
                full(8, conv_width),
                full(n, width),
            ],
            [
                pltpu.VMEM((block + 8, conv_width), F32),
                pltpu.VMEM((4 * CHUNK + 16, 2 * width), BF16),
                pltpu.VMEM((CHUNK, 2 * width), BF16),
                pltpu.VMEM((LANES, CHUNK), F32),
            ],
            "mix_back",
            3 * count,
            aliases={len(ins) - 2: 0, len(ins) - 1: 1},
        )

    order_a, order_b = (0, 1, 2, 3), (0, 1, 2, 3)
    grad_out = mm_tn(gz, dbr).astype(BF16)
    grad_gate = mm_tn(normed, dgp).astype(BF16)
    keep, send, gain_part = whole(
        partial(pack_early_kernel, order=order_a),
        (scalars, grad_out, grad_gate, proj_gate),
        [low(width, model), low(width, model), full(8, model)],
        [],
        "pack_early",
        3,
    )

    def halve(keep, send, bit):
        got = swap_dp(send, bit)
        h = keep.shape[0] // 2
        return add_low(keep[:h], got[:h]), add_low(keep[h:], got[h:])

    def finish(keep, send, bit):
        return rest_of_dp(add_low(keep, swap_dp(send, bit)))

    def rest_of_dp(x):
        extra = SHARDS
        while extra < lax.axis_size("dp"):
            x = add_low(x, swap_dp(x, extra.bit_length() - 1))
            extra *= 2
        return x

    zeros = (
        jnp.zeros((8, conv_width), F32),
        jnp.zeros((n, width), F32),
        jnp.zeros((8, conv_width), F32),
        jnp.zeros((8, LANES), F32),
    )
    keep, send = halve(keep, send, order_a[0])
    state = (
        *zeros,
        jnp.zeros((rows, conv_width + LANES), BF16),
        jnp.zeros((8, rows), F32),
    )
    parts = 4
    count = rows // BACK_BLOCK // parts
    g = after(g, send)
    sent, x = swap_dp(send, order_a[1]), None
    for k in range(parts):
        outs = back_part((parts - k) * count - 1, count, g, state)
        rest, rd_rest, gconv, ghead, ext_carry, carry = outs
        if k == 1:
            sent, carry, branch_got = lax.optimization_barrier((sent, carry, branch_got))
        elif k == 2:
            sent, carry = lax.optimization_barrier((sent, carry))
        elif k == 3:
            sent, rest = lax.optimization_barrier((sent, rest))
        if k > 0:
            h = keep.shape[0] // 2
            if k < 3:
                keep, send = add_low(keep[:h], sent[:h]), add_low(keep[h:], sent[h:])
                carry = after(carry, send)
                sent = swap_dp(send, order_a[k + 1])
            else:
                x = rest_of_dp(add_low(keep, sent))
                sent = swap_dp(x, order_a[3])
        state = (ext_carry, carry, gconv, ghead, rest, rd_rest)

    grad_inner = mm_tn(normed, rest[:, :width]).astype(BF16)
    grad_state = mm_tn(rest[:, width:], normed).astype(BF16)
    keep, send = whole(
        partial(pack_late_kernel, order=order_b, heads=heads, state_width=state_width),
        (
            scalars, grad_inner, grad_state, proj_inner, w_state_t, gain, gain_part, gconv, ghead,
            small, gather,
        ),
        [low(LATE_ROWS * SHARDS // 2, model), low(LATE_ROWS * SHARDS // 2, model)],
        [pltpu.VMEM((8 * SHARDS, model), F32)],
        "pack_late",
        3,
    )

    def halve_with(keep, send, bit, *work):
        got = after(swap_dp(send, bit), *work)
        h = keep.shape[0] // 2
        return add_low(keep[:h], got[:h]), add_low(keep[h:], got[h:])

    back_args = (scalars, dgp, after(rest, send), gate_v, inner_v, state_v, step_weight)
    dn_oth = whole(
        partial(back_project_kernel, other=True), back_args, [low(rows, width_own)], [], "back_oth", 4
    )[0]
    rd_part = rd_gate[0] + rd_rest[0]
    keep, send = halve_with(keep, send, order_b[0], dn_oth, rd_part)
    x = jnp.concatenate([x, sent])
    send, x = lax.optimization_barrier((send, x))
    dn_got = swap_mp(dn_oth)
    oth_rd = swap_mp(rd_part.reshape(8, rows // 8)).reshape(rows)

    sent = swap_dp(x, order_a[2])
    dn_own = whole(
        partial(back_project_kernel, other=False), back_args, [full(rows, width_own)], [], "back_own", 4
    )[0]
    keep, send = halve_with(keep, send, order_b[1], dn_own)
    x = jnp.concatenate([x, sent])
    send, x, gz_late, tokens_late, oth_late = lax.optimization_barrier((send, x, gz, tokens, oth_tokens))

    sent = swap_dp(x, order_a[1])
    branch_own = whole(
        partial(branch_kernel, other=False), (scalars, gz_late, out_v), [full(rows, width_own)], [], "branch_own", 3
    )[0]
    keep, send = halve_with(keep, send, order_b[2], branch_own, dn_got)

    seq_mask = (jnp.arange(rows) < lengths[0]).astype(F32)[:, None]
    gate_inv = lax.rsqrt(sums[0] / inner_width + EPSILON)[:, None]
    tokens_f = tokens_late.astype(F32)
    block_out = (tokens_f + seq_mask * gate_inv * (branch_own + branch_got.astype(F32))).astype(BF16)
    z = rest_of_dp(add_low(keep, after(swap_dp(send, order_b[3]), block_out)))
    part = model // SHARDS
    tail = z[part:]
    tail_row = lax.broadcasted_iota(jnp.int32, (LATE_ROWS - part, 1), 0)
    alone = (tail_row >= LATE_ROWS - part - 8) & (tail_row < LATE_ROWS - part - 4)
    tail_f = tail.astype(F32)
    tail = jnp.where(alone, tail_f, tail_f + swap_mp(tail).astype(F32)).astype(BF16)
    x = jnp.concatenate([x, sent])
    z, x = lax.optimization_barrier((jnp.concatenate([z[:part], tail]), x))
    sent = swap_dp(x, order_a[0])

    oth_f = oth_late.astype(F32)
    square = jnp.sum(tokens_f * tokens_f, axis=1, keepdims=True) + jnp.sum(
        oth_f * oth_f, axis=1, keepdims=True
    )
    inv = lax.rsqrt(square / model + EPSILON)
    grad_full = dn_own + dn_got.astype(F32)
    grad_tokens = (
        cotangent.astype(F32)
        + inv * (grad_full * norm_gain.astype(F32)[None])
        - tokens_f * (inv * inv * ((rd_part + oth_rd)[:, None] / model))
    )

    z = jnp.concatenate([z, after(swap_dp(z, order_b[3]), grad_tokens)])
    grad_proj_out, grad_proj_gate = whole(
        partial(unpack_early_kernel, order=order_a),
        (scalars, x, after(sent, z)),
        [full(width, model), full(model, width)],
        [],
        "unpack_early",
        4,
        in_vmem=False,
    )
    z = jnp.concatenate([z, after(swap_dp(z, order_b[2]), grad_proj_out)])
    z = jnp.concatenate([z, swap_dp(z, order_b[1])])
    (
        grad_proj_inner,
        grad_proj_state,
        step,
        grad_conv_inner,
        grad_conv_inner_bias,
        grad_conv_state,
        grad_conv_state_bias,
        grad_gate_gain,
        grad_step_bias,
        grad_decay_log,
        grad_skip,
        grad_norm_gain,
    ) = whole(
        partial(unpack_late_kernel, order=order_b, heads=heads),
        (scalars, z, swap_dp(z, order_b[0])),
        [
            full(model, width),
            full(model, state_width),
            full(heads, 2, model),
            full(4, width),
            full(1, width),
            full(4, state_width),
            full(1, state_width),
            full(1, width),
            full(2, heads),
            full(2, heads),
            full(1, heads),
            full(1, width_own),
        ],
        [pltpu.VMEM((state_width, model), F32), pltpu.VMEM((8 * SHARDS, model), F32)],
        "unpack_late",
        4,
        in_vmem=False,
    )
    return (
        block_out,
        grad_tokens,
        grad_norm_gain[0],
        grad_proj_gate,
        grad_proj_inner,
        grad_proj_state,
        step.transpose(2, 1, 0),
        grad_conv_inner,
        grad_conv_inner_bias[0],
        grad_conv_state,
        grad_conv_state_bias[0],
        grad_step_bias,
        grad_decay_log,
        grad_skip[0],
        grad_gate_gain[0],
        grad_proj_out,
    )


def solution(mesh):
    in_specs = (
        P("dp", "mp"),
        P("mp"),
        P(None, "mp"),
        P(None, "mp"),
        P(),
        P(None, None, "mp"),
        P(None, "mp"),
        P("mp"),
        P(),
        P(),
        P(None, "mp"),
        P(None, "mp"),
        P("mp"),
        P("mp"),
        P("mp", None),
        P("dp"),
        P("dp", "mp"),
    )
    out_specs = (
        P("dp", "mp"),
        P("dp", "mp"),
        P("mp"),
        P(None, "mp"),
        P(None, "mp"),
        P(),
        P(None, None, "mp"),
        P(None, "mp"),
        P("mp"),
        P(),
        P(),
        P(None, "mp"),
        P(None, "mp"),
        P("mp"),
        P("mp"),
        P("mp", None),
    )
    return jax.shard_map(body, mesh=mesh, in_specs=in_specs, out_specs=out_specs, check_vma=False)
```

```python
from functools import partial

import jax
import jax.numpy as jnp
from jax import lax
from jax.experimental import pallas as pl
from jax.experimental.pallas import tpu as pltpu
from jax.sharding import PartitionSpec as P

EPSILON = 1e-05
CHUNK = 128
PROJECT_BLOCK, MIX_BLOCK, GATE_BLOCK, BACK_BLOCK = 256, 256, 256, 128
LANES = 128
F32 = jnp.float32
BF16 = jnp.bfloat16
HIGHEST = lax.Precision.HIGHEST
VMEM_LIMIT = 12 * 1024 * 1024
SHARDS = 16
LOG2_E = 1.4426950408889634
LATE_ROWS = 72


def mm(a, b):
    return jnp.dot(a, b, preferred_element_type=F32)


def mm_nt(a, b):
    return lax.dot_general(a, b, (((1,), (1,)), ((), ())), preferred_element_type=F32)


def mm_tn(a, b):
    return lax.dot_general(a, b, (((0,), (0,)), ((), ())), preferred_element_type=F32)


def split_two(v):
    hi = v.astype(BF16)
    return hi, (v - hi.astype(F32)).astype(BF16)


def split_three(v):
    hi, mid = split_two(v)
    return hi, mid, (v - hi.astype(F32) - mid.astype(F32)).astype(BF16)


def expand(v, spread):
    hi, lo = split_two(v)
    return mm(jnp.concatenate([hi, lo], axis=1), spread)


def row_mask(block, rows, length):
    pos = block * rows + lax.broadcasted_iota(jnp.int32, (rows, 1), 0)
    return (pos < length).astype(F32)


def to_row(col_a, col_b):
    rows = col_a.shape[0]
    lane = lax.broadcasted_iota(jnp.int32, (rows, LANES), 1)
    tile = jnp.where(lane == 0, col_a, jnp.where(lane == 1, col_b, 0.0))
    return jnp.transpose(tile)[0:8, :]


def sigmoid(v):
    return 0.5 * jnp.tanh(0.5 * v) + 0.5


def natural(rank, own, oth):
    return jnp.where(
        rank == 0, jnp.concatenate([own, oth], axis=1), jnp.concatenate([oth, own], axis=1)
    )


def eight(row):
    return jnp.broadcast_to(row, (8, row.shape[1]))


def stage_kernel(w_state, w_step, *refs, count, head_dim):
    sources, outs, sems = refs[:count], refs[count:-1], refs[-1]
    spread, gather, w_state_t = outs[count:]
    copies = [
        pltpu.make_async_copy(src, dst, sems.at[k]) for k, (src, dst) in enumerate(zip(sources, outs))
    ]
    for copy in copies:
        copy.start()
    state_width = w_state.shape[1]
    w_state_t[:state_width, :] = jnp.transpose(w_state[...].astype(F32)).astype(BF16)
    w_state_t[state_width:, :] = jnp.transpose(w_step[...].astype(F32)).astype(BF16)
    head = lax.broadcasted_iota(jnp.int32, spread.shape, 1) // head_dim
    row = lax.broadcasted_iota(jnp.int32, spread.shape, 0) % LANES
    spread[...] = jnp.where(head == row, 1.0, 0.0).astype(BF16)
    head = lax.broadcasted_iota(jnp.int32, gather.shape, 0) // head_dim
    lane = lax.broadcasted_iota(jnp.int32, gather.shape, 1)
    gather[...] = jnp.where(head == lane, 1.0, 0.0).astype(BF16)
    for copy in copies:
        copy.wait()


def project_kernel(
    i, scalars, own, oth, gain, w_gate, w_inner, w_state, w_step, conv, head_par, spread,
    normed_ref, gate_ref, pre_ref, slope_ref, hs_ref, act_ref, sact_ref, xd_ref, hf_ref, sb_ref,
    ext, carry, *, heads, width, state_width, block,
):
    @pl.when(i == 0)
    def _():
        ext[0:8, :] = jnp.zeros((8, ext.shape[1]), F32)
        carry[...] = jnp.zeros_like(carry)

    x = natural(scalars[1], own[...], oth[...]).astype(F32)
    inv = lax.rsqrt(jnp.mean(x * x, axis=-1, keepdims=True) + EPSILON)
    normed = (x * inv * gain[...]).astype(BF16)
    normed_ref[...] = normed
    step_pre = mm(normed, w_step[...])
    z = step_pre + head_par[0:1, :]
    dt = jnp.maximum(z, 0.0) + jnp.log1p(jnp.exp(-jnp.abs(z)))
    rate = head_par[1:2, :] * dt
    dtm = dt * row_mask(i, block, scalars[0])
    hs_ref[:, 0:LANES] = z
    hs_ref[:, LANES : 2 * LANES] = dt
    tri_r = lax.broadcasted_iota(jnp.int32, (CHUNK, CHUNK), 0)
    tri_c = lax.broadcasted_iota(jnp.int32, (CHUNK, CHUNK), 1)
    tri = (tri_c <= tri_r).astype(F32)
    is_fwd = lax.broadcasted_iota(jnp.int32, (CHUNK, LANES), 1) < heads
    per = block // CHUNK
    to_spread = [dtm]
    keeps = []
    for c_idx in range(per):
        rows = slice(c_idx * CHUNK, (c_idx + 1) * CHUNK)
        rate_c = rate[rows]
        cum = jnp.dot(tri, rate_c, precision=HIGHEST, preferred_element_type=F32)
        tot = cum[CHUNK - 1 : CHUNK, :]
        cumx = jnp.where(is_fwd, cum, cum - rate_c)
        hs_ref[rows, 2 * LANES : 3 * LANES] = cumx
        hs_ref[rows, 3 * LANES :] = jnp.broadcast_to(tot, (CHUNK, LANES))
        to_spread.append(dtm[rows] * jnp.exp(jnp.where(is_fwd, tot - cumx, cumx)))
        keeps.append(eight(jnp.exp(tot)))
    wide = expand(jnp.concatenate(to_spread + keeps, axis=0), spread[...])

    ext[8 : 8 + block, 0:width] = mm(normed, w_inner[...])
    ext[8 : 8 + block, width:] = mm(normed, w_state[...])
    gate_ref[...] = mm(normed, w_gate[...])
    whole_ext = ext[...]
    pre = whole_ext[8:]
    pre_ref[...] = pre.astype(BF16)
    c = conv[4:5, :] + conv[3:4, :] * pre
    for j in range(3):
        c = c + conv[j : j + 1, :] * pltpu.roll(whole_ext, 3 - j, 0)[8:]
    sg = sigmoid(c)
    both = c * sg
    slope_ref[...] = (sg * (1.0 + c * (1.0 - sg))).astype(BF16)
    ext[0:8, :] = ext[block : block + 8, :]
    act = both[:, :width]
    act_ref[...] = act
    sact = both[:, width:].astype(BF16)
    sact_ref[...] = sact
    xd_ref[:, 0:width] = (act * wide[0:block, :width]).astype(BF16)
    xd_ref[:, width:] = (act * wide[0:block, width:]).astype(BF16)
    n = state_width // 4
    for c_idx in range(per):
        rows = slice(c_idx * CHUNK, (c_idx + 1) * CHUNK)
        coef = wide[block + c_idx * CHUNK : block + (c_idx + 1) * CHUNK]
        keep = wide[2 * block + 8 * c_idx : 2 * block + 8 * c_idx + 1, :width]
        hf_ref[c_idx] = carry[...].astype(BF16)
        carry[...] = carry[...] * keep + mm_tn(
            sact[rows, 0:n], (act[rows] * coef[:, :width]).astype(BF16)
        )
        sb_ref[c_idx] = mm_tn(
            sact[rows, 2 * n : 3 * n], (act[rows] * coef[:, width:]).astype(BF16)
        )


def pair_tiles(pair):
    lane = lax.broadcasted_iota(jnp.int32, (1, pair.shape[1]), 1)
    first = (lane < pair.shape[1] // 2).astype(F32)
    keep_a, keep_b = first.astype(BF16), (1.0 - first).astype(BF16)
    return jnp.concatenate([pair * keep_a, pair * keep_b], axis=0)


def mix_kernel(
    i, scalars, act, sact, hs, xd, hf, sb, head_par, spread, y_ref, hb_ref, carry,
    *, heads, width, state_width, block,
):
    @pl.when(i == 0)
    def _():
        carry[...] = jnp.zeros_like(carry)

    n = state_width // 4
    per = block // CHUNK
    r = lax.broadcasted_iota(jnp.int32, (CHUNK, CHUNK), 0)
    c = lax.broadcasted_iota(jnp.int32, (CHUNK, CHUNK), 1)
    lower = c < r
    upper = c > r
    is_fwd = lax.broadcasted_iota(jnp.int32, (block, LANES), 1) < heads
    cum_all = hs[:, 2 * LANES : 3 * LANES]
    tot_all = hs[:, 3 * LANES :]
    wide = expand(
        jnp.concatenate(
            [jnp.exp(jnp.where(is_fwd, cum_all, tot_all - cum_all))]
            + [jnp.exp(tot_all[k * CHUNK : k * CHUNK + 8]) for k in range(per)]
            + [eight(head_par[2:3, :])],
            axis=0,
        ),
        spread[...],
    )
    skip = wide[block + 8 * per : block + 8 * per + 1]
    for c_idx in reversed(range(per)):
        rows = slice(c_idx * CHUNK, (c_idx + 1) * CHUNK)
        cumx = cum_all[rows] * LOG2_E
        cum_t = jnp.transpose(cumx)
        sact_c = sact[rows, :]
        b_f, c_f = sact_c[:, 0:n], sact_c[:, n : 2 * n]
        b_b, c_b = sact_c[:, 2 * n : 3 * n], sact_c[:, 3 * n :]
        s_f = jnp.where(lower, mm_nt(c_f, b_f), 0.0)
        s_b = jnp.where(upper, mm_nt(c_b, b_b), 0.0)
        hb = carry[...].astype(BF16)
        hb_ref[c_idx] = hb
        in_f = mm(c_f, hf[c_idx])
        in_b = mm(c_b, hb)
        keep = wide[block + 8 * c_idx : block + 8 * c_idx + 1, width:]
        carry[...] = carry[...] * keep + sb[c_idx]
        for p in range(heads // 2):
            lanes = slice(p * LANES, (p + 1) * LANES)
            lanes_b = slice(width + p * LANES, width + (p + 1) * LANES)
            w_f, w_b = [], []
            for h in (2 * p, 2 * p + 1):
                damp = jnp.exp2(
                    jnp.minimum(
                        cumx[:, h : h + 1] - cum_t[h : h + 1, :],
                        cum_t[heads + h : heads + h + 1, :] - cumx[:, heads + h : heads + h + 1],
                    )
                )
                w_f.append((s_f * damp).astype(BF16))
                w_b.append((s_b * damp).astype(BF16))
            out = mm(
                jnp.concatenate(w_f + w_b, axis=1),
                jnp.concatenate([pair_tiles(xd[rows, lanes]), pair_tiles(xd[rows, lanes_b])], axis=0),
            )
            y_ref[rows, lanes] = (
                out
                + wide[rows, lanes] * in_f[:, lanes]
                + wide[rows, lanes_b] * in_b[:, lanes]
                + skip[:, lanes] * act[rows, lanes]
            )


def gate_kernel(i, scalars, y, gate, cown, coth, po, gg, dgn_ref, gz_ref, sums_ref, *, block):
    gp = gate[...]
    gated = y[...] * (gp * sigmoid(gp))
    mask = row_mask(i, block, scalars[0])
    cot = natural(scalars[1], cown[...], coth[...])
    dgn = mm_nt((cot.astype(F32) * mask).astype(BF16), po[...])
    dgn_ref[...] = dgn
    scaled = gated * gg[...]
    gz_ref[...] = scaled.astype(BF16)
    sums_ref[...] = to_row(
        jnp.sum(gated * gated, axis=1, keepdims=True), jnp.sum(dgn * scaled, axis=1, keepdims=True)
    )


def gate_back_kernel(
    i, scalars, sums, gate, y, act, dgn, cown, coth, hs, sact, hf, hb, gg, spread, gather,
    g_ref, dgp_ref, dbr_ref, dc_ref, gb_ref, gf_ref, rd_ref, rows_ref, small_ref, carry, prod,
    *, heads, width, state_width, block, inner_width,
):
    @pl.when(i == 0)
    def _():
        carry[...] = jnp.zeros_like(carry)
        small_ref[...] = jnp.zeros_like(small_ref)

    per = block // CHUNK
    is_fwd = lax.broadcasted_iota(jnp.int32, (block, LANES), 1) < heads
    cum_all = hs[:, 2 * LANES : 3 * LANES]
    tot_all = hs[:, 3 * LANES :]
    wide = expand(
        jnp.concatenate(
            [jnp.exp(jnp.where(is_fwd, cum_all, tot_all - cum_all))]
            + [jnp.exp(tot_all[k * CHUNK : k * CHUNK + 8]) for k in range(per)],
            axis=0,
        ),
        spread[...],
    )
    cols = jnp.transpose(sums[...])
    gate_inv = lax.rsqrt(cols[:, 0:1] / inner_width + EPSILON)
    gate_dot = cols[:, 1:2] / inner_width
    gp = gate[...]
    sg = sigmoid(gp)
    act_gate = gp * sg
    yv = y[...]
    gated = yv * act_gate
    dg = dgn[...]
    small_ref[0:1, :] += jnp.sum(dg * gated * gate_inv, axis=0, keepdims=True)
    d_gated = gate_inv * (dg * gg[...]) - gated * (gate_inv * gate_inv * gate_inv * gate_dot)
    d_gp = d_gated * yv * (sg * (1.0 + gp * (1.0 - sg)))
    dgp_ref[...] = d_gp.astype(BF16)
    rd = jnp.sum(d_gp * gp, axis=1, keepdims=True)
    rd_ref[...] = to_row(rd, jnp.zeros_like(rd))
    d_y = d_gated * act_gate
    g_ref[...] = d_y.astype(BF16)
    small_ref[1:2, :] += jnp.sum(d_y * act[...], axis=0, keepdims=True)
    mask = row_mask(i, block, scalars[0])
    cot = natural(scalars[1], cown[...], coth[...])
    dbr_ref[...] = (cot.astype(F32) * (mask * gate_inv)).astype(BF16)
    n = state_width // 4
    for c_idx in range(per):
        rows = slice(c_idx * CHUNK, (c_idx + 1) * CHUNK)
        dy_c = d_y[rows]
        dyf = dy_c * wide[rows, :width]
        dyb = dy_c * wide[rows, width:]
        prod[rows, 0:width] = (dyf * mm(sact[rows, n : 2 * n], hf[c_idx])).astype(BF16)
        prod[rows, width:] = (dyb * mm(sact[rows, 3 * n :], hb[c_idx])).astype(BF16)
        dyf = dyf.astype(BF16)
        dyb = dyb.astype(BF16)
        dc_ref[rows, 0:n] = mm_nt(dyf, hf[c_idx])
        dc_ref[rows, n : 2 * n] = mm_nt(dyb, hb[c_idx])
        gb_ref[c_idx] = carry[...].astype(BF16)
        keep = wide[block + 8 * c_idx : block + 8 * c_idx + 1, width:]
        carry[...] = carry[...] * keep + mm_tn(sact[rows, 3 * n :], dyb)
        gf_ref[c_idx] = mm_tn(sact[rows, n : 2 * n], dyf)
    rows_ref[...] = mm(prod[...], gather[...])


def back_kernel(
    i, scalars, g, act, sact, hs, xd, row_in, hf, hb, gb, gf, dc, pre, slope, conv, head_par, spread, gather,
    ext_in, carry_in, gconv_in, _rest, _rates, _rd, rest_ref, rates_ref, rd_ref, gconv_ref, ext_out,
    carry, ext, stack, xs, rsum, csum,
    *, heads, width, state_width, block, top,
):
    blk = top - i
    per = block // CHUNK

    @pl.when(i == 0)
    def _():
        ext[block:, :] = ext_in[...]
        carry[...] = carry_in[...]
        gconv_ref[...] = gconv_in[...]
        rsum[...] = jnp.zeros_like(rsum)
        csum[...] = jnp.zeros_like(csum)

    n = state_width // 4
    r = lax.broadcasted_iota(jnp.int32, (CHUNK, CHUNK), 0)
    c = lax.broadcasted_iota(jnp.int32, (CHUNK, CHUNK), 1)
    later = c > r
    earlier = c < r
    is_fwd_all = lax.broadcasted_iota(jnp.int32, (block, LANES), 1) < heads
    is_fwd = lax.broadcasted_iota(jnp.int32, (CHUNK, LANES), 1) < heads
    mask = row_mask(blk, block, scalars[0])
    cum_all = hs[:, 2 * LANES : 3 * LANES]
    tot_all = hs[:, 3 * LANES :]
    wide = expand(
        jnp.concatenate(
            [jnp.exp(jnp.where(is_fwd_all, tot_all - cum_all, cum_all)), hs[:, LANES : 2 * LANES] * mask]
            + [jnp.exp(tot_all[k * CHUNK : k * CHUNK + 8]) for k in range(per)]
            + [eight(head_par[2:3, :])],
            axis=0,
        ),
        spread[...],
    )
    skip = wide[2 * block + 8 * per : 2 * block + 8 * per + 1]
    for c_idx in reversed(range(per)):
        rows = slice(c_idx * CHUNK, (c_idx + 1) * CHUNK)
        rows_dt = slice(block + c_idx * CHUNK, block + (c_idx + 1) * CHUNK)
        cumx = cum_all[rows] * LOG2_E
        cum_t = jnp.transpose(cumx)
        sact_c = sact[rows, :]
        b_f, c_f = sact_c[:, 0:n], sact_c[:, n : 2 * n]
        b_b, c_b = sact_c[:, 2 * n : 3 * n], sact_c[:, 3 * n :]
        s_f = jnp.where(later, mm_nt(b_f, c_f), 0.0)
        s_b = jnp.where(earlier, mm_nt(b_b, c_b), 0.0)
        s_all = s_f + s_b
        grad_f = carry[...]
        grad_f_low = grad_f.astype(BF16)
        grad_b_low = gb[c_idx]
        keep = wide[2 * block + 8 * c_idx : 2 * block + 8 * c_idx + 1]
        keep_f = keep[:, :width]
        edge_f = keep_f * jnp.sum(grad_f * hf[c_idx].astype(F32), axis=0, keepdims=True)
        edge_b = keep[:, width:] * jnp.sum(
            hb[c_idx].astype(F32) * grad_b_low.astype(F32), axis=0, keepdims=True
        )
        e_hi, e_lo = split_two(eight(jnp.concatenate([edge_f, edge_b], axis=1)))
        stack[2 * CHUNK :, :] = jnp.concatenate([e_hi, e_lo], axis=0)
        carry[...] = grad_f * keep_f + gf[c_idx]
        in_f = mm(b_f, grad_f_low)
        in_b = mm(b_b, grad_b_low)
        d_scores = jnp.zeros((CHUNK, CHUNK), F32)
        for p in range(heads // 2):
            lanes = slice(p * LANES, (p + 1) * LANES)
            lanes_b = slice(width + p * LANES, width + (p + 1) * LANES)
            g_pair = g[rows, lanes]
            xf_pair = xd[rows, lanes]
            xb_pair = xd[rows, lanes_b]
            dw = mm_nt(
                jnp.concatenate([pair_tiles(xf_pair), pair_tiles(xb_pair)], axis=0), g_pair
            )
            w_f, w_b = [], []
            for q, h in enumerate((2 * p, 2 * p + 1)):
                damp = jnp.exp2(
                    jnp.minimum(
                        cum_t[h : h + 1, :] - cumx[:, h : h + 1],
                        cumx[:, heads + h : heads + h + 1] - cum_t[heads + h : heads + h + 1, :],
                    )
                )
                w_f.append((s_f * damp).astype(BF16))
                w_b.append((s_b * damp).astype(BF16))
                part = jnp.where(
                    later, dw[q * CHUNK : (q + 1) * CHUNK], dw[(2 + q) * CHUNK : (3 + q) * CHUNK]
                )
                part = part * damp
                d_scores = d_scores + part
                e_all = part * s_all
                e_fwd = jnp.where(later, e_all, 0.0)
                sum_all = jnp.sum(e_all, axis=0, keepdims=True)
                sum_fwd = jnp.sum(e_fwd, axis=0, keepdims=True)
                rsum[h : h + 1, :] = sum_fwd
                rsum[heads + h : heads + h + 1, :] = sum_fwd - sum_all
                sum_all = jnp.sum(e_all, axis=1, keepdims=True)
                sum_fwd = jnp.sum(e_fwd, axis=1, keepdims=True)
                csum[:, h : h + 1] = -sum_fwd
                csum[:, heads + h : heads + h + 1] = sum_all - sum_fwd
            dx = mm(
                jnp.concatenate(
                    [jnp.concatenate(w_f, axis=1), jnp.concatenate(w_b, axis=1)], axis=0
                ),
                pair_tiles(g_pair),
            )
            edge_pf = wide[rows, lanes]
            edge_pb = wide[rows, lanes_b]
            inter_f = edge_pf * in_f[:, lanes]
            inter_b = edge_pb * in_b[:, lanes]
            dx_f = dx[:CHUNK] + inter_f
            dx_b = dx[CHUNK:] + inter_b
            xf = xf_pair.astype(F32)
            xb = xb_pair.astype(F32)
            xs[:, lanes] = (xf * edge_pf).astype(BF16)
            xs[:, lanes_b] = (xb * edge_pb).astype(BF16)
            act_p = act[rows, lanes]
            stack[0:CHUNK, lanes] = (act_p * dx_f).astype(BF16)
            stack[0:CHUNK, lanes_b] = (act_p * dx_b).astype(BF16)
            stack[CHUNK : 2 * CHUNK, lanes] = (xf * inter_f).astype(BF16)
            stack[CHUNK : 2 * CHUNK, lanes_b] = (xb * inter_b).astype(BF16)
            d_inner = (
                skip[:, lanes] * g_pair.astype(F32)
                + wide[rows_dt, lanes] * dx_f
                + wide[rows_dt, lanes_b] * dx_b
            )
            ext[rows, lanes] = d_inner * slope[rows, lanes].astype(F32)
        low_f = jnp.where(later, d_scores, 0.0).astype(BF16)
        low_b = jnp.where(earlier, d_scores, 0.0).astype(BF16)
        d_bf = mm(low_f, c_f) + mm_nt(xs[:, :width], grad_f_low)
        d_cf = mm_tn(low_f, b_f) + dc[rows, 0:n]
        d_bb = mm(low_b, c_b) + mm_nt(xs[:, width:], grad_b_low)
        d_cb = mm_tn(low_b, b_b) + dc[rows, n : 2 * n]
        d_state = jnp.concatenate([d_bf, d_cf, d_bb, d_cb], axis=1)
        ext[rows, width:] = d_state * slope[rows, width:].astype(F32)
        head_sums = mm(stack[...], gather[...])
        rin = row_in[rows, :]
        ahead = head_sums[CHUNK : 2 * CHUNK]
        rates_ref[rows, 0:LANES] = (
            jnp.transpose(rsum[...]) + csum[...] + jnp.where(is_fwd, rin, ahead)
        )
        rates_ref[rows, LANES : 2 * LANES] = jnp.where(is_fwd, ahead, rin)
        rates_ref[rows, 2 * LANES : 3 * LANES] = head_sums[0:CHUNK] * mask[rows]
        edge = head_sums[2 * CHUNK : 2 * CHUNK + 1] + head_sums[2 * CHUNK + 8 : 2 * CHUNK + 9]
        rates_ref[rows, 3 * LANES :] = jnp.broadcast_to(edge, (CHUNK, LANES))

    prev = pre[...].astype(F32)
    whole_ext = ext[...]
    moved = whole_ext[:block]
    acc = conv[3:4, :] * moved
    gconv_ref[4:5, :] += jnp.sum(moved, axis=0, keepdims=True)
    gconv_ref[3:4, :] += jnp.sum(moved * prev, axis=0, keepdims=True)
    for j in range(3):
        moved = pltpu.roll(whole_ext, block + 8 - (3 - j), 0)[:block]
        acc = acc + conv[j : j + 1, :] * moved
        gconv_ref[j : j + 1, :] += jnp.sum(moved * prev, axis=0, keepdims=True)
    rest_ref[...] = acc.astype(BF16)
    rd = jnp.sum(acc * prev, axis=1, keepdims=True)
    rd_ref[...] = to_row(rd, jnp.zeros_like(rd))
    ext[block:, :] = ext[0:8, :]
    ext_out[...] = ext[0:8, :]


def rates_kernel(i, scalars, rates, hs, rd_a, rd_b, head_par, dz_ref, ghead_ref, rd_ref, *, heads, block):
    @pl.when(i == 0)
    def _():
        ghead_ref[...] = jnp.zeros_like(ghead_ref)

    r = lax.broadcasted_iota(jnp.int32, (CHUNK, CHUNK), 0)
    c = lax.broadcasted_iota(jnp.int32, (CHUNK, CHUNK), 1)
    tri = jnp.where(c <= r, 1.0, 0.0).astype(BF16)
    is_fwd = lax.broadcasted_iota(jnp.int32, (CHUNK, LANES), 1) < heads
    neg = head_par[1:2, :]
    for c_idx in range(block // CHUNK):
        rows = slice(c_idx * CHUNK, (c_idx + 1) * CHUNK)
        d_cum = rates[rows, 0:LANES]
        d_run = rates[rows, LANES : 2 * LANES]
        sums = mm(tri, jnp.concatenate([*split_three(d_cum), *split_two(d_run)], axis=1))
        ahead = sums[:, 0:LANES] + sums[:, LANES : 2 * LANES] + sums[:, 2 * LANES : 3 * LANES]
        run = sums[:, 3 * LANES : 4 * LANES] + sums[:, 4 * LANES :]
        behind = ahead[CHUNK - 1 :, :] - ahead
        d_rate = jnp.where(is_fwd, behind + d_cum + run - d_run, behind + run)
        d_rate = d_rate + rates[rows, 3 * LANES :]
        z = hs[rows, 0:LANES]
        d_step = neg * d_rate + rates[rows, 2 * LANES : 3 * LANES]
        d_z = d_step / (1.0 + jnp.exp(-z))
        dt = hs[rows, LANES : 2 * LANES]
        ghead_ref[0:1, :] += jnp.sum(d_rate * (neg * dt), axis=0, keepdims=True)
        ghead_ref[1:2, :] += jnp.sum(d_z, axis=0, keepdims=True)
        dz_ref[rows, :] = d_z.astype(BF16)
        rd = jnp.sum(d_z * (z - head_par[0:1, :]), axis=1, keepdims=True)
        rd_ref[:, rows] = rd_a[:, rows] + rd_b[:, rows] + to_row(rd, jnp.zeros_like(rd))


def columns_of(scalars, other, size):
    rank = scalars[1]
    return pl.ds(pl.multiple_of((1 - rank if other else rank) * size, LANES), size)


def branch_kernel(scalars, gz, po, out_ref, *, other):
    cols = columns_of(scalars, other, out_ref.shape[1])
    out_ref[...] = mm(gz[...], po[:, cols]).astype(out_ref.dtype)


def back_project_kernel(
    scalars, dgp, rest, dz, rd, w_gate, w_inner, w_state, w_step, out_ref, *, other
):
    rows, size = dgp.shape[0], out_ref.shape[1]
    at = columns_of(scalars, other, size)
    a = w_inner.shape[1]
    out_ref[0:rows, :] = (
        mm_nt(dgp[...], w_gate[at, :])
        + mm_nt(rest[:, 0:a], w_inner[at, :])
        + mm_nt(rest[:, a:], w_state[at, :])
        + mm_nt(dz[...], w_step[at, :])
    ).astype(out_ref.dtype)
    if other:
        part = rows // 4
        lines = jnp.concatenate([rd[0:1, k * part : (k + 1) * part] for k in range(4)], axis=0)
        lines = jnp.concatenate(split_three(lines) + (jnp.zeros((4, part), BF16),), axis=0)
        out_ref[rows : rows + 16, 0:part] = lines
        out_ref[rows : rows + 16, part:] = jnp.zeros((16, size - part), BF16)


def home_of(r, me, order):
    j = me % SHARDS
    levels = len(order)
    for p, bit in enumerate(order):
        if (r >> (levels - 1 - p)) & 1:
            j = jnp.bitwise_xor(j, 1 << bit)
    return j


def pack_early_kernel(
    scalars, grad_out, grad_gate, w_gate, keep_ref, send_ref, gain_ref, *, order
):
    hi, lo = split_two(grad_gate[...].astype(F32) * w_gate[...].astype(F32))
    ones = jnp.ones((8, hi.shape[1]), BF16)
    gain_ref[...] = mm_nt(ones, hi) + mm_nt(ones, lo)
    part = grad_out.shape[0] // SHARDS
    for r in range(SHARDS):
        j = home_of(r, scalars[2], order)
        out = keep_ref if r < SHARDS // 2 else send_ref
        at = (r % (SHARDS // 2)) * 2 * part
        src = pl.ds(pl.multiple_of(j * part, part), part)
        out[at : at + part, :] = grad_out[src, :]
        out[at + part : at + 2 * part, :] = grad_gate[src, :]


def unpack_early_kernel(scalars, first, second, out_ref, gate_ref, *, order):
    part = out_ref.shape[0] // SHARDS
    for r in range(SHARDS):
        j = home_of(r, scalars[2], order)
        src = first if r < SHARDS // 2 else second
        at = (r % (SHARDS // 2)) * 2 * part
        dst = pl.ds(pl.multiple_of(j * part, part), part)
        out_ref[dst, :] = src[at : at + part, :].astype(F32)
        gate_ref[dst, :] = src[at + part : at + 2 * part, :].astype(F32)


def pack_late_kernel(
    scalars, inner, state, step_low, w_inner, w_state_t, gain, gain_part, gconv, ghead, small, gather,
    keep_ref, send_ref, misc, *, order, heads, state_width,
):
    model, width = w_inner.shape
    hi, lo = split_two(inner[...].astype(F32) * w_inner[...].astype(F32))
    ones = jnp.ones((8, hi.shape[1]), BF16)
    gain_row = (mm_nt(ones, hi) + mm_nt(ones, lo) + gain_part[...])[0:1]
    step = step_low[...].astype(F32)
    w_t = w_state_t[...].astype(F32)
    gain_row += jnp.sum(state[...].astype(F32) * w_t[:state_width], axis=0, keepdims=True)
    gain_row += jnp.sum(step * w_t[state_width:], axis=0, keepdims=True)
    gain_row = gain_row / gain[...]
    misc[...] = jnp.zeros_like(misc)

    def put_single(k, row):
        at = (k // 2) * 8 + k % 2
        misc[at : at + 1, :] = row

    for k in range(2 * heads):
        put_single(k, step[k : k + 1, :])
    at = 2 * heads
    for k in range(5):
        put_single(at + k, gconv[k : k + 1, 0:width])
    put_single(at + 5, small[0:1, :])
    hi, lo = split_two(eight(small[1:2, :]))
    skip = mm(hi, gather[0:width, :]) + mm(lo, gather[0:width, :])
    at = ((at + 6) // 2) * 8 + (at + 6) % 2
    misc[at : at + 1, 2 * LANES : 3 * LANES] = skip[0:1]
    misc[at : at + 1, 0:LANES] = ghead[0:1, :]
    misc[at : at + 1, LANES : 2 * LANES] = ghead[1:2, :]
    fit = model // state_width
    for k in range(5):
        at = (k // fit) * 8 + 4
        lanes = slice((k % fit) * state_width, (k % fit + 1) * state_width)
        misc[at : at + 1, lanes] = gconv[k : k + 1, width:]
    at = (-(-5 // fit)) * 8 + 4
    misc[at : at + 1, :] = gain_row
    part = model // SHARDS
    part_s = state_width // SHARDS
    rows = part + part_s + 8
    for r in range(SHARDS):
        j = home_of(r, scalars[2], order)
        out = keep_ref if r < SHARDS // 2 else send_ref
        at = (r % (SHARDS // 2)) * rows
        out[at : at + part, :] = inner[pl.ds(pl.multiple_of(j * part, part), part), :]
        out[at + part : at + part + part_s, :] = state[
            pl.ds(pl.multiple_of(j * part_s, part_s), part_s), :
        ]
        out[at + part + part_s : at + rows, :] = misc[
            pl.ds(pl.multiple_of(j * 8, 8), 8), :
        ].astype(BF16)


def unpack_late_kernel(
    scalars, first, second, inner_ref, state_ref, step_ref, convi_ref, convi_b_ref, convs_ref, convs_b_ref,
    gg_ref, bias_ref, decay_ref, skip_ref, gain_ref, state, misc, *, order, heads,
):
    model = inner_ref.shape[0]
    state_width = state_ref.shape[1]
    part = model // SHARDS
    part_s = state_width // SHARDS
    rows = part + part_s + 8
    for r in range(SHARDS):
        j = home_of(r, scalars[2], order)
        src = first if r < SHARDS // 2 else second
        at = (r % (SHARDS // 2)) * rows
        inner_ref[pl.ds(pl.multiple_of(j * part, part), part), :] = src[at : at + part, :].astype(F32)
        state[pl.ds(pl.multiple_of(j * part_s, part_s), part_s), :] = src[
            at + part : at + part + part_s, :
        ].astype(F32)
        misc[pl.ds(pl.multiple_of(j * 8, 8), 8), :] = src[at + part + part_s : at + rows, :].astype(F32)
    state_ref[...] = jnp.transpose(state[...])

    def single(k):
        at = (k // 2) * 8 + k % 2
        return misc[at : at + 1, :]

    for h in range(heads):
        for d in range(2):
            step_ref[h, d : d + 1, :] = single(d * heads + h)
    at = 2 * heads
    for k in range(4):
        convi_ref[k : k + 1, :] = single(at + k)
    convi_b_ref[...] = single(at + 4)
    gg_ref[...] = single(at + 5)
    head_row = single(at + 6)
    for d in range(2):
        decay_ref[d : d + 1, :] = head_row[:, d * heads : (d + 1) * heads]
        bias_ref[d : d + 1, :] = head_row[:, LANES + d * heads : LANES + (d + 1) * heads]
    skip_ref[...] = head_row[:, 2 * LANES : 2 * LANES + heads]
    fit = model // state_width
    for k in range(5):
        at = (k // fit) * 8 + 4
        lanes = slice((k % fit) * state_width, (k % fit + 1) * state_width)
        out, row = (convs_ref, k) if k < 4 else (convs_b_ref, 0)
        out[row : row + 1, :] = misc[at : at + 1, lanes]
    at = (-(-5 // fit)) * 8 + 4
    half = model // 2
    gain_ref[...] = jnp.where(
        scalars[1] == 0, misc[at : at + 1, :half], misc[at : at + 1, half:]
    )


def place(i, top):
    return i if top is None else top - i


def rows_of(block, top=None):
    return lambda ref, i: ref.at[pl.ds(pl.multiple_of(place(i, top) * block, block), block)]


def lanes_of(block, top=None):
    return lambda ref, i: ref.at[:, pl.ds(pl.multiple_of(place(i, top) * block, block), block)]


def states_of(block, top=None):
    per = block // CHUNK
    return lambda ref, i: ref.at[pl.ds(place(i, top) * per, per)]


def fixed(ref, i):
    return ref


def call(kernel, blocks, ins, out_views, out_shape, scratch, name, aliases=None, us=0.0):
    views = [view for _, view in ins[1:]] + out_views
    arrays = [ins[0]] + [
        pltpu.with_memory_space_constraint(x, pltpu.VMEM) if view is not fixed else x
        for x, view in ins[1:]
    ]

    def looped(scalars, *refs):
        def step(i, _):
            blocks_of = [view(ref, i) for view, ref in zip(views, refs)]
            kernel(i, scalars, *blocks_of, *refs[len(views) :])
            return 0

        lax.fori_loop(0, blocks, step, 0)

    vmem = pl.BlockSpec(memory_space=pltpu.VMEM)
    return pl.pallas_call(
        looped,
        out_shape=[pltpu.VMEM(o.shape, o.dtype) for o in out_shape],
        in_specs=[pl.BlockSpec(memory_space=pltpu.SMEM)] + [vmem] * (len(arrays) - 1),
        out_specs=[vmem] * len(out_shape),
        scratch_shapes=scratch,
        compiler_params=pltpu.CompilerParams(vmem_limit_bytes=VMEM_LIMIT),
        cost_estimate=pl.CostEstimate(
            flops=int(us * 5e8), transcendentals=0, bytes_accessed=int(us * 3e6)
        ),
        name=name,
        input_output_aliases=aliases or {},
    )(*arrays)


def whole(kernel, args, out_shape, scratch, name, in_vmem=True, us=0.0):
    vmem = pl.BlockSpec(memory_space=pltpu.VMEM)
    return pl.pallas_call(
        kernel,
        out_shape=[pltpu.VMEM(o.shape, o.dtype) if in_vmem else o for o in out_shape],
        in_specs=[pl.BlockSpec(memory_space=pltpu.SMEM)] + [vmem] * (len(args) - 1),
        out_specs=[vmem] * len(out_shape),
        scratch_shapes=scratch,
        compiler_params=pltpu.CompilerParams(vmem_limit_bytes=VMEM_LIMIT),
        cost_estimate=pl.CostEstimate(
            flops=int(us * 5e8), transcendentals=0, bytes_accessed=int(us * 3e6)
        ),
        name=name,
    )(*args)


def swap_mp(x):
    return lax.ppermute(x, "mp", [(0, 1), (1, 0)])


def swap_dp(x, bit):
    size = lax.axis_size("dp")
    return lax.ppermute(x, "dp", [(i, i ^ (1 << bit)) for i in range(size)])


def add_low(a, b):
    return (a.astype(F32) + b.astype(F32)).astype(BF16)


def after(x, *others):
    return lax.optimization_barrier((x, *others))[0]


def body(
    tokens,
    norm_gain,
    proj_gate,
    proj_inner,
    proj_state,
    proj_step,
    conv_inner,
    conv_inner_bias,
    conv_state,
    conv_state_bias,
    step_bias,
    decay_log,
    skip_gain,
    gate_gain,
    proj_out,
    lengths,
    cotangent,
):
    rows, width_own = tokens.shape
    model = 2 * width_own
    heads = skip_gain.shape[0]
    width = proj_inner.shape[1]
    head_dim = width // heads
    state_width = proj_state.shape[1]
    n = state_width // 4
    conv_width = width + state_width
    inner_width = width * lax.axis_size("mp")
    chunks = rows // CHUNK
    rank = lax.axis_index("mp")
    shape = jax.ShapeDtypeStruct

    oth_tokens = swap_mp(tokens)
    oth_gain = swap_mp(norm_gain.reshape(1, width_own))
    oth_cot = swap_mp(after(cotangent, oth_tokens))

    scalars = jnp.stack([lengths[0], rank, lax.axis_index("dp")]).astype(jnp.int32)
    step_weight = proj_step.reshape(model, 2 * heads)
    step_weight = jnp.pad(step_weight, ((0, 0), (0, LANES - 2 * heads)))
    own_gain = norm_gain.reshape(1, width_own)
    gain = natural(rank, own_gain, oth_gain).astype(F32)
    conv = jnp.concatenate(
        [
            jnp.concatenate([conv_inner, conv_state], axis=1),
            jnp.concatenate([conv_inner_bias, conv_state_bias])[None],
            jnp.zeros((3, conv_width), F32),
        ]
    )
    head_par = jnp.stack(
        [
            step_bias.reshape(-1),
            -jnp.exp(decay_log.reshape(-1)),
            jnp.pad(skip_gain, (0, heads)),
        ]
    )
    head_par = jnp.pad(head_par, ((0, 5), (0, LANES - 2 * heads)))
    staged = (tokens, cotangent, proj_gate, proj_inner, proj_state, proj_out)
    hbm = pl.BlockSpec(memory_space=pl.ANY)
    vmem = pl.BlockSpec(memory_space=pltpu.VMEM)
    tokens_v, cot_v, gate_v, inner_v, state_v, out_v, spread, gather, w_state_t = pl.pallas_call(
        partial(stage_kernel, count=len(staged), head_dim=head_dim),
        out_shape=[pltpu.VMEM(x.shape, x.dtype) for x in staged]
        + [
            pltpu.VMEM((2 * LANES, 2 * width), BF16),
            pltpu.VMEM((2 * width, LANES), BF16),
            pltpu.VMEM((state_width + LANES, model), BF16),
        ],
        in_specs=[vmem, vmem] + [hbm] * len(staged),
        out_specs=[vmem] * (len(staged) + 3),
        scratch_shapes=[pltpu.SemaphoreType.DMA((len(staged),))],
        compiler_params=pltpu.CompilerParams(vmem_limit_bytes=VMEM_LIMIT),
        name="stage",
    )(proj_state, step_weight, *staged)
    gg = gate_gain[None]

    sizes = dict(heads=heads, width=width, state_width=state_width)
    low = lambda *dims: shape(dims, BF16)
    full = lambda *dims: shape(dims, F32)
    block = PROJECT_BLOCK
    up, states = rows_of(block), states_of(block)
    normed, gate_pre, pre, slope, hs, act, sact, xd, hf, sb = call(
        partial(project_kernel, block=block, **sizes),
        rows // block,
        [
            scalars,
            (tokens_v, up),
            (oth_tokens, up),
            (gain, fixed),
            (gate_v, fixed),
            (inner_v, fixed),
            (state_v, fixed),
            (step_weight, fixed),
            (conv, fixed),
            (head_par, fixed),
            (spread, fixed),
        ],
        [up, up, up, up, up, up, up, up, states, states],
        [
            low(rows, model),
            full(rows, width),
            low(rows, conv_width),
            low(rows, conv_width),
            full(rows, 4 * LANES),
            full(rows, width),
            low(rows, state_width),
            low(rows, 2 * width),
            low(chunks, n, width),
            full(chunks, n, width),
        ],
        [pltpu.VMEM((block + 8, conv_width), F32), pltpu.VMEM((n, width), F32)],
        "project",
        us=12,
    )

    block = MIX_BLOCK
    top = rows // block - 1
    down, states_down = rows_of(block, top), states_of(block, top)
    y, hb = call(
        partial(mix_kernel, block=block, **sizes),
        rows // block,
        [
            scalars,
            (act, down),
            (sact, down),
            (hs, down),
            (xd, down),
            (hf, states_down),
            (sb, states_down),
            (head_par, fixed),
            (spread, fixed),
        ],
        [down, states_down],
        [full(rows, width), low(chunks, n, width)],
        [pltpu.VMEM((n, width), F32)],
        "mix",
        us=7,
    )

    block = GATE_BLOCK
    up, states, up_lanes = rows_of(block), states_of(block), lanes_of(block)
    dgn, gz, sums = call(
        partial(gate_kernel, block=block),
        rows // block,
        [
            scalars,
            (y, up),
            (gate_pre, up),
            (cot_v, up),
            (oth_cot, up),
            (out_v, fixed),
            (gg, fixed),
        ],
        [up, up, up_lanes],
        [full(rows, width), low(rows, width), full(8, rows)],
        [],
        "gate",
        us=3,
    )

    oth_sums = swap_mp(sums)
    branch_oth = whole(
        partial(branch_kernel, other=True), (scalars, gz, out_v), [low(rows, width_own)], [], "branch_oth", us=3
    )[0]
    sums = sums + oth_sums
    branch_got = swap_mp(after(branch_oth, sums))
    sums_in = after(sums, branch_oth)

    g, dgp, dbr, dc, gb, gf, rd_gate, row_sums, small = call(
        partial(gate_back_kernel, block=block, inner_width=inner_width, **sizes),
        rows // block,
        [
            scalars,
            (sums_in, up_lanes),
            (gate_pre, up),
            (y, up),
            (act, up),
            (dgn, up),
            (cot_v, up),
            (oth_cot, up),
            (hs, up),
            (sact, up),
            (hf, states),
            (hb, states),
            (gg, fixed),
            (spread, fixed),
            (gather, fixed),
        ],
        [up, up, up, up, states, states, up_lanes, up, fixed],
        [
            low(rows, width),
            low(rows, width),
            low(rows, model),
            full(rows, 2 * n),
            low(chunks, n, width),
            full(chunks, n, width),
            full(8, rows),
            full(rows, LANES),
            full(8, width),
        ],
        [pltpu.VMEM((n, width), F32), pltpu.VMEM((block, 2 * width), BF16)],
        "gate_back",
        us=8,
    )

    def back_part(first, count, g, state):
        block = BACK_BLOCK
        here, states_here, here_lanes = rows_of(block, first), states_of(block, first), lanes_of(block, first)
        ins = [
            scalars,
            (g, here),
            (act, here),
            (sact, here),
            (hs, here),
            (xd, here),
            (row_sums, here),
            (hf, states_here),
            (hb, states_here),
            (gb, states_here),
            (gf, states_here),
            (dc, here),
            (pre, here),
            (slope, here),
            (conv, fixed),
            (head_par, fixed),
            (spread, fixed),
            (gather, fixed),
            *[(x, fixed) for x in state[:3]],
            (state[3], here),
            (state[4], here),
            (state[5], here_lanes),
        ]
        return call(
            partial(back_kernel, block=block, top=first, **sizes),
            count,
            ins,
            [here, here, here_lanes, fixed, fixed, fixed],
            [
                low(rows, conv_width),
                full(rows, 4 * LANES),
                full(8, rows),
                full(8, conv_width),
                full(8, conv_width),
                full(n, width),
            ],
            [
                pltpu.VMEM((block + 8, conv_width), F32),
                pltpu.VMEM((2 * CHUNK + 16, 2 * width), BF16),
                pltpu.VMEM((CHUNK, 2 * width), BF16),
                pltpu.VMEM((LANES, CHUNK), F32),
                pltpu.VMEM((CHUNK, LANES), F32),
            ],
            "mix_back",
            us=3 * count,
            aliases={len(ins) - 3: 0, len(ins) - 2: 1, len(ins) - 1: 2},
        )

    order_a, order_b = (0, 1, 2, 3), (0, 1, 2, 3)
    grad_out = mm_tn(gz, dbr).astype(BF16)
    grad_gate = mm_tn(normed, dgp).astype(BF16)
    keep, send, gain_part = whole(
        partial(pack_early_kernel, order=order_a),
        (scalars, grad_out, grad_gate, proj_gate),
        [low(width, model), low(width, model), full(8, model)],
        [],
        "pack_early",
    )

    def halve(keep, send, bit):
        got = swap_dp(send, bit)
        h = keep.shape[0] // 2
        return add_low(keep[:h], got[:h]), add_low(keep[h:], got[h:])

    def finish(keep, send, bit):
        return rest_of_dp(add_low(keep, swap_dp(send, bit)))

    def rest_of_dp(x):
        extra = SHARDS
        while extra < lax.axis_size("dp"):
            x = add_low(x, swap_dp(x, extra.bit_length() - 1))
            extra *= 2
        return x

    zeros = (
        jnp.zeros((8, conv_width), F32),
        jnp.zeros((n, width), F32),
        jnp.zeros((8, conv_width), F32),
    )
    keep, send = halve(keep, send, order_a[0])
    state = (
        *zeros,
        jnp.zeros((rows, conv_width), BF16),
        jnp.zeros((rows, 4 * LANES), F32),
        jnp.zeros((8, rows), F32),
    )
    parts = 4
    count = rows // BACK_BLOCK // parts
    g = after(g, send)
    sent, x = swap_dp(send, order_a[1]), None
    for k in range(parts):
        outs = back_part((parts - k) * count - 1, count, g, state)
        rest, rates, rd_rest, gconv, ext_carry, carry = outs
        if k == 1:
            sent, carry = lax.optimization_barrier((sent, carry))
        elif k == 2:
            sent, carry, branch_got = lax.optimization_barrier((sent, carry, branch_got))
        elif k == 3:
            sent, rest = lax.optimization_barrier((sent, rest))
        if k > 0:
            h = keep.shape[0] // 2
            if k < 3:
                keep, send = add_low(keep[:h], sent[:h]), add_low(keep[h:], sent[h:])
                carry = after(carry, send)
                sent = swap_dp(send, order_a[k + 1])
            else:
                x = rest_of_dp(add_low(keep, sent))
        state = (ext_carry, carry, gconv, rest, rates, rd_rest)

    block = GATE_BLOCK
    rates, x, rest = lax.optimization_barrier((rates, x, rest))
    sent = swap_dp(x, order_a[3])
    dz, ghead, rd_part = call(
        partial(rates_kernel, heads=heads, block=block),
        rows // block,
        [
            scalars,
            (rates, rows_of(block)),
            (hs, rows_of(block)),
            (rd_gate, lanes_of(block)),
            (rd_rest, lanes_of(block)),
            (head_par, fixed),
        ],
        [rows_of(block), fixed, lanes_of(block)],
        [low(rows, LANES), full(8, LANES), full(8, rows)],
        [],
        "rates",
    )
    grad_inner = mm_tn(normed, rest[:, :width]).astype(BF16)
    grad_state = mm_tn(rest[:, width:], normed).astype(BF16)
    grad_step = mm_tn(dz, normed).astype(BF16)
    keep, send = whole(
        partial(pack_late_kernel, order=order_b, heads=heads, state_width=state_width),
        (
            scalars, grad_inner, grad_state, grad_step, inner_v, w_state_t, gain, gain_part, gconv, ghead,
            small, gather,
        ),
        [low(LATE_ROWS * SHARDS // 2, model), low(LATE_ROWS * SHARDS // 2, model)],
        [pltpu.VMEM((8 * SHARDS, model), F32)],
        "pack_late",
    )

    def halve_with(keep, send, bit, *work):
        got = after(swap_dp(send, bit), *work)
        h = keep.shape[0] // 2
        return add_low(keep[:h], got[:h]), add_low(keep[h:], got[h:])

    x = jnp.concatenate([x, sent])
    send, x = lax.optimization_barrier((send, x))
    keep, send = halve_with(keep, send, order_b[0])
    send, x, rest = lax.optimization_barrier((send, x, rest))
    back_args = (scalars, dgp, rest, dz, rd_part, gate_v, inner_v, state_v, step_weight)
    dn_oth = whole(
        partial(back_project_kernel, other=True), back_args, [low(rows + 16, width_own)], [], "back_oth"
    )[0]
    dn_got = swap_mp(dn_oth)

    sent = swap_dp(x, order_a[2])
    dn_own = whole(
        partial(back_project_kernel, other=False), (*back_args[:2], after(rest, dn_oth), *back_args[3:]), [full(rows, width_own)], [], "back_own"
    )[0]
    keep, send = halve_with(keep, send, order_b[1], dn_own)
    x = jnp.concatenate([x, sent])
    send, x, gz_late, tokens_late, oth_late = lax.optimization_barrier((send, x, gz, tokens, oth_tokens))

    sent = swap_dp(x, order_a[1])
    branch_own = whole(
        partial(branch_kernel, other=False), (scalars, gz_late, out_v), [full(rows, width_own)], [], "branch_own"
    )[0]
    keep, send = halve_with(keep, send, order_b[2], branch_own)

    seq_mask = (jnp.arange(rows) < lengths[0]).astype(F32)[:, None]
    gate_inv = lax.rsqrt(sums[0] / inner_width + EPSILON)[:, None]
    tokens_f = tokens_late.astype(F32)
    block_out = (tokens_f + seq_mask * gate_inv * (branch_own + branch_got.astype(F32))).astype(BF16)
    z = rest_of_dp(add_low(keep, after(swap_dp(send, order_b[3]), block_out, dn_got)))
    part = model // SHARDS
    tail = z[part:]
    tail_row = lax.broadcasted_iota(jnp.int32, (LATE_ROWS - part, 1), 0)
    alone = (tail_row >= LATE_ROWS - part - 8) & (tail_row < LATE_ROWS - part - 4)
    tail_f = tail.astype(F32)
    tail = jnp.where(alone, tail_f, tail_f + swap_mp(tail).astype(F32)).astype(BF16)
    x = jnp.concatenate([x, sent])
    z, x = lax.optimization_barrier((jnp.concatenate([z[:part], tail]), x))
    sent = swap_dp(x, order_a[0])

    oth_f = oth_late.astype(F32)
    square = jnp.sum(tokens_f * tokens_f, axis=1, keepdims=True) + jnp.sum(
        oth_f * oth_f, axis=1, keepdims=True
    )
    inv = lax.rsqrt(square / model + EPSILON)
    part = rows // 4
    lines = dn_got[rows:, :part].astype(F32)
    oth_rd = (lines[0:4] + lines[4:8] + lines[8:12]).reshape(rows)
    rd_both = rd_part[0] + oth_rd
    grad_full = dn_own + dn_got[:rows].astype(F32)
    grad_tokens = (
        cotangent.astype(F32)
        + inv * (grad_full * norm_gain.astype(F32)[None])
        - tokens_f * (inv * inv * (rd_both[:, None] / model))
    )

    z = jnp.concatenate([z, after(swap_dp(z, order_b[3]), grad_tokens)])
    grad_proj_out, grad_proj_gate = whole(
        partial(unpack_early_kernel, order=order_a),
        (scalars, x, after(sent, z)),
        [full(width, model), full(model, width)],
        [],
        "unpack_early",
        in_vmem=False,
    )
    z = jnp.concatenate([z, after(swap_dp(z, order_b[2]), grad_proj_out)])
    z = jnp.concatenate([z, swap_dp(z, order_b[1])])
    (
        grad_proj_inner,
        grad_proj_state,
        step,
        grad_conv_inner,
        grad_conv_inner_bias,
        grad_conv_state,
        grad_conv_state_bias,
        grad_gate_gain,
        grad_step_bias,
        grad_decay_log,
        grad_skip,
        grad_norm_gain,
    ) = whole(
        partial(unpack_late_kernel, order=order_b, heads=heads),
        (scalars, z, swap_dp(z, order_b[0])),
        [
            full(model, width),
            full(model, state_width),
            full(heads, 2, model),
            full(4, width),
            full(1, width),
            full(4, state_width),
            full(1, state_width),
            full(1, width),
            full(2, heads),
            full(2, heads),
            full(1, heads),
            full(1, width_own),
        ],
        [pltpu.VMEM((state_width, model), F32), pltpu.VMEM((8 * SHARDS, model), F32)],
        "unpack_late",
        in_vmem=False,
    )
    return (
        block_out,
        grad_tokens,
        grad_norm_gain[0],
        grad_proj_gate,
        grad_proj_inner,
        grad_proj_state,
        step.transpose(2, 1, 0),
        grad_conv_inner,
        grad_conv_inner_bias[0],
        grad_conv_state,
        grad_conv_state_bias[0],
        grad_step_bias,
        grad_decay_log,
        grad_skip[0],
        grad_gate_gain[0],
        grad_proj_out,
    )


def solution(mesh):
    in_specs = (
        P("dp", "mp"),
        P("mp"),
        P(None, "mp"),
        P(None, "mp"),
        P(),
        P(None, None, "mp"),
        P(None, "mp"),
        P("mp"),
        P(),
        P(),
        P(None, "mp"),
        P(None, "mp"),
        P("mp"),
        P("mp"),
        P("mp", None),
        P("dp"),
        P("dp", "mp"),
    )
    out_specs = (
        P("dp", "mp"),
        P("dp", "mp"),
        P("mp"),
        P(None, "mp"),
        P(None, "mp"),
        P(),
        P(None, None, "mp"),
        P(None, "mp"),
        P("mp"),
        P(),
        P(),
        P(None, "mp"),
        P(None, "mp"),
        P("mp"),
        P("mp"),
        P("mp", None),
    )
    return jax.shard_map(body, mesh=mesh, in_specs=in_specs, out_specs=out_specs, check_vma=False)
```

```python
from functools import partial

import jax
import jax.numpy as jnp
from jax import lax
from jax.experimental import pallas as pl
from jax.experimental.pallas import tpu as pltpu
from jax.sharding import PartitionSpec as P

EPSILON = 1e-05
CHUNK = 128
PROJECT_BLOCK, MIX_BLOCK, GATE_BLOCK, BACK_BLOCK, RATES_BLOCK = 256, 256, 256, 128, 512
LANES = 128
F32 = jnp.float32
BF16 = jnp.bfloat16
HIGHEST = lax.Precision.HIGHEST
VMEM_LIMIT = 12 * 1024 * 1024
SHARDS = 16
LOG2_E = 1.4426950408889634
LATE_ROWS = 72


def mm(a, b):
    return jnp.dot(a, b, preferred_element_type=F32)


def mm_nt(a, b):
    return lax.dot_general(a, b, (((1,), (1,)), ((), ())), preferred_element_type=F32)


def mm_tn(a, b):
    return lax.dot_general(a, b, (((0,), (0,)), ((), ())), preferred_element_type=F32)


def split_two(v):
    hi = v.astype(BF16)
    return hi, (v - hi.astype(F32)).astype(BF16)


def split_three(v):
    hi, mid = split_two(v)
    return hi, mid, (v - hi.astype(F32) - mid.astype(F32)).astype(BF16)


def expand(v, spread):
    hi, lo = split_two(v)
    return mm(jnp.concatenate([hi, lo], axis=1), spread)


def row_mask(block, rows, length):
    pos = block * rows + lax.broadcasted_iota(jnp.int32, (rows, 1), 0)
    return (pos < length).astype(F32)


def to_row(col_a, col_b):
    rows = col_a.shape[0]
    lane = lax.broadcasted_iota(jnp.int32, (rows, LANES), 1)
    tile = jnp.where(lane == 0, col_a, jnp.where(lane == 1, col_b, 0.0))
    return jnp.transpose(tile)[0:8, :]


def sigmoid(v):
    return 0.5 * jnp.tanh(0.5 * v) + 0.5


def natural(rank, own, oth):
    return jnp.where(
        rank == 0, jnp.concatenate([own, oth], axis=1), jnp.concatenate([oth, own], axis=1)
    )


def eight(row):
    return jnp.broadcast_to(row, (8, row.shape[1]))


def stage_kernel(w_state, w_step, *refs, count, head_dim):
    sources, outs, sems = refs[:count], refs[count:-1], refs[-1]
    spread, gather, w_state_t = outs[count:]
    copies = [
        pltpu.make_async_copy(src, dst, sems.at[k]) for k, (src, dst) in enumerate(zip(sources, outs))
    ]
    for copy in copies:
        copy.start()
    state_width = w_state.shape[1]
    w_state_t[:state_width, :] = jnp.transpose(w_state[...].astype(F32)).astype(BF16)
    w_state_t[state_width:, :] = jnp.transpose(w_step[...].astype(F32)).astype(BF16)
    head = lax.broadcasted_iota(jnp.int32, spread.shape, 1) // head_dim
    row = lax.broadcasted_iota(jnp.int32, spread.shape, 0) % LANES
    spread[...] = jnp.where(head == row, 1.0, 0.0).astype(BF16)
    head = lax.broadcasted_iota(jnp.int32, gather.shape, 0) // head_dim
    lane = lax.broadcasted_iota(jnp.int32, gather.shape, 1)
    gather[...] = jnp.where(head == lane, 1.0, 0.0).astype(BF16)
    for copy in copies:
        copy.wait()


def project_kernel(
    i, scalars, own, oth, gain, w_gate, w_inner, w_state, w_step, conv, head_par, spread,
    normed_ref, gate_ref, pre_ref, slope_ref, hs_ref, act_ref, sact_ref, xd_ref, hf_ref, sb_ref,
    ext, carry, *, heads, width, state_width, block,
):
    @pl.when(i == 0)
    def _():
        ext[0:8, :] = jnp.zeros((8, ext.shape[1]), F32)
        carry[...] = jnp.zeros_like(carry)

    x = natural(scalars[1], own[...], oth[...]).astype(F32)
    inv = lax.rsqrt(jnp.mean(x * x, axis=-1, keepdims=True) + EPSILON)
    normed = (x * inv * gain[...]).astype(BF16)
    normed_ref[...] = normed
    step_pre = mm(normed, w_step[...])
    z = step_pre + head_par[0:1, :]
    dt = jnp.maximum(z, 0.0) + jnp.log1p(jnp.exp(-jnp.abs(z)))
    rate = head_par[1:2, :] * dt
    dtm = dt * row_mask(i, block, scalars[0])
    hs_ref[:, 0:LANES] = z
    hs_ref[:, LANES : 2 * LANES] = dt
    tri_r = lax.broadcasted_iota(jnp.int32, (CHUNK, CHUNK), 0)
    tri_c = lax.broadcasted_iota(jnp.int32, (CHUNK, CHUNK), 1)
    tri = (tri_c <= tri_r).astype(F32)
    is_fwd = lax.broadcasted_iota(jnp.int32, (CHUNK, LANES), 1) < heads
    per = block // CHUNK
    to_spread = [dtm]
    keeps = []
    for c_idx in range(per):
        rows = slice(c_idx * CHUNK, (c_idx + 1) * CHUNK)
        rate_c = rate[rows]
        cum = jnp.dot(tri, rate_c, precision=HIGHEST, preferred_element_type=F32)
        tot = cum[CHUNK - 1 : CHUNK, :]
        cumx = jnp.where(is_fwd, cum, cum - rate_c)
        hs_ref[rows, 2 * LANES : 3 * LANES] = cumx
        hs_ref[rows, 3 * LANES :] = jnp.broadcast_to(tot, (CHUNK, LANES))
        to_spread.append(dtm[rows] * jnp.exp(jnp.where(is_fwd, tot - cumx, cumx)))
        keeps.append(eight(jnp.exp(tot)))
    wide = expand(jnp.concatenate(to_spread + keeps, axis=0), spread[...])

    ext[8 : 8 + block, 0:width] = mm(normed, w_inner[...])
    ext[8 : 8 + block, width:] = mm(normed, w_state[...])
    gate_ref[...] = mm(normed, w_gate[...])
    whole_ext = ext[...]
    pre = whole_ext[8:]
    pre_ref[...] = pre.astype(BF16)
    c = conv[4:5, :] + conv[3:4, :] * pre
    for j in range(3):
        c = c + conv[j : j + 1, :] * pltpu.roll(whole_ext, 3 - j, 0)[8:]
    sg = sigmoid(c)
    both = c * sg
    slope_ref[...] = (sg * (1.0 + c * (1.0 - sg))).astype(BF16)
    ext[0:8, :] = ext[block : block + 8, :]
    act = both[:, :width]
    act_ref[...] = act
    sact = both[:, width:].astype(BF16)
    sact_ref[...] = sact
    xd_ref[:, 0:width] = (act * wide[0:block, :width]).astype(BF16)
    xd_ref[:, width:] = (act * wide[0:block, width:]).astype(BF16)
    n = state_width // 4
    for c_idx in range(per):
        rows = slice(c_idx * CHUNK, (c_idx + 1) * CHUNK)
        coef = wide[block + c_idx * CHUNK : block + (c_idx + 1) * CHUNK]
        keep = wide[2 * block + 8 * c_idx : 2 * block + 8 * c_idx + 1, :width]
        hf_ref[c_idx] = carry[...].astype(BF16)
        carry[...] = carry[...] * keep + mm_tn(
            sact[rows, 0:n], (act[rows] * coef[:, :width]).astype(BF16)
        )
        sb_ref[c_idx] = mm_tn(
            sact[rows, 2 * n : 3 * n], (act[rows] * coef[:, width:]).astype(BF16)
        )


def pair_tiles(pair):
    lane = lax.broadcasted_iota(jnp.int32, (1, pair.shape[1]), 1)
    first = (lane < pair.shape[1] // 2).astype(F32)
    keep_a, keep_b = first.astype(BF16), (1.0 - first).astype(BF16)
    return jnp.concatenate([pair * keep_a, pair * keep_b], axis=0)


def mix_kernel(
    i, scalars, act, sact, hs, xd, hf, sb, head_par, spread, y_ref, hb_ref, carry,
    *, heads, width, state_width, block,
):
    @pl.when(i == 0)
    def _():
        carry[...] = jnp.zeros_like(carry)

    n = state_width // 4
    per = block // CHUNK
    r = lax.broadcasted_iota(jnp.int32, (CHUNK, CHUNK), 0)
    c = lax.broadcasted_iota(jnp.int32, (CHUNK, CHUNK), 1)
    lower = c < r
    upper = c > r
    is_fwd = lax.broadcasted_iota(jnp.int32, (block, LANES), 1) < heads
    cum_all = hs[:, 2 * LANES : 3 * LANES]
    tot_all = hs[:, 3 * LANES :]
    wide = expand(
        jnp.concatenate(
            [jnp.exp(jnp.where(is_fwd, cum_all, tot_all - cum_all))]
            + [jnp.exp(tot_all[k * CHUNK : k * CHUNK + 8]) for k in range(per)]
            + [eight(head_par[2:3, :])],
            axis=0,
        ),
        spread[...],
    )
    skip = wide[block + 8 * per : block + 8 * per + 1]
    for c_idx in reversed(range(per)):
        rows = slice(c_idx * CHUNK, (c_idx + 1) * CHUNK)
        cumx = cum_all[rows] * LOG2_E
        cum_t = jnp.transpose(cumx)
        sact_c = sact[rows, :]
        b_f, c_f = sact_c[:, 0:n], sact_c[:, n : 2 * n]
        b_b, c_b = sact_c[:, 2 * n : 3 * n], sact_c[:, 3 * n :]
        s_f = jnp.where(lower, mm_nt(c_f, b_f), 0.0)
        s_b = jnp.where(upper, mm_nt(c_b, b_b), 0.0)
        hb = carry[...].astype(BF16)
        hb_ref[c_idx] = hb
        in_f = mm(c_f, hf[c_idx])
        in_b = mm(c_b, hb)
        keep = wide[block + 8 * c_idx : block + 8 * c_idx + 1, width:]
        carry[...] = carry[...] * keep + sb[c_idx]
        for p in range(heads // 2):
            lanes = slice(p * LANES, (p + 1) * LANES)
            lanes_b = slice(width + p * LANES, width + (p + 1) * LANES)
            w_f, w_b = [], []
            for h in (2 * p, 2 * p + 1):
                damp = jnp.exp2(
                    jnp.minimum(
                        cumx[:, h : h + 1] - cum_t[h : h + 1, :],
                        cum_t[heads + h : heads + h + 1, :] - cumx[:, heads + h : heads + h + 1],
                    )
                )
                w_f.append((s_f * damp).astype(BF16))
                w_b.append((s_b * damp).astype(BF16))
            out = mm(
                jnp.concatenate(w_f + w_b, axis=1),
                jnp.concatenate([pair_tiles(xd[rows, lanes]), pair_tiles(xd[rows, lanes_b])], axis=0),
            )
            y_ref[rows, lanes] = (
                out
                + wide[rows, lanes] * in_f[:, lanes]
                + wide[rows, lanes_b] * in_b[:, lanes]
                + skip[:, lanes] * act[rows, lanes]
            )


def gate_kernel(i, scalars, y, gate, cown, coth, po, gg, dgn_ref, gz_ref, sums_ref, *, block):
    gp = gate[...]
    gated = y[...] * (gp * sigmoid(gp))
    mask = row_mask(i, block, scalars[0])
    cot = natural(scalars[1], cown[...], coth[...])
    dgn = mm_nt((cot.astype(F32) * mask).astype(BF16), po[...])
    dgn_ref[...] = dgn
    scaled = gated * gg[...]
    gz_ref[...] = scaled.astype(BF16)
    sums_ref[...] = to_row(
        jnp.sum(gated * gated, axis=1, keepdims=True), jnp.sum(dgn * scaled, axis=1, keepdims=True)
    )


def gate_back_kernel(
    i, scalars, sums, gate, y, act, dgn, cown, coth, hs, sact, hf, hb, gg, spread, gather,
    g_ref, dgp_ref, dbr_ref, dc_ref, gb_ref, gf_ref, rd_ref, rows_ref, small_ref, carry, prod,
    *, heads, width, state_width, block, inner_width,
):
    @pl.when(i == 0)
    def _():
        carry[...] = jnp.zeros_like(carry)
        small_ref[...] = jnp.zeros_like(small_ref)

    per = block // CHUNK
    is_fwd = lax.broadcasted_iota(jnp.int32, (block, LANES), 1) < heads
    cum_all = hs[:, 2 * LANES : 3 * LANES]
    tot_all = hs[:, 3 * LANES :]
    wide = expand(
        jnp.concatenate(
            [jnp.exp(jnp.where(is_fwd, cum_all, tot_all - cum_all))]
            + [jnp.exp(tot_all[k * CHUNK : k * CHUNK + 8]) for k in range(per)],
            axis=0,
        ),
        spread[...],
    )
    cols = jnp.transpose(sums[...])
    gate_inv = lax.rsqrt(cols[:, 0:1] / inner_width + EPSILON)
    gate_dot = cols[:, 1:2] / inner_width
    gp = gate[...]
    sg = sigmoid(gp)
    act_gate = gp * sg
    yv = y[...]
    gated = yv * act_gate
    dg = dgn[...]
    small_ref[0:1, :] += jnp.sum(dg * gated * gate_inv, axis=0, keepdims=True)
    d_gated = gate_inv * (dg * gg[...]) - gated * (gate_inv * gate_inv * gate_inv * gate_dot)
    d_gp = d_gated * yv * (sg * (1.0 + gp * (1.0 - sg)))
    dgp_ref[...] = d_gp.astype(BF16)
    rd = jnp.sum(d_gp * gp, axis=1, keepdims=True)
    rd_ref[...] = to_row(rd, jnp.zeros_like(rd))
    d_y = d_gated * act_gate
    g_ref[...] = d_y.astype(BF16)
    small_ref[1:2, :] += jnp.sum(d_y * act[...], axis=0, keepdims=True)
    mask = row_mask(i, block, scalars[0])
    cot = natural(scalars[1], cown[...], coth[...])
    dbr_ref[...] = (cot.astype(F32) * (mask * gate_inv)).astype(BF16)
    n = state_width // 4
    for c_idx in range(per):
        rows = slice(c_idx * CHUNK, (c_idx + 1) * CHUNK)
        dy_c = d_y[rows]
        dyf = dy_c * wide[rows, :width]
        dyb = dy_c * wide[rows, width:]
        prod[rows, 0:width] = (dyf * mm(sact[rows, n : 2 * n], hf[c_idx])).astype(BF16)
        prod[rows, width:] = (dyb * mm(sact[rows, 3 * n :], hb[c_idx])).astype(BF16)
        dyf = dyf.astype(BF16)
        dyb = dyb.astype(BF16)
        dc_ref[rows, 0:n] = mm_nt(dyf, hf[c_idx])
        dc_ref[rows, n : 2 * n] = mm_nt(dyb, hb[c_idx])
        gb_ref[c_idx] = carry[...].astype(BF16)
        keep = wide[block + 8 * c_idx : block + 8 * c_idx + 1, width:]
        carry[...] = carry[...] * keep + mm_tn(sact[rows, 3 * n :], dyb)
        gf_ref[c_idx] = mm_tn(sact[rows, n : 2 * n], dyf)
    rows_ref[...] = mm(prod[...], gather[...])


def back_kernel(
    i, scalars, g, act, sact, hs, xd, row_in, hf, hb, gb, gf, dc, pre, slope, conv, head_par, spread, gather,
    ext_in, carry_in, gconv_in, _rest, _rates, _rd, rest_ref, rates_ref, rd_ref, gconv_ref, ext_out,
    carry, ext, stack, xs, rsum, csum,
    *, heads, width, state_width, block, top,
):
    blk = top - i
    per = block // CHUNK

    @pl.when(i == 0)
    def _():
        ext[block:, :] = ext_in[...]
        carry[...] = carry_in[...]
        gconv_ref[...] = gconv_in[...]
        rsum[...] = jnp.zeros_like(rsum)
        csum[...] = jnp.zeros_like(csum)

    n = state_width // 4
    r = lax.broadcasted_iota(jnp.int32, (CHUNK, CHUNK), 0)
    c = lax.broadcasted_iota(jnp.int32, (CHUNK, CHUNK), 1)
    later = c > r
    earlier = c < r
    is_fwd_all = lax.broadcasted_iota(jnp.int32, (block, LANES), 1) < heads
    is_fwd = lax.broadcasted_iota(jnp.int32, (CHUNK, LANES), 1) < heads
    mask = row_mask(blk, block, scalars[0])
    cum_all = hs[:, 2 * LANES : 3 * LANES]
    tot_all = hs[:, 3 * LANES :]
    wide = expand(
        jnp.concatenate(
            [jnp.exp(jnp.where(is_fwd_all, tot_all - cum_all, cum_all)), hs[:, LANES : 2 * LANES] * mask]
            + [jnp.exp(tot_all[k * CHUNK : k * CHUNK + 8]) for k in range(per)]
            + [eight(head_par[2:3, :])],
            axis=0,
        ),
        spread[...],
    )
    skip = wide[2 * block + 8 * per : 2 * block + 8 * per + 1]
    for c_idx in reversed(range(per)):
        rows = slice(c_idx * CHUNK, (c_idx + 1) * CHUNK)
        rows_dt = slice(block + c_idx * CHUNK, block + (c_idx + 1) * CHUNK)
        cumx = cum_all[rows] * LOG2_E
        cum_t = jnp.transpose(cumx)
        sact_c = sact[rows, :]
        b_f, c_f = sact_c[:, 0:n], sact_c[:, n : 2 * n]
        b_b, c_b = sact_c[:, 2 * n : 3 * n], sact_c[:, 3 * n :]
        s_f = jnp.where(later, mm_nt(b_f, c_f), 0.0)
        s_b = jnp.where(earlier, mm_nt(b_b, c_b), 0.0)
        s_all = s_f + s_b
        grad_f = carry[...]
        grad_f_low = grad_f.astype(BF16)
        grad_b_low = gb[c_idx]
        keep = wide[2 * block + 8 * c_idx : 2 * block + 8 * c_idx + 1]
        keep_f = keep[:, :width]
        edge_f = keep_f * jnp.sum(grad_f * hf[c_idx].astype(F32), axis=0, keepdims=True)
        edge_b = keep[:, width:] * jnp.sum(
            hb[c_idx].astype(F32) * grad_b_low.astype(F32), axis=0, keepdims=True
        )
        e_hi, e_lo = split_two(eight(jnp.concatenate([edge_f, edge_b], axis=1)))
        stack[2 * CHUNK :, :] = jnp.concatenate([e_hi, e_lo], axis=0)
        carry[...] = grad_f * keep_f + gf[c_idx]
        in_f = mm(b_f, grad_f_low)
        in_b = mm(b_b, grad_b_low)
        d_scores = jnp.zeros((CHUNK, CHUNK), F32)
        for p in range(heads // 2):
            lanes = slice(p * LANES, (p + 1) * LANES)
            lanes_b = slice(width + p * LANES, width + (p + 1) * LANES)
            g_pair = g[rows, lanes]
            xf_pair = xd[rows, lanes]
            xb_pair = xd[rows, lanes_b]
            dw = mm_nt(
                jnp.concatenate([pair_tiles(xf_pair), pair_tiles(xb_pair)], axis=0), g_pair
            )
            w_f, w_b = [], []
            for q, h in enumerate((2 * p, 2 * p + 1)):
                damp = jnp.exp2(
                    jnp.minimum(
                        cum_t[h : h + 1, :] - cumx[:, h : h + 1],
                        cumx[:, heads + h : heads + h + 1] - cum_t[heads + h : heads + h + 1, :],
                    )
                )
                w_f.append((s_f * damp).astype(BF16))
                w_b.append((s_b * damp).astype(BF16))
                part = jnp.where(
                    later, dw[q * CHUNK : (q + 1) * CHUNK], dw[(2 + q) * CHUNK : (3 + q) * CHUNK]
                )
                part = part * damp
                d_scores = d_scores + part
                e_all = part * s_all
                e_fwd = jnp.where(later, e_all, 0.0)
                sum_all = jnp.sum(e_all, axis=0, keepdims=True)
                sum_fwd = jnp.sum(e_fwd, axis=0, keepdims=True)
                rsum[h : h + 1, :] = sum_fwd
                rsum[heads + h : heads + h + 1, :] = sum_fwd - sum_all
                sum_all = jnp.sum(e_all, axis=1, keepdims=True)
                sum_fwd = jnp.sum(e_fwd, axis=1, keepdims=True)
                csum[:, h : h + 1] = -sum_fwd
                csum[:, heads + h : heads + h + 1] = sum_all - sum_fwd
            dx = mm(
                jnp.concatenate(
                    [jnp.concatenate(w_f, axis=1), jnp.concatenate(w_b, axis=1)], axis=0
                ),
                pair_tiles(g_pair),
            )
            edge_pf = wide[rows, lanes]
            edge_pb = wide[rows, lanes_b]
            inter_f = edge_pf * in_f[:, lanes]
            inter_b = edge_pb * in_b[:, lanes]
            dx_f = dx[:CHUNK] + inter_f
            dx_b = dx[CHUNK:] + inter_b
            xf = xf_pair.astype(F32)
            xb = xb_pair.astype(F32)
            xs[:, lanes] = (xf * edge_pf).astype(BF16)
            xs[:, lanes_b] = (xb * edge_pb).astype(BF16)
            act_p = act[rows, lanes]
            stack[0:CHUNK, lanes] = (act_p * dx_f).astype(BF16)
            stack[0:CHUNK, lanes_b] = (act_p * dx_b).astype(BF16)
            stack[CHUNK : 2 * CHUNK, lanes] = (xf * inter_f).astype(BF16)
            stack[CHUNK : 2 * CHUNK, lanes_b] = (xb * inter_b).astype(BF16)
            d_inner = (
                skip[:, lanes] * g_pair.astype(F32)
                + wide[rows_dt, lanes] * dx_f
                + wide[rows_dt, lanes_b] * dx_b
            )
            ext[rows, lanes] = d_inner * slope[rows, lanes].astype(F32)
        low_f = jnp.where(later, d_scores, 0.0).astype(BF16)
        low_b = jnp.where(earlier, d_scores, 0.0).astype(BF16)
        d_bf = mm(low_f, c_f) + mm_nt(xs[:, :width], grad_f_low)
        d_cf = mm_tn(low_f, b_f) + dc[rows, 0:n]
        d_bb = mm(low_b, c_b) + mm_nt(xs[:, width:], grad_b_low)
        d_cb = mm_tn(low_b, b_b) + dc[rows, n : 2 * n]
        d_state = jnp.concatenate([d_bf, d_cf, d_bb, d_cb], axis=1)
        ext[rows, width:] = d_state * slope[rows, width:].astype(F32)
        head_sums = mm(stack[...], gather[...])
        rin = row_in[rows, :]
        ahead = head_sums[CHUNK : 2 * CHUNK]
        rates_ref[rows, 0:LANES] = (
            jnp.transpose(rsum[...]) + csum[...] + jnp.where(is_fwd, rin, ahead)
        )
        rates_ref[rows, LANES : 2 * LANES] = jnp.where(is_fwd, ahead, rin)
        rates_ref[rows, 2 * LANES : 3 * LANES] = head_sums[0:CHUNK] * mask[rows]
        edge = head_sums[2 * CHUNK : 2 * CHUNK + 1] + head_sums[2 * CHUNK + 8 : 2 * CHUNK + 9]
        rates_ref[rows, 3 * LANES :] = jnp.broadcast_to(edge, (CHUNK, LANES))

    prev = pre[...].astype(F32)
    whole_ext = ext[...]
    moved = whole_ext[:block]
    acc = conv[3:4, :] * moved
    gconv_ref[4:5, :] += jnp.sum(moved, axis=0, keepdims=True)
    gconv_ref[3:4, :] += jnp.sum(moved * prev, axis=0, keepdims=True)
    for j in range(3):
        moved = pltpu.roll(whole_ext, block + 8 - (3 - j), 0)[:block]
        acc = acc + conv[j : j + 1, :] * moved
        gconv_ref[j : j + 1, :] += jnp.sum(moved * prev, axis=0, keepdims=True)
    rest_ref[...] = acc.astype(BF16)
    rd = jnp.sum(acc * prev, axis=1, keepdims=True)
    rd_ref[...] = to_row(rd, jnp.zeros_like(rd))
    ext[block:, :] = ext[0:8, :]
    ext_out[...] = ext[0:8, :]


def rates_kernel(i, scalars, rates, hs, rd_a, rd_b, head_par, dz_ref, ghead_ref, rd_ref, *, heads, block):
    @pl.when(i == 0)
    def _():
        ghead_ref[...] = jnp.zeros_like(ghead_ref)

    r = lax.broadcasted_iota(jnp.int32, (CHUNK, CHUNK), 0)
    c = lax.broadcasted_iota(jnp.int32, (CHUNK, CHUNK), 1)
    tri = jnp.where(c <= r, 1.0, 0.0).astype(BF16)
    is_fwd = lax.broadcasted_iota(jnp.int32, (CHUNK, LANES), 1) < heads
    neg = head_par[1:2, :]
    for c_idx in range(block // CHUNK):
        rows = slice(c_idx * CHUNK, (c_idx + 1) * CHUNK)
        d_cum = rates[rows, 0:LANES]
        d_run = rates[rows, LANES : 2 * LANES]
        sums = mm(tri, jnp.concatenate([*split_three(d_cum), *split_two(d_run)], axis=1))
        ahead = sums[:, 0:LANES] + sums[:, LANES : 2 * LANES] + sums[:, 2 * LANES : 3 * LANES]
        run = sums[:, 3 * LANES : 4 * LANES] + sums[:, 4 * LANES :]
        behind = ahead[CHUNK - 1 :, :] - ahead
        d_rate = jnp.where(is_fwd, behind + d_cum + run - d_run, behind + run)
        d_rate = d_rate + rates[rows, 3 * LANES :]
        z = hs[rows, 0:LANES]
        d_step = neg * d_rate + rates[rows, 2 * LANES : 3 * LANES]
        d_z = d_step / (1.0 + jnp.exp(-z))
        dt = hs[rows, LANES : 2 * LANES]
        ghead_ref[0:1, :] += jnp.sum(d_rate * (neg * dt), axis=0, keepdims=True)
        ghead_ref[1:2, :] += jnp.sum(d_z, axis=0, keepdims=True)
        dz_ref[rows, :] = d_z.astype(BF16)
        rd = jnp.sum(d_z * (z - head_par[0:1, :]), axis=1, keepdims=True)
        rd_ref[:, rows] = rd_a[:, rows] + rd_b[:, rows] + to_row(rd, jnp.zeros_like(rd))


def columns_of(scalars, other, size):
    rank = scalars[1]
    return pl.ds(pl.multiple_of((1 - rank if other else rank) * size, LANES), size)


def branch_kernel(scalars, gz, po, out_ref, *, other):
    cols = columns_of(scalars, other, out_ref.shape[1])
    out_ref[...] = mm(gz[...], po[:, cols]).astype(out_ref.dtype)


def back_project_kernel(
    scalars, dgp, rest, dz, rd, w_gate, w_inner, w_state, w_step, out_ref, *, other
):
    rows, size = dgp.shape[0], out_ref.shape[1]
    at = columns_of(scalars, other, size)
    a = w_inner.shape[1]
    out_ref[0:rows, :] = (
        mm_nt(dgp[...], w_gate[at, :])
        + mm_nt(rest[:, 0:a], w_inner[at, :])
        + mm_nt(rest[:, a:], w_state[at, :])
        + mm_nt(dz[...], w_step[at, :])
    ).astype(out_ref.dtype)
    if other:
        part = rows // 4
        lines = jnp.concatenate([rd[0:1, k * part : (k + 1) * part] for k in range(4)], axis=0)
        lines = jnp.concatenate(split_three(lines) + (jnp.zeros((4, part), BF16),), axis=0)
        out_ref[rows : rows + 16, 0:part] = lines
        out_ref[rows : rows + 16, part:] = jnp.zeros((16, size - part), BF16)


def home_of(r, me, order):
    j = me % SHARDS
    levels = len(order)
    for p, bit in enumerate(order):
        if (r >> (levels - 1 - p)) & 1:
            j = jnp.bitwise_xor(j, 1 << bit)
    return j


def lanes_in(orders, width):
    size = width // len(orders)
    return [
        (r, slice(k * size, (k + 1) * size), order) for k, order in enumerate(orders) for r in range(SHARDS)
    ]


def pack_early_kernel(
    scalars, grad_out, grad_gate, w_gate, keep_ref, send_ref, gain_ref, *, order
):
    hi, lo = split_two(grad_gate[...].astype(F32) * w_gate[...].astype(F32))
    ones = jnp.ones((8, hi.shape[1]), BF16)
    gain_ref[...] = mm_nt(ones, hi) + mm_nt(ones, lo)
    part = grad_out.shape[0] // SHARDS
    for r in range(SHARDS):
        j = home_of(r, scalars[2], order)
        out = keep_ref if r < SHARDS // 2 else send_ref
        at = (r % (SHARDS // 2)) * 2 * part
        src = pl.ds(pl.multiple_of(j * part, part), part)
        out[at : at + part, :] = grad_out[src, :]
        out[at + part : at + 2 * part, :] = grad_gate[src, :]


def unpack_early_kernel(scalars, first, second, out_ref, gate_ref, *, order):
    part = out_ref.shape[0] // SHARDS
    for r in range(SHARDS):
        j = home_of(r, scalars[2], order)
        src = first if r < SHARDS // 2 else second
        at = (r % (SHARDS // 2)) * 2 * part
        dst = pl.ds(pl.multiple_of(j * part, part), part)
        out_ref[dst, :] = src[at : at + part, :].astype(F32)
        gate_ref[dst, :] = src[at + part : at + 2 * part, :].astype(F32)


def pack_late_kernel(
    scalars, inner, state, step_low, w_inner, w_state_t, gain, gain_part, gconv, ghead, small, gather,
    keep_ref, send_ref, misc, *, orders, heads, state_width,
):
    model, width = w_inner.shape
    hi, lo = split_two(inner[...].astype(F32) * w_inner[...].astype(F32))
    ones = jnp.ones((8, hi.shape[1]), BF16)
    gain_row = (mm_nt(ones, hi) + mm_nt(ones, lo) + gain_part[...])[0:1]
    step = step_low[...].astype(F32)
    w_t = w_state_t[...].astype(F32)
    gain_row += jnp.sum(state[...].astype(F32) * w_t[:state_width], axis=0, keepdims=True)
    gain_row += jnp.sum(step * w_t[state_width:], axis=0, keepdims=True)
    gain_row = gain_row / gain[...]
    misc[...] = jnp.zeros_like(misc)

    def put_single(k, row):
        at = (k // 2) * 8 + k % 2
        misc[at : at + 1, :] = row

    for k in range(2 * heads):
        put_single(k, step[k : k + 1, :])
    at = 2 * heads
    for k in range(5):
        put_single(at + k, gconv[k : k + 1, 0:width])
    put_single(at + 5, small[0:1, :])
    hi, lo = split_two(eight(small[1:2, :]))
    skip = mm(hi, gather[0:width, :]) + mm(lo, gather[0:width, :])
    at = ((at + 6) // 2) * 8 + (at + 6) % 2
    misc[at : at + 1, 2 * LANES : 3 * LANES] = skip[0:1]
    misc[at : at + 1, 0:LANES] = ghead[0:1, :]
    misc[at : at + 1, LANES : 2 * LANES] = ghead[1:2, :]
    fit = model // state_width
    for k in range(5):
        at = (k // fit) * 8 + 4
        lanes = slice((k % fit) * state_width, (k % fit + 1) * state_width)
        misc[at : at + 1, lanes] = gconv[k : k + 1, width:]
    at = (-(-5 // fit)) * 8 + 4
    misc[at : at + 1, :] = gain_row
    part = model // SHARDS
    part_s = state_width // SHARDS
    rows = part + part_s + 8
    for r, cols, order in lanes_in(orders, model):
        j = home_of(r, scalars[2], order)
        out = keep_ref if r < SHARDS // 2 else send_ref
        at = (r % (SHARDS // 2)) * rows
        out[at : at + part, cols] = inner[pl.ds(pl.multiple_of(j * part, part), part), cols]
        out[at + part : at + part + part_s, cols] = state[
            pl.ds(pl.multiple_of(j * part_s, part_s), part_s), cols
        ]
        out[at + part + part_s : at + rows, cols] = misc[
            pl.ds(pl.multiple_of(j * 8, 8), 8), cols
        ].astype(BF16)


def unpack_late_kernel(
    scalars, first, second, inner_ref, state_ref, step_ref, convi_ref, convi_b_ref, convs_ref, convs_b_ref,
    gg_ref, bias_ref, decay_ref, skip_ref, gain_ref, state, misc, *, orders, heads,
):
    model = inner_ref.shape[0]
    state_width = state_ref.shape[1]
    part = model // SHARDS
    part_s = state_width // SHARDS
    rows = part + part_s + 8
    for r, cols, order in lanes_in(orders, model):
        j = home_of(r, scalars[2], order)
        src = first if r < SHARDS // 2 else second
        at = (r % (SHARDS // 2)) * rows
        inner_ref[pl.ds(pl.multiple_of(j * part, part), part), cols] = src[at : at + part, cols].astype(
            F32
        )
        state[pl.ds(pl.multiple_of(j * part_s, part_s), part_s), cols] = src[
            at + part : at + part + part_s, cols
        ].astype(F32)
        misc[pl.ds(pl.multiple_of(j * 8, 8), 8), cols] = src[at + part + part_s : at + rows, cols].astype(
            F32
        )
    state_ref[...] = jnp.transpose(state[...])

    def single(k):
        at = (k // 2) * 8 + k % 2
        return misc[at : at + 1, :]

    for h in range(heads):
        for d in range(2):
            step_ref[h, d : d + 1, :] = single(d * heads + h)
    at = 2 * heads
    for k in range(4):
        convi_ref[k : k + 1, :] = single(at + k)
    convi_b_ref[...] = single(at + 4).reshape(convi_b_ref.shape)
    gg_ref[...] = single(at + 5).reshape(gg_ref.shape)
    head_row = single(at + 6)
    for d in range(2):
        decay_ref[d : d + 1, :] = head_row[:, d * heads : (d + 1) * heads]
        bias_ref[d : d + 1, :] = head_row[:, LANES + d * heads : LANES + (d + 1) * heads]
    skip_ref[...] = head_row[:, 2 * LANES : 2 * LANES + heads]
    fit = model // state_width
    for k in range(5):
        at = (k // fit) * 8 + 4
        lanes = slice((k % fit) * state_width, (k % fit + 1) * state_width)
        out, row = (convs_ref, k) if k < 4 else (convs_b_ref, 0)
        out[row : row + 1, :] = misc[at : at + 1, lanes]
    at = (-(-5 // fit)) * 8 + 4
    half = model // 2
    gain_ref[...] = jnp.where(
        scalars[1] == 0, misc[at : at + 1, :half], misc[at : at + 1, half:]
    ).reshape(gain_ref.shape)


def place(i, top):
    return i if top is None else top - i


def rows_of(block, top=None):
    return lambda ref, i: ref.at[pl.ds(pl.multiple_of(place(i, top) * block, block), block)]


def lanes_of(block, top=None):
    return lambda ref, i: ref.at[:, pl.ds(pl.multiple_of(place(i, top) * block, block), block)]


def states_of(block, top=None):
    per = block // CHUNK
    return lambda ref, i: ref.at[pl.ds(place(i, top) * per, per)]


def fixed(ref, i):
    return ref


def call(kernel, blocks, ins, out_views, out_shape, scratch, name, aliases=None, us=0.0):
    views = [view for _, view in ins[1:]] + out_views
    arrays = [ins[0]] + [
        pltpu.with_memory_space_constraint(x, pltpu.VMEM) if view is not fixed else x
        for x, view in ins[1:]
    ]

    def looped(scalars, *refs):
        def step(i, _):
            blocks_of = [view(ref, i) for view, ref in zip(views, refs)]
            kernel(i, scalars, *blocks_of, *refs[len(views) :])
            return 0

        lax.fori_loop(0, blocks, step, 0)

    vmem = pl.BlockSpec(memory_space=pltpu.VMEM)
    return pl.pallas_call(
        looped,
        out_shape=[pltpu.VMEM(o.shape, o.dtype) for o in out_shape],
        in_specs=[pl.BlockSpec(memory_space=pltpu.SMEM)] + [vmem] * (len(arrays) - 1),
        out_specs=[vmem] * len(out_shape),
        scratch_shapes=scratch,
        compiler_params=pltpu.CompilerParams(vmem_limit_bytes=VMEM_LIMIT),
        cost_estimate=pl.CostEstimate(
            flops=int(us * 5e8), transcendentals=0, bytes_accessed=int(us * 3e6)
        ),
        name=name,
        input_output_aliases=aliases or {},
    )(*arrays)


def whole(kernel, args, out_shape, scratch, name, in_vmem=True, us=0.0):
    vmem = pl.BlockSpec(memory_space=pltpu.VMEM)
    return pl.pallas_call(
        kernel,
        out_shape=[pltpu.VMEM(o.shape, o.dtype) if in_vmem else o for o in out_shape],
        in_specs=[pl.BlockSpec(memory_space=pltpu.SMEM)] + [vmem] * (len(args) - 1),
        out_specs=[vmem] * len(out_shape),
        scratch_shapes=scratch,
        compiler_params=pltpu.CompilerParams(vmem_limit_bytes=VMEM_LIMIT),
        cost_estimate=pl.CostEstimate(
            flops=int(us * 5e8), transcendentals=0, bytes_accessed=int(us * 3e6)
        ),
        name=name,
    )(*args)


def swap_mp(x):
    return lax.ppermute(x, "mp", [(0, 1), (1, 0)])


def swap_dp(x, bit):
    size = lax.axis_size("dp")
    return lax.ppermute(x, "dp", [(i, i ^ (1 << bit)) for i in range(size)])


def add_low(a, b):
    return (a.astype(F32) + b.astype(F32)).astype(BF16)


def after(x, *others):
    return lax.optimization_barrier((x, *others))[0]


def body(
    tokens,
    norm_gain,
    proj_gate,
    proj_inner,
    proj_state,
    proj_step,
    conv_inner,
    conv_inner_bias,
    conv_state,
    conv_state_bias,
    step_bias,
    decay_log,
    skip_gain,
    gate_gain,
    proj_out,
    lengths,
    cotangent,
):
    rows, width_own = tokens.shape
    model = 2 * width_own
    heads = skip_gain.shape[0]
    width = proj_inner.shape[1]
    head_dim = width // heads
    state_width = proj_state.shape[1]
    n = state_width // 4
    conv_width = width + state_width
    inner_width = width * lax.axis_size("mp")
    chunks = rows // CHUNK
    rank = lax.axis_index("mp")
    shape = jax.ShapeDtypeStruct

    oth_tokens = swap_mp(tokens)
    oth_gain = swap_mp(norm_gain.reshape(1, width_own))
    oth_cot = swap_mp(after(cotangent, oth_tokens))

    scalars = jnp.stack([lengths[0], rank, lax.axis_index("dp")]).astype(jnp.int32)
    step_weight = proj_step.reshape(model, 2 * heads)
    step_weight = jnp.pad(step_weight, ((0, 0), (0, LANES - 2 * heads)))
    own_gain = norm_gain.reshape(1, width_own)
    gain = natural(rank, own_gain, oth_gain).astype(F32)
    conv = jnp.concatenate(
        [
            jnp.concatenate([conv_inner, conv_state], axis=1),
            jnp.concatenate([conv_inner_bias, conv_state_bias])[None],
            jnp.zeros((3, conv_width), F32),
        ]
    )
    head_par = jnp.stack(
        [
            step_bias.reshape(-1),
            -jnp.exp(decay_log.reshape(-1)),
            jnp.pad(skip_gain, (0, heads)),
        ]
    )
    head_par = jnp.pad(head_par, ((0, 5), (0, LANES - 2 * heads)))
    staged = (tokens, cotangent, proj_gate, proj_inner, proj_state, proj_out)
    hbm = pl.BlockSpec(memory_space=pl.ANY)
    vmem = pl.BlockSpec(memory_space=pltpu.VMEM)
    tokens_v, cot_v, gate_v, inner_v, state_v, out_v, spread, gather, w_state_t = pl.pallas_call(
        partial(stage_kernel, count=len(staged), head_dim=head_dim),
        out_shape=[pltpu.VMEM(x.shape, x.dtype) for x in staged]
        + [
            pltpu.VMEM((2 * LANES, 2 * width), BF16),
            pltpu.VMEM((2 * width, LANES), BF16),
            pltpu.VMEM((state_width + LANES, model), BF16),
        ],
        in_specs=[vmem, vmem] + [hbm] * len(staged),
        out_specs=[vmem] * (len(staged) + 3),
        scratch_shapes=[pltpu.SemaphoreType.DMA((len(staged),))],
        compiler_params=pltpu.CompilerParams(vmem_limit_bytes=VMEM_LIMIT),
        name="stage",
    )(proj_state, step_weight, *staged)
    gg = gate_gain[None]

    sizes = dict(heads=heads, width=width, state_width=state_width)
    low = lambda *dims: shape(dims, BF16)
    full = lambda *dims: shape(dims, F32)
    block = PROJECT_BLOCK
    up, states = rows_of(block), states_of(block)
    normed, gate_pre, pre, slope, hs, act, sact, xd, hf, sb = call(
        partial(project_kernel, block=block, **sizes),
        rows // block,
        [
            scalars,
            (tokens_v, up),
            (oth_tokens, up),
            (gain, fixed),
            (gate_v, fixed),
            (inner_v, fixed),
            (state_v, fixed),
            (step_weight, fixed),
            (conv, fixed),
            (head_par, fixed),
            (spread, fixed),
        ],
        [up, up, up, up, up, up, up, up, states, states],
        [
            low(rows, model),
            full(rows, width),
            low(rows, conv_width),
            low(rows, conv_width),
            full(rows, 4 * LANES),
            full(rows, width),
            low(rows, state_width),
            low(rows, 2 * width),
            low(chunks, n, width),
            full(chunks, n, width),
        ],
        [pltpu.VMEM((block + 8, conv_width), F32), pltpu.VMEM((n, width), F32)],
        "project",
        us=12,
    )

    block = MIX_BLOCK
    top = rows // block - 1
    down, states_down = rows_of(block, top), states_of(block, top)
    y, hb = call(
        partial(mix_kernel, block=block, **sizes),
        rows // block,
        [
            scalars,
            (act, down),
            (sact, down),
            (hs, down),
            (xd, down),
            (hf, states_down),
            (sb, states_down),
            (head_par, fixed),
            (spread, fixed),
        ],
        [down, states_down],
        [full(rows, width), low(chunks, n, width)],
        [pltpu.VMEM((n, width), F32)],
        "mix",
        us=7,
    )

    block = GATE_BLOCK
    up, states, up_lanes = rows_of(block), states_of(block), lanes_of(block)
    dgn, gz, sums = call(
        partial(gate_kernel, block=block),
        rows // block,
        [
            scalars,
            (y, up),
            (gate_pre, up),
            (cot_v, up),
            (oth_cot, up),
            (out_v, fixed),
            (gg, fixed),
        ],
        [up, up, up_lanes],
        [full(rows, width), low(rows, width), full(8, rows)],
        [],
        "gate",
        us=3,
    )

    oth_sums = swap_mp(sums)
    branch_oth = whole(
        partial(branch_kernel, other=True), (scalars, gz, out_v), [low(rows, width_own)], [], "branch_oth", us=3
    )[0]
    sums = sums + oth_sums
    branch_got = swap_mp(after(branch_oth, sums))
    sums_in = after(sums, branch_oth)

    g, dgp, dbr, dc, gb, gf, rd_gate, row_sums, small = call(
        partial(gate_back_kernel, block=block, inner_width=inner_width, **sizes),
        rows // block,
        [
            scalars,
            (sums_in, up_lanes),
            (gate_pre, up),
            (y, up),
            (act, up),
            (dgn, up),
            (cot_v, up),
            (oth_cot, up),
            (hs, up),
            (sact, up),
            (hf, states),
            (hb, states),
            (gg, fixed),
            (spread, fixed),
            (gather, fixed),
        ],
        [up, up, up, up, states, states, up_lanes, up, fixed],
        [
            low(rows, width),
            low(rows, width),
            low(rows, model),
            full(rows, 2 * n),
            low(chunks, n, width),
            full(chunks, n, width),
            full(8, rows),
            full(rows, LANES),
            full(8, width),
        ],
        [pltpu.VMEM((n, width), F32), pltpu.VMEM((block, 2 * width), BF16)],
        "gate_back",
        us=8,
    )

    def back_part(first, count, g, state):
        block = BACK_BLOCK
        here, states_here, here_lanes = rows_of(block, first), states_of(block, first), lanes_of(block, first)
        ins = [
            scalars,
            (g, here),
            (act, here),
            (sact, here),
            (hs, here),
            (xd, here),
            (row_sums, here),
            (hf, states_here),
            (hb, states_here),
            (gb, states_here),
            (gf, states_here),
            (dc, here),
            (pre, here),
            (slope, here),
            (conv, fixed),
            (head_par, fixed),
            (spread, fixed),
            (gather, fixed),
            *[(x, fixed) for x in state[:3]],
            (state[3], here),
            (state[4], here),
            (state[5], here_lanes),
        ]
        return call(
            partial(back_kernel, block=block, top=first, **sizes),
            count,
            ins,
            [here, here, here_lanes, fixed, fixed, fixed],
            [
                low(rows, conv_width),
                full(rows, 4 * LANES),
                full(8, rows),
                full(8, conv_width),
                full(8, conv_width),
                full(n, width),
            ],
            [
                pltpu.VMEM((block + 8, conv_width), F32),
                pltpu.VMEM((2 * CHUNK + 16, 2 * width), BF16),
                pltpu.VMEM((CHUNK, 2 * width), BF16),
                pltpu.VMEM((LANES, CHUNK), F32),
                pltpu.VMEM((CHUNK, LANES), F32),
            ],
            "mix_back",
            us=3 * count,
            aliases={len(ins) - 3: 0, len(ins) - 2: 1, len(ins) - 1: 2},
        )

    order_a, orders_b = (0, 1, 2, 3), ((0, 1, 2, 3), (0, 2, 1, 3))
    grad_out = mm_tn(gz, dbr).astype(BF16)
    grad_gate = mm_tn(normed, dgp).astype(BF16)
    keep, send, gain_part = whole(
        partial(pack_early_kernel, order=order_a),
        (scalars, grad_out, grad_gate, proj_gate),
        [low(width, model), low(width, model), full(8, model)],
        [],
        "pack_early",
    )

    def halve(keep, send, bit):
        got = swap_dp(send, bit)
        h = keep.shape[0] // 2
        return add_low(keep[:h], got[:h]), add_low(keep[h:], got[h:])

    def finish(keep, send, bit):
        return rest_of_dp(add_low(keep, swap_dp(send, bit)))

    def rest_of_dp(x):
        extra = SHARDS
        while extra < lax.axis_size("dp"):
            x = add_low(x, swap_dp(x, extra.bit_length() - 1))
            extra *= 2
        return x

    zeros = (
        jnp.zeros((8, conv_width), F32),
        jnp.zeros((n, width), F32),
        jnp.zeros((8, conv_width), F32),
    )
    keep, send = halve(keep, send, order_a[0])
    state = (
        *zeros,
        jnp.zeros((rows, conv_width), BF16),
        jnp.zeros((rows, 4 * LANES), F32),
        jnp.zeros((8, rows), F32),
    )
    parts = 4
    count = rows // BACK_BLOCK // parts
    g = after(g, send)
    sent, x = swap_dp(send, order_a[1]), None
    for k in range(parts):
        outs = back_part((parts - k) * count - 1, count, g, state)
        rest, rates, rd_rest, gconv, ext_carry, carry = outs
        if k == 1:
            sent, carry = lax.optimization_barrier((sent, carry))
        elif k == 2:
            sent, carry, branch_got = lax.optimization_barrier((sent, carry, branch_got))
        elif k == 3:
            sent, rest = lax.optimization_barrier((sent, rest))
        if k > 0:
            h = keep.shape[0] // 2
            if k < 3:
                keep, send = add_low(keep[:h], sent[:h]), add_low(keep[h:], sent[h:])
                carry = after(carry, send)
                sent = swap_dp(send, order_a[k + 1])
            else:
                x = rest_of_dp(add_low(keep, sent))
        state = (ext_carry, carry, gconv, rest, rates, rd_rest)

    block = RATES_BLOCK
    rates, x, rest = lax.optimization_barrier((rates, x, rest))
    sent = swap_dp(x, order_a[3])
    dz, ghead, rd_part = call(
        partial(rates_kernel, heads=heads, block=block),
        rows // block,
        [
            scalars,
            (rates, rows_of(block)),
            (hs, rows_of(block)),
            (rd_gate, lanes_of(block)),
            (rd_rest, lanes_of(block)),
            (head_par, fixed),
        ],
        [rows_of(block), fixed, lanes_of(block)],
        [low(rows, LANES), full(8, LANES), full(8, rows)],
        [],
        "rates",
    )
    grad_inner = mm_tn(normed, rest[:, :width]).astype(BF16)
    grad_state = mm_tn(rest[:, width:], normed).astype(BF16)
    grad_step = mm_tn(dz, normed).astype(BF16)
    keep, send = whole(
        partial(pack_late_kernel, orders=orders_b, heads=heads, state_width=state_width),
        (
            scalars, grad_inner, grad_state, grad_step, inner_v, w_state_t, gain, gain_part, gconv, ghead,
            small, gather,
        ),
        [low(LATE_ROWS * SHARDS // 2, model), low(LATE_ROWS * SHARDS // 2, model)],
        [pltpu.VMEM((8 * SHARDS, model), F32)],
        "pack_late",
    )

    back_args = (scalars, dgp, rest, dz, rd_part, gate_v, inner_v, state_v, step_weight)
    dn_oth = whole(
        partial(back_project_kernel, other=True), back_args, [low(rows + 16, width_own)], [], "back_oth"
    )[0]
    x = jnp.concatenate([x, sent])
    send, x, dn_oth = lax.optimization_barrier((send, x, dn_oth))
    got = swap_dp(send, 0)
    sent = swap_dp(x, order_a[2])
    h, c = keep.shape[0] // 2, model // 2
    keeps = [add_low(keep[:h, :c], got[:h, :c]), add_low(keep[:h, c:], got[:h, c:])]
    sends = [add_low(keep[h:, :c], got[h:, :c]), add_low(keep[h:, c:], got[h:, c:])]
    sends[0], sends[1], rest, gz_late = lax.optimization_barrier((sends[0], sends[1], rest, gz))
    dn_got = swap_mp(dn_oth)

    dn_own = whole(
        partial(back_project_kernel, other=False), (*back_args[:2], rest, *back_args[3:]),
        [full(rows, width_own)], [], "back_own"
    )[0]
    branch_own = whole(
        partial(branch_kernel, other=False), (scalars, gz_late, out_v), [full(rows, width_own)], [],
        "branch_own"
    )[0]
    for level in (1, 2):
        gots = [swap_dp(v, order[level]) for v, order in zip(sends, orders_b)]
        if level == 1:
            gots[0], gots[1], dn_own, branch_own = lax.optimization_barrier(
                (gots[0], gots[1], dn_own, branch_own)
            )
        else:
            x = jnp.concatenate([x, sent])
            gots[0], gots[1], x = lax.optimization_barrier((gots[0], gots[1], x))
        h = keeps[0].shape[0] // 2
        pairs = list(zip(keeps, gots))
        if level == 1:
            keeps = [add_low(k[:h], v[:h]) for k, v in pairs]
            sends = [add_low(k[h:], v[h:]) for k, v in pairs]
        else:
            keep = jnp.concatenate([add_low(k[:h], v[:h]) for k, v in pairs], axis=1)
            send = jnp.concatenate([add_low(k[h:], v[h:]) for k, v in pairs], axis=1)
    send, x, tokens_late, oth_late = lax.optimization_barrier((send, x, tokens, oth_tokens))
    sent = swap_dp(x, order_a[1])

    seq_mask = (jnp.arange(rows) < lengths[0]).astype(F32)[:, None]
    gate_inv = lax.rsqrt(sums[0] / inner_width + EPSILON)[:, None]
    tokens_f = tokens_late.astype(F32)
    block_out = (tokens_f + seq_mask * gate_inv * (branch_own + branch_got.astype(F32))).astype(BF16)

    got, block_out, dn_got = lax.optimization_barrier((swap_dp(send, 3), block_out, dn_got))
    z = rest_of_dp(add_low(keep, got))
    part = model // SHARDS
    tail = z[part:]
    tail_row = lax.broadcasted_iota(jnp.int32, (LATE_ROWS - part, 1), 0)
    alone = (tail_row >= LATE_ROWS - part - 8) & (tail_row < LATE_ROWS - part - 4)
    tail_f = tail.astype(F32)
    tail = jnp.where(alone, tail_f, tail_f + swap_mp(tail).astype(F32)).astype(BF16)
    z = jnp.concatenate([z[:part], tail])
    oth_f = oth_late.astype(F32)
    square = jnp.sum(tokens_f * tokens_f, axis=1, keepdims=True) + jnp.sum(
        oth_f * oth_f, axis=1, keepdims=True
    )
    inv = lax.rsqrt(square / model + EPSILON)
    part = rows // 4
    lines = dn_got[rows:, :part].astype(F32)
    oth_rd = (lines[0:4] + lines[4:8] + lines[8:12]).reshape(rows)
    rd_both = rd_part[0] + oth_rd
    grad_full = dn_own + dn_got[:rows].astype(F32)
    grad_tokens = (
        cotangent.astype(F32)
        + inv * (grad_full * norm_gain.astype(F32)[None])
        - tokens_f * (inv * inv * (rd_both[:, None] / model))
    )

    x = jnp.concatenate([x, sent])
    got, grad_tokens, x = lax.optimization_barrier((swap_dp(z, 3), grad_tokens, x))
    sent = swap_dp(x, order_a[0])
    z = jnp.concatenate([z, got])
    zs = [z[:, :c], z[:, c:]]
    gots = [swap_dp(v, order[2]) for v, order in zip(zs, orders_b)]
    zs = [jnp.concatenate([v, g]) for v, g in zip(zs, gots)]
    grad_proj_out, grad_proj_gate = whole(
        partial(unpack_early_kernel, order=order_a),
        (scalars, x, after(sent, *zs)),
        [full(width, model), full(model, width)],
        [],
        "unpack_early",
        in_vmem=False,
    )
    gots = [swap_dp(v, order[1]) for v, order in zip(zs, orders_b)]
    gots[0], gots[1], grad_proj_out = lax.optimization_barrier((gots[0], gots[1], grad_proj_out))
    z = jnp.concatenate([jnp.concatenate([v, g]) for v, g in zip(zs, gots)], axis=1)
    (
        grad_proj_inner,
        grad_proj_state,
        step,
        grad_conv_inner,
        grad_conv_inner_bias,
        grad_conv_state,
        grad_conv_state_bias,
        grad_gate_gain,
        grad_step_bias,
        grad_decay_log,
        grad_skip,
        grad_norm_gain,
    ) = whole(
        partial(unpack_late_kernel, orders=orders_b, heads=heads),
        (scalars, z, swap_dp(z, 0)),
        [
            full(model, width),
            full(model, state_width),
            full(heads, 2, model),
            full(4, width),
            full(width),
            full(4, state_width),
            full(1, state_width),
            full(width),
            full(2, heads),
            full(2, heads),
            full(1, heads),
            full(width_own),
        ],
        [pltpu.VMEM((state_width, model), F32), pltpu.VMEM((8 * SHARDS, model), F32)],
        "unpack_late",
        in_vmem=False,
    )
    return (
        block_out,
        grad_tokens,
        grad_norm_gain,
        grad_proj_gate,
        grad_proj_inner,
        grad_proj_state,
        step.transpose(2, 1, 0),
        grad_conv_inner,
        grad_conv_inner_bias,
        grad_conv_state,
        grad_conv_state_bias[0],
        grad_step_bias,
        grad_decay_log,
        grad_skip[0],
        grad_gate_gain,
        grad_proj_out,
    )


def solution(mesh):
    in_specs = (
        P("dp", "mp"),
        P("mp"),
        P(None, "mp"),
        P(None, "mp"),
        P(),
        P(None, None, "mp"),
        P(None, "mp"),
        P("mp"),
        P(),
        P(),
        P(None, "mp"),
        P(None, "mp"),
        P("mp"),
        P("mp"),
        P("mp", None),
        P("dp"),
        P("dp", "mp"),
    )
    out_specs = (
        P("dp", "mp"),
        P("dp", "mp"),
        P("mp"),
        P(None, "mp"),
        P(None, "mp"),
        P(),
        P(None, None, "mp"),
        P(None, "mp"),
        P("mp"),
        P(),
        P(),
        P(None, "mp"),
        P(None, "mp"),
        P("mp"),
        P("mp"),
        P("mp", None),
    )
    return jax.shard_map(body, mesh=mesh, in_specs=in_specs, out_specs=out_specs, check_vma=False)
```

```python
from functools import partial

import jax
import jax.numpy as jnp
from jax import lax
from jax.experimental import pallas as pl
from jax.experimental.pallas import tpu as pltpu
from jax.sharding import PartitionSpec as P

EPSILON = 1e-05
CHUNK = 128
PROJECT_BLOCK, MIX_BLOCK, GATE_BLOCK, BACK_BLOCK, RATES_BLOCK = 256, 256, 256, 128, 512
LANES = 128
F32 = jnp.float32
BF16 = jnp.bfloat16
HIGHEST = lax.Precision.HIGHEST
VMEM_LIMIT = 12 * 1024 * 1024
SHARDS = 16
LOG2_E = 1.4426950408889634
LATE_ROWS = 72


def mm(a, b):
    return jnp.dot(a, b, preferred_element_type=F32)


def mm_nt(a, b):
    return lax.dot_general(a, b, (((1,), (1,)), ((), ())), preferred_element_type=F32)


def mm_tn(a, b):
    return lax.dot_general(a, b, (((0,), (0,)), ((), ())), preferred_element_type=F32)


def split_two(v):
    hi = v.astype(BF16)
    return hi, (v - hi.astype(F32)).astype(BF16)


def split_three(v):
    hi, mid = split_two(v)
    return hi, mid, (v - hi.astype(F32) - mid.astype(F32)).astype(BF16)


def expand(v, spread):
    hi, lo = split_two(v)
    return mm(jnp.concatenate([hi, lo], axis=1), spread)


def row_mask(block, rows, length):
    pos = block * rows + lax.broadcasted_iota(jnp.int32, (rows, 1), 0)
    return (pos < length).astype(F32)


def to_row(col_a, col_b):
    rows = col_a.shape[0]
    lane = lax.broadcasted_iota(jnp.int32, (rows, LANES), 1)
    tile = jnp.where(lane == 0, col_a, jnp.where(lane == 1, col_b, 0.0))
    return jnp.transpose(tile)[0:8, :]


def sigmoid(v):
    return 0.5 * jnp.tanh(0.5 * v) + 0.5


def natural(rank, own, oth):
    return jnp.where(
        rank == 0, jnp.concatenate([own, oth], axis=1), jnp.concatenate([oth, own], axis=1)
    )


def eight(row):
    return jnp.broadcast_to(row, (8, row.shape[1]))


def stage_kernel(w_state, w_step, *refs, count, head_dim):
    sources, outs, sems = refs[:count], refs[count:-1], refs[-1]
    spread, gather, w_state_t = outs[count:]
    copies = [
        pltpu.make_async_copy(src, dst, sems.at[k]) for k, (src, dst) in enumerate(zip(sources, outs))
    ]
    for copy in copies:
        copy.start()
    state_width = w_state.shape[1]
    w_state_t[:state_width, :] = jnp.transpose(w_state[...].astype(F32)).astype(BF16)
    w_state_t[state_width:, :] = jnp.transpose(w_step[...].astype(F32)).astype(BF16)
    head = lax.broadcasted_iota(jnp.int32, spread.shape, 1) // head_dim
    row = lax.broadcasted_iota(jnp.int32, spread.shape, 0) % LANES
    spread[...] = jnp.where(head == row, 1.0, 0.0).astype(BF16)
    head = lax.broadcasted_iota(jnp.int32, gather.shape, 0) // head_dim
    lane = lax.broadcasted_iota(jnp.int32, gather.shape, 1)
    gather[...] = jnp.where(head == lane, 1.0, 0.0).astype(BF16)
    for copy in copies:
        copy.wait()


def project_kernel(
    i, scalars, own, oth, gain, w_gate, w_inner, w_state, w_step, conv, head_par, spread,
    normed_ref, gate_ref, pre_ref, slope_ref, hs_ref, act_ref, sact_ref, xd_ref, hf_ref, sb_ref,
    ext, carry, *, heads, width, state_width, block,
):
    @pl.when(i == 0)
    def _():
        ext[0:8, :] = jnp.zeros((8, ext.shape[1]), F32)
        carry[...] = jnp.zeros_like(carry)

    x = natural(scalars[1], own[...], oth[...]).astype(F32)
    inv = lax.rsqrt(jnp.mean(x * x, axis=-1, keepdims=True) + EPSILON)
    normed = (x * inv * gain[...]).astype(BF16)
    normed_ref[...] = normed
    step_pre = mm(normed, w_step[...])
    z = step_pre + head_par[0:1, :]
    dt = jnp.maximum(z, 0.0) + jnp.log1p(jnp.exp(-jnp.abs(z)))
    rate = head_par[1:2, :] * dt
    dtm = dt * row_mask(i, block, scalars[0])
    hs_ref[:, 0:LANES] = z
    hs_ref[:, LANES : 2 * LANES] = dt
    tri_r = lax.broadcasted_iota(jnp.int32, (CHUNK, CHUNK), 0)
    tri_c = lax.broadcasted_iota(jnp.int32, (CHUNK, CHUNK), 1)
    tri = (tri_c <= tri_r).astype(F32)
    is_fwd = lax.broadcasted_iota(jnp.int32, (CHUNK, LANES), 1) < heads
    per = block // CHUNK
    to_spread = [dtm]
    keeps = []
    for c_idx in range(per):
        rows = slice(c_idx * CHUNK, (c_idx + 1) * CHUNK)
        rate_c = rate[rows]
        cum = jnp.dot(tri, rate_c, precision=HIGHEST, preferred_element_type=F32)
        tot = cum[CHUNK - 1 : CHUNK, :]
        cumx = jnp.where(is_fwd, cum, cum - rate_c)
        hs_ref[rows, 2 * LANES : 3 * LANES] = cumx
        hs_ref[rows, 3 * LANES :] = jnp.broadcast_to(tot, (CHUNK, LANES))
        to_spread.append(dtm[rows] * jnp.exp(jnp.where(is_fwd, tot - cumx, cumx)))
        keeps.append(eight(jnp.exp(tot)))
    wide = expand(jnp.concatenate(to_spread + keeps, axis=0), spread[...])

    ext[8 : 8 + block, 0:width] = mm(normed, w_inner[...])
    ext[8 : 8 + block, width:] = mm(normed, w_state[...])
    gate_ref[...] = mm(normed, w_gate[...])
    whole_ext = ext[...]
    pre = whole_ext[8:]
    pre_ref[...] = pre.astype(BF16)
    c = conv[4:5, :] + conv[3:4, :] * pre
    for j in range(3):
        c = c + conv[j : j + 1, :] * pltpu.roll(whole_ext, 3 - j, 0)[8:]
    sg = sigmoid(c)
    both = c * sg
    slope_ref[...] = (sg * (1.0 + c * (1.0 - sg))).astype(BF16)
    ext[0:8, :] = ext[block : block + 8, :]
    act = both[:, :width]
    act_ref[...] = act
    sact = both[:, width:].astype(BF16)
    sact_ref[...] = sact
    xd_ref[:, 0:width] = (act * wide[0:block, :width]).astype(BF16)
    xd_ref[:, width:] = (act * wide[0:block, width:]).astype(BF16)
    n = state_width // 4
    for c_idx in range(per):
        rows = slice(c_idx * CHUNK, (c_idx + 1) * CHUNK)
        coef = wide[block + c_idx * CHUNK : block + (c_idx + 1) * CHUNK]
        keep = wide[2 * block + 8 * c_idx : 2 * block + 8 * c_idx + 1, :width]
        hf_ref[c_idx] = carry[...].astype(BF16)
        carry[...] = carry[...] * keep + mm_tn(
            sact[rows, 0:n], (act[rows] * coef[:, :width]).astype(BF16)
        )
        sb_ref[c_idx] = mm_tn(
            sact[rows, 2 * n : 3 * n], (act[rows] * coef[:, width:]).astype(BF16)
        )


def pair_tiles(pair):
    lane = lax.broadcasted_iota(jnp.int32, (1, pair.shape[1]), 1)
    first = (lane < pair.shape[1] // 2).astype(F32)
    keep_a, keep_b = first.astype(BF16), (1.0 - first).astype(BF16)
    return jnp.concatenate([pair * keep_a, pair * keep_b], axis=0)


def mix_kernel(
    i, scalars, act, sact, hs, xd, hf, sb, head_par, spread, y_ref, hb_ref, carry,
    *, heads, width, state_width, block,
):
    @pl.when(i == 0)
    def _():
        carry[...] = jnp.zeros_like(carry)

    n = state_width // 4
    per = block // CHUNK
    r = lax.broadcasted_iota(jnp.int32, (CHUNK, CHUNK), 0)
    c = lax.broadcasted_iota(jnp.int32, (CHUNK, CHUNK), 1)
    lower = c < r
    upper = c > r
    is_fwd = lax.broadcasted_iota(jnp.int32, (block, LANES), 1) < heads
    cum_all = hs[:, 2 * LANES : 3 * LANES]
    tot_all = hs[:, 3 * LANES :]
    wide = expand(
        jnp.concatenate(
            [jnp.exp(jnp.where(is_fwd, cum_all, tot_all - cum_all))]
            + [jnp.exp(tot_all[k * CHUNK : k * CHUNK + 8]) for k in range(per)]
            + [eight(head_par[2:3, :])],
            axis=0,
        ),
        spread[...],
    )
    skip = wide[block + 8 * per : block + 8 * per + 1]
    for c_idx in reversed(range(per)):
        rows = slice(c_idx * CHUNK, (c_idx + 1) * CHUNK)
        cumx = cum_all[rows] * LOG2_E
        cum_t = jnp.transpose(cumx)
        sact_c = sact[rows, :]
        b_f, c_f = sact_c[:, 0:n], sact_c[:, n : 2 * n]
        b_b, c_b = sact_c[:, 2 * n : 3 * n], sact_c[:, 3 * n :]
        s_f = jnp.where(lower, mm_nt(c_f, b_f), 0.0)
        s_b = jnp.where(upper, mm_nt(c_b, b_b), 0.0)
        hb = carry[...].astype(BF16)
        hb_ref[c_idx] = hb
        in_f = mm(c_f, hf[c_idx])
        in_b = mm(c_b, hb)
        keep = wide[block + 8 * c_idx : block + 8 * c_idx + 1, width:]
        carry[...] = carry[...] * keep + sb[c_idx]
        for p in range(heads // 2):
            lanes = slice(p * LANES, (p + 1) * LANES)
            lanes_b = slice(width + p * LANES, width + (p + 1) * LANES)
            w_f, w_b = [], []
            for h in (2 * p, 2 * p + 1):
                damp = jnp.exp2(
                    jnp.minimum(
                        cumx[:, h : h + 1] - cum_t[h : h + 1, :],
                        cum_t[heads + h : heads + h + 1, :] - cumx[:, heads + h : heads + h + 1],
                    )
                )
                w_f.append((s_f * damp).astype(BF16))
                w_b.append((s_b * damp).astype(BF16))
            out = mm(
                jnp.concatenate(w_f + w_b, axis=1),
                jnp.concatenate([pair_tiles(xd[rows, lanes]), pair_tiles(xd[rows, lanes_b])], axis=0),
            )
            y_ref[rows, lanes] = (
                out
                + wide[rows, lanes] * in_f[:, lanes]
                + wide[rows, lanes_b] * in_b[:, lanes]
                + skip[:, lanes] * act[rows, lanes]
            )


def gate_kernel(i, scalars, y, gate, cown, coth, po, gg, dgn_ref, gz_ref, sums_ref, *, block):
    gp = gate[...]
    gated = y[...] * (gp * sigmoid(gp))
    mask = row_mask(i, block, scalars[0])
    cot = natural(scalars[1], cown[...], coth[...])
    dgn = mm_nt((cot.astype(F32) * mask).astype(BF16), po[...])
    dgn_ref[...] = dgn
    scaled = gated * gg[...]
    gz_ref[...] = scaled.astype(BF16)
    sums_ref[...] = to_row(
        jnp.sum(gated * gated, axis=1, keepdims=True), jnp.sum(dgn * scaled, axis=1, keepdims=True)
    )


def gate_back_kernel(
    i, scalars, sums, gate, y, act, dgn, cown, coth, hs, sact, hf, hb, gg, spread, gather,
    g_ref, dgp_ref, dbr_ref, dc_ref, gb_ref, gf_ref, rd_ref, rows_ref, small_ref, carry, prod,
    *, heads, width, state_width, block, inner_width,
):
    @pl.when(i == 0)
    def _():
        carry[...] = jnp.zeros_like(carry)
        small_ref[...] = jnp.zeros_like(small_ref)

    per = block // CHUNK
    is_fwd = lax.broadcasted_iota(jnp.int32, (block, LANES), 1) < heads
    cum_all = hs[:, 2 * LANES : 3 * LANES]
    tot_all = hs[:, 3 * LANES :]
    wide = expand(
        jnp.concatenate(
            [jnp.exp(jnp.where(is_fwd, cum_all, tot_all - cum_all))]
            + [jnp.exp(tot_all[k * CHUNK : k * CHUNK + 8]) for k in range(per)],
            axis=0,
        ),
        spread[...],
    )
    cols = jnp.transpose(sums[...])
    gate_inv = lax.rsqrt(cols[:, 0:1] / inner_width + EPSILON)
    gate_dot = cols[:, 1:2] / inner_width
    gp = gate[...]
    sg = sigmoid(gp)
    act_gate = gp * sg
    yv = y[...]
    gated = yv * act_gate
    dg = dgn[...]
    small_ref[0:1, :] += jnp.sum(dg * gated * gate_inv, axis=0, keepdims=True)
    d_gated = gate_inv * (dg * gg[...]) - gated * (gate_inv * gate_inv * gate_inv * gate_dot)
    d_gp = d_gated * yv * (sg * (1.0 + gp * (1.0 - sg)))
    dgp_ref[...] = d_gp.astype(BF16)
    rd = jnp.sum(d_gp * gp, axis=1, keepdims=True)
    rd_ref[...] = to_row(rd, jnp.zeros_like(rd))
    d_y = d_gated * act_gate
    g_ref[...] = d_y.astype(BF16)
    small_ref[1:2, :] += jnp.sum(d_y * act[...], axis=0, keepdims=True)
    mask = row_mask(i, block, scalars[0])
    cot = natural(scalars[1], cown[...], coth[...])
    dbr_ref[...] = (cot.astype(F32) * (mask * gate_inv)).astype(BF16)
    n = state_width // 4
    for c_idx in range(per):
        rows = slice(c_idx * CHUNK, (c_idx + 1) * CHUNK)
        dy_c = d_y[rows]
        dyf = dy_c * wide[rows, :width]
        dyb = dy_c * wide[rows, width:]
        prod[rows, 0:width] = (dyf * mm(sact[rows, n : 2 * n], hf[c_idx])).astype(BF16)
        prod[rows, width:] = (dyb * mm(sact[rows, 3 * n :], hb[c_idx])).astype(BF16)
        dyf = dyf.astype(BF16)
        dyb = dyb.astype(BF16)
        dc_ref[rows, 0:n] = mm_nt(dyf, hf[c_idx])
        dc_ref[rows, n : 2 * n] = mm_nt(dyb, hb[c_idx])
        gb_ref[c_idx] = carry[...].astype(BF16)
        keep = wide[block + 8 * c_idx : block + 8 * c_idx + 1, width:]
        carry[...] = carry[...] * keep + mm_tn(sact[rows, 3 * n :], dyb)
        gf_ref[c_idx] = mm_tn(sact[rows, n : 2 * n], dyf)
    rows_ref[...] = mm(prod[...], gather[...])


def back_kernel(
    i, scalars, g, act, sact, hs, xd, row_in, hf, hb, gb, gf, dc, pre, slope, conv, head_par, spread, gather,
    ext_in, carry_in, gconv_in, _rest, _rates, _rd, rest_ref, rates_ref, rd_ref, gconv_ref, ext_out,
    carry, ext, stack, xs, rsum, csum,
    *, heads, width, state_width, block, top,
):
    blk = top - i
    per = block // CHUNK

    @pl.when(i == 0)
    def _():
        ext[block:, :] = ext_in[...]
        carry[...] = carry_in[...]
        gconv_ref[...] = gconv_in[...]
        rsum[...] = jnp.zeros_like(rsum)
        csum[...] = jnp.zeros_like(csum)

    n = state_width // 4
    r = lax.broadcasted_iota(jnp.int32, (CHUNK, CHUNK), 0)
    c = lax.broadcasted_iota(jnp.int32, (CHUNK, CHUNK), 1)
    later = c > r
    earlier = c < r
    is_fwd_all = lax.broadcasted_iota(jnp.int32, (block, LANES), 1) < heads
    is_fwd = lax.broadcasted_iota(jnp.int32, (CHUNK, LANES), 1) < heads
    mask = row_mask(blk, block, scalars[0])
    cum_all = hs[:, 2 * LANES : 3 * LANES]
    tot_all = hs[:, 3 * LANES :]
    wide = expand(
        jnp.concatenate(
            [jnp.exp(jnp.where(is_fwd_all, tot_all - cum_all, cum_all)), hs[:, LANES : 2 * LANES] * mask]
            + [jnp.exp(tot_all[k * CHUNK : k * CHUNK + 8]) for k in range(per)]
            + [eight(head_par[2:3, :])],
            axis=0,
        ),
        spread[...],
    )
    skip = wide[2 * block + 8 * per : 2 * block + 8 * per + 1]
    for c_idx in reversed(range(per)):
        rows = slice(c_idx * CHUNK, (c_idx + 1) * CHUNK)
        rows_dt = slice(block + c_idx * CHUNK, block + (c_idx + 1) * CHUNK)
        cumx = cum_all[rows] * LOG2_E
        cum_t = jnp.transpose(cumx)
        sact_c = sact[rows, :]
        b_f, c_f = sact_c[:, 0:n], sact_c[:, n : 2 * n]
        b_b, c_b = sact_c[:, 2 * n : 3 * n], sact_c[:, 3 * n :]
        s_f = jnp.where(later, mm_nt(b_f, c_f), 0.0)
        s_b = jnp.where(earlier, mm_nt(b_b, c_b), 0.0)
        s_all = s_f + s_b
        grad_f = carry[...]
        grad_f_low = grad_f.astype(BF16)
        grad_b_low = gb[c_idx]
        keep = wide[2 * block + 8 * c_idx : 2 * block + 8 * c_idx + 1]
        keep_f = keep[:, :width]
        edge_f = keep_f * jnp.sum(grad_f * hf[c_idx].astype(F32), axis=0, keepdims=True)
        edge_b = keep[:, width:] * jnp.sum(
            hb[c_idx].astype(F32) * grad_b_low.astype(F32), axis=0, keepdims=True
        )
        e_hi, e_lo = split_two(eight(jnp.concatenate([edge_f, edge_b], axis=1)))
        stack[2 * CHUNK :, :] = jnp.concatenate([e_hi, e_lo], axis=0)
        carry[...] = grad_f * keep_f + gf[c_idx]
        in_f = mm(b_f, grad_f_low)
        in_b = mm(b_b, grad_b_low)
        d_scores = jnp.zeros((CHUNK, CHUNK), F32)
        for p in range(heads // 2):
            lanes = slice(p * LANES, (p + 1) * LANES)
            lanes_b = slice(width + p * LANES, width + (p + 1) * LANES)
            g_pair = g[rows, lanes]
            xf_pair = xd[rows, lanes]
            xb_pair = xd[rows, lanes_b]
            dw = mm_nt(
                jnp.concatenate([pair_tiles(xf_pair), pair_tiles(xb_pair)], axis=0), g_pair
            )
            w_f, w_b = [], []
            for q, h in enumerate((2 * p, 2 * p + 1)):
                damp = jnp.exp2(
                    jnp.minimum(
                        cum_t[h : h + 1, :] - cumx[:, h : h + 1],
                        cumx[:, heads + h : heads + h + 1] - cum_t[heads + h : heads + h + 1, :],
                    )
                )
                w_f.append((s_f * damp).astype(BF16))
                w_b.append((s_b * damp).astype(BF16))
                part = jnp.where(
                    later, dw[q * CHUNK : (q + 1) * CHUNK], dw[(2 + q) * CHUNK : (3 + q) * CHUNK]
                )
                part = part * damp
                d_scores = d_scores + part
                e_all = part * s_all
                e_fwd = jnp.where(later, e_all, 0.0)
                sum_all = jnp.sum(e_all, axis=0, keepdims=True)
                sum_fwd = jnp.sum(e_fwd, axis=0, keepdims=True)
                rsum[h : h + 1, :] = sum_fwd
                rsum[heads + h : heads + h + 1, :] = sum_fwd - sum_all
                sum_all = jnp.sum(e_all, axis=1, keepdims=True)
                sum_fwd = jnp.sum(e_fwd, axis=1, keepdims=True)
                csum[:, h : h + 1] = -sum_fwd
                csum[:, heads + h : heads + h + 1] = sum_all - sum_fwd
            dx = mm(
                jnp.concatenate(
                    [jnp.concatenate(w_f, axis=1), jnp.concatenate(w_b, axis=1)], axis=0
                ),
                pair_tiles(g_pair),
            )
            edge_pf = wide[rows, lanes]
            edge_pb = wide[rows, lanes_b]
            inter_f = edge_pf * in_f[:, lanes]
            inter_b = edge_pb * in_b[:, lanes]
            dx_f = dx[:CHUNK] + inter_f
            dx_b = dx[CHUNK:] + inter_b
            xf = xf_pair.astype(F32)
            xb = xb_pair.astype(F32)
            xs[:, lanes] = (xf * edge_pf).astype(BF16)
            xs[:, lanes_b] = (xb * edge_pb).astype(BF16)
            act_p = act[rows, lanes]
            stack[0:CHUNK, lanes] = (act_p * dx_f).astype(BF16)
            stack[0:CHUNK, lanes_b] = (act_p * dx_b).astype(BF16)
            stack[CHUNK : 2 * CHUNK, lanes] = (xf * inter_f).astype(BF16)
            stack[CHUNK : 2 * CHUNK, lanes_b] = (xb * inter_b).astype(BF16)
            d_inner = (
                skip[:, lanes] * g_pair.astype(F32)
                + wide[rows_dt, lanes] * dx_f
                + wide[rows_dt, lanes_b] * dx_b
            )
            ext[rows, lanes] = d_inner * slope[rows, lanes].astype(F32)
        low_f = jnp.where(later, d_scores, 0.0).astype(BF16)
        low_b = jnp.where(earlier, d_scores, 0.0).astype(BF16)
        d_bf = mm(low_f, c_f) + mm_nt(xs[:, :width], grad_f_low)
        d_cf = mm_tn(low_f, b_f) + dc[rows, 0:n]
        d_bb = mm(low_b, c_b) + mm_nt(xs[:, width:], grad_b_low)
        d_cb = mm_tn(low_b, b_b) + dc[rows, n : 2 * n]
        d_state = jnp.concatenate([d_bf, d_cf, d_bb, d_cb], axis=1)
        ext[rows, width:] = d_state * slope[rows, width:].astype(F32)
        head_sums = mm(stack[...], gather[...])
        rin = row_in[rows, :]
        ahead = head_sums[CHUNK : 2 * CHUNK]
        rates_ref[rows, 0:LANES] = (
            jnp.transpose(rsum[...]) + csum[...] + jnp.where(is_fwd, rin, ahead)
        )
        rates_ref[rows, LANES : 2 * LANES] = jnp.where(is_fwd, ahead, rin)
        rates_ref[rows, 2 * LANES : 3 * LANES] = head_sums[0:CHUNK] * mask[rows]
        edge = head_sums[2 * CHUNK : 2 * CHUNK + 1] + head_sums[2 * CHUNK + 8 : 2 * CHUNK + 9]
        rates_ref[rows, 3 * LANES :] = jnp.broadcast_to(edge, (CHUNK, LANES))

    prev = pre[...].astype(F32)
    whole_ext = ext[...]
    moved = whole_ext[:block]
    acc = conv[3:4, :] * moved
    gconv_ref[4:5, :] += jnp.sum(moved, axis=0, keepdims=True)
    gconv_ref[3:4, :] += jnp.sum(moved * prev, axis=0, keepdims=True)
    for j in range(3):
        moved = pltpu.roll(whole_ext, block + 8 - (3 - j), 0)[:block]
        acc = acc + conv[j : j + 1, :] * moved
        gconv_ref[j : j + 1, :] += jnp.sum(moved * prev, axis=0, keepdims=True)
    rest_ref[...] = acc.astype(BF16)
    rd = jnp.sum(acc * prev, axis=1, keepdims=True)
    rd_ref[...] = to_row(rd, jnp.zeros_like(rd))
    ext[block:, :] = ext[0:8, :]
    ext_out[...] = ext[0:8, :]


def rates_kernel(i, scalars, rates, hs, rd_a, rd_b, head_par, dz_ref, ghead_ref, rd_ref, *, heads, block):
    @pl.when(i == 0)
    def _():
        ghead_ref[...] = jnp.zeros_like(ghead_ref)

    r = lax.broadcasted_iota(jnp.int32, (CHUNK, CHUNK), 0)
    c = lax.broadcasted_iota(jnp.int32, (CHUNK, CHUNK), 1)
    tri = jnp.where(c <= r, 1.0, 0.0).astype(BF16)
    is_fwd = lax.broadcasted_iota(jnp.int32, (CHUNK, LANES), 1) < heads
    neg = head_par[1:2, :]
    for c_idx in range(block // CHUNK):
        rows = slice(c_idx * CHUNK, (c_idx + 1) * CHUNK)
        d_cum = rates[rows, 0:LANES]
        d_run = rates[rows, LANES : 2 * LANES]
        sums = mm(tri, jnp.concatenate([*split_three(d_cum), *split_two(d_run)], axis=1))
        ahead = sums[:, 0:LANES] + sums[:, LANES : 2 * LANES] + sums[:, 2 * LANES : 3 * LANES]
        run = sums[:, 3 * LANES : 4 * LANES] + sums[:, 4 * LANES :]
        behind = ahead[CHUNK - 1 :, :] - ahead
        d_rate = jnp.where(is_fwd, behind + d_cum + run - d_run, behind + run)
        d_rate = d_rate + rates[rows, 3 * LANES :]
        z = hs[rows, 0:LANES]
        d_step = neg * d_rate + rates[rows, 2 * LANES : 3 * LANES]
        d_z = d_step / (1.0 + jnp.exp(-z))
        dt = hs[rows, LANES : 2 * LANES]
        ghead_ref[0:1, :] += jnp.sum(d_rate * (neg * dt), axis=0, keepdims=True)
        ghead_ref[1:2, :] += jnp.sum(d_z, axis=0, keepdims=True)
        dz_ref[rows, :] = d_z.astype(BF16)
        rd = jnp.sum(d_z * (z - head_par[0:1, :]), axis=1, keepdims=True)
        rd_ref[:, rows] = rd_a[:, rows] + rd_b[:, rows] + to_row(rd, jnp.zeros_like(rd))


def columns_of(scalars, other, size):
    rank = scalars[1]
    return pl.ds(pl.multiple_of((1 - rank if other else rank) * size, LANES), size)


def branch_kernel(scalars, gz, po, out_ref, *, other):
    cols = columns_of(scalars, other, out_ref.shape[1])
    out_ref[...] = mm(gz[...], po[:, cols]).astype(out_ref.dtype)


def back_project_kernel(
    scalars, dgp, rest, dz, rd, w_gate, w_inner, w_state, w_step, out_ref, *, other
):
    rows, size = dgp.shape[0], out_ref.shape[1]
    at = columns_of(scalars, other, size)
    a = w_inner.shape[1]
    out_ref[0:rows, :] = (
        mm_nt(dgp[...], w_gate[at, :])
        + mm_nt(rest[:, 0:a], w_inner[at, :])
        + mm_nt(rest[:, a:], w_state[at, :])
        + mm_nt(dz[...], w_step[at, :])
    ).astype(out_ref.dtype)
    if other:
        part = rows // 4
        lines = jnp.concatenate([rd[0:1, k * part : (k + 1) * part] for k in range(4)], axis=0)
        lines = jnp.concatenate(split_three(lines) + (jnp.zeros((4, part), BF16),), axis=0)
        out_ref[rows : rows + 16, 0:part] = lines
        out_ref[rows : rows + 16, part:] = jnp.zeros((16, size - part), BF16)


def home_of(r, me, order):
    j = me % SHARDS
    levels = len(order)
    for p, bit in enumerate(order):
        if (r >> (levels - 1 - p)) & 1:
            j = jnp.bitwise_xor(j, 1 << bit)
    return j


def lanes_in(orders, width):
    size = width // len(orders)
    return [
        (r, slice(k * size, (k + 1) * size), order) for k, order in enumerate(orders) for r in range(SHARDS)
    ]


def pack_early_kernel(
    scalars, grad_out, grad_gate, w_gate, keep_ref, send_ref, gain_ref, *, order
):
    hi, lo = split_two(grad_gate[...].astype(F32) * w_gate[...].astype(F32))
    ones = jnp.ones((8, hi.shape[1]), BF16)
    gain_ref[...] = mm_nt(ones, hi) + mm_nt(ones, lo)
    part = grad_out.shape[0] // SHARDS
    for r in range(SHARDS):
        j = home_of(r, scalars[2], order)
        out = keep_ref if r < SHARDS // 2 else send_ref
        at = (r % (SHARDS // 2)) * 2 * part
        src = pl.ds(pl.multiple_of(j * part, part), part)
        out[at : at + part, :] = grad_out[src, :]
        out[at + part : at + 2 * part, :] = grad_gate[src, :]


def unpack_early_kernel(scalars, first, second, out_ref, gate_ref, *, order):
    part = out_ref.shape[0] // SHARDS
    for r in range(SHARDS):
        j = home_of(r, scalars[2], order)
        src = first if r < SHARDS // 2 else second
        at = (r % (SHARDS // 2)) * 2 * part
        dst = pl.ds(pl.multiple_of(j * part, part), part)
        out_ref[dst, :] = src[at : at + part, :].astype(F32)
        gate_ref[dst, :] = src[at + part : at + 2 * part, :].astype(F32)


def pack_late_kernel(
    scalars, inner, state, step_low, w_inner, w_state_t, gain, gain_part, gconv, ghead, small, gather,
    keep_ref, send_ref, misc, *, orders, heads, state_width,
):
    model, width = w_inner.shape
    hi, lo = split_two(inner[...].astype(F32) * w_inner[...].astype(F32))
    ones = jnp.ones((8, hi.shape[1]), BF16)
    gain_row = (mm_nt(ones, hi) + mm_nt(ones, lo) + gain_part[...])[0:1]
    step = step_low[...].astype(F32)
    w_t = w_state_t[...].astype(F32)
    gain_row += jnp.sum(state[...].astype(F32) * w_t[:state_width], axis=0, keepdims=True)
    gain_row += jnp.sum(step * w_t[state_width:], axis=0, keepdims=True)
    gain_row = gain_row / gain[...]
    misc[...] = jnp.zeros_like(misc)

    def put_single(k, row):
        at = (k // 2) * 8 + k % 2
        misc[at : at + 1, :] = row

    for k in range(2 * heads):
        put_single(k, step[k : k + 1, :])
    at = 2 * heads
    for k in range(5):
        put_single(at + k, gconv[k : k + 1, 0:width])
    put_single(at + 5, small[0:1, :])
    hi, lo = split_two(eight(small[1:2, :]))
    skip = mm(hi, gather[0:width, :]) + mm(lo, gather[0:width, :])
    at = ((at + 6) // 2) * 8 + (at + 6) % 2
    misc[at : at + 1, 2 * LANES : 3 * LANES] = skip[0:1]
    misc[at : at + 1, 0:LANES] = ghead[0:1, :]
    misc[at : at + 1, LANES : 2 * LANES] = ghead[1:2, :]
    fit = model // state_width
    for k in range(5):
        at = (k // fit) * 8 + 4
        lanes = slice((k % fit) * state_width, (k % fit + 1) * state_width)
        misc[at : at + 1, lanes] = gconv[k : k + 1, width:]
    at = (-(-5 // fit)) * 8 + 4
    misc[at : at + 1, :] = gain_row
    part = model // SHARDS
    part_s = state_width // SHARDS
    rows = part + part_s + 8
    for r, cols, order in lanes_in(orders, model):
        j = home_of(r, scalars[2], order)
        out = keep_ref if r < SHARDS // 2 else send_ref
        at = (r % (SHARDS // 2)) * rows
        out[at : at + part, cols] = inner[pl.ds(pl.multiple_of(j * part, part), part), cols]
        out[at + part : at + part + part_s, cols] = state[
            pl.ds(pl.multiple_of(j * part_s, part_s), part_s), cols
        ]
        out[at + part + part_s : at + rows, cols] = misc[
            pl.ds(pl.multiple_of(j * 8, 8), 8), cols
        ].astype(BF16)


def unpack_late_kernel(
    scalars, first, second, inner_ref, state_ref, step_ref, convi_ref, convi_b_ref, convs_ref, convs_b_ref,
    gg_ref, bias_ref, decay_ref, skip_ref, gain_ref, state, misc, *, orders, heads,
):
    model = inner_ref.shape[0]
    state_width = state_ref.shape[1]
    part = model // SHARDS
    part_s = state_width // SHARDS
    rows = part + part_s + 8
    for r, cols, order in lanes_in(orders, model):
        j = home_of(r, scalars[2], order)
        src = first if r < SHARDS // 2 else second
        at = (r % (SHARDS // 2)) * rows
        inner_ref[pl.ds(pl.multiple_of(j * part, part), part), cols] = src[at : at + part, cols].astype(
            F32
        )
        state[pl.ds(pl.multiple_of(j * part_s, part_s), part_s), cols] = src[
            at + part : at + part + part_s, cols
        ].astype(F32)
        misc[pl.ds(pl.multiple_of(j * 8, 8), 8), cols] = src[at + part + part_s : at + rows, cols].astype(
            F32
        )
    state_ref[...] = jnp.transpose(state[...])

    def single(k):
        at = (k // 2) * 8 + k % 2
        return misc[at : at + 1, :]

    for h in range(heads):
        for d in range(2):
            step_ref[h, d : d + 1, :] = single(d * heads + h)
    at = 2 * heads
    for k in range(4):
        convi_ref[k : k + 1, :] = single(at + k)
    convi_b_ref[...] = single(at + 4).reshape(convi_b_ref.shape)
    gg_ref[...] = single(at + 5).reshape(gg_ref.shape)
    head_row = single(at + 6)
    for d in range(2):
        decay_ref[d : d + 1, :] = head_row[:, d * heads : (d + 1) * heads]
        bias_ref[d : d + 1, :] = head_row[:, LANES + d * heads : LANES + (d + 1) * heads]
    skip_ref[...] = head_row[:, 2 * LANES : 2 * LANES + heads]
    fit = model // state_width
    for k in range(5):
        at = (k // fit) * 8 + 4
        lanes = slice((k % fit) * state_width, (k % fit + 1) * state_width)
        out, row = (convs_ref, k) if k < 4 else (convs_b_ref, 0)
        out[row : row + 1, :] = misc[at : at + 1, lanes]
    at = (-(-5 // fit)) * 8 + 4
    half = model // 2
    gain_ref[...] = jnp.where(
        scalars[1] == 0, misc[at : at + 1, :half], misc[at : at + 1, half:]
    ).reshape(gain_ref.shape)


def place(i, top):
    return i if top is None else top - i


def rows_of(block, top=None):
    return lambda ref, i: ref.at[pl.ds(pl.multiple_of(place(i, top) * block, block), block)]


def lanes_of(block, top=None):
    return lambda ref, i: ref.at[:, pl.ds(pl.multiple_of(place(i, top) * block, block), block)]


def states_of(block, top=None):
    per = block // CHUNK
    return lambda ref, i: ref.at[pl.ds(place(i, top) * per, per)]


def fixed(ref, i):
    return ref


def call(kernel, blocks, ins, out_views, out_shape, scratch, name, aliases=None, us=0.0):
    views = [view for _, view in ins[1:]] + out_views
    arrays = [ins[0]] + [
        pltpu.with_memory_space_constraint(x, pltpu.VMEM) if view is not fixed else x
        for x, view in ins[1:]
    ]

    def looped(scalars, *refs):
        def step(i, _):
            blocks_of = [view(ref, i) for view, ref in zip(views, refs)]
            kernel(i, scalars, *blocks_of, *refs[len(views) :])
            return 0

        lax.fori_loop(0, blocks, step, 0)

    vmem = pl.BlockSpec(memory_space=pltpu.VMEM)
    return pl.pallas_call(
        looped,
        out_shape=[pltpu.VMEM(o.shape, o.dtype) for o in out_shape],
        in_specs=[pl.BlockSpec(memory_space=pltpu.SMEM)] + [vmem] * (len(arrays) - 1),
        out_specs=[vmem] * len(out_shape),
        scratch_shapes=scratch,
        compiler_params=pltpu.CompilerParams(vmem_limit_bytes=VMEM_LIMIT),
        cost_estimate=pl.CostEstimate(
            flops=int(us * 5e8), transcendentals=0, bytes_accessed=int(us * 3e6)
        ),
        name=name,
        input_output_aliases=aliases or {},
    )(*arrays)


def whole(kernel, args, out_shape, scratch, name, in_vmem=True, us=0.0):
    vmem = pl.BlockSpec(memory_space=pltpu.VMEM)
    return pl.pallas_call(
        kernel,
        out_shape=[pltpu.VMEM(o.shape, o.dtype) if in_vmem else o for o in out_shape],
        in_specs=[pl.BlockSpec(memory_space=pltpu.SMEM)] + [vmem] * (len(args) - 1),
        out_specs=[vmem] * len(out_shape),
        scratch_shapes=scratch,
        compiler_params=pltpu.CompilerParams(vmem_limit_bytes=VMEM_LIMIT),
        cost_estimate=pl.CostEstimate(
            flops=int(us * 5e8), transcendentals=0, bytes_accessed=int(us * 3e6)
        ),
        name=name,
    )(*args)


def swap_mp(x):
    return lax.ppermute(x, "mp", [(0, 1), (1, 0)])


def swap_dp(x, bit):
    size = lax.axis_size("dp")
    return lax.ppermute(x, "dp", [(i, i ^ (1 << bit)) for i in range(size)])


def add_low(a, b):
    return (a.astype(F32) + b.astype(F32)).astype(BF16)


def after(x, *others):
    return lax.optimization_barrier((x, *others))[0]


def body(
    tokens,
    norm_gain,
    proj_gate,
    proj_inner,
    proj_state,
    proj_step,
    conv_inner,
    conv_inner_bias,
    conv_state,
    conv_state_bias,
    step_bias,
    decay_log,
    skip_gain,
    gate_gain,
    proj_out,
    lengths,
    cotangent,
):
    rows, width_own = tokens.shape
    model = 2 * width_own
    heads = skip_gain.shape[0]
    width = proj_inner.shape[1]
    head_dim = width // heads
    state_width = proj_state.shape[1]
    n = state_width // 4
    conv_width = width + state_width
    inner_width = width * lax.axis_size("mp")
    chunks = rows // CHUNK
    rank = lax.axis_index("mp")
    shape = jax.ShapeDtypeStruct

    oth_tokens = swap_mp(tokens)
    oth_gain = swap_mp(norm_gain.reshape(1, width_own))
    oth_cot = swap_mp(after(cotangent, oth_tokens))

    scalars = jnp.stack([lengths[0], rank, lax.axis_index("dp")]).astype(jnp.int32)
    step_weight = proj_step.reshape(model, 2 * heads)
    step_weight = jnp.pad(step_weight, ((0, 0), (0, LANES - 2 * heads)))
    own_gain = norm_gain.reshape(1, width_own)
    gain = natural(rank, own_gain, oth_gain).astype(F32)
    conv = jnp.concatenate(
        [
            jnp.concatenate([conv_inner, conv_state], axis=1),
            jnp.concatenate([conv_inner_bias, conv_state_bias])[None],
            jnp.zeros((3, conv_width), F32),
        ]
    )
    head_par = jnp.stack(
        [
            step_bias.reshape(-1),
            -jnp.exp(decay_log.reshape(-1)),
            jnp.pad(skip_gain, (0, heads)),
        ]
    )
    head_par = jnp.pad(head_par, ((0, 5), (0, LANES - 2 * heads)))
    staged = (tokens, cotangent, proj_gate, proj_inner, proj_state, proj_out)
    hbm = pl.BlockSpec(memory_space=pl.ANY)
    vmem = pl.BlockSpec(memory_space=pltpu.VMEM)
    tokens_v, cot_v, gate_v, inner_v, state_v, out_v, spread, gather, w_state_t = pl.pallas_call(
        partial(stage_kernel, count=len(staged), head_dim=head_dim),
        out_shape=[pltpu.VMEM(x.shape, x.dtype) for x in staged]
        + [
            pltpu.VMEM((2 * LANES, 2 * width), BF16),
            pltpu.VMEM((2 * width, LANES), BF16),
            pltpu.VMEM((state_width + LANES, model), BF16),
        ],
        in_specs=[vmem, vmem] + [hbm] * len(staged),
        out_specs=[vmem] * (len(staged) + 3),
        scratch_shapes=[pltpu.SemaphoreType.DMA((len(staged),))],
        compiler_params=pltpu.CompilerParams(vmem_limit_bytes=VMEM_LIMIT),
        name="stage",
    )(proj_state, step_weight, *staged)
    gg = gate_gain[None]

    sizes = dict(heads=heads, width=width, state_width=state_width)
    low = lambda *dims: shape(dims, BF16)
    full = lambda *dims: shape(dims, F32)
    block = PROJECT_BLOCK
    up, states = rows_of(block), states_of(block)
    normed, gate_pre, pre, slope, hs, act, sact, xd, hf, sb = call(
        partial(project_kernel, block=block, **sizes),
        rows // block,
        [
            scalars,
            (tokens_v, up),
            (oth_tokens, up),
            (gain, fixed),
            (gate_v, fixed),
            (inner_v, fixed),
            (state_v, fixed),
            (step_weight, fixed),
            (conv, fixed),
            (head_par, fixed),
            (spread, fixed),
        ],
        [up, up, up, up, up, up, up, up, states, states],
        [
            low(rows, model),
            full(rows, width),
            low(rows, conv_width),
            low(rows, conv_width),
            full(rows, 4 * LANES),
            full(rows, width),
            low(rows, state_width),
            low(rows, 2 * width),
            low(chunks, n, width),
            full(chunks, n, width),
        ],
        [pltpu.VMEM((block + 8, conv_width), F32), pltpu.VMEM((n, width), F32)],
        "project",
        us=12,
    )

    block = MIX_BLOCK
    top = rows // block - 1
    down, states_down = rows_of(block, top), states_of(block, top)
    y, hb = call(
        partial(mix_kernel, block=block, **sizes),
        rows // block,
        [
            scalars,
            (act, down),
            (sact, down),
            (hs, down),
            (xd, down),
            (hf, states_down),
            (sb, states_down),
            (head_par, fixed),
            (spread, fixed),
        ],
        [down, states_down],
        [full(rows, width), low(chunks, n, width)],
        [pltpu.VMEM((n, width), F32)],
        "mix",
        us=7,
    )

    block = GATE_BLOCK
    up, states, up_lanes = rows_of(block), states_of(block), lanes_of(block)
    dgn, gz, sums = call(
        partial(gate_kernel, block=block),
        rows // block,
        [
            scalars,
            (y, up),
            (gate_pre, up),
            (cot_v, up),
            (oth_cot, up),
            (out_v, fixed),
            (gg, fixed),
        ],
        [up, up, up_lanes],
        [full(rows, width), low(rows, width), full(8, rows)],
        [],
        "gate",
        us=3,
    )

    oth_sums = swap_mp(sums)
    branch_oth = whole(
        partial(branch_kernel, other=True), (scalars, gz, out_v), [low(rows, width_own)], [], "branch_oth", us=3
    )[0]
    sums = sums + oth_sums
    branch_got = swap_mp(after(branch_oth, sums))
    sums_in = after(sums, branch_oth)

    g, dgp, dbr, dc, gb, gf, rd_gate, row_sums, small = call(
        partial(gate_back_kernel, block=block, inner_width=inner_width, **sizes),
        rows // block,
        [
            scalars,
            (sums_in, up_lanes),
            (gate_pre, up),
            (y, up),
            (act, up),
            (dgn, up),
            (cot_v, up),
            (oth_cot, up),
            (hs, up),
            (sact, up),
            (hf, states),
            (hb, states),
            (gg, fixed),
            (spread, fixed),
            (gather, fixed),
        ],
        [up, up, up, up, states, states, up_lanes, up, fixed],
        [
            low(rows, width),
            low(rows, width),
            low(rows, model),
            full(rows, 2 * n),
            low(chunks, n, width),
            full(chunks, n, width),
            full(8, rows),
            full(rows, LANES),
            full(8, width),
        ],
        [pltpu.VMEM((n, width), F32), pltpu.VMEM((block, 2 * width), BF16)],
        "gate_back",
        us=8,
    )

    def back_part(first, count, g, state):
        block = BACK_BLOCK
        here, states_here, here_lanes = rows_of(block, first), states_of(block, first), lanes_of(block, first)
        ins = [
            scalars,
            (g, here),
            (act, here),
            (sact, here),
            (hs, here),
            (xd, here),
            (row_sums, here),
            (hf, states_here),
            (hb, states_here),
            (gb, states_here),
            (gf, states_here),
            (dc, here),
            (pre, here),
            (slope, here),
            (conv, fixed),
            (head_par, fixed),
            (spread, fixed),
            (gather, fixed),
            *[(x, fixed) for x in state[:3]],
            (state[3], here),
            (state[4], here),
            (state[5], here_lanes),
        ]
        return call(
            partial(back_kernel, block=block, top=first, **sizes),
            count,
            ins,
            [here, here, here_lanes, fixed, fixed, fixed],
            [
                low(rows, conv_width),
                full(rows, 4 * LANES),
                full(8, rows),
                full(8, conv_width),
                full(8, conv_width),
                full(n, width),
            ],
            [
                pltpu.VMEM((block + 8, conv_width), F32),
                pltpu.VMEM((2 * CHUNK + 16, 2 * width), BF16),
                pltpu.VMEM((CHUNK, 2 * width), BF16),
                pltpu.VMEM((LANES, CHUNK), F32),
                pltpu.VMEM((CHUNK, LANES), F32),
            ],
            "mix_back",
            us=3 * count,
            aliases={len(ins) - 3: 0, len(ins) - 2: 1, len(ins) - 1: 2},
        )

    order_a, orders_b = (0, 1, 2, 3), ((0, 1, 2, 3), (0, 2, 1, 3))
    grad_out = mm_tn(gz, dbr).astype(BF16)
    grad_gate = mm_tn(normed, dgp).astype(BF16)
    keep, send, gain_part = whole(
        partial(pack_early_kernel, order=order_a),
        (scalars, grad_out, grad_gate, proj_gate),
        [low(width, model), low(width, model), full(8, model)],
        [],
        "pack_early",
    )

    def rest_of_dp(x):
        extra = SHARDS
        while extra < lax.axis_size("dp"):
            x = add_low(x, swap_dp(x, extra.bit_length() - 1))
            extra *= 2
        return x

    zeros = (
        jnp.zeros((8, conv_width), F32),
        jnp.zeros((n, width), F32),
        jnp.zeros((8, conv_width), F32),
    )
    branch_own = whole(
        partial(branch_kernel, other=False), (scalars, after(gz, send), out_v), [full(rows, width_own)], [],
        "branch_own"
    )[0]
    got, branch_own = lax.optimization_barrier((swap_dp(send, order_a[0]), branch_own))
    h = keep.shape[0] // 2
    keep, send = add_low(keep[:h], got[:h]), add_low(keep[h:], got[h:])
    state = (
        *zeros,
        jnp.zeros((rows, conv_width), BF16),
        jnp.zeros((rows, 4 * LANES), F32),
        jnp.zeros((8, rows), F32),
    )
    parts = 4
    count = rows // BACK_BLOCK // parts
    g = after(g, send)
    sent, x = swap_dp(send, order_a[1]), None
    for k in range(parts):
        outs = back_part((parts - k) * count - 1, count, g, state)
        rest, rates, rd_rest, gconv, ext_carry, carry = outs
        if k == 1:
            sent, carry = lax.optimization_barrier((sent, carry))
        elif k == 2:
            sent, carry, branch_got = lax.optimization_barrier((sent, carry, branch_got))
        elif k == 3:
            sent, rest = lax.optimization_barrier((sent, rest))
        if k > 0:
            h = keep.shape[0] // 2
            if k < 3:
                keep, send = add_low(keep[:h], sent[:h]), add_low(keep[h:], sent[h:])
                carry = after(carry, send)
                sent = swap_dp(send, order_a[k + 1])
            else:
                x = rest_of_dp(add_low(keep, sent))
        state = (ext_carry, carry, gconv, rest, rates, rd_rest)

    block = RATES_BLOCK
    rates, x, rest = lax.optimization_barrier((rates, x, rest))
    sent = swap_dp(x, order_a[3])
    dz, ghead, rd_part = call(
        partial(rates_kernel, heads=heads, block=block),
        rows // block,
        [
            scalars,
            (rates, rows_of(block)),
            (hs, rows_of(block)),
            (rd_gate, lanes_of(block)),
            (rd_rest, lanes_of(block)),
            (head_par, fixed),
        ],
        [rows_of(block), fixed, lanes_of(block)],
        [low(rows, LANES), full(8, LANES), full(8, rows)],
        [],
        "rates",
    )
    grad_inner = mm_tn(normed, rest[:, :width]).astype(BF16)
    grad_state = mm_tn(rest[:, width:], normed).astype(BF16)
    grad_step = mm_tn(dz, normed).astype(BF16)
    keep, send = whole(
        partial(pack_late_kernel, orders=orders_b, heads=heads, state_width=state_width),
        (
            scalars, grad_inner, grad_state, grad_step, inner_v, w_state_t, gain, gain_part, gconv, ghead,
            small, gather,
        ),
        [low(LATE_ROWS * SHARDS // 2, model), low(LATE_ROWS * SHARDS // 2, model)],
        [pltpu.VMEM((8 * SHARDS, model), F32)],
        "pack_late",
    )

    back_args = (scalars, dgp, rest, dz, rd_part, gate_v, inner_v, state_v, step_weight)
    dn_oth = whole(
        partial(back_project_kernel, other=True), back_args, [low(rows + 16, width_own)], [], "back_oth"
    )[0]
    x = jnp.concatenate([x, sent])
    send, x, dn_oth = lax.optimization_barrier((send, x, dn_oth))
    got = swap_dp(send, 0)
    sent = swap_dp(x, order_a[2])
    h, c = keep.shape[0] // 2, model // 2
    keeps = [add_low(keep[:h, :c], got[:h, :c]), add_low(keep[:h, c:], got[:h, c:])]
    sends = [add_low(keep[h:, :c], got[h:, :c]), add_low(keep[h:, c:], got[h:, c:])]
    sends[0], sends[1], rest = lax.optimization_barrier((sends[0], sends[1], rest))
    dn_got = swap_mp(dn_oth)

    dn_own = whole(
        partial(back_project_kernel, other=False), (*back_args[:2], rest, *back_args[3:]),
        [full(rows, width_own)], [], "back_own"
    )[0]
    for level in (1, 2):
        gots = [swap_dp(v, order[level]) for v, order in zip(sends, orders_b)]
        if level == 1:
            gots[0], gots[1], dn_own, sent = lax.optimization_barrier((gots[0], gots[1], dn_own, sent))
            x = jnp.concatenate([x, sent])
        h = keeps[0].shape[0] // 2
        pairs = list(zip(keeps, gots))
        if level == 1:
            keeps = [add_low(k[:h], v[:h]) for k, v in pairs]
            sends = [add_low(k[h:], v[h:]) for k, v in pairs]
        else:
            keep = jnp.concatenate([add_low(k[:h], v[:h]) for k, v in pairs], axis=1)
            send = jnp.concatenate([add_low(k[h:], v[h:]) for k, v in pairs], axis=1)
    send, x, tokens_late, oth_late = lax.optimization_barrier((send, x, tokens, oth_tokens))
    sent = swap_dp(x, order_a[1])

    seq_mask = (jnp.arange(rows) < lengths[0]).astype(F32)[:, None]
    gate_inv = lax.rsqrt(sums[0] / inner_width + EPSILON)[:, None]
    tokens_f = tokens_late.astype(F32)
    block_out = (tokens_f + seq_mask * gate_inv * (branch_own + branch_got.astype(F32))).astype(BF16)

    got, block_out, dn_got = lax.optimization_barrier((swap_dp(send, 3), block_out, dn_got))
    z = rest_of_dp(add_low(keep, got))
    part = model // SHARDS
    tail = z[part:]
    tail_row = lax.broadcasted_iota(jnp.int32, (LATE_ROWS - part, 1), 0)
    alone = (tail_row >= LATE_ROWS - part - 8) & (tail_row < LATE_ROWS - part - 4)
    tail_f = tail.astype(F32)
    tail = jnp.where(alone, tail_f, tail_f + swap_mp(tail).astype(F32)).astype(BF16)
    z = jnp.concatenate([z[:part], tail])
    oth_f = oth_late.astype(F32)
    square = jnp.sum(tokens_f * tokens_f, axis=1, keepdims=True) + jnp.sum(
        oth_f * oth_f, axis=1, keepdims=True
    )
    inv = lax.rsqrt(square / model + EPSILON)
    part = rows // 4
    lines = dn_got[rows:, :part].astype(F32)
    oth_rd = (lines[0:4] + lines[4:8] + lines[8:12]).reshape(rows)
    rd_both = rd_part[0] + oth_rd
    grad_full = dn_own + dn_got[:rows].astype(F32)
    grad_tokens = (
        cotangent.astype(F32)
        + inv * (grad_full * norm_gain.astype(F32)[None])
        - tokens_f * (inv * inv * (rd_both[:, None] / model))
    )

    got, grad_tokens, sent = lax.optimization_barrier((swap_dp(z, 3), grad_tokens, sent))
    x = jnp.concatenate([x, sent])
    sent = swap_dp(x, order_a[0])
    z = jnp.concatenate([z, got])
    zs = [z[:, :c], z[:, c:]]
    gots = [swap_dp(v, order[2]) for v, order in zip(zs, orders_b)]
    zs = [jnp.concatenate([v, g]) for v, g in zip(zs, gots)]
    grad_proj_out, grad_proj_gate = whole(
        partial(unpack_early_kernel, order=order_a),
        (scalars, x, after(sent, *zs)),
        [full(width, model), full(model, width)],
        [],
        "unpack_early",
        in_vmem=False,
    )
    gots = [swap_dp(v, order[1]) for v, order in zip(zs, orders_b)]
    gots[0], gots[1], grad_proj_out = lax.optimization_barrier((gots[0], gots[1], grad_proj_out))
    z = jnp.concatenate([jnp.concatenate([v, g]) for v, g in zip(zs, gots)], axis=1)
    (
        grad_proj_inner,
        grad_proj_state,
        step,
        grad_conv_inner,
        grad_conv_inner_bias,
        grad_conv_state,
        grad_conv_state_bias,
        grad_gate_gain,
        grad_step_bias,
        grad_decay_log,
        grad_skip,
        grad_norm_gain,
    ) = whole(
        partial(unpack_late_kernel, orders=orders_b, heads=heads),
        (scalars, z, swap_dp(z, 0)),
        [
            full(model, width),
            full(model, state_width),
            full(heads, 2, model),
            full(4, width),
            full(width),
            full(4, state_width),
            full(1, state_width),
            full(width),
            full(2, heads),
            full(2, heads),
            full(1, heads),
            full(width_own),
        ],
        [pltpu.VMEM((state_width, model), F32), pltpu.VMEM((8 * SHARDS, model), F32)],
        "unpack_late",
        in_vmem=False,
    )
    return (
        block_out,
        grad_tokens,
        grad_norm_gain,
        grad_proj_gate,
        grad_proj_inner,
        grad_proj_state,
        step.transpose(2, 1, 0),
        grad_conv_inner,
        grad_conv_inner_bias,
        grad_conv_state,
        grad_conv_state_bias[0],
        grad_step_bias,
        grad_decay_log,
        grad_skip[0],
        grad_gate_gain,
        grad_proj_out,
    )


def solution(mesh):
    in_specs = (
        P("dp", "mp"),
        P("mp"),
        P(None, "mp"),
        P(None, "mp"),
        P(),
        P(None, None, "mp"),
        P(None, "mp"),
        P("mp"),
        P(),
        P(),
        P(None, "mp"),
        P(None, "mp"),
        P("mp"),
        P("mp"),
        P("mp", None),
        P("dp"),
        P("dp", "mp"),
    )
    out_specs = (
        P("dp", "mp"),
        P("dp", "mp"),
        P("mp"),
        P(None, "mp"),
        P(None, "mp"),
        P(),
        P(None, None, "mp"),
        P(None, "mp"),
        P("mp"),
        P(),
        P(),
        P(None, "mp"),
        P(None, "mp"),
        P("mp"),
        P("mp"),
        P("mp", None),
    )
    return jax.shard_map(body, mesh=mesh, in_specs=in_specs, out_specs=out_specs, check_vma=False)
```

```python
from functools import partial

import jax
import jax.numpy as jnp
from jax import lax
from jax.experimental import pallas as pl
from jax.experimental.pallas import tpu as pltpu
from jax.sharding import PartitionSpec as P

EPSILON = 1e-05
CHUNK = 128
PROJECT_BLOCK, MIX_BLOCK, GATE_BLOCK, GATE_BACK_BLOCK, BACK_BLOCK, RATES_BLOCK = 256, 256, 512, 256, 128, 512
LANES = 128
F32 = jnp.float32
BF16 = jnp.bfloat16
HIGHEST = lax.Precision.HIGHEST
VMEM_LIMIT = 12 * 1024 * 1024
SHARDS = 16
LOG2_E = 1.4426950408889634
LATE_ROWS = 72


def mm(a, b):
    return jnp.dot(a, b, preferred_element_type=F32)


def mm_nt(a, b):
    return lax.dot_general(a, b, (((1,), (1,)), ((), ())), preferred_element_type=F32)


def mm_tn(a, b):
    return lax.dot_general(a, b, (((0,), (0,)), ((), ())), preferred_element_type=F32)


def split_two(v):
    hi = v.astype(BF16)
    return hi, (v - hi.astype(F32)).astype(BF16)


def split_three(v):
    hi, mid = split_two(v)
    return hi, mid, (v - hi.astype(F32) - mid.astype(F32)).astype(BF16)


def expand(v, spread):
    hi, lo = split_two(v)
    return mm(jnp.concatenate([hi, lo], axis=1), spread)


def row_mask(block, rows, length):
    pos = block * rows + lax.broadcasted_iota(jnp.int32, (rows, 1), 0)
    return (pos < length).astype(F32)


def to_row(col_a, col_b):
    rows = col_a.shape[0]
    lane = lax.broadcasted_iota(jnp.int32, (rows, LANES), 1)
    tile = jnp.where(lane == 0, col_a, jnp.where(lane == 1, col_b, 0.0))
    return jnp.transpose(tile)[0:8, :]


def sigmoid(v):
    return 0.5 * jnp.tanh(0.5 * v) + 0.5


def natural(rank, own, oth):
    return jnp.where(
        rank == 0, jnp.concatenate([own, oth], axis=1), jnp.concatenate([oth, own], axis=1)
    )


def eight(row):
    return jnp.broadcast_to(row, (8, row.shape[1]))


def stage_kernel(w_state, w_step, *refs, count, head_dim):
    sources, outs, sems = refs[:count], refs[count:-1], refs[-1]
    spread, gather, w_state_t = outs[count:]
    copies = [
        pltpu.make_async_copy(src, dst, sems.at[k]) for k, (src, dst) in enumerate(zip(sources, outs))
    ]
    for copy in copies:
        copy.start()
    state_width = w_state.shape[1]
    w_state_t[:state_width, :] = jnp.transpose(w_state[...].astype(F32)).astype(BF16)
    w_state_t[state_width:, :] = jnp.transpose(w_step[...].astype(F32)).astype(BF16)
    head = lax.broadcasted_iota(jnp.int32, spread.shape, 1) // head_dim
    row = lax.broadcasted_iota(jnp.int32, spread.shape, 0) % LANES
    spread[...] = jnp.where(head == row, 1.0, 0.0).astype(BF16)
    head = lax.broadcasted_iota(jnp.int32, gather.shape, 0) // head_dim
    lane = lax.broadcasted_iota(jnp.int32, gather.shape, 1)
    gather[...] = jnp.where(head == lane, 1.0, 0.0).astype(BF16)
    for copy in copies:
        copy.wait()


def project_kernel(
    i, scalars, own, oth, gain, w_gate, w_inner, w_state, w_step, conv, head_par, spread,
    normed_ref, gate_ref, pre_ref, slope_ref, hs_ref, act_ref, sact_ref, xd_ref, hf_ref, sb_ref,
    ext, carry, *, heads, width, state_width, block,
):
    @pl.when(i == 0)
    def _():
        ext[0:8, :] = jnp.zeros((8, ext.shape[1]), F32)
        carry[...] = jnp.zeros_like(carry)

    x = natural(scalars[1], own[...], oth[...]).astype(F32)
    inv = lax.rsqrt(jnp.mean(x * x, axis=-1, keepdims=True) + EPSILON)
    normed = (x * inv * gain[...]).astype(BF16)
    normed_ref[...] = normed
    step_pre = mm(normed, w_step[...])
    z = step_pre + head_par[0:1, :]
    dt = jnp.maximum(z, 0.0) + jnp.log1p(jnp.exp(-jnp.abs(z)))
    rate = head_par[1:2, :] * dt
    dtm = dt * row_mask(i, block, scalars[0])
    hs_ref[:, 0:LANES] = z
    hs_ref[:, LANES : 2 * LANES] = dt
    tri_r = lax.broadcasted_iota(jnp.int32, (CHUNK, CHUNK), 0)
    tri_c = lax.broadcasted_iota(jnp.int32, (CHUNK, CHUNK), 1)
    tri = (tri_c <= tri_r).astype(F32)
    is_fwd = lax.broadcasted_iota(jnp.int32, (CHUNK, LANES), 1) < heads
    per = block // CHUNK
    to_spread = [dtm]
    keeps = []
    for c_idx in range(per):
        rows = slice(c_idx * CHUNK, (c_idx + 1) * CHUNK)
        rate_c = rate[rows]
        cum = jnp.dot(tri, rate_c, precision=HIGHEST, preferred_element_type=F32)
        tot = cum[CHUNK - 1 : CHUNK, :]
        cumx = jnp.where(is_fwd, cum, cum - rate_c)
        hs_ref[rows, 2 * LANES : 3 * LANES] = cumx
        hs_ref[rows, 3 * LANES :] = jnp.broadcast_to(tot, (CHUNK, LANES))
        to_spread.append(dtm[rows] * jnp.exp(jnp.where(is_fwd, tot - cumx, cumx)))
        keeps.append(eight(jnp.exp(tot)))
    wide = expand(jnp.concatenate(to_spread + keeps, axis=0), spread[...])

    ext[8 : 8 + block, 0:width] = mm(normed, w_inner[...])
    ext[8 : 8 + block, width:] = mm(normed, w_state[...])
    gate_ref[...] = mm(normed, w_gate[...])
    whole_ext = ext[...]
    pre = whole_ext[8:]
    pre_ref[...] = pre.astype(BF16)
    c = conv[4:5, :] + conv[3:4, :] * pre
    for j in range(3):
        c = c + conv[j : j + 1, :] * pltpu.roll(whole_ext, 3 - j, 0)[8:]
    sg = sigmoid(c)
    both = c * sg
    slope_ref[...] = (sg * (1.0 + c * (1.0 - sg))).astype(BF16)
    ext[0:8, :] = ext[block : block + 8, :]
    act = both[:, :width]
    act_ref[...] = act
    sact = both[:, width:].astype(BF16)
    sact_ref[...] = sact
    xd_ref[:, 0:width] = (act * wide[0:block, :width]).astype(BF16)
    xd_ref[:, width:] = (act * wide[0:block, width:]).astype(BF16)
    n = state_width // 4
    for c_idx in range(per):
        rows = slice(c_idx * CHUNK, (c_idx + 1) * CHUNK)
        coef = wide[block + c_idx * CHUNK : block + (c_idx + 1) * CHUNK]
        keep = wide[2 * block + 8 * c_idx : 2 * block + 8 * c_idx + 1, :width]
        hf_ref[c_idx] = carry[...].astype(BF16)
        carry[...] = carry[...] * keep + mm_tn(
            sact[rows, 0:n], (act[rows] * coef[:, :width]).astype(BF16)
        )
        sb_ref[c_idx] = mm_tn(
            sact[rows, 2 * n : 3 * n], (act[rows] * coef[:, width:]).astype(BF16)
        )


def pair_tiles(pair):
    lane = lax.broadcasted_iota(jnp.int32, (1, pair.shape[1]), 1)
    first = (lane < pair.shape[1] // 2).astype(F32)
    keep_a, keep_b = first.astype(BF16), (1.0 - first).astype(BF16)
    return jnp.concatenate([pair * keep_a, pair * keep_b], axis=0)


def mix_kernel(
    i, scalars, act, sact, hs, xd, hf, sb, head_par, spread, y_ref, hb_ref, carry,
    *, heads, width, state_width, block,
):
    @pl.when(i == 0)
    def _():
        carry[...] = jnp.zeros_like(carry)

    n = state_width // 4
    per = block // CHUNK
    r = lax.broadcasted_iota(jnp.int32, (CHUNK, CHUNK), 0)
    c = lax.broadcasted_iota(jnp.int32, (CHUNK, CHUNK), 1)
    lower = c < r
    upper = c > r
    is_fwd = lax.broadcasted_iota(jnp.int32, (block, LANES), 1) < heads
    cum_all = hs[:, 2 * LANES : 3 * LANES]
    tot_all = hs[:, 3 * LANES :]
    wide = expand(
        jnp.concatenate(
            [jnp.exp(jnp.where(is_fwd, cum_all, tot_all - cum_all))]
            + [jnp.exp(tot_all[k * CHUNK : k * CHUNK + 8]) for k in range(per)]
            + [eight(head_par[2:3, :])],
            axis=0,
        ),
        spread[...],
    )
    skip = wide[block + 8 * per : block + 8 * per + 1]
    for c_idx in reversed(range(per)):
        rows = slice(c_idx * CHUNK, (c_idx + 1) * CHUNK)
        cumx = cum_all[rows] * LOG2_E
        cum_t = jnp.transpose(cumx)
        sact_c = sact[rows, :]
        b_f, c_f = sact_c[:, 0:n], sact_c[:, n : 2 * n]
        b_b, c_b = sact_c[:, 2 * n : 3 * n], sact_c[:, 3 * n :]
        s_f = jnp.where(lower, mm_nt(c_f, b_f), 0.0)
        s_b = jnp.where(upper, mm_nt(c_b, b_b), 0.0)
        hb = carry[...].astype(BF16)
        hb_ref[c_idx] = hb
        in_f = mm(c_f, hf[c_idx])
        in_b = mm(c_b, hb)
        keep = wide[block + 8 * c_idx : block + 8 * c_idx + 1, width:]
        carry[...] = carry[...] * keep + sb[c_idx]
        for p in range(heads // 2):
            lanes = slice(p * LANES, (p + 1) * LANES)
            lanes_b = slice(width + p * LANES, width + (p + 1) * LANES)
            w_f, w_b = [], []
            for h in (2 * p, 2 * p + 1):
                damp = jnp.exp2(
                    jnp.minimum(
                        cumx[:, h : h + 1] - cum_t[h : h + 1, :],
                        cum_t[heads + h : heads + h + 1, :] - cumx[:, heads + h : heads + h + 1],
                    )
                )
                w_f.append((s_f * damp).astype(BF16))
                w_b.append((s_b * damp).astype(BF16))
            out = mm(
                jnp.concatenate(w_f + w_b, axis=1),
                jnp.concatenate([pair_tiles(xd[rows, lanes]), pair_tiles(xd[rows, lanes_b])], axis=0),
            )
            y_ref[rows, lanes] = (
                out
                + wide[rows, lanes] * in_f[:, lanes]
                + wide[rows, lanes_b] * in_b[:, lanes]
                + skip[:, lanes] * act[rows, lanes]
            )


def gate_kernel(i, scalars, y, gate, cown, coth, po, gg, dgn_ref, gz_ref, sums_ref, *, block):
    gp = gate[...]
    gated = y[...] * (gp * sigmoid(gp))
    mask = row_mask(i, block, scalars[0])
    cot = natural(scalars[1], cown[...], coth[...])
    dgn = mm_nt((cot.astype(F32) * mask).astype(BF16), po[...])
    dgn_ref[...] = dgn
    scaled = gated * gg[...]
    gz_ref[...] = scaled.astype(BF16)
    sums_ref[...] = to_row(
        jnp.sum(gated * gated, axis=1, keepdims=True), jnp.sum(dgn * scaled, axis=1, keepdims=True)
    )


def gate_back_kernel(
    i, scalars, sums, gate, y, act, dgn, cown, coth, hs, sact, hf, hb, gg, spread, gather,
    g_ref, dgp_ref, dbr_ref, dc_ref, gb_ref, gf_ref, rd_ref, rows_ref, small_ref, carry, prod,
    *, heads, width, state_width, block, inner_width,
):
    @pl.when(i == 0)
    def _():
        carry[...] = jnp.zeros_like(carry)
        small_ref[...] = jnp.zeros_like(small_ref)

    per = block // CHUNK
    is_fwd = lax.broadcasted_iota(jnp.int32, (block, LANES), 1) < heads
    cum_all = hs[:, 2 * LANES : 3 * LANES]
    tot_all = hs[:, 3 * LANES :]
    wide = expand(
        jnp.concatenate(
            [jnp.exp(jnp.where(is_fwd, cum_all, tot_all - cum_all))]
            + [jnp.exp(tot_all[k * CHUNK : k * CHUNK + 8]) for k in range(per)],
            axis=0,
        ),
        spread[...],
    )
    cols = jnp.transpose(sums[...])
    gate_inv = lax.rsqrt(cols[:, 0:1] / inner_width + EPSILON)
    gate_dot = cols[:, 1:2] / inner_width
    gp = gate[...]
    sg = sigmoid(gp)
    act_gate = gp * sg
    yv = y[...]
    gated = yv * act_gate
    dg = dgn[...]
    small_ref[0:1, :] += jnp.sum(dg * gated * gate_inv, axis=0, keepdims=True)
    d_gated = gate_inv * (dg * gg[...]) - gated * (gate_inv * gate_inv * gate_inv * gate_dot)
    d_gp = d_gated * yv * (sg * (1.0 + gp * (1.0 - sg)))
    dgp_ref[...] = d_gp.astype(BF16)
    rd = jnp.sum(d_gp * gp, axis=1, keepdims=True)
    rd_ref[...] = to_row(rd, jnp.zeros_like(rd))
    d_y = d_gated * act_gate
    g_ref[...] = d_y.astype(BF16)
    small_ref[1:2, :] += jnp.sum(d_y * act[...], axis=0, keepdims=True)
    mask = row_mask(i, block, scalars[0])
    cot = natural(scalars[1], cown[...], coth[...])
    dbr_ref[...] = (cot.astype(F32) * (mask * gate_inv)).astype(BF16)
    n = state_width // 4
    for c_idx in range(per):
        rows = slice(c_idx * CHUNK, (c_idx + 1) * CHUNK)
        dy_c = d_y[rows]
        dyf = dy_c * wide[rows, :width]
        dyb = dy_c * wide[rows, width:]
        prod[rows, 0:width] = (dyf * mm(sact[rows, n : 2 * n], hf[c_idx])).astype(BF16)
        prod[rows, width:] = (dyb * mm(sact[rows, 3 * n :], hb[c_idx])).astype(BF16)
        dyf = dyf.astype(BF16)
        dyb = dyb.astype(BF16)
        dc_ref[rows, 0:n] = mm_nt(dyf, hf[c_idx])
        dc_ref[rows, n : 2 * n] = mm_nt(dyb, hb[c_idx])
        gb_ref[c_idx] = carry[...].astype(BF16)
        keep = wide[block + 8 * c_idx : block + 8 * c_idx + 1, width:]
        carry[...] = carry[...] * keep + mm_tn(sact[rows, 3 * n :], dyb)
        gf_ref[c_idx] = mm_tn(sact[rows, n : 2 * n], dyf)
    rows_ref[...] = mm(prod[...], gather[...])


def back_kernel(
    i, scalars, g, act, sact, hs, xd, row_in, hf, hb, gb, gf, dc, pre, slope, conv, head_par, spread, gather,
    ext_in, carry_in, gconv_in, _rest, _rates, _rd, rest_ref, rates_ref, rd_ref, gconv_ref, ext_out,
    carry, ext, stack, xs, rsum, csum,
    *, heads, width, state_width, block, top,
):
    blk = top - i
    per = block // CHUNK

    @pl.when(i == 0)
    def _():
        ext[block:, :] = ext_in[...]
        carry[...] = carry_in[...]
        gconv_ref[...] = gconv_in[...]
        rsum[...] = jnp.zeros_like(rsum)
        csum[...] = jnp.zeros_like(csum)

    n = state_width // 4
    r = lax.broadcasted_iota(jnp.int32, (CHUNK, CHUNK), 0)
    c = lax.broadcasted_iota(jnp.int32, (CHUNK, CHUNK), 1)
    later = c > r
    earlier = c < r
    is_fwd_all = lax.broadcasted_iota(jnp.int32, (block, LANES), 1) < heads
    is_fwd = lax.broadcasted_iota(jnp.int32, (CHUNK, LANES), 1) < heads
    mask = row_mask(blk, block, scalars[0])
    cum_all = hs[:, 2 * LANES : 3 * LANES]
    tot_all = hs[:, 3 * LANES :]
    wide = expand(
        jnp.concatenate(
            [jnp.exp(jnp.where(is_fwd_all, tot_all - cum_all, cum_all)), hs[:, LANES : 2 * LANES] * mask]
            + [jnp.exp(tot_all[k * CHUNK : k * CHUNK + 8]) for k in range(per)]
            + [eight(head_par[2:3, :])],
            axis=0,
        ),
        spread[...],
    )
    skip = wide[2 * block + 8 * per : 2 * block + 8 * per + 1]
    for c_idx in reversed(range(per)):
        rows = slice(c_idx * CHUNK, (c_idx + 1) * CHUNK)
        rows_dt = slice(block + c_idx * CHUNK, block + (c_idx + 1) * CHUNK)
        cumx = cum_all[rows] * LOG2_E
        cum_t = jnp.transpose(cumx)
        sact_c = sact[rows, :]
        b_f, c_f = sact_c[:, 0:n], sact_c[:, n : 2 * n]
        b_b, c_b = sact_c[:, 2 * n : 3 * n], sact_c[:, 3 * n :]
        s_f = jnp.where(later, mm_nt(b_f, c_f), 0.0)
        s_b = jnp.where(earlier, mm_nt(b_b, c_b), 0.0)
        s_all = s_f + s_b
        grad_f = carry[...]
        grad_f_low = grad_f.astype(BF16)
        grad_b_low = gb[c_idx]
        keep = wide[2 * block + 8 * c_idx : 2 * block + 8 * c_idx + 1]
        keep_f = keep[:, :width]
        edge_f = keep_f * jnp.sum(grad_f * hf[c_idx].astype(F32), axis=0, keepdims=True)
        edge_b = keep[:, width:] * jnp.sum(
            hb[c_idx].astype(F32) * grad_b_low.astype(F32), axis=0, keepdims=True
        )
        e_hi, e_lo = split_two(eight(jnp.concatenate([edge_f, edge_b], axis=1)))
        stack[2 * CHUNK :, :] = jnp.concatenate([e_hi, e_lo], axis=0)
        carry[...] = grad_f * keep_f + gf[c_idx]
        in_f = mm(b_f, grad_f_low)
        in_b = mm(b_b, grad_b_low)
        d_scores = jnp.zeros((CHUNK, CHUNK), F32)
        for p in range(heads // 2):
            lanes = slice(p * LANES, (p + 1) * LANES)
            lanes_b = slice(width + p * LANES, width + (p + 1) * LANES)
            g_pair = g[rows, lanes]
            xf_pair = xd[rows, lanes]
            xb_pair = xd[rows, lanes_b]
            dw = mm_nt(
                jnp.concatenate([pair_tiles(xf_pair), pair_tiles(xb_pair)], axis=0), g_pair
            )
            w_f, w_b = [], []
            for q, h in enumerate((2 * p, 2 * p + 1)):
                damp = jnp.exp2(
                    jnp.minimum(
                        cum_t[h : h + 1, :] - cumx[:, h : h + 1],
                        cumx[:, heads + h : heads + h + 1] - cum_t[heads + h : heads + h + 1, :],
                    )
                )
                w_f.append((s_f * damp).astype(BF16))
                w_b.append((s_b * damp).astype(BF16))
                part = jnp.where(
                    later, dw[q * CHUNK : (q + 1) * CHUNK], dw[(2 + q) * CHUNK : (3 + q) * CHUNK]
                )
                part = part * damp
                d_scores = d_scores + part
                e_all = part * s_all
                e_fwd = jnp.where(later, e_all, 0.0)
                sum_all = jnp.sum(e_all, axis=0, keepdims=True)
                sum_fwd = jnp.sum(e_fwd, axis=0, keepdims=True)
                rsum[h : h + 1, :] = sum_fwd
                rsum[heads + h : heads + h + 1, :] = sum_fwd - sum_all
                sum_all = jnp.sum(e_all, axis=1, keepdims=True)
                sum_fwd = jnp.sum(e_fwd, axis=1, keepdims=True)
                csum[:, h : h + 1] = -sum_fwd
                csum[:, heads + h : heads + h + 1] = sum_all - sum_fwd
            dx = mm(
                jnp.concatenate(
                    [jnp.concatenate(w_f, axis=1), jnp.concatenate(w_b, axis=1)], axis=0
                ),
                pair_tiles(g_pair),
            )
            edge_pf = wide[rows, lanes]
            edge_pb = wide[rows, lanes_b]
            inter_f = edge_pf * in_f[:, lanes]
            inter_b = edge_pb * in_b[:, lanes]
            dx_f = dx[:CHUNK] + inter_f
            dx_b = dx[CHUNK:] + inter_b
            xf = xf_pair.astype(F32)
            xb = xb_pair.astype(F32)
            xs[:, lanes] = (xf * edge_pf).astype(BF16)
            xs[:, lanes_b] = (xb * edge_pb).astype(BF16)
            act_p = act[rows, lanes]
            stack[0:CHUNK, lanes] = (act_p * dx_f).astype(BF16)
            stack[0:CHUNK, lanes_b] = (act_p * dx_b).astype(BF16)
            stack[CHUNK : 2 * CHUNK, lanes] = (xf * inter_f).astype(BF16)
            stack[CHUNK : 2 * CHUNK, lanes_b] = (xb * inter_b).astype(BF16)
            d_inner = (
                skip[:, lanes] * g_pair.astype(F32)
                + wide[rows_dt, lanes] * dx_f
                + wide[rows_dt, lanes_b] * dx_b
            )
            ext[rows, lanes] = d_inner * slope[rows, lanes].astype(F32)
        low_f = jnp.where(later, d_scores, 0.0).astype(BF16)
        low_b = jnp.where(earlier, d_scores, 0.0).astype(BF16)
        d_bf = mm(low_f, c_f) + mm_nt(xs[:, :width], grad_f_low)
        d_cf = mm_tn(low_f, b_f) + dc[rows, 0:n]
        d_bb = mm(low_b, c_b) + mm_nt(xs[:, width:], grad_b_low)
        d_cb = mm_tn(low_b, b_b) + dc[rows, n : 2 * n]
        d_state = jnp.concatenate([d_bf, d_cf, d_bb, d_cb], axis=1)
        ext[rows, width:] = d_state * slope[rows, width:].astype(F32)
        head_sums = mm(stack[...], gather[...])
        rin = row_in[rows, :]
        ahead = head_sums[CHUNK : 2 * CHUNK]
        rates_ref[rows, 0:LANES] = (
            jnp.transpose(rsum[...]) + csum[...] + jnp.where(is_fwd, rin, ahead)
        )
        rates_ref[rows, LANES : 2 * LANES] = jnp.where(is_fwd, ahead, rin)
        rates_ref[rows, 2 * LANES : 3 * LANES] = head_sums[0:CHUNK] * mask[rows]
        edge = head_sums[2 * CHUNK : 2 * CHUNK + 1] + head_sums[2 * CHUNK + 8 : 2 * CHUNK + 9]
        rates_ref[rows, 3 * LANES :] = jnp.broadcast_to(edge, (CHUNK, LANES))

    prev = pre[...].astype(F32)
    whole_ext = ext[...]
    moved = whole_ext[:block]
    acc = conv[3:4, :] * moved
    gconv_ref[4:5, :] += jnp.sum(moved, axis=0, keepdims=True)
    gconv_ref[3:4, :] += jnp.sum(moved * prev, axis=0, keepdims=True)
    for j in range(3):
        moved = pltpu.roll(whole_ext, block + 8 - (3 - j), 0)[:block]
        acc = acc + conv[j : j + 1, :] * moved
        gconv_ref[j : j + 1, :] += jnp.sum(moved * prev, axis=0, keepdims=True)
    rest_ref[...] = acc.astype(BF16)
    rd = jnp.sum(acc * prev, axis=1, keepdims=True)
    rd_ref[...] = to_row(rd, jnp.zeros_like(rd))
    ext[block:, :] = ext[0:8, :]
    ext_out[...] = ext[0:8, :]


def rates_kernel(i, scalars, rates, hs, rd_a, rd_b, head_par, dz_ref, ghead_ref, rd_ref, *, heads, block):
    @pl.when(i == 0)
    def _():
        ghead_ref[...] = jnp.zeros_like(ghead_ref)

    r = lax.broadcasted_iota(jnp.int32, (CHUNK, CHUNK), 0)
    c = lax.broadcasted_iota(jnp.int32, (CHUNK, CHUNK), 1)
    tri = jnp.where(c <= r, 1.0, 0.0).astype(BF16)
    is_fwd = lax.broadcasted_iota(jnp.int32, (CHUNK, LANES), 1) < heads
    neg = head_par[1:2, :]
    for c_idx in range(block // CHUNK):
        rows = slice(c_idx * CHUNK, (c_idx + 1) * CHUNK)
        d_cum = rates[rows, 0:LANES]
        d_run = rates[rows, LANES : 2 * LANES]
        sums = mm(tri, jnp.concatenate([*split_three(d_cum), *split_two(d_run)], axis=1))
        ahead = sums[:, 0:LANES] + sums[:, LANES : 2 * LANES] + sums[:, 2 * LANES : 3 * LANES]
        run = sums[:, 3 * LANES : 4 * LANES] + sums[:, 4 * LANES :]
        behind = ahead[CHUNK - 1 :, :] - ahead
        d_rate = jnp.where(is_fwd, behind + d_cum + run - d_run, behind + run)
        d_rate = d_rate + rates[rows, 3 * LANES :]
        z = hs[rows, 0:LANES]
        d_step = neg * d_rate + rates[rows, 2 * LANES : 3 * LANES]
        d_z = d_step / (1.0 + jnp.exp(-z))
        dt = hs[rows, LANES : 2 * LANES]
        ghead_ref[0:1, :] += jnp.sum(d_rate * (neg * dt), axis=0, keepdims=True)
        ghead_ref[1:2, :] += jnp.sum(d_z, axis=0, keepdims=True)
        dz_ref[rows, :] = d_z.astype(BF16)
        rd = jnp.sum(d_z * (z - head_par[0:1, :]), axis=1, keepdims=True)
        rd_ref[:, rows] = rd_a[:, rows] + rd_b[:, rows] + to_row(rd, jnp.zeros_like(rd))


def columns_of(scalars, other, size):
    rank = scalars[1]
    return pl.ds(pl.multiple_of((1 - rank if other else rank) * size, LANES), size)


def branch_kernel(scalars, gz, po, out_ref, *, other):
    cols = columns_of(scalars, other, out_ref.shape[1])
    out_ref[...] = mm(gz[...], po[:, cols]).astype(out_ref.dtype)


def back_project_kernel(
    scalars, dgp, rest, dz, rd, w_gate, w_inner, w_state, w_step, out_ref, *, other
):
    rows, size = dgp.shape[0], out_ref.shape[1]
    at = columns_of(scalars, other, size)
    a = w_inner.shape[1]
    out_ref[0:rows, :] = (
        mm_nt(dgp[...], w_gate[at, :])
        + mm_nt(rest[:, 0:a], w_inner[at, :])
        + mm_nt(rest[:, a:], w_state[at, :])
        + mm_nt(dz[...], w_step[at, :])
    ).astype(out_ref.dtype)
    if other:
        part = rows // 4
        lines = jnp.concatenate([rd[0:1, k * part : (k + 1) * part] for k in range(4)], axis=0)
        lines = jnp.concatenate(split_three(lines) + (jnp.zeros((4, part), BF16),), axis=0)
        out_ref[rows : rows + 16, 0:part] = lines
        out_ref[rows : rows + 16, part:] = jnp.zeros((16, size - part), BF16)


def home_of(r, me, order):
    j = me % SHARDS
    levels = len(order)
    for p, bit in enumerate(order):
        if (r >> (levels - 1 - p)) & 1:
            j = jnp.bitwise_xor(j, 1 << bit)
    return j


def lanes_in(orders, width):
    size = width // len(orders)
    return [
        (r, slice(k * size, (k + 1) * size), order) for k, order in enumerate(orders) for r in range(SHARDS)
    ]


def pack_early_kernel(
    scalars, grad_out, grad_gate, w_gate, keep_ref, send_ref, gain_ref, *, order
):
    hi, lo = split_two(grad_gate[...].astype(F32) * w_gate[...].astype(F32))
    ones = jnp.ones((8, hi.shape[1]), BF16)
    gain_ref[...] = mm_nt(ones, hi) + mm_nt(ones, lo)
    part = grad_out.shape[0] // SHARDS
    for r in range(SHARDS):
        j = home_of(r, scalars[2], order)
        out = keep_ref if r < SHARDS // 2 else send_ref
        at = (r % (SHARDS // 2)) * 2 * part
        src = pl.ds(pl.multiple_of(j * part, part), part)
        out[at : at + part, :] = grad_out[src, :]
        out[at + part : at + 2 * part, :] = grad_gate[src, :]


def unpack_early_kernel(scalars, first, second, out_ref, gate_ref, *, order):
    part = out_ref.shape[0] // SHARDS
    for r in range(SHARDS):
        j = home_of(r, scalars[2], order)
        src = first if r < SHARDS // 2 else second
        at = (r % (SHARDS // 2)) * 2 * part
        dst = pl.ds(pl.multiple_of(j * part, part), part)
        out_ref[dst, :] = src[at : at + part, :].astype(F32)
        gate_ref[dst, :] = src[at + part : at + 2 * part, :].astype(F32)


def pack_late_kernel(
    scalars, inner, state, step_low, w_inner, w_state_t, gain, gain_part, gconv, ghead, small, gather,
    keep_ref, send_ref, misc, *, orders, heads, state_width,
):
    model, width = w_inner.shape
    hi, lo = split_two(inner[...].astype(F32) * w_inner[...].astype(F32))
    ones = jnp.ones((8, hi.shape[1]), BF16)
    gain_row = (mm_nt(ones, hi) + mm_nt(ones, lo) + gain_part[...])[0:1]
    step = step_low[...].astype(F32)
    w_t = w_state_t[...].astype(F32)
    gain_row += jnp.sum(state[...].astype(F32) * w_t[:state_width], axis=0, keepdims=True)
    gain_row += jnp.sum(step * w_t[state_width:], axis=0, keepdims=True)
    gain_row = gain_row / gain[...]
    misc[...] = jnp.zeros_like(misc)

    def put_single(k, row):
        at = (k // 2) * 8 + k % 2
        misc[at : at + 1, :] = row

    for k in range(2 * heads):
        put_single(k, step[k : k + 1, :])
    at = 2 * heads
    for k in range(5):
        put_single(at + k, gconv[k : k + 1, 0:width])
    put_single(at + 5, small[0:1, :])
    hi, lo = split_two(eight(small[1:2, :]))
    skip = mm(hi, gather[0:width, :]) + mm(lo, gather[0:width, :])
    at = ((at + 6) // 2) * 8 + (at + 6) % 2
    misc[at : at + 1, 2 * LANES : 3 * LANES] = skip[0:1]
    misc[at : at + 1, 0:LANES] = ghead[0:1, :]
    misc[at : at + 1, LANES : 2 * LANES] = ghead[1:2, :]
    fit = model // state_width
    for k in range(5):
        at = (k // fit) * 8 + 4
        lanes = slice((k % fit) * state_width, (k % fit + 1) * state_width)
        misc[at : at + 1, lanes] = gconv[k : k + 1, width:]
    at = (-(-5 // fit)) * 8 + 4
    misc[at : at + 1, :] = gain_row
    part = model // SHARDS
    part_s = state_width // SHARDS
    rows = part + part_s + 8
    for r, cols, order in lanes_in(orders, model):
        j = home_of(r, scalars[2], order)
        out = keep_ref if r < SHARDS // 2 else send_ref
        at = (r % (SHARDS // 2)) * rows
        out[at : at + part, cols] = inner[pl.ds(pl.multiple_of(j * part, part), part), cols]
        out[at + part : at + part + part_s, cols] = state[
            pl.ds(pl.multiple_of(j * part_s, part_s), part_s), cols
        ]
        out[at + part + part_s : at + rows, cols] = misc[
            pl.ds(pl.multiple_of(j * 8, 8), 8), cols
        ].astype(BF16)


def unpack_late_kernel(
    scalars, first, second, inner_ref, state_ref, step_ref, convi_ref, convi_b_ref, convs_ref, convs_b_ref,
    gg_ref, bias_ref, decay_ref, skip_ref, gain_ref, state, misc, *, orders, heads,
):
    model = inner_ref.shape[0]
    state_width = state_ref.shape[1]
    part = model // SHARDS
    part_s = state_width // SHARDS
    rows = part + part_s + 8
    for r, cols, order in lanes_in(orders, model):
        j = home_of(r, scalars[2], order)
        src = first if r < SHARDS // 2 else second
        at = (r % (SHARDS // 2)) * rows
        inner_ref[pl.ds(pl.multiple_of(j * part, part), part), cols] = src[at : at + part, cols].astype(
            F32
        )
        state[pl.ds(pl.multiple_of(j * part_s, part_s), part_s), cols] = src[
            at + part : at + part + part_s, cols
        ].astype(F32)
        misc[pl.ds(pl.multiple_of(j * 8, 8), 8), cols] = src[at + part + part_s : at + rows, cols].astype(
            F32
        )
    state_ref[...] = jnp.transpose(state[...])

    def single(k):
        at = (k // 2) * 8 + k % 2
        return misc[at : at + 1, :]

    for h in range(heads):
        for d in range(2):
            step_ref[h, d : d + 1, :] = single(d * heads + h)
    at = 2 * heads
    for k in range(4):
        convi_ref[k : k + 1, :] = single(at + k)
    convi_b_ref[...] = single(at + 4).reshape(convi_b_ref.shape)
    gg_ref[...] = single(at + 5).reshape(gg_ref.shape)
    head_row = single(at + 6)
    for d in range(2):
        decay_ref[d : d + 1, :] = head_row[:, d * heads : (d + 1) * heads]
        bias_ref[d : d + 1, :] = head_row[:, LANES + d * heads : LANES + (d + 1) * heads]
    skip_ref[...] = head_row[:, 2 * LANES : 2 * LANES + heads]
    fit = model // state_width
    for k in range(5):
        at = (k // fit) * 8 + 4
        lanes = slice((k % fit) * state_width, (k % fit + 1) * state_width)
        out, row = (convs_ref, k) if k < 4 else (convs_b_ref, 0)
        out[row : row + 1, :] = misc[at : at + 1, lanes]
    at = (-(-5 // fit)) * 8 + 4
    half = model // 2
    gain_ref[...] = jnp.where(
        scalars[1] == 0, misc[at : at + 1, :half], misc[at : at + 1, half:]
    ).reshape(gain_ref.shape)


def place(i, top):
    return i if top is None else top - i


def rows_of(block, top=None):
    return lambda ref, i: ref.at[pl.ds(pl.multiple_of(place(i, top) * block, block), block)]


def lanes_of(block, top=None):
    return lambda ref, i: ref.at[:, pl.ds(pl.multiple_of(place(i, top) * block, block), block)]


def states_of(block, top=None):
    per = block // CHUNK
    return lambda ref, i: ref.at[pl.ds(place(i, top) * per, per)]


def fixed(ref, i):
    return ref


def call(kernel, blocks, ins, out_views, out_shape, scratch, name, aliases=None, us=0.0):
    views = [view for _, view in ins[1:]] + out_views
    arrays = [ins[0]] + [
        pltpu.with_memory_space_constraint(x, pltpu.VMEM) if view is not fixed else x
        for x, view in ins[1:]
    ]

    def looped(scalars, *refs):
        def step(i, _):
            blocks_of = [view(ref, i) for view, ref in zip(views, refs)]
            kernel(i, scalars, *blocks_of, *refs[len(views) :])
            return 0

        lax.fori_loop(0, blocks, step, 0)

    vmem = pl.BlockSpec(memory_space=pltpu.VMEM)
    return pl.pallas_call(
        looped,
        out_shape=[pltpu.VMEM(o.shape, o.dtype) for o in out_shape],
        in_specs=[pl.BlockSpec(memory_space=pltpu.SMEM)] + [vmem] * (len(arrays) - 1),
        out_specs=[vmem] * len(out_shape),
        scratch_shapes=scratch,
        compiler_params=pltpu.CompilerParams(vmem_limit_bytes=VMEM_LIMIT),
        cost_estimate=pl.CostEstimate(
            flops=int(us * 5e8), transcendentals=0, bytes_accessed=int(us * 3e6)
        ),
        name=name,
        input_output_aliases=aliases or {},
    )(*arrays)


def whole(kernel, args, out_shape, scratch, name, in_vmem=True, us=0.0):
    vmem = pl.BlockSpec(memory_space=pltpu.VMEM)
    return pl.pallas_call(
        kernel,
        out_shape=[pltpu.VMEM(o.shape, o.dtype) if in_vmem else o for o in out_shape],
        in_specs=[pl.BlockSpec(memory_space=pltpu.SMEM)] + [vmem] * (len(args) - 1),
        out_specs=[vmem] * len(out_shape),
        scratch_shapes=scratch,
        compiler_params=pltpu.CompilerParams(vmem_limit_bytes=VMEM_LIMIT),
        cost_estimate=pl.CostEstimate(
            flops=int(us * 5e8), transcendentals=0, bytes_accessed=int(us * 3e6)
        ),
        name=name,
    )(*args)


def swap_mp(x):
    return lax.ppermute(x, "mp", [(0, 1), (1, 0)])


def swap_dp(x, bit):
    size = lax.axis_size("dp")
    return lax.ppermute(x, "dp", [(i, i ^ (1 << bit)) for i in range(size)])


def add_low(a, b):
    return (a.astype(F32) + b.astype(F32)).astype(BF16)


def after(x, *others):
    return lax.optimization_barrier((x, *others))[0]


def body(
    tokens,
    norm_gain,
    proj_gate,
    proj_inner,
    proj_state,
    proj_step,
    conv_inner,
    conv_inner_bias,
    conv_state,
    conv_state_bias,
    step_bias,
    decay_log,
    skip_gain,
    gate_gain,
    proj_out,
    lengths,
    cotangent,
):
    rows, width_own = tokens.shape
    model = 2 * width_own
    heads = skip_gain.shape[0]
    width = proj_inner.shape[1]
    head_dim = width // heads
    state_width = proj_state.shape[1]
    n = state_width // 4
    conv_width = width + state_width
    inner_width = width * lax.axis_size("mp")
    chunks = rows // CHUNK
    rank = lax.axis_index("mp")
    shape = jax.ShapeDtypeStruct

    oth_tokens = swap_mp(tokens)
    oth_gain = swap_mp(norm_gain.reshape(1, width_own))
    oth_cot = swap_mp(after(cotangent, oth_tokens))

    scalars = jnp.stack([lengths[0], rank, lax.axis_index("dp")]).astype(jnp.int32)
    step_weight = proj_step.reshape(model, 2 * heads)
    step_weight = jnp.pad(step_weight, ((0, 0), (0, LANES - 2 * heads)))
    own_gain = norm_gain.reshape(1, width_own)
    gain = natural(rank, own_gain, oth_gain).astype(F32)
    conv = jnp.concatenate(
        [
            jnp.concatenate([conv_inner, conv_state], axis=1),
            jnp.concatenate([conv_inner_bias, conv_state_bias])[None],
            jnp.zeros((3, conv_width), F32),
        ]
    )
    head_par = jnp.stack(
        [
            step_bias.reshape(-1),
            -jnp.exp(decay_log.reshape(-1)),
            jnp.pad(skip_gain, (0, heads)),
        ]
    )
    head_par = jnp.pad(head_par, ((0, 5), (0, LANES - 2 * heads)))
    staged = (tokens, cotangent, proj_gate, proj_inner, proj_state, proj_out)
    hbm = pl.BlockSpec(memory_space=pl.ANY)
    vmem = pl.BlockSpec(memory_space=pltpu.VMEM)
    tokens_v, cot_v, gate_v, inner_v, state_v, out_v, spread, gather, w_state_t = pl.pallas_call(
        partial(stage_kernel, count=len(staged), head_dim=head_dim),
        out_shape=[pltpu.VMEM(x.shape, x.dtype) for x in staged]
        + [
            pltpu.VMEM((2 * LANES, 2 * width), BF16),
            pltpu.VMEM((2 * width, LANES), BF16),
            pltpu.VMEM((state_width + LANES, model), BF16),
        ],
        in_specs=[vmem, vmem] + [hbm] * len(staged),
        out_specs=[vmem] * (len(staged) + 3),
        scratch_shapes=[pltpu.SemaphoreType.DMA((len(staged),))],
        compiler_params=pltpu.CompilerParams(vmem_limit_bytes=VMEM_LIMIT),
        name="stage",
    )(proj_state, step_weight, *staged)
    gg = gate_gain[None]

    sizes = dict(heads=heads, width=width, state_width=state_width)
    low = lambda *dims: shape(dims, BF16)
    full = lambda *dims: shape(dims, F32)
    block = PROJECT_BLOCK
    up, states = rows_of(block), states_of(block)
    normed, gate_pre, pre, slope, hs, act, sact, xd, hf, sb = call(
        partial(project_kernel, block=block, **sizes),
        rows // block,
        [
            scalars,
            (tokens_v, up),
            (oth_tokens, up),
            (gain, fixed),
            (gate_v, fixed),
            (inner_v, fixed),
            (state_v, fixed),
            (step_weight, fixed),
            (conv, fixed),
            (head_par, fixed),
            (spread, fixed),
        ],
        [up, up, up, up, up, up, up, up, states, states],
        [
            low(rows, model),
            full(rows, width),
            low(rows, conv_width),
            low(rows, conv_width),
            full(rows, 4 * LANES),
            full(rows, width),
            low(rows, state_width),
            low(rows, 2 * width),
            low(chunks, n, width),
            full(chunks, n, width),
        ],
        [pltpu.VMEM((block + 8, conv_width), F32), pltpu.VMEM((n, width), F32)],
        "project",
        us=12,
    )

    block = MIX_BLOCK
    top = rows // block - 1
    down, states_down = rows_of(block, top), states_of(block, top)
    y, hb = call(
        partial(mix_kernel, block=block, **sizes),
        rows // block,
        [
            scalars,
            (act, down),
            (sact, down),
            (hs, down),
            (xd, down),
            (hf, states_down),
            (sb, states_down),
            (head_par, fixed),
            (spread, fixed),
        ],
        [down, states_down],
        [full(rows, width), low(chunks, n, width)],
        [pltpu.VMEM((n, width), F32)],
        "mix",
        us=7,
    )

    block = GATE_BLOCK
    up, states, up_lanes = rows_of(block), states_of(block), lanes_of(block)
    dgn, gz, sums = call(
        partial(gate_kernel, block=block),
        rows // block,
        [
            scalars,
            (y, up),
            (gate_pre, up),
            (cot_v, up),
            (oth_cot, up),
            (out_v, fixed),
            (gg, fixed),
        ],
        [up, up, up_lanes],
        [full(rows, width), low(rows, width), full(8, rows)],
        [],
        "gate",
        us=3,
    )

    oth_sums = swap_mp(sums)
    branch_oth = whole(
        partial(branch_kernel, other=True), (scalars, gz, out_v), [low(rows, width_own)], [], "branch_oth", us=3
    )[0]
    sums = sums + oth_sums
    branch_got = swap_mp(after(branch_oth, sums))
    sums_in = after(sums, branch_oth)

    block = GATE_BACK_BLOCK
    up, states, up_lanes = rows_of(block), states_of(block), lanes_of(block)
    g, dgp, dbr, dc, gb, gf, rd_gate, row_sums, small = call(
        partial(gate_back_kernel, block=block, inner_width=inner_width, **sizes),
        rows // block,
        [
            scalars,
            (sums_in, up_lanes),
            (gate_pre, up),
            (y, up),
            (act, up),
            (dgn, up),
            (cot_v, up),
            (oth_cot, up),
            (hs, up),
            (sact, up),
            (hf, states),
            (hb, states),
            (gg, fixed),
            (spread, fixed),
            (gather, fixed),
        ],
        [up, up, up, up, states, states, up_lanes, up, fixed],
        [
            low(rows, width),
            low(rows, width),
            low(rows, model),
            full(rows, 2 * n),
            low(chunks, n, width),
            full(chunks, n, width),
            full(8, rows),
            full(rows, LANES),
            full(8, width),
        ],
        [pltpu.VMEM((n, width), F32), pltpu.VMEM((block, 2 * width), BF16)],
        "gate_back",
        us=8,
    )

    def back_part(first, count, g, state):
        block = BACK_BLOCK
        here, states_here, here_lanes = rows_of(block, first), states_of(block, first), lanes_of(block, first)
        ins = [
            scalars,
            (g, here),
            (act, here),
            (sact, here),
            (hs, here),
            (xd, here),
            (row_sums, here),
            (hf, states_here),
            (hb, states_here),
            (gb, states_here),
            (gf, states_here),
            (dc, here),
            (pre, here),
            (slope, here),
            (conv, fixed),
            (head_par, fixed),
            (spread, fixed),
            (gather, fixed),
            *[(x, fixed) for x in state[:3]],
            (state[3], here),
            (state[4], here),
            (state[5], here_lanes),
        ]
        return call(
            partial(back_kernel, block=block, top=first, **sizes),
            count,
            ins,
            [here, here, here_lanes, fixed, fixed, fixed],
            [
                low(rows, conv_width),
                full(rows, 4 * LANES),
                full(8, rows),
                full(8, conv_width),
                full(8, conv_width),
                full(n, width),
            ],
            [
                pltpu.VMEM((block + 8, conv_width), F32),
                pltpu.VMEM((2 * CHUNK + 16, 2 * width), BF16),
                pltpu.VMEM((CHUNK, 2 * width), BF16),
                pltpu.VMEM((LANES, CHUNK), F32),
                pltpu.VMEM((CHUNK, LANES), F32),
            ],
            "mix_back",
            us=3 * count,
            aliases={len(ins) - 3: 0, len(ins) - 2: 1, len(ins) - 1: 2},
        )

    order_a, orders_b = (0, 1, 2, 3), ((0, 1, 2, 3), (0, 2, 1, 3))
    grad_out = mm_tn(gz, dbr).astype(BF16)
    grad_gate = mm_tn(normed, dgp).astype(BF16)
    keep, send, gain_part = whole(
        partial(pack_early_kernel, order=order_a),
        (scalars, grad_out, grad_gate, proj_gate),
        [low(width, model), low(width, model), full(8, model)],
        [],
        "pack_early",
    )

    def rest_of_dp(x):
        extra = SHARDS
        while extra < lax.axis_size("dp"):
            x = add_low(x, swap_dp(x, extra.bit_length() - 1))
            extra *= 2
        return x

    zeros = (
        jnp.zeros((8, conv_width), F32),
        jnp.zeros((n, width), F32),
        jnp.zeros((8, conv_width), F32),
    )
    branch_own = whole(
        partial(branch_kernel, other=False), (scalars, after(gz, send), out_v), [full(rows, width_own)], [],
        "branch_own"
    )[0]
    got, branch_own = lax.optimization_barrier((swap_dp(send, order_a[0]), branch_own))
    h = keep.shape[0] // 2
    keep, send = add_low(keep[:h], got[:h]), add_low(keep[h:], got[h:])
    state = (
        *zeros,
        jnp.zeros((rows, conv_width), BF16),
        jnp.zeros((rows, 4 * LANES), F32),
        jnp.zeros((8, rows), F32),
    )
    g = after(g, send)
    sent, x = swap_dp(send, order_a[1]), None
    left = rows // BACK_BLOCK
    for k, share in enumerate((2, 4, 4)):
        count = rows // BACK_BLOCK // share
        outs = back_part(left - 1, count, g, state)
        left -= count
        rest, rates, rd_rest, gconv, ext_carry, carry = outs
        h = keep.shape[0] // 2
        if k < 2:
            sent, carry = lax.optimization_barrier((sent, carry))
            if k == 1:
                carry, branch_got = lax.optimization_barrier((carry, branch_got))
            keep, send = add_low(keep[:h], sent[:h]), add_low(keep[h:], sent[h:])
            carry = after(carry, send)
            sent = swap_dp(send, order_a[k + 2])
        else:
            sent, rest = lax.optimization_barrier((sent, rest))
            x = rest_of_dp(add_low(keep, sent))
        state = (ext_carry, carry, gconv, rest, rates, rd_rest)

    block = RATES_BLOCK
    rates, x, rest = lax.optimization_barrier((rates, x, rest))
    sent = swap_dp(x, order_a[3])
    dz, ghead, rd_part = call(
        partial(rates_kernel, heads=heads, block=block),
        rows // block,
        [
            scalars,
            (rates, rows_of(block)),
            (hs, rows_of(block)),
            (rd_gate, lanes_of(block)),
            (rd_rest, lanes_of(block)),
            (head_par, fixed),
        ],
        [rows_of(block), fixed, lanes_of(block)],
        [low(rows, LANES), full(8, LANES), full(8, rows)],
        [],
        "rates",
    )
    grad_inner = mm_tn(normed, rest[:, :width]).astype(BF16)
    grad_state = mm_tn(rest[:, width:], normed).astype(BF16)
    grad_step = mm_tn(dz, normed).astype(BF16)
    keep, send = whole(
        partial(pack_late_kernel, orders=orders_b, heads=heads, state_width=state_width),
        (
            scalars, grad_inner, grad_state, grad_step, inner_v, w_state_t, gain, gain_part, gconv, ghead,
            small, gather,
        ),
        [low(LATE_ROWS * SHARDS // 2, model), low(LATE_ROWS * SHARDS // 2, model)],
        [pltpu.VMEM((8 * SHARDS, model), F32)],
        "pack_late",
    )

    back_args = (scalars, dgp, rest, dz, rd_part, gate_v, inner_v, state_v, step_weight)
    dn_oth = whole(
        partial(back_project_kernel, other=True), back_args, [low(rows + 16, width_own)], [], "back_oth"
    )[0]
    x = jnp.concatenate([x, sent])
    send, x, dn_oth = lax.optimization_barrier((send, x, dn_oth))
    got = swap_dp(send, 0)
    sent = swap_dp(x, order_a[2])
    h, c = keep.shape[0] // 2, model // 2
    keeps = [add_low(keep[:h, :c], got[:h, :c]), add_low(keep[:h, c:], got[:h, c:])]
    sends = [add_low(keep[h:, :c], got[h:, :c]), add_low(keep[h:, c:], got[h:, c:])]
    sends[0], sends[1], rest = lax.optimization_barrier((sends[0], sends[1], rest))
    dn_got = swap_mp(dn_oth)

    dn_own = whole(
        partial(back_project_kernel, other=False), (*back_args[:2], rest, *back_args[3:]),
        [full(rows, width_own)], [], "back_own"
    )[0]
    for level in (1, 2):
        gots = [swap_dp(v, order[level]) for v, order in zip(sends, orders_b)]
        if level == 1:
            gots[0], gots[1], dn_own, sent = lax.optimization_barrier((gots[0], gots[1], dn_own, sent))
            x = jnp.concatenate([x, sent])
        h = keeps[0].shape[0] // 2
        pairs = list(zip(keeps, gots))
        if level == 1:
            keeps = [add_low(k[:h], v[:h]) for k, v in pairs]
            sends = [add_low(k[h:], v[h:]) for k, v in pairs]
        else:
            keep = jnp.concatenate([add_low(k[:h], v[:h]) for k, v in pairs], axis=1)
            send = jnp.concatenate([add_low(k[h:], v[h:]) for k, v in pairs], axis=1)
    send, x, tokens_late, oth_late = lax.optimization_barrier((send, x, tokens, oth_tokens))
    sent = swap_dp(x, order_a[1])

    seq_mask = (jnp.arange(rows) < lengths[0]).astype(F32)[:, None]
    gate_inv = lax.rsqrt(sums[0] / inner_width + EPSILON)[:, None]
    tokens_f = tokens_late.astype(F32)
    block_out = (tokens_f + seq_mask * gate_inv * (branch_own + branch_got.astype(F32))).astype(BF16)

    got, block_out, dn_got = lax.optimization_barrier((swap_dp(send, 3), block_out, dn_got))
    z = rest_of_dp(add_low(keep, got))
    part = model // SHARDS
    tail = z[part:]
    tail_row = lax.broadcasted_iota(jnp.int32, (LATE_ROWS - part, 1), 0)
    alone = (tail_row >= LATE_ROWS - part - 8) & (tail_row < LATE_ROWS - part - 4)
    tail_f = tail.astype(F32)
    tail = jnp.where(alone, tail_f, tail_f + swap_mp(tail).astype(F32)).astype(BF16)
    z = jnp.concatenate([z[:part], tail])
    oth_f = oth_late.astype(F32)
    square = jnp.sum(tokens_f * tokens_f, axis=1, keepdims=True) + jnp.sum(
        oth_f * oth_f, axis=1, keepdims=True
    )
    inv = lax.rsqrt(square / model + EPSILON)
    part = rows // 4
    lines = dn_got[rows:, :part].astype(F32)
    oth_rd = (lines[0:4] + lines[4:8] + lines[8:12]).reshape(rows)
    rd_both = rd_part[0] + oth_rd
    grad_full = dn_own + dn_got[:rows].astype(F32)
    grad_tokens = (
        cotangent.astype(F32)
        + inv * (grad_full * norm_gain.astype(F32)[None])
        - tokens_f * (inv * inv * (rd_both[:, None] / model))
    )

    got, grad_tokens, sent = lax.optimization_barrier((swap_dp(z, 3), grad_tokens, sent))
    x = jnp.concatenate([x, sent])
    sent = swap_dp(x, order_a[0])
    z = jnp.concatenate([z, got])
    zs = [z[:, :c], z[:, c:]]
    gots = [swap_dp(v, order[2]) for v, order in zip(zs, orders_b)]
    zs = [jnp.concatenate([v, g]) for v, g in zip(zs, gots)]
    grad_proj_out, grad_proj_gate = whole(
        partial(unpack_early_kernel, order=order_a),
        (scalars, x, after(sent, *zs)),
        [full(width, model), full(model, width)],
        [],
        "unpack_early",
        in_vmem=False,
    )
    gots = [swap_dp(v, order[1]) for v, order in zip(zs, orders_b)]
    gots[0], gots[1], grad_proj_out = lax.optimization_barrier((gots[0], gots[1], grad_proj_out))
    z = jnp.concatenate([jnp.concatenate([v, g]) for v, g in zip(zs, gots)], axis=1)
    (
        grad_proj_inner,
        grad_proj_state,
        step,
        grad_conv_inner,
        grad_conv_inner_bias,
        grad_conv_state,
        grad_conv_state_bias,
        grad_gate_gain,
        grad_step_bias,
        grad_decay_log,
        grad_skip,
        grad_norm_gain,
    ) = whole(
        partial(unpack_late_kernel, orders=orders_b, heads=heads),
        (scalars, z, swap_dp(z, 0)),
        [
            full(model, width),
            full(model, state_width),
            full(heads, 2, model),
            full(4, width),
            full(width),
            full(4, state_width),
            full(1, state_width),
            full(width),
            full(2, heads),
            full(2, heads),
            full(1, heads),
            full(width_own),
        ],
        [pltpu.VMEM((state_width, model), F32), pltpu.VMEM((8 * SHARDS, model), F32)],
        "unpack_late",
        in_vmem=False,
    )
    return (
        block_out,
        grad_tokens,
        grad_norm_gain,
        grad_proj_gate,
        grad_proj_inner,
        grad_proj_state,
        step.transpose(2, 1, 0),
        grad_conv_inner,
        grad_conv_inner_bias,
        grad_conv_state,
        grad_conv_state_bias[0],
        grad_step_bias,
        grad_decay_log,
        grad_skip[0],
        grad_gate_gain,
        grad_proj_out,
    )


def solution(mesh):
    in_specs = (
        P("dp", "mp"),
        P("mp"),
        P(None, "mp"),
        P(None, "mp"),
        P(),
        P(None, None, "mp"),
        P(None, "mp"),
        P("mp"),
        P(),
        P(),
        P(None, "mp"),
        P(None, "mp"),
        P("mp"),
        P("mp"),
        P("mp", None),
        P("dp"),
        P("dp", "mp"),
    )
    out_specs = (
        P("dp", "mp"),
        P("dp", "mp"),
        P("mp"),
        P(None, "mp"),
        P(None, "mp"),
        P(),
        P(None, None, "mp"),
        P(None, "mp"),
        P("mp"),
        P(),
        P(),
        P(None, "mp"),
        P(None, "mp"),
        P("mp"),
        P("mp"),
        P("mp", None),
    )
    return jax.shard_map(body, mesh=mesh, in_specs=in_specs, out_specs=out_specs, check_vma=False)
```

```python
from functools import partial

import jax
import jax.numpy as jnp
from jax import lax
from jax.experimental import pallas as pl
from jax.experimental.pallas import tpu as pltpu
from jax.sharding import PartitionSpec as P

EPSILON = 1e-05
CHUNK = 128
PROJECT_BLOCK, MIX_BLOCK, GATE_BLOCK, GATE_BACK_BLOCK, BACK_BLOCK, RATES_BLOCK = 256, 512, 512, 256, 128, 1024
LANES = 128
F32 = jnp.float32
BF16 = jnp.bfloat16
HIGHEST = lax.Precision.HIGHEST
VMEM_LIMIT = 12 * 1024 * 1024
SHARDS = 16
LOG2_E = 1.4426950408889634
LATE_ROWS = 72


def mm(a, b):
    return jnp.dot(a, b, preferred_element_type=F32)


def mm_nt(a, b):
    return lax.dot_general(a, b, (((1,), (1,)), ((), ())), preferred_element_type=F32)


def mm_tn(a, b):
    return lax.dot_general(a, b, (((0,), (0,)), ((), ())), preferred_element_type=F32)


def split_two(v):
    hi = v.astype(BF16)
    return hi, (v - hi.astype(F32)).astype(BF16)


def split_three(v):
    hi, mid = split_two(v)
    return hi, mid, (v - hi.astype(F32) - mid.astype(F32)).astype(BF16)


def expand(v, spread):
    hi, lo = split_two(v)
    return mm(jnp.concatenate([hi, lo], axis=1), spread)


def row_mask(block, rows, length):
    pos = block * rows + lax.broadcasted_iota(jnp.int32, (rows, 1), 0)
    return (pos < length).astype(F32)


def to_row(col_a, col_b):
    rows = col_a.shape[0]
    lane = lax.broadcasted_iota(jnp.int32, (rows, LANES), 1)
    tile = jnp.where(lane == 0, col_a, jnp.where(lane == 1, col_b, 0.0))
    return jnp.transpose(tile)[0:8, :]


def sigmoid(v):
    return 0.5 * jnp.tanh(0.5 * v) + 0.5


def natural(rank, own, oth):
    return jnp.where(
        rank == 0, jnp.concatenate([own, oth], axis=1), jnp.concatenate([oth, own], axis=1)
    )


def eight(row):
    return jnp.broadcast_to(row, (8, row.shape[1]))


def stage_kernel(w_state, w_step, *refs, count, head_dim):
    sources, outs, sems = refs[:count], refs[count:-1], refs[-1]
    spread, gather, w_state_t = outs[count:]
    copies = [
        pltpu.make_async_copy(src, dst, sems.at[k]) for k, (src, dst) in enumerate(zip(sources, outs))
    ]
    for copy in copies:
        copy.start()
    state_width = w_state.shape[1]
    w_state_t[:state_width, :] = jnp.transpose(w_state[...].astype(F32)).astype(BF16)
    w_state_t[state_width:, :] = jnp.transpose(w_step[...].astype(F32)).astype(BF16)
    head = lax.broadcasted_iota(jnp.int32, spread.shape, 1) // head_dim
    row = lax.broadcasted_iota(jnp.int32, spread.shape, 0) % LANES
    spread[...] = jnp.where(head == row, 1.0, 0.0).astype(BF16)
    head = lax.broadcasted_iota(jnp.int32, gather.shape, 0) // head_dim
    lane = lax.broadcasted_iota(jnp.int32, gather.shape, 1)
    gather[...] = jnp.where(head == lane, 1.0, 0.0).astype(BF16)
    for copy in copies:
        copy.wait()


def project_kernel(
    i, scalars, own, oth, gain, w_gate, w_inner, w_state, w_step, conv, head_par, spread,
    normed_ref, gate_ref, pre_ref, slope_ref, hs_ref, act_ref, sact_ref, xd_ref, hf_ref, sb_ref,
    ext, carry, *, heads, width, state_width, block,
):
    @pl.when(i == 0)
    def _():
        ext[0:8, :] = jnp.zeros((8, ext.shape[1]), F32)
        carry[...] = jnp.zeros_like(carry)

    x = natural(scalars[1], own[...], oth[...]).astype(F32)
    inv = lax.rsqrt(jnp.mean(x * x, axis=-1, keepdims=True) + EPSILON)
    normed = (x * inv * gain[...]).astype(BF16)
    normed_ref[...] = normed
    step_pre = mm(normed, w_step[...])
    z = step_pre + head_par[0:1, :]
    dt = jnp.maximum(z, 0.0) + jnp.log1p(jnp.exp(-jnp.abs(z)))
    rate = head_par[1:2, :] * dt
    dtm = dt * row_mask(i, block, scalars[0])
    hs_ref[:, 0:LANES] = z
    hs_ref[:, LANES : 2 * LANES] = dt
    tri_r = lax.broadcasted_iota(jnp.int32, (CHUNK, CHUNK), 0)
    tri_c = lax.broadcasted_iota(jnp.int32, (CHUNK, CHUNK), 1)
    tri = (tri_c <= tri_r).astype(F32)
    is_fwd = lax.broadcasted_iota(jnp.int32, (CHUNK, LANES), 1) < heads
    per = block // CHUNK
    to_spread = [dtm]
    keeps = []
    for c_idx in range(per):
        rows = slice(c_idx * CHUNK, (c_idx + 1) * CHUNK)
        rate_c = rate[rows]
        cum = jnp.dot(tri, rate_c, precision=HIGHEST, preferred_element_type=F32)
        tot = cum[CHUNK - 1 : CHUNK, :]
        cumx = jnp.where(is_fwd, cum, cum - rate_c)
        hs_ref[rows, 2 * LANES : 3 * LANES] = cumx
        hs_ref[rows, 3 * LANES :] = jnp.broadcast_to(tot, (CHUNK, LANES))
        to_spread.append(dtm[rows] * jnp.exp(jnp.where(is_fwd, tot - cumx, cumx)))
        keeps.append(eight(jnp.exp(tot)))
    wide = expand(jnp.concatenate(to_spread + keeps, axis=0), spread[...])

    ext[8 : 8 + block, 0:width] = mm(normed, w_inner[...])
    ext[8 : 8 + block, width:] = mm(normed, w_state[...])
    gate_ref[...] = mm(normed, w_gate[...])
    whole_ext = ext[...]
    pre = whole_ext[8:]
    pre_ref[...] = pre.astype(BF16)
    c = conv[4:5, :] + conv[3:4, :] * pre
    for j in range(3):
        c = c + conv[j : j + 1, :] * pltpu.roll(whole_ext, 3 - j, 0)[8:]
    sg = sigmoid(c)
    both = c * sg
    slope_ref[...] = (sg * (1.0 + c * (1.0 - sg))).astype(BF16)
    ext[0:8, :] = ext[block : block + 8, :]
    act = both[:, :width]
    act_ref[...] = act
    sact = both[:, width:].astype(BF16)
    sact_ref[...] = sact
    xd_ref[:, 0:width] = (act * wide[0:block, :width]).astype(BF16)
    xd_ref[:, width:] = (act * wide[0:block, width:]).astype(BF16)
    n = state_width // 4
    for c_idx in range(per):
        rows = slice(c_idx * CHUNK, (c_idx + 1) * CHUNK)
        coef = wide[block + c_idx * CHUNK : block + (c_idx + 1) * CHUNK]
        keep = wide[2 * block + 8 * c_idx : 2 * block + 8 * c_idx + 1, :width]
        hf_ref[c_idx] = carry[...].astype(BF16)
        carry[...] = carry[...] * keep + mm_tn(
            sact[rows, 0:n], (act[rows] * coef[:, :width]).astype(BF16)
        )
        sb_ref[c_idx] = mm_tn(
            sact[rows, 2 * n : 3 * n], (act[rows] * coef[:, width:]).astype(BF16)
        )


def pair_tiles(pair):
    lane = lax.broadcasted_iota(jnp.int32, (1, pair.shape[1]), 1)
    first = (lane < pair.shape[1] // 2).astype(F32)
    keep_a, keep_b = first.astype(BF16), (1.0 - first).astype(BF16)
    return jnp.concatenate([pair * keep_a, pair * keep_b], axis=0)


def mix_kernel(
    i, scalars, act, sact, hs, xd, hf, sb, head_par, spread, y_ref, hb_ref, carry,
    *, heads, width, state_width, block,
):
    @pl.when(i == 0)
    def _():
        carry[...] = jnp.zeros_like(carry)

    n = state_width // 4
    per = block // CHUNK
    r = lax.broadcasted_iota(jnp.int32, (CHUNK, CHUNK), 0)
    c = lax.broadcasted_iota(jnp.int32, (CHUNK, CHUNK), 1)
    lower = c < r
    upper = c > r
    is_fwd = lax.broadcasted_iota(jnp.int32, (block, LANES), 1) < heads
    cum_all = hs[:, 2 * LANES : 3 * LANES]
    tot_all = hs[:, 3 * LANES :]
    wide = expand(
        jnp.concatenate(
            [jnp.exp(jnp.where(is_fwd, cum_all, tot_all - cum_all))]
            + [jnp.exp(tot_all[k * CHUNK : k * CHUNK + 8]) for k in range(per)]
            + [eight(head_par[2:3, :])],
            axis=0,
        ),
        spread[...],
    )
    skip = wide[block + 8 * per : block + 8 * per + 1]
    for c_idx in reversed(range(per)):
        rows = slice(c_idx * CHUNK, (c_idx + 1) * CHUNK)
        cumx = cum_all[rows] * LOG2_E
        cum_t = jnp.transpose(cumx)
        sact_c = sact[rows, :]
        b_f, c_f = sact_c[:, 0:n], sact_c[:, n : 2 * n]
        b_b, c_b = sact_c[:, 2 * n : 3 * n], sact_c[:, 3 * n :]
        s_f = jnp.where(lower, mm_nt(c_f, b_f), 0.0)
        s_b = jnp.where(upper, mm_nt(c_b, b_b), 0.0)
        hb = carry[...].astype(BF16)
        hb_ref[c_idx] = hb
        in_f = mm(c_f, hf[c_idx])
        in_b = mm(c_b, hb)
        keep = wide[block + 8 * c_idx : block + 8 * c_idx + 1, width:]
        carry[...] = carry[...] * keep + sb[c_idx]
        for p in range(heads // 2):
            lanes = slice(p * LANES, (p + 1) * LANES)
            lanes_b = slice(width + p * LANES, width + (p + 1) * LANES)
            w_f, w_b = [], []
            for h in (2 * p, 2 * p + 1):
                damp = jnp.exp2(
                    jnp.minimum(
                        cumx[:, h : h + 1] - cum_t[h : h + 1, :],
                        cum_t[heads + h : heads + h + 1, :] - cumx[:, heads + h : heads + h + 1],
                    )
                )
                w_f.append((s_f * damp).astype(BF16))
                w_b.append((s_b * damp).astype(BF16))
            out = mm(
                jnp.concatenate(w_f + w_b, axis=1),
                jnp.concatenate([pair_tiles(xd[rows, lanes]), pair_tiles(xd[rows, lanes_b])], axis=0),
            )
            y_ref[rows, lanes] = (
                out
                + wide[rows, lanes] * in_f[:, lanes]
                + wide[rows, lanes_b] * in_b[:, lanes]
                + skip[:, lanes] * act[rows, lanes]
            )


def gate_kernel(i, scalars, y, gate, cown, coth, po, gg, dgn_ref, gz_ref, sums_ref, *, block):
    gp = gate[...]
    gated = y[...] * (gp * sigmoid(gp))
    mask = row_mask(i, block, scalars[0])
    cot = natural(scalars[1], cown[...], coth[...])
    dgn = mm_nt((cot.astype(F32) * mask).astype(BF16), po[...])
    dgn_ref[...] = dgn
    scaled = gated * gg[...]
    gz_ref[...] = scaled.astype(BF16)
    sums_ref[...] = to_row(
        jnp.sum(gated * gated, axis=1, keepdims=True), jnp.sum(dgn * scaled, axis=1, keepdims=True)
    )


def gate_back_kernel(
    i, scalars, sums, gate, y, act, dgn, cown, coth, hs, sact, hf, hb, gg, spread, gather,
    g_ref, dgp_ref, dbr_ref, dc_ref, gb_ref, gf_ref, rd_ref, rows_ref, small_ref, carry, prod,
    *, heads, width, state_width, block, inner_width,
):
    @pl.when(i == 0)
    def _():
        carry[...] = jnp.zeros_like(carry)
        small_ref[...] = jnp.zeros_like(small_ref)

    per = block // CHUNK
    is_fwd = lax.broadcasted_iota(jnp.int32, (block, LANES), 1) < heads
    cum_all = hs[:, 2 * LANES : 3 * LANES]
    tot_all = hs[:, 3 * LANES :]
    wide = expand(
        jnp.concatenate(
            [jnp.exp(jnp.where(is_fwd, cum_all, tot_all - cum_all))]
            + [jnp.exp(tot_all[k * CHUNK : k * CHUNK + 8]) for k in range(per)],
            axis=0,
        ),
        spread[...],
    )
    cols = jnp.transpose(sums[...])
    gate_inv = lax.rsqrt(cols[:, 0:1] / inner_width + EPSILON)
    gate_dot = cols[:, 1:2] / inner_width
    gp = gate[...]
    sg = sigmoid(gp)
    act_gate = gp * sg
    yv = y[...]
    gated = yv * act_gate
    dg = dgn[...]
    small_ref[0:1, :] += jnp.sum(dg * gated * gate_inv, axis=0, keepdims=True)
    d_gated = gate_inv * (dg * gg[...]) - gated * (gate_inv * gate_inv * gate_inv * gate_dot)
    d_gp = d_gated * yv * (sg * (1.0 + gp * (1.0 - sg)))
    dgp_ref[...] = d_gp.astype(BF16)
    rd = jnp.sum(d_gp * gp, axis=1, keepdims=True)
    rd_ref[...] = to_row(rd, jnp.zeros_like(rd))
    d_y = d_gated * act_gate
    g_ref[...] = d_y.astype(BF16)
    small_ref[1:2, :] += jnp.sum(d_y * act[...], axis=0, keepdims=True)
    mask = row_mask(i, block, scalars[0])
    cot = natural(scalars[1], cown[...], coth[...])
    dbr_ref[...] = (cot.astype(F32) * (mask * gate_inv)).astype(BF16)
    n = state_width // 4
    for c_idx in range(per):
        rows = slice(c_idx * CHUNK, (c_idx + 1) * CHUNK)
        dy_c = d_y[rows]
        dyf = dy_c * wide[rows, :width]
        dyb = dy_c * wide[rows, width:]
        prod[rows, 0:width] = (dyf * mm(sact[rows, n : 2 * n], hf[c_idx])).astype(BF16)
        prod[rows, width:] = (dyb * mm(sact[rows, 3 * n :], hb[c_idx])).astype(BF16)
        dyf = dyf.astype(BF16)
        dyb = dyb.astype(BF16)
        dc_ref[rows, 0:n] = mm_nt(dyf, hf[c_idx])
        dc_ref[rows, n : 2 * n] = mm_nt(dyb, hb[c_idx])
        gb_ref[c_idx] = carry[...].astype(BF16)
        keep = wide[block + 8 * c_idx : block + 8 * c_idx + 1, width:]
        carry[...] = carry[...] * keep + mm_tn(sact[rows, 3 * n :], dyb)
        gf_ref[c_idx] = mm_tn(sact[rows, n : 2 * n], dyf)
    rows_ref[...] = mm(prod[...], gather[...])


def back_kernel(
    i, scalars, g, act, sact, hs, xd, row_in, hf, hb, gb, gf, dc, pre, slope, conv, head_par, spread, gather,
    ext_in, carry_in, gconv_in, _rest, _rates, _rd, rest_ref, rates_ref, rd_ref, gconv_ref, ext_out,
    carry, ext, stack, xs, rsum, csum,
    *, heads, width, state_width, block, top,
):
    blk = top - i
    per = block // CHUNK

    @pl.when(i == 0)
    def _():
        ext[block:, :] = ext_in[...]
        carry[...] = carry_in[...]
        gconv_ref[...] = gconv_in[...]
        rsum[...] = jnp.zeros_like(rsum)
        csum[...] = jnp.zeros_like(csum)

    n = state_width // 4
    r = lax.broadcasted_iota(jnp.int32, (CHUNK, CHUNK), 0)
    c = lax.broadcasted_iota(jnp.int32, (CHUNK, CHUNK), 1)
    later = c > r
    earlier = c < r
    is_fwd_all = lax.broadcasted_iota(jnp.int32, (block, LANES), 1) < heads
    is_fwd = lax.broadcasted_iota(jnp.int32, (CHUNK, LANES), 1) < heads
    mask = row_mask(blk, block, scalars[0])
    cum_all = hs[:, 2 * LANES : 3 * LANES]
    tot_all = hs[:, 3 * LANES :]
    wide = expand(
        jnp.concatenate(
            [jnp.exp(jnp.where(is_fwd_all, tot_all - cum_all, cum_all)), hs[:, LANES : 2 * LANES] * mask]
            + [jnp.exp(tot_all[k * CHUNK : k * CHUNK + 8]) for k in range(per)]
            + [eight(head_par[2:3, :])],
            axis=0,
        ),
        spread[...],
    )
    skip = wide[2 * block + 8 * per : 2 * block + 8 * per + 1]
    for c_idx in reversed(range(per)):
        rows = slice(c_idx * CHUNK, (c_idx + 1) * CHUNK)
        rows_dt = slice(block + c_idx * CHUNK, block + (c_idx + 1) * CHUNK)
        cumx = cum_all[rows] * LOG2_E
        cum_t = jnp.transpose(cumx)
        sact_c = sact[rows, :]
        b_f, c_f = sact_c[:, 0:n], sact_c[:, n : 2 * n]
        b_b, c_b = sact_c[:, 2 * n : 3 * n], sact_c[:, 3 * n :]
        s_f = jnp.where(later, mm_nt(b_f, c_f), 0.0)
        s_b = jnp.where(earlier, mm_nt(b_b, c_b), 0.0)
        s_all = s_f + s_b
        grad_f = carry[...]
        grad_f_low = grad_f.astype(BF16)
        grad_b_low = gb[c_idx]
        keep = wide[2 * block + 8 * c_idx : 2 * block + 8 * c_idx + 1]
        keep_f = keep[:, :width]
        edge_f = keep_f * jnp.sum(grad_f * hf[c_idx].astype(F32), axis=0, keepdims=True)
        edge_b = keep[:, width:] * jnp.sum(
            hb[c_idx].astype(F32) * grad_b_low.astype(F32), axis=0, keepdims=True
        )
        e_hi, e_lo = split_two(eight(jnp.concatenate([edge_f, edge_b], axis=1)))
        stack[2 * CHUNK :, :] = jnp.concatenate([e_hi, e_lo], axis=0)
        carry[...] = grad_f * keep_f + gf[c_idx]
        in_f = mm(b_f, grad_f_low)
        in_b = mm(b_b, grad_b_low)
        d_scores = jnp.zeros((CHUNK, CHUNK), F32)
        for p in range(heads // 2):
            lanes = slice(p * LANES, (p + 1) * LANES)
            lanes_b = slice(width + p * LANES, width + (p + 1) * LANES)
            g_pair = g[rows, lanes]
            xf_pair = xd[rows, lanes]
            xb_pair = xd[rows, lanes_b]
            dw = mm_nt(
                jnp.concatenate([pair_tiles(xf_pair), pair_tiles(xb_pair)], axis=0), g_pair
            )
            w_f, w_b = [], []
            for q, h in enumerate((2 * p, 2 * p + 1)):
                damp = jnp.exp2(
                    jnp.minimum(
                        cum_t[h : h + 1, :] - cumx[:, h : h + 1],
                        cumx[:, heads + h : heads + h + 1] - cum_t[heads + h : heads + h + 1, :],
                    )
                )
                w_f.append((s_f * damp).astype(BF16))
                w_b.append((s_b * damp).astype(BF16))
                part = jnp.where(
                    later, dw[q * CHUNK : (q + 1) * CHUNK], dw[(2 + q) * CHUNK : (3 + q) * CHUNK]
                )
                part = part * damp
                d_scores = d_scores + part
                e_all = part * s_all
                e_fwd = jnp.where(later, e_all, 0.0)
                sum_all = jnp.sum(e_all, axis=0, keepdims=True)
                sum_fwd = jnp.sum(e_fwd, axis=0, keepdims=True)
                rsum[h : h + 1, :] = sum_fwd
                rsum[heads + h : heads + h + 1, :] = sum_fwd - sum_all
                sum_all = jnp.sum(e_all, axis=1, keepdims=True)
                sum_fwd = jnp.sum(e_fwd, axis=1, keepdims=True)
                csum[:, h : h + 1] = -sum_fwd
                csum[:, heads + h : heads + h + 1] = sum_all - sum_fwd
            dx = mm(
                jnp.concatenate(
                    [jnp.concatenate(w_f, axis=1), jnp.concatenate(w_b, axis=1)], axis=0
                ),
                pair_tiles(g_pair),
            )
            edge_pf = wide[rows, lanes]
            edge_pb = wide[rows, lanes_b]
            inter_f = edge_pf * in_f[:, lanes]
            inter_b = edge_pb * in_b[:, lanes]
            dx_f = dx[:CHUNK] + inter_f
            dx_b = dx[CHUNK:] + inter_b
            xf = xf_pair.astype(F32)
            xb = xb_pair.astype(F32)
            xs[:, lanes] = (xf * edge_pf).astype(BF16)
            xs[:, lanes_b] = (xb * edge_pb).astype(BF16)
            act_p = act[rows, lanes]
            stack[0:CHUNK, lanes] = (act_p * dx_f).astype(BF16)
            stack[0:CHUNK, lanes_b] = (act_p * dx_b).astype(BF16)
            stack[CHUNK : 2 * CHUNK, lanes] = (xf * inter_f).astype(BF16)
            stack[CHUNK : 2 * CHUNK, lanes_b] = (xb * inter_b).astype(BF16)
            d_inner = (
                skip[:, lanes] * g_pair.astype(F32)
                + wide[rows_dt, lanes] * dx_f
                + wide[rows_dt, lanes_b] * dx_b
            )
            ext[rows, lanes] = d_inner * slope[rows, lanes].astype(F32)
        low_f = jnp.where(later, d_scores, 0.0).astype(BF16)
        low_b = jnp.where(earlier, d_scores, 0.0).astype(BF16)
        d_bf = mm(low_f, c_f) + mm_nt(xs[:, :width], grad_f_low)
        d_cf = mm_tn(low_f, b_f) + dc[rows, 0:n]
        d_bb = mm(low_b, c_b) + mm_nt(xs[:, width:], grad_b_low)
        d_cb = mm_tn(low_b, b_b) + dc[rows, n : 2 * n]
        d_state = jnp.concatenate([d_bf, d_cf, d_bb, d_cb], axis=1)
        ext[rows, width:] = d_state * slope[rows, width:].astype(F32)
        head_sums = mm(stack[...], gather[...])
        rin = row_in[rows, :]
        ahead = head_sums[CHUNK : 2 * CHUNK]
        rates_ref[rows, 0:LANES] = (
            jnp.transpose(rsum[...]) + csum[...] + jnp.where(is_fwd, rin, ahead)
        )
        rates_ref[rows, LANES : 2 * LANES] = jnp.where(is_fwd, ahead, rin)
        rates_ref[rows, 2 * LANES : 3 * LANES] = head_sums[0:CHUNK] * mask[rows]
        edge = head_sums[2 * CHUNK : 2 * CHUNK + 1] + head_sums[2 * CHUNK + 8 : 2 * CHUNK + 9]
        rates_ref[rows, 3 * LANES :] = jnp.broadcast_to(edge, (CHUNK, LANES))

    prev = pre[...].astype(F32)
    whole_ext = ext[...]
    moved = whole_ext[:block]
    acc = conv[3:4, :] * moved
    gconv_ref[4:5, :] += jnp.sum(moved, axis=0, keepdims=True)
    gconv_ref[3:4, :] += jnp.sum(moved * prev, axis=0, keepdims=True)
    for j in range(3):
        moved = pltpu.roll(whole_ext, block + 8 - (3 - j), 0)[:block]
        acc = acc + conv[j : j + 1, :] * moved
        gconv_ref[j : j + 1, :] += jnp.sum(moved * prev, axis=0, keepdims=True)
    rest_ref[...] = acc.astype(BF16)
    rd = jnp.sum(acc * prev, axis=1, keepdims=True)
    rd_ref[...] = to_row(rd, jnp.zeros_like(rd))
    ext[block:, :] = ext[0:8, :]
    ext_out[...] = ext[0:8, :]


def rates_kernel(i, scalars, rates, hs, rd_a, rd_b, head_par, dz_ref, ghead_ref, rd_ref, *, heads, block):
    @pl.when(i == 0)
    def _():
        ghead_ref[...] = jnp.zeros_like(ghead_ref)

    r = lax.broadcasted_iota(jnp.int32, (CHUNK, CHUNK), 0)
    c = lax.broadcasted_iota(jnp.int32, (CHUNK, CHUNK), 1)
    tri = jnp.where(c <= r, 1.0, 0.0).astype(BF16)
    is_fwd = lax.broadcasted_iota(jnp.int32, (CHUNK, LANES), 1) < heads
    neg = head_par[1:2, :]
    for c_idx in range(block // CHUNK):
        rows = slice(c_idx * CHUNK, (c_idx + 1) * CHUNK)
        d_cum = rates[rows, 0:LANES]
        d_run = rates[rows, LANES : 2 * LANES]
        sums = mm(tri, jnp.concatenate([*split_three(d_cum), *split_two(d_run)], axis=1))
        ahead = sums[:, 0:LANES] + sums[:, LANES : 2 * LANES] + sums[:, 2 * LANES : 3 * LANES]
        run = sums[:, 3 * LANES : 4 * LANES] + sums[:, 4 * LANES :]
        behind = ahead[CHUNK - 1 :, :] - ahead
        d_rate = jnp.where(is_fwd, behind + d_cum + run - d_run, behind + run)
        d_rate = d_rate + rates[rows, 3 * LANES :]
        z = hs[rows, 0:LANES]
        d_step = neg * d_rate + rates[rows, 2 * LANES : 3 * LANES]
        d_z = d_step / (1.0 + jnp.exp(-z))
        dt = hs[rows, LANES : 2 * LANES]
        ghead_ref[0:1, :] += jnp.sum(d_rate * (neg * dt), axis=0, keepdims=True)
        ghead_ref[1:2, :] += jnp.sum(d_z, axis=0, keepdims=True)
        dz_ref[rows, :] = d_z.astype(BF16)
        rd = jnp.sum(d_z * (z - head_par[0:1, :]), axis=1, keepdims=True)
        rd_ref[:, rows] = rd_a[:, rows] + rd_b[:, rows] + to_row(rd, jnp.zeros_like(rd))


def columns_of(scalars, other, size):
    rank = scalars[1]
    return pl.ds(pl.multiple_of((1 - rank if other else rank) * size, LANES), size)


def branch_kernel(scalars, gz, po, out_ref, *, other):
    cols = columns_of(scalars, other, out_ref.shape[1])
    out_ref[...] = mm(gz[...], po[:, cols]).astype(out_ref.dtype)


def back_project_kernel(
    scalars, dgp, rest, dz, rd, w_gate, w_inner, w_state, w_step, out_ref, *, other
):
    rows, size = dgp.shape[0], out_ref.shape[1]
    at = columns_of(scalars, other, size)
    a = w_inner.shape[1]
    out_ref[0:rows, :] = (
        mm_nt(dgp[...], w_gate[at, :])
        + mm_nt(rest[:, 0:a], w_inner[at, :])
        + mm_nt(rest[:, a:], w_state[at, :])
        + mm_nt(dz[...], w_step[at, :])
    ).astype(out_ref.dtype)
    if other:
        part = rows // 4
        lines = jnp.concatenate([rd[0:1, k * part : (k + 1) * part] for k in range(4)], axis=0)
        lines = jnp.concatenate(split_three(lines) + (jnp.zeros((4, part), BF16),), axis=0)
        out_ref[rows : rows + 16, 0:part] = lines
        out_ref[rows : rows + 16, part:] = jnp.zeros((16, size - part), BF16)


def home_of(r, me, order):
    j = me % SHARDS
    levels = len(order)
    for p, bit in enumerate(order):
        if (r >> (levels - 1 - p)) & 1:
            j = jnp.bitwise_xor(j, 1 << bit)
    return j


def lanes_in(orders, width):
    size = width // len(orders)
    return [
        (r, slice(k * size, (k + 1) * size), order) for k, order in enumerate(orders) for r in range(SHARDS)
    ]


def pack_early_kernel(
    scalars, grad_out, grad_gate, w_gate, keep_ref, send_ref, gain_ref, *, order
):
    hi, lo = split_two(grad_gate[...].astype(F32) * w_gate[...].astype(F32))
    ones = jnp.ones((8, hi.shape[1]), BF16)
    gain_ref[...] = mm_nt(ones, hi) + mm_nt(ones, lo)
    part = grad_out.shape[0] // SHARDS
    for r in range(SHARDS):
        j = home_of(r, scalars[2], order)
        out = keep_ref if r < SHARDS // 2 else send_ref
        at = (r % (SHARDS // 2)) * 2 * part
        src = pl.ds(pl.multiple_of(j * part, part), part)
        out[at : at + part, :] = grad_out[src, :]
        out[at + part : at + 2 * part, :] = grad_gate[src, :]


def unpack_early_kernel(scalars, first, second, out_ref, gate_ref, *, order):
    part = out_ref.shape[0] // SHARDS
    for r in range(SHARDS):
        j = home_of(r, scalars[2], order)
        src = first if r < SHARDS // 2 else second
        at = (r % (SHARDS // 2)) * 2 * part
        dst = pl.ds(pl.multiple_of(j * part, part), part)
        out_ref[dst, :] = src[at : at + part, :].astype(F32)
        gate_ref[dst, :] = src[at + part : at + 2 * part, :].astype(F32)


def pack_late_kernel(
    scalars, inner, state, step_low, w_inner, w_state_t, gain, gain_part, gconv, ghead, small, gather,
    keep_ref, send_ref, misc, *, orders, heads, state_width,
):
    model, width = w_inner.shape
    hi, lo = split_two(inner[...].astype(F32) * w_inner[...].astype(F32))
    ones = jnp.ones((8, hi.shape[1]), BF16)
    gain_row = (mm_nt(ones, hi) + mm_nt(ones, lo) + gain_part[...])[0:1]
    step = step_low[...].astype(F32)
    w_t = w_state_t[...].astype(F32)
    gain_row += jnp.sum(state[...].astype(F32) * w_t[:state_width], axis=0, keepdims=True)
    gain_row += jnp.sum(step * w_t[state_width:], axis=0, keepdims=True)
    gain_row = gain_row / gain[...]
    misc[...] = jnp.zeros_like(misc)

    def put_single(k, row):
        at = (k // 2) * 8 + k % 2
        misc[at : at + 1, :] = row

    for k in range(2 * heads):
        put_single(k, step[k : k + 1, :])
    at = 2 * heads
    for k in range(5):
        put_single(at + k, gconv[k : k + 1, 0:width])
    put_single(at + 5, small[0:1, :])
    hi, lo = split_two(eight(small[1:2, :]))
    skip = mm(hi, gather[0:width, :]) + mm(lo, gather[0:width, :])
    at = ((at + 6) // 2) * 8 + (at + 6) % 2
    misc[at : at + 1, 2 * LANES : 3 * LANES] = skip[0:1]
    misc[at : at + 1, 0:LANES] = ghead[0:1, :]
    misc[at : at + 1, LANES : 2 * LANES] = ghead[1:2, :]
    fit = model // state_width
    for k in range(5):
        at = (k // fit) * 8 + 4
        lanes = slice((k % fit) * state_width, (k % fit + 1) * state_width)
        misc[at : at + 1, lanes] = gconv[k : k + 1, width:]
    at = (-(-5 // fit)) * 8 + 4
    misc[at : at + 1, :] = gain_row
    part = model // SHARDS
    part_s = state_width // SHARDS
    rows = part + part_s + 8
    for r, cols, order in lanes_in(orders, model):
        j = home_of(r, scalars[2], order)
        out = keep_ref if r < SHARDS // 2 else send_ref
        at = (r % (SHARDS // 2)) * rows
        out[at : at + part, cols] = inner[pl.ds(pl.multiple_of(j * part, part), part), cols]
        out[at + part : at + part + part_s, cols] = state[
            pl.ds(pl.multiple_of(j * part_s, part_s), part_s), cols
        ]
        out[at + part + part_s : at + rows, cols] = misc[
            pl.ds(pl.multiple_of(j * 8, 8), 8), cols
        ].astype(BF16)


def unpack_late_kernel(
    scalars, first, second, inner_ref, state_ref, step_ref, convi_ref, convi_b_ref, convs_ref, convs_b_ref,
    gg_ref, bias_ref, decay_ref, skip_ref, gain_ref, state, misc, *, orders, heads,
):
    model = inner_ref.shape[0]
    state_width = state_ref.shape[1]
    part = model // SHARDS
    part_s = state_width // SHARDS
    rows = part + part_s + 8
    for r, cols, order in lanes_in(orders, model):
        j = home_of(r, scalars[2], order)
        src = first if r < SHARDS // 2 else second
        at = (r % (SHARDS // 2)) * rows
        inner_ref[pl.ds(pl.multiple_of(j * part, part), part), cols] = src[at : at + part, cols].astype(
            F32
        )
        state[pl.ds(pl.multiple_of(j * part_s, part_s), part_s), cols] = src[
            at + part : at + part + part_s, cols
        ].astype(F32)
        misc[pl.ds(pl.multiple_of(j * 8, 8), 8), cols] = src[at + part + part_s : at + rows, cols].astype(
            F32
        )
    state_ref[...] = jnp.transpose(state[...])

    def single(k):
        at = (k // 2) * 8 + k % 2
        return misc[at : at + 1, :]

    for h in range(heads):
        for d in range(2):
            step_ref[h, d : d + 1, :] = single(d * heads + h)
    at = 2 * heads
    for k in range(4):
        convi_ref[k : k + 1, :] = single(at + k)
    convi_b_ref[...] = single(at + 4).reshape(convi_b_ref.shape)
    gg_ref[...] = single(at + 5).reshape(gg_ref.shape)
    head_row = single(at + 6)
    for d in range(2):
        decay_ref[d : d + 1, :] = head_row[:, d * heads : (d + 1) * heads]
        bias_ref[d : d + 1, :] = head_row[:, LANES + d * heads : LANES + (d + 1) * heads]
    skip_ref[...] = head_row[:, 2 * LANES : 2 * LANES + heads]
    fit = model // state_width
    for k in range(5):
        at = (k // fit) * 8 + 4
        lanes = slice((k % fit) * state_width, (k % fit + 1) * state_width)
        out, row = (convs_ref, k) if k < 4 else (convs_b_ref, 0)
        out[row : row + 1, :] = misc[at : at + 1, lanes]
    at = (-(-5 // fit)) * 8 + 4
    half = model // 2
    gain_ref[...] = jnp.where(
        scalars[1] == 0, misc[at : at + 1, :half], misc[at : at + 1, half:]
    ).reshape(gain_ref.shape)


def place(i, top):
    return i if top is None else top - i


def rows_of(block, top=None):
    return lambda ref, i: ref.at[pl.ds(pl.multiple_of(place(i, top) * block, block), block)]


def lanes_of(block, top=None):
    return lambda ref, i: ref.at[:, pl.ds(pl.multiple_of(place(i, top) * block, block), block)]


def states_of(block, top=None):
    per = block // CHUNK
    return lambda ref, i: ref.at[pl.ds(place(i, top) * per, per)]


def fixed(ref, i):
    return ref


def call(kernel, blocks, ins, out_views, out_shape, scratch, name, aliases=None, us=0.0):
    views = [view for _, view in ins[1:]] + out_views
    arrays = [ins[0]] + [
        pltpu.with_memory_space_constraint(x, pltpu.VMEM) if view is not fixed else x
        for x, view in ins[1:]
    ]

    def looped(scalars, *refs):
        def step(i, _):
            blocks_of = [view(ref, i) for view, ref in zip(views, refs)]
            kernel(i, scalars, *blocks_of, *refs[len(views) :])
            return 0

        lax.fori_loop(0, blocks, step, 0)

    vmem = pl.BlockSpec(memory_space=pltpu.VMEM)
    return pl.pallas_call(
        looped,
        out_shape=[pltpu.VMEM(o.shape, o.dtype) for o in out_shape],
        in_specs=[pl.BlockSpec(memory_space=pltpu.SMEM)] + [vmem] * (len(arrays) - 1),
        out_specs=[vmem] * len(out_shape),
        scratch_shapes=scratch,
        compiler_params=pltpu.CompilerParams(vmem_limit_bytes=VMEM_LIMIT),
        cost_estimate=pl.CostEstimate(
            flops=int(us * 5e8), transcendentals=0, bytes_accessed=int(us * 3e6)
        ),
        name=name,
        input_output_aliases=aliases or {},
    )(*arrays)


def whole(kernel, args, out_shape, scratch, name, in_vmem=True, us=0.0):
    vmem = pl.BlockSpec(memory_space=pltpu.VMEM)
    return pl.pallas_call(
        kernel,
        out_shape=[pltpu.VMEM(o.shape, o.dtype) if in_vmem else o for o in out_shape],
        in_specs=[pl.BlockSpec(memory_space=pltpu.SMEM)] + [vmem] * (len(args) - 1),
        out_specs=[vmem] * len(out_shape),
        scratch_shapes=scratch,
        compiler_params=pltpu.CompilerParams(vmem_limit_bytes=VMEM_LIMIT),
        cost_estimate=pl.CostEstimate(
            flops=int(us * 5e8), transcendentals=0, bytes_accessed=int(us * 3e6)
        ),
        name=name,
    )(*args)


def swap_mp(x):
    return lax.ppermute(x, "mp", [(0, 1), (1, 0)])


def swap_dp(x, bit):
    size = lax.axis_size("dp")
    return lax.ppermute(x, "dp", [(i, i ^ (1 << bit)) for i in range(size)])


def add_low(a, b):
    return (a.astype(F32) + b.astype(F32)).astype(BF16)


def after(x, *others):
    return lax.optimization_barrier((x, *others))[0]


def body(
    tokens,
    norm_gain,
    proj_gate,
    proj_inner,
    proj_state,
    proj_step,
    conv_inner,
    conv_inner_bias,
    conv_state,
    conv_state_bias,
    step_bias,
    decay_log,
    skip_gain,
    gate_gain,
    proj_out,
    lengths,
    cotangent,
):
    rows, width_own = tokens.shape
    model = 2 * width_own
    heads = skip_gain.shape[0]
    width = proj_inner.shape[1]
    head_dim = width // heads
    state_width = proj_state.shape[1]
    n = state_width // 4
    conv_width = width + state_width
    inner_width = width * lax.axis_size("mp")
    chunks = rows // CHUNK
    rank = lax.axis_index("mp")
    shape = jax.ShapeDtypeStruct

    oth_tokens = swap_mp(tokens)
    oth_gain = swap_mp(norm_gain.reshape(1, width_own))
    oth_cot = swap_mp(after(cotangent, oth_tokens))

    scalars = jnp.stack([lengths[0], rank, lax.axis_index("dp")]).astype(jnp.int32)
    step_weight = proj_step.reshape(model, 2 * heads)
    step_weight = jnp.pad(step_weight, ((0, 0), (0, LANES - 2 * heads)))
    own_gain = norm_gain.reshape(1, width_own)
    gain = natural(rank, own_gain, oth_gain).astype(F32)
    conv = jnp.concatenate(
        [
            jnp.concatenate([conv_inner, conv_state], axis=1),
            jnp.concatenate([conv_inner_bias, conv_state_bias])[None],
            jnp.zeros((3, conv_width), F32),
        ]
    )
    head_par = jnp.stack(
        [
            step_bias.reshape(-1),
            -jnp.exp(decay_log.reshape(-1)),
            jnp.pad(skip_gain, (0, heads)),
        ]
    )
    head_par = jnp.pad(head_par, ((0, 5), (0, LANES - 2 * heads)))
    staged = (tokens, cotangent, proj_gate, proj_inner, proj_state, proj_out)
    hbm = pl.BlockSpec(memory_space=pl.ANY)
    vmem = pl.BlockSpec(memory_space=pltpu.VMEM)
    tokens_v, cot_v, gate_v, inner_v, state_v, out_v, spread, gather, w_state_t = pl.pallas_call(
        partial(stage_kernel, count=len(staged), head_dim=head_dim),
        out_shape=[pltpu.VMEM(x.shape, x.dtype) for x in staged]
        + [
            pltpu.VMEM((2 * LANES, 2 * width), BF16),
            pltpu.VMEM((2 * width, LANES), BF16),
            pltpu.VMEM((state_width + LANES, model), BF16),
        ],
        in_specs=[vmem, vmem] + [hbm] * len(staged),
        out_specs=[vmem] * (len(staged) + 3),
        scratch_shapes=[pltpu.SemaphoreType.DMA((len(staged),))],
        compiler_params=pltpu.CompilerParams(vmem_limit_bytes=VMEM_LIMIT),
        name="stage",
    )(proj_state, step_weight, *staged)
    gg = gate_gain[None]

    sizes = dict(heads=heads, width=width, state_width=state_width)
    low = lambda *dims: shape(dims, BF16)
    full = lambda *dims: shape(dims, F32)
    block = PROJECT_BLOCK
    up, states = rows_of(block), states_of(block)
    normed, gate_pre, pre, slope, hs, act, sact, xd, hf, sb = call(
        partial(project_kernel, block=block, **sizes),
        rows // block,
        [
            scalars,
            (tokens_v, up),
            (oth_tokens, up),
            (gain, fixed),
            (gate_v, fixed),
            (inner_v, fixed),
            (state_v, fixed),
            (step_weight, fixed),
            (conv, fixed),
            (head_par, fixed),
            (spread, fixed),
        ],
        [up, up, up, up, up, up, up, up, states, states],
        [
            low(rows, model),
            full(rows, width),
            low(rows, conv_width),
            low(rows, conv_width),
            full(rows, 4 * LANES),
            full(rows, width),
            low(rows, state_width),
            low(rows, 2 * width),
            low(chunks, n, width),
            full(chunks, n, width),
        ],
        [pltpu.VMEM((block + 8, conv_width), F32), pltpu.VMEM((n, width), F32)],
        "project",
        us=12,
    )

    block = MIX_BLOCK
    top = rows // block - 1
    down, states_down = rows_of(block, top), states_of(block, top)
    y, hb = call(
        partial(mix_kernel, block=block, **sizes),
        rows // block,
        [
            scalars,
            (act, down),
            (sact, down),
            (hs, down),
            (xd, down),
            (hf, states_down),
            (sb, states_down),
            (head_par, fixed),
            (spread, fixed),
        ],
        [down, states_down],
        [full(rows, width), low(chunks, n, width)],
        [pltpu.VMEM((n, width), F32)],
        "mix",
        us=7,
    )

    block = GATE_BLOCK
    up, states, up_lanes = rows_of(block), states_of(block), lanes_of(block)
    dgn, gz, sums = call(
        partial(gate_kernel, block=block),
        rows // block,
        [
            scalars,
            (y, up),
            (gate_pre, up),
            (cot_v, up),
            (oth_cot, up),
            (out_v, fixed),
            (gg, fixed),
        ],
        [up, up, up_lanes],
        [full(rows, width), low(rows, width), full(8, rows)],
        [],
        "gate",
        us=3,
    )

    oth_sums = swap_mp(sums)
    branch_oth = whole(
        partial(branch_kernel, other=True), (scalars, gz, out_v), [low(rows, width_own)], [], "branch_oth", us=3
    )[0]
    sums = sums + oth_sums
    branch_got = swap_mp(after(branch_oth, sums))
    sums_in = after(sums, branch_oth)

    block = GATE_BACK_BLOCK
    up, states, up_lanes = rows_of(block), states_of(block), lanes_of(block)
    g, dgp, dbr, dc, gb, gf, rd_gate, row_sums, small = call(
        partial(gate_back_kernel, block=block, inner_width=inner_width, **sizes),
        rows // block,
        [
            scalars,
            (sums_in, up_lanes),
            (gate_pre, up),
            (y, up),
            (act, up),
            (dgn, up),
            (cot_v, up),
            (oth_cot, up),
            (hs, up),
            (sact, up),
            (hf, states),
            (hb, states),
            (gg, fixed),
            (spread, fixed),
            (gather, fixed),
        ],
        [up, up, up, up, states, states, up_lanes, up, fixed],
        [
            low(rows, width),
            low(rows, width),
            low(rows, model),
            full(rows, 2 * n),
            low(chunks, n, width),
            full(chunks, n, width),
            full(8, rows),
            full(rows, LANES),
            full(8, width),
        ],
        [pltpu.VMEM((n, width), F32), pltpu.VMEM((block, 2 * width), BF16)],
        "gate_back",
        us=8,
    )

    def back_part(first, count, g, state):
        block = BACK_BLOCK
        here, states_here, here_lanes = rows_of(block, first), states_of(block, first), lanes_of(block, first)
        ins = [
            scalars,
            (g, here),
            (act, here),
            (sact, here),
            (hs, here),
            (xd, here),
            (row_sums, here),
            (hf, states_here),
            (hb, states_here),
            (gb, states_here),
            (gf, states_here),
            (dc, here),
            (pre, here),
            (slope, here),
            (conv, fixed),
            (head_par, fixed),
            (spread, fixed),
            (gather, fixed),
            *[(x, fixed) for x in state[:3]],
            (state[3], here),
            (state[4], here),
            (state[5], here_lanes),
        ]
        return call(
            partial(back_kernel, block=block, top=first, **sizes),
            count,
            ins,
            [here, here, here_lanes, fixed, fixed, fixed],
            [
                low(rows, conv_width),
                full(rows, 4 * LANES),
                full(8, rows),
                full(8, conv_width),
                full(8, conv_width),
                full(n, width),
            ],
            [
                pltpu.VMEM((block + 8, conv_width), F32),
                pltpu.VMEM((2 * CHUNK + 16, 2 * width), BF16),
                pltpu.VMEM((CHUNK, 2 * width), BF16),
                pltpu.VMEM((LANES, CHUNK), F32),
                pltpu.VMEM((CHUNK, LANES), F32),
            ],
            "mix_back",
            us=3 * count,
            aliases={len(ins) - 3: 0, len(ins) - 2: 1, len(ins) - 1: 2},
        )

    order_a, orders_b = (0, 1, 2, 3), ((0, 1, 2, 3), (0, 2, 1, 3))
    grad_out = mm_tn(gz, dbr).astype(BF16)
    grad_gate = mm_tn(normed, dgp).astype(BF16)
    keep, send, gain_part = whole(
        partial(pack_early_kernel, order=order_a),
        (scalars, grad_out, grad_gate, proj_gate),
        [low(width, model), low(width, model), full(8, model)],
        [],
        "pack_early",
    )

    def rest_of_dp(x):
        extra = SHARDS
        while extra < lax.axis_size("dp"):
            x = add_low(x, swap_dp(x, extra.bit_length() - 1))
            extra *= 2
        return x

    zeros = (
        jnp.zeros((8, conv_width), F32),
        jnp.zeros((n, width), F32),
        jnp.zeros((8, conv_width), F32),
    )
    branch_own = whole(
        partial(branch_kernel, other=False), (scalars, after(gz, send), out_v), [full(rows, width_own)], [],
        "branch_own"
    )[0]
    got, branch_own = lax.optimization_barrier((swap_dp(send, order_a[0]), branch_own))
    h = keep.shape[0] // 2
    keep, send = add_low(keep[:h], got[:h]), add_low(keep[h:], got[h:])
    state = (
        *zeros,
        jnp.zeros((rows, conv_width), BF16),
        jnp.zeros((rows, 4 * LANES), F32),
        jnp.zeros((8, rows), F32),
    )
    g = after(g, send)
    sent, x = swap_dp(send, order_a[1]), None
    left = rows // BACK_BLOCK
    for k, share in enumerate((2, 4, 4)):
        count = rows // BACK_BLOCK // share
        outs = back_part(left - 1, count, g, state)
        left -= count
        rest, rates, rd_rest, gconv, ext_carry, carry = outs
        h = keep.shape[0] // 2
        if k < 2:
            sent, carry = lax.optimization_barrier((sent, carry))
            if k == 1:
                carry, branch_got = lax.optimization_barrier((carry, branch_got))
            keep, send = add_low(keep[:h], sent[:h]), add_low(keep[h:], sent[h:])
            carry = after(carry, send)
            sent = swap_dp(send, order_a[k + 2])
        else:
            sent, rest = lax.optimization_barrier((sent, rest))
            x = rest_of_dp(add_low(keep, sent))
        state = (ext_carry, carry, gconv, rest, rates, rd_rest)

    block = RATES_BLOCK
    rates, x, rest = lax.optimization_barrier((rates, x, rest))
    sent = swap_dp(x, order_a[3])
    dz, ghead, rd_part = call(
        partial(rates_kernel, heads=heads, block=block),
        rows // block,
        [
            scalars,
            (rates, rows_of(block)),
            (hs, rows_of(block)),
            (rd_gate, lanes_of(block)),
            (rd_rest, lanes_of(block)),
            (head_par, fixed),
        ],
        [rows_of(block), fixed, lanes_of(block)],
        [low(rows, LANES), full(8, LANES), full(8, rows)],
        [],
        "rates",
    )
    grad_inner = mm_tn(normed, rest[:, :width]).astype(BF16)
    grad_state = mm_tn(rest[:, width:], normed).astype(BF16)
    grad_step = mm_tn(dz, normed).astype(BF16)
    keep, send = whole(
        partial(pack_late_kernel, orders=orders_b, heads=heads, state_width=state_width),
        (
            scalars, grad_inner, grad_state, grad_step, inner_v, w_state_t, gain, gain_part, gconv, ghead,
            small, gather,
        ),
        [low(LATE_ROWS * SHARDS // 2, model), low(LATE_ROWS * SHARDS // 2, model)],
        [pltpu.VMEM((8 * SHARDS, model), F32)],
        "pack_late",
    )

    back_args = (scalars, dgp, rest, dz, rd_part, gate_v, inner_v, state_v, step_weight)
    dn_oth = whole(
        partial(back_project_kernel, other=True), back_args, [low(rows + 16, width_own)], [], "back_oth"
    )[0]
    x = jnp.concatenate([x, sent])
    send, x, dn_oth = lax.optimization_barrier((send, x, dn_oth))
    got = swap_dp(send, 0)
    sent = swap_dp(x, order_a[2])
    h, c = keep.shape[0] // 2, model // 2
    keeps = [add_low(keep[:h, :c], got[:h, :c]), add_low(keep[:h, c:], got[:h, c:])]
    sends = [add_low(keep[h:, :c], got[h:, :c]), add_low(keep[h:, c:], got[h:, c:])]
    sends[0], sends[1], rest = lax.optimization_barrier((sends[0], sends[1], rest))
    dn_got = swap_mp(dn_oth)

    dn_own = whole(
        partial(back_project_kernel, other=False), (*back_args[:2], rest, *back_args[3:]),
        [full(rows, width_own)], [], "back_own"
    )[0]
    for level in (1, 2):
        gots = [swap_dp(v, order[level]) for v, order in zip(sends, orders_b)]
        if level == 1:
            gots[0], gots[1], dn_own, sent = lax.optimization_barrier((gots[0], gots[1], dn_own, sent))
            x = jnp.concatenate([x, sent])
        h = keeps[0].shape[0] // 2
        pairs = list(zip(keeps, gots))
        if level == 1:
            keeps = [add_low(k[:h], v[:h]) for k, v in pairs]
            sends = [add_low(k[h:], v[h:]) for k, v in pairs]
        else:
            keep = jnp.concatenate([add_low(k[:h], v[:h]) for k, v in pairs], axis=1)
            send = jnp.concatenate([add_low(k[h:], v[h:]) for k, v in pairs], axis=1)
    send, x, tokens_late, oth_late = lax.optimization_barrier((send, x, tokens, oth_tokens))
    sent = swap_dp(x, order_a[1])

    seq_mask = (jnp.arange(rows) < lengths[0]).astype(F32)[:, None]
    gate_inv = lax.rsqrt(sums[0] / inner_width + EPSILON)[:, None]
    tokens_f = tokens_late.astype(F32)
    block_out = (tokens_f + seq_mask * gate_inv * (branch_own + branch_got.astype(F32))).astype(BF16)

    got, block_out, dn_got = lax.optimization_barrier((swap_dp(send, 3), block_out, dn_got))
    z = rest_of_dp(add_low(keep, got))
    part = model // SHARDS
    tail = z[part:]
    tail_row = lax.broadcasted_iota(jnp.int32, (LATE_ROWS - part, 1), 0)
    alone = (tail_row >= LATE_ROWS - part - 8) & (tail_row < LATE_ROWS - part - 4)
    tail_f = tail.astype(F32)
    tail = jnp.where(alone, tail_f, tail_f + swap_mp(tail).astype(F32)).astype(BF16)
    z = jnp.concatenate([z[:part], tail])
    oth_f = oth_late.astype(F32)
    square = jnp.sum(tokens_f * tokens_f, axis=1, keepdims=True) + jnp.sum(
        oth_f * oth_f, axis=1, keepdims=True
    )
    inv = lax.rsqrt(square / model + EPSILON)
    part = rows // 4
    lines = dn_got[rows:, :part].astype(F32)
    oth_rd = (lines[0:4] + lines[4:8] + lines[8:12]).reshape(rows)
    rd_both = rd_part[0] + oth_rd
    grad_full = dn_own + dn_got[:rows].astype(F32)
    grad_tokens = (
        cotangent.astype(F32)
        + inv * (grad_full * norm_gain.astype(F32)[None])
        - tokens_f * (inv * inv * (rd_both[:, None] / model))
    )

    got, grad_tokens, sent = lax.optimization_barrier((swap_dp(z, 3), grad_tokens, sent))
    x = jnp.concatenate([x, sent])
    sent = swap_dp(x, order_a[0])
    z = jnp.concatenate([z, got])
    zs = [z[:, :c], z[:, c:]]
    gots = [swap_dp(v, order[2]) for v, order in zip(zs, orders_b)]
    zs = [jnp.concatenate([v, g]) for v, g in zip(zs, gots)]
    grad_proj_out, grad_proj_gate = whole(
        partial(unpack_early_kernel, order=order_a),
        (scalars, x, after(sent, *zs)),
        [full(width, model), full(model, width)],
        [],
        "unpack_early",
        in_vmem=False,
    )
    gots = [swap_dp(v, order[1]) for v, order in zip(zs, orders_b)]
    gots[0], gots[1], grad_proj_out = lax.optimization_barrier((gots[0], gots[1], grad_proj_out))
    z = jnp.concatenate([jnp.concatenate([v, g]) for v, g in zip(zs, gots)], axis=1)
    (
        grad_proj_inner,
        grad_proj_state,
        step,
        grad_conv_inner,
        grad_conv_inner_bias,
        grad_conv_state,
        grad_conv_state_bias,
        grad_gate_gain,
        grad_step_bias,
        grad_decay_log,
        grad_skip,
        grad_norm_gain,
    ) = whole(
        partial(unpack_late_kernel, orders=orders_b, heads=heads),
        (scalars, z, swap_dp(z, 0)),
        [
            full(model, width),
            full(model, state_width),
            full(heads, 2, model),
            full(4, width),
            full(width),
            full(4, state_width),
            full(1, state_width),
            full(width),
            full(2, heads),
            full(2, heads),
            full(1, heads),
            full(width_own),
        ],
        [pltpu.VMEM((state_width, model), F32), pltpu.VMEM((8 * SHARDS, model), F32)],
        "unpack_late",
        in_vmem=False,
    )
    return (
        block_out,
        grad_tokens,
        grad_norm_gain,
        grad_proj_gate,
        grad_proj_inner,
        grad_proj_state,
        step.transpose(2, 1, 0),
        grad_conv_inner,
        grad_conv_inner_bias,
        grad_conv_state,
        grad_conv_state_bias[0],
        grad_step_bias,
        grad_decay_log,
        grad_skip[0],
        grad_gate_gain,
        grad_proj_out,
    )


def solution(mesh):
    in_specs = (
        P("dp", "mp"),
        P("mp"),
        P(None, "mp"),
        P(None, "mp"),
        P(),
        P(None, None, "mp"),
        P(None, "mp"),
        P("mp"),
        P(),
        P(),
        P(None, "mp"),
        P(None, "mp"),
        P("mp"),
        P("mp"),
        P("mp", None),
        P("dp"),
        P("dp", "mp"),
    )
    out_specs = (
        P("dp", "mp"),
        P("dp", "mp"),
        P("mp"),
        P(None, "mp"),
        P(None, "mp"),
        P(),
        P(None, None, "mp"),
        P(None, "mp"),
        P("mp"),
        P(),
        P(),
        P(None, "mp"),
        P(None, "mp"),
        P("mp"),
        P("mp"),
        P("mp", None),
    )
    return jax.shard_map(body, mesh=mesh, in_specs=in_specs, out_specs=out_specs, check_vma=False)
```
